32 devices in a mesh: ctx: 8 (over z, x), head: 4 (over y, core).
Axes of the slice: x: 2, y: 2, z: 4, core: 2. Of those that a mesh axis runs over, the one named last changes fastest.
Arguments:
- queries: bfloat16 [4096, 4096], P('ctx', 'head'), may hold values from -5 to 5
- keys: bfloat16 [4096, 512], P('ctx', 'head'), may hold values from -5 to 5
- values: bfloat16 [4096, 512], P('ctx', 'head'), may hold values from -8 to 8
- feature_map: bfloat16 [4, 128, 16], P('head'), may hold values from -0.5 to 0.5
- out_proj: bfloat16 [4096, 8192], P('ctx', 'head'), may hold values from -0.09375 to 0.09375
- teacher: bfloat16 [4096, 8192], P('ctx', 'head'), may hold values from -16 to 16
Outputs:
- student_out: bfloat16 [4096, 8192], P('ctx', 'head')
- loss: float32 [], replicated
- feature_grad: float32 [4, 128, 16], P('head')
The draws below stay inside these ranges and needn't reach their ends.
All inputs are finite; a program needn't handle non-finite values.
Results may differ from the reference program's by a relative error of at most 0.006.
Values may be sent and summed in bfloat16 or wider, within the bound.
A program may use at most 128 MiB of HBM per device.

```python
import math
import jax
import jax.numpy as jnp
from jax import lax

D = 8192
HEAD_DIM = 128
GROUP = 8
KV_HEADS = 4
Q_HEADS = 32
COL_DEV = 2048
FEAT = 16
WIN = 64
TOK_DEV = 512
LENGTH = 4096


def draw_queries(key, part):
    drawn = jax.random.normal(jax.random.fold_in(key, 11), (LENGTH, KV_HEADS, GROUP, HEAD_DIM), jnp.float32)
    return jnp.clip(drawn, -5.0, 5.0).reshape(LENGTH, Q_HEADS * HEAD_DIM).astype(jnp.bfloat16)


def draw_keys(key, part):
    drawn = jax.random.normal(jax.random.fold_in(key, 21), (LENGTH, KV_HEADS, HEAD_DIM), jnp.float32)
    return jnp.clip(drawn, -5.0, 5.0).reshape(LENGTH, KV_HEADS * HEAD_DIM).astype(jnp.bfloat16)


def draw_values(key, part):
    region = max(TOK_DEV // 2, 1)
    region_count = LENGTH // region
    offsets = jax.random.normal(jax.random.fold_in(key, 41), (region_count, 1, KV_HEADS * HEAD_DIM), jnp.float32) * 1.5
    jitter = jax.random.normal(jax.random.fold_in(key, 42), (region_count, region, KV_HEADS * HEAD_DIM), jnp.float32)
    return jnp.clip(offsets + jitter, -8.0, 8.0).reshape(LENGTH, KV_HEADS * HEAD_DIM).astype(jnp.bfloat16)


def draw_teacher(key, part):
    position = jnp.arange(LENGTH, dtype=jnp.float32)
    rising = 1.0 + 2.0 * position / LENGTH
    drawn = jnp.clip(jax.random.normal(jax.random.fold_in(key, 51), (LENGTH, D), jnp.float32), -4.0, 4.0)
    return jnp.clip(drawn * rising[:, None], -16.0, 16.0).astype(jnp.bfloat16)


def steps_of(rng, dims, split, smallest, top_value):
    gain = 1.0
    for axis_at, parts in split:
        heights = jax.random.uniform(jax.random.fold_in(jax.random.fold_in(rng, 6), axis_at), (parts,), jnp.float32, smallest / len(split), top_value / len(split))
        gain = gain * jnp.repeat(jnp.exp(heights), dims[axis_at] // parts).reshape((-1,) + (1,) * (len(dims) - 1 - axis_at))
    return gain


def normal_values(rng, shape, scale, reach, split=(), kind=jnp.bfloat16):
    values = scale * jax.random.normal(rng, shape, jnp.float32)
    if split:
        values = values * steps_of(rng, shape, split, -0.22, 0.18)
    return jnp.clip(values, -reach, reach).astype(kind)


def setup_inputs(seed: int = 0) -> dict:
    splits = jax.random.split(jax.random.key(seed), 7)
    return {
        "queries": draw_queries(jax.random.fold_in(splits[6], 71), 0),
        "keys": draw_keys(jax.random.fold_in(splits[6], 71), 0),
        "values": draw_values(jax.random.fold_in(splits[6], 71), 0),
        "feature_map": normal_values(splits[3], (KV_HEADS, HEAD_DIM, FEAT), HEAD_DIM ** -0.5, 0.5, ((0, 4),)),
        "out_proj": normal_values(splits[4], (Q_HEADS * HEAD_DIM, D), (Q_HEADS * HEAD_DIM) ** -0.5, 0.09375, ((0, 8), (1, 4))),
        "teacher": draw_teacher(jax.random.fold_in(splits[6], 71), 0),
    }


exact_mode = lax.Precision.HIGHEST

def taylor_square(features):
    feature_count = features.shape[-1]
    outer = features[..., :, None] * features[..., None, :]
    return outer.reshape(features.shape[:-1] + (feature_count * feature_count,))

def taylor_linear(query_float, key_float, value_float, feature_weights):
    query_features = jnp.einsum('lgqe,gef->lgqf', query_float, feature_weights, precision=exact_mode)
    key_features = jnp.einsum('lge,gef->lgf', key_float, feature_weights, precision=exact_mode)
    blocks = LENGTH // TOK_DEV
    query_blocks = query_features.reshape(blocks, TOK_DEV, KV_HEADS, GROUP, FEAT)
    key_blocks = key_features.reshape(blocks, TOK_DEV, KV_HEADS, FEAT)
    value_blocks = value_float.reshape(blocks, TOK_DEV, KV_HEADS, HEAD_DIM)
    causal = lax.broadcasted_iota(jnp.int32, (TOK_DEV, TOK_DEV), 0) >= lax.broadcasted_iota(jnp.int32, (TOK_DEV, TOK_DEV), 1)
    initial = (jnp.zeros((KV_HEADS, FEAT * FEAT, HEAD_DIM), jnp.float32), jnp.zeros((KV_HEADS, FEAT, HEAD_DIM), jnp.float32), jnp.zeros((KV_HEADS, HEAD_DIM), jnp.float32), jnp.zeros((KV_HEADS, FEAT * FEAT), jnp.float32), jnp.zeros((KV_HEADS, FEAT), jnp.float32), jnp.zeros((KV_HEADS,), jnp.float32))

    def one_step(carried, block):
        past_square_v, past_linear_v, past_values, past_square_k, past_linear_k, past_count = carried
        query_block, key_block, value_block = block
        qk_inner = jnp.einsum('tgqf,sgf->gqts', query_block, key_block, precision=exact_mode) / 4.0
        kernel = jnp.where(causal, 1.0 + qk_inner + 0.5 * qk_inner * qk_inner, 0.0)
        numerator = jnp.einsum('gqts,sge->tgqe', kernel, value_block, precision=exact_mode)
        denominator = jnp.transpose(lax.optimization_barrier(jnp.sum(kernel, axis=-1)), (2, 0, 1))
        query_square = taylor_square(query_block)
        numerator = numerator + jnp.einsum('tgqk,gke->tgqe', query_square, past_square_v, precision=exact_mode) / 32.0 + jnp.einsum('tgqf,gfe->tgqe', query_block, past_linear_v, precision=exact_mode) / 4.0 + past_values[None, :, None, :]
        denominator = denominator + jnp.einsum('tgqk,gk->tgq', query_square, past_square_k, precision=exact_mode) / 32.0 + jnp.einsum('tgqf,gf->tgq', query_block, past_linear_k, precision=exact_mode) / 4.0 + past_count[None, :, None]
        key_square = taylor_square(key_block)
        updated = (past_square_v + jnp.einsum('sgk,sge->gke', key_square, value_block, precision=exact_mode), past_linear_v + jnp.einsum('sgf,sge->gfe', key_block, value_block, precision=exact_mode), past_values + lax.optimization_barrier(jnp.sum(value_block, axis=0)), past_square_k + lax.optimization_barrier(jnp.sum(key_square, axis=0)), past_linear_k + lax.optimization_barrier(jnp.sum(key_block, axis=0)), past_count + float(TOK_DEV))
        return (updated, numerator / denominator[..., None])
    finals, outputs = lax.scan(jax.checkpoint(one_step), initial, (query_blocks, key_blocks, value_blocks))
    return outputs.reshape(LENGTH, KV_HEADS, GROUP, HEAD_DIM)

def window_attention(query_heads, key_heads, value_heads):
    blocks = LENGTH // TOK_DEV
    pad_rows = jnp.zeros((WIN, KV_HEADS, HEAD_DIM), jnp.bfloat16)
    key_padded = jnp.concatenate([pad_rows, key_heads], 0)
    value_padded = jnp.concatenate([pad_rows, value_heads], 0)
    query_pos = lax.broadcasted_iota(jnp.int32, (TOK_DEV, TOK_DEV + WIN), 0)
    key_pos = lax.broadcasted_iota(jnp.int32, (TOK_DEV, TOK_DEV + WIN), 1)
    distance = query_pos + WIN - key_pos

    def one_block(block_id):
        first_row = (block_id * TOK_DEV).astype(jnp.int32)
        query_block = lax.dynamic_slice_in_dim(query_heads, first_row, TOK_DEV, 0)
        key_block = lax.dynamic_slice_in_dim(key_padded, first_row, TOK_DEV + WIN, 0)
        value_block = lax.dynamic_slice_in_dim(value_padded, first_row, TOK_DEV + WIN, 0)
        scores = jnp.einsum('tgqe,sge->gqts', query_block.astype(jnp.float32), key_block.astype(jnp.float32), precision=exact_mode) / math.sqrt(HEAD_DIM)
        allowed = (distance >= 0) & (distance < WIN) & (first_row + key_pos - WIN >= 0)
        scores = jnp.where(allowed, scores, -jnp.inf)
        row_max = lax.optimization_barrier(jnp.max(scores, axis=-1, keepdims=True))
        weights = jnp.where(allowed, jnp.exp(scores - row_max), 0.0)
        attn_weights = (weights / lax.optimization_barrier(jnp.sum(weights, axis=-1, keepdims=True))).astype(jnp.bfloat16)
        return jnp.einsum('gqts,sge->tgqe', attn_weights.astype(jnp.float32), value_block.astype(jnp.float32), precision=exact_mode)
    outputs = lax.map(one_block, jnp.arange(blocks, dtype=jnp.int32))
    return outputs.reshape(LENGTH, KV_HEADS, GROUP, HEAD_DIM)

def head_gradient(d_student, out_proj):
    column_blocks = D // COL_DEV

    def add_block(block_id, running):
        first_col = (block_id * COL_DEV).astype(jnp.int32)
        grad_cols = lax.dynamic_slice_in_dim(d_student, first_col, COL_DEV, 1)
        weight_cols = lax.dynamic_slice_in_dim(out_proj, first_col, COL_DEV, 1)
        partial_sum = lax.dot_general(grad_cols, weight_cols, (((1,), (1,)), ((), ())), preferred_element_type=jnp.float32)
        rounded = lax.optimization_barrier(partial_sum.astype(jnp.bfloat16))
        return running + rounded.astype(jnp.float32)
    start = jnp.zeros((LENGTH, Q_HEADS * HEAD_DIM), jnp.float32)
    return lax.fori_loop(jnp.int32(0), jnp.int32(column_blocks), add_block, start)

def reference(queries, keys, values, feature_map, out_proj, teacher):
    query_heads = queries.reshape(LENGTH, KV_HEADS, GROUP, HEAD_DIM)
    key_heads = keys.reshape(LENGTH, KV_HEADS, HEAD_DIM)
    value_heads = values.reshape(LENGTH, KV_HEADS, HEAD_DIM)
    window_out = window_attention(query_heads, key_heads, value_heads)
    query_float = query_heads.astype(jnp.float32)
    key_float = key_heads.astype(jnp.float32)
    value_float = value_heads.astype(jnp.float32)

    def linear_part(feature_weights):
        return taylor_linear(query_float, key_float, value_float, feature_weights)
    linear_out, pullback = jax.vjp(linear_part, feature_map.astype(jnp.float32))
    head_out = (linear_out + window_out).astype(jnp.bfloat16).reshape(LENGTH, Q_HEADS * HEAD_DIM)
    student_out = jnp.dot(head_out, out_proj, preferred_element_type=jnp.float32).astype(jnp.bfloat16)
    residual = student_out.astype(jnp.float32) - teacher.astype(jnp.float32)
    loss = jnp.sum(residual * residual) / (LENGTH * D)
    d_student = (2.0 * residual / LENGTH).astype(jnp.bfloat16)
    d_head = head_gradient(d_student, out_proj)
    grads = pullback(d_head.reshape(LENGTH, KV_HEADS, GROUP, HEAD_DIM))
    return (student_out, loss, grads[0])
```

```python
import functools
import math

import jax
import jax.numpy as jnp
import numpy as np
from jax import lax
from jax.experimental import pallas as pl
from jax.experimental.pallas import tpu as pltpu
from jax.sharding import PartitionSpec as P

D = 8192
HEAD_DIM = 128
GROUP = 8
WIN = 64


exact_mode = lax.Precision.HIGHEST


def shifted(block, axis, distance):
    devices = range(lax.axis_size(axis))
    route = [(i - distance, i) for i in devices if i - distance in devices]
    return lax.ppermute(block, axis, route)


def taylor_square(features):
    feature_count = features.shape[-1]
    outer = features[..., :, None] * features[..., None, :]
    return outer.reshape(features.shape[:-1] + (feature_count * feature_count,))


def two_terms(x):
    high = lax.reduce_precision(x, 8, 7)
    return jnp.concatenate([high.astype(jnp.bfloat16), (x - high).astype(jnp.bfloat16)], -1)


def joined(pair):
    half = pair.shape[-1] // 2
    return pair[..., :half] + pair[..., half:]


def square_grad(grad_square, features):
    feature_count = features.shape[-1]
    matrix = grad_square.reshape(features.shape + (feature_count,))
    return jnp.einsum("...fh,...h->...f", matrix, features, precision=exact_mode) + jnp.einsum(
        "...hf,...h->...f", matrix, features, precision=exact_mode
    )


def exchange_kernel(count, head_count, mode, x_ref, row_ref, out_ref, row_out, buf, row_buf, send, recv, row_send, row_recv):
    me = lax.axis_index("ctx")
    head = lax.axis_index("head")
    mesh_ids = pl.DeviceIdType.MESH
    barrier = pltpu.get_barrier_semaphore()
    for d in range(1, count):
        pl.semaphore_signal(
            barrier, inc=1, device_id=(lax.rem(me + d, count), head), device_id_type=mesh_ids
        )
    for d in range(1, head_count):
        pl.semaphore_signal(
            barrier, inc=1, device_id=(me, lax.rem(head + d, head_count)), device_id_type=mesh_ids
        )
    pl.semaphore_wait(barrier, count + head_count - 2)

    def wanted(source, target):
        return {"lower": source < target, "upper": source > target, "all": source != target}[mode]

    def ctx_copy(d):
        return pltpu.make_async_remote_copy(
            src_ref=x_ref,
            dst_ref=buf.at[me],
            send_sem=send.at[d],
            recv_sem=recv.at[me],
            device_id=(lax.rem(me + d, count), head),
            device_id_type=mesh_ids,
        )

    def row_copy(d):
        return pltpu.make_async_remote_copy(
            src_ref=row_ref,
            dst_ref=row_buf.at[head],
            send_sem=row_send.at[d],
            recv_sem=row_recv.at[head],
            device_id=(me, lax.rem(head + d, head_count)),
            device_id_type=mesh_ids,
        )

    def ctx_arrival(source):
        return pltpu.make_async_remote_copy(
            src_ref=x_ref,
            dst_ref=buf.at[source],
            send_sem=send.at[0],
            recv_sem=recv.at[source],
            device_id=(source, head),
            device_id_type=mesh_ids,
        )

    def row_arrival(source):
        return pltpu.make_async_remote_copy(
            src_ref=row_ref,
            dst_ref=row_buf.at[source],
            send_sem=row_send.at[0],
            recv_sem=row_recv.at[source],
            device_id=(me, source),
            device_id_type=mesh_ids,
        )

    for d in range(1, count):

        @pl.when(wanted(me, lax.rem(me + d, count)))
        def _():
            ctx_copy(d).start()

    for d in range(1, head_count):
        row_copy(d).start()

    row_out[...] = jnp.zeros_like(row_out)
    for source in range(head_count):

        @pl.when(source == head)
        def _():
            row_out[...] += row_ref[...]

        @pl.when(source != head)
        def _():
            row_arrival(source).wait_recv()
            row_out[...] += row_buf[source]

    out_ref[...] = jnp.zeros_like(out_ref)
    for source in range(count):
        if mode == "all":

            @pl.when(source == me)
            def _():
                out_ref[...] += x_ref[...].astype(jnp.float32)

        @pl.when(wanted(source, me))
        def _():
            ctx_arrival(source).wait_recv()
            out_ref[...] += buf[source].astype(jnp.float32)

    for d in range(1, count):

        @pl.when(wanted(me, lax.rem(me + d, count)))
        def _():
            ctx_copy(d).wait_send()

    for d in range(1, head_count):
        row_copy(d).wait_send()


def exchange(x, row, mode, collective_id):
    count = lax.axis_size("ctx")
    head_count = lax.axis_size("head")
    vmem = pl.BlockSpec(memory_space=pltpu.VMEM)
    return pl.pallas_call(
        functools.partial(exchange_kernel, count, head_count, mode),
        out_shape=(
            jax.ShapeDtypeStruct(x.shape, jnp.float32),
            jax.ShapeDtypeStruct(row.shape, jnp.float32),
        ),
        in_specs=[vmem, vmem],
        out_specs=(vmem, vmem),
        scratch_shapes=[
            pltpu.VMEM((count,) + x.shape, x.dtype),
            pltpu.VMEM((head_count,) + row.shape, jnp.float32),
            pltpu.SemaphoreType.DMA((count,)),
            pltpu.SemaphoreType.DMA((count,)),
            pltpu.SemaphoreType.DMA((head_count,)),
            pltpu.SemaphoreType.DMA((head_count,)),
        ],
        compiler_params=pltpu.CompilerParams(collective_id=collective_id, has_side_effects=True),
        cost_estimate=pl.CostEstimate(
            flops=count * x.size, bytes_accessed=40 * count * x.size, transcendentals=0
        ),
    )(x, row)


def pack(square, linear, square_den, linear_den, flat):
    groups, feature_count = linear_den.shape
    squares = feature_count * feature_count
    square_rows = square_den.reshape(groups, squares // HEAD_DIM, HEAD_DIM)
    linear_rows = jnp.pad(linear_den, ((0, 0), (0, HEAD_DIM - feature_count)))[:, None]
    small = jnp.concatenate([flat[:, None], linear_rows, square_rows], 1)
    small = jnp.pad(small, ((0, 0), (0, -small.shape[1] % 16), (0, 0)))
    return jnp.concatenate([square, linear, small], 1).reshape(-1, HEAD_DIM)


def unpack(packed, groups, feature_count):
    squares = feature_count * feature_count
    packed = packed.reshape(groups, -1, HEAD_DIM)
    top = squares + feature_count
    square_den = packed[:, top + 2 : top + 2 + squares // HEAD_DIM].reshape(groups, squares)
    return (
        packed[:, :squares],
        packed[:, squares:top],
        square_den,
        packed[:, top + 1, :feature_count],
        packed[:, top],
    )


def ring_gather(block):
    count = lax.axis_size("ctx")
    me = lax.axis_index("ctx")
    rows = block.shape[0]
    half = rows // 2
    ring = list(range(0, count, 2)) + list(range(1, count, 2))[::-1]
    place = [ring.index(i) for i in range(count)]
    position = jnp.array(place, jnp.int32)[me]
    ring_table = jnp.array(ring, jnp.int32)
    up_route = [(ring[p], ring[(p + 1) % count]) for p in range(count)]
    down_route = [(ring[(p + 1) % count], ring[p]) for p in range(count)]
    up, down = block[:half], block[half:]
    pieces = [(me, up, down, me)]
    for step in range(1, count):
        up = lax.ppermute(up, "ctx", up_route)
        down = lax.ppermute(down, "ctx", down_route)
        pieces.append(
            (
                ring_table[(position - step) % count],
                up,
                down,
                ring_table[(position + step) % count],
            )
        )
    return pieces


def after_hop(pieces, hop, *members):
    if hop >= len(pieces):
        return members
    up_owner, up, down, down_owner = pieces[hop]
    up, down, *members = lax.optimization_barrier((up, down, *members))
    pieces[hop] = (up_owner, up, down, down_owner)
    return members


def assemble(pieces, zero, rows):
    half = rows // 2
    count = len(pieces)
    full = jnp.broadcast_to(zero, (count * rows, pieces[0][1].shape[1]))
    for up_owner, up, down, down_owner in pieces:
        full = lax.dynamic_update_slice(full, up, (up_owner * rows, 0))
        full = lax.dynamic_update_slice(full, down, (down_owner * rows + half, 0))
    return full


def flipped(block, bit):
    return lax.ppermute(block, "head", [(i, i ^ bit) for i in range(4)])


def sum_heads(row):
    if lax.axis_size("head") != 4:
        return lax.psum(row, "head")
    row = row + flipped(row, 1)
    return row + flipped(row, 2)


def sum_from(block, sign):
    count = lax.axis_size("ctx")
    devices = range(count)
    total = jnp.zeros_like(block)
    for distance in range(1, count):
        route = [(i, i + sign * distance) for i in devices if i + sign * distance in devices]
        total = total + lax.ppermute(block, "ctx", route)
    return total


def gather_heads(block):
    if lax.axis_size("head") != 4:
        return lax.all_gather(block, "head", axis=1, tiled=True)
    head = lax.axis_index("head")
    rows, width = block.shape
    far = flipped(block, 2)
    near = flipped(block, 1)
    diagonal = flipped(far, 1)
    full = jnp.zeros((rows, 4 * width), block.dtype)
    for bit, member in ((0, block), (2, far), (1, near), (3, diagonal)):
        full = lax.dynamic_update_slice(full, member, (0, (head ^ bit) * width))
    return full


def scatter_heads(d_student, proj_full):
    def product(weights):
        return lax.dot_general(
            d_student, weights, (((1,), (1,)), ((), ())), preferred_element_type=jnp.float32
        ).astype(jnp.bfloat16)

    if lax.axis_size("head") != 4:
        terms = product(proj_full)
        return lax.psum_scatter(terms, "head", scatter_dimension=1, tiled=True).astype(jnp.float32)
    head = lax.axis_index("head")
    width = proj_full.shape[0] // 4

    def block(bit):
        return product(lax.dynamic_slice_in_dim(proj_full, (head ^ bit) * width, width, 0))

    diagonal = flipped(block(3), 1)
    far = block(2)
    pair = (far.astype(jnp.float32) + diagonal.astype(jnp.float32)).astype(jnp.bfloat16)
    far_sum = flipped(pair, 2)
    near = flipped(block(1), 1)
    own = block(0)
    return own.astype(jnp.float32) + near.astype(jnp.float32) + far_sum.astype(jnp.float32)


def window_tiles(extended, tok_rows):
    tile_count = tok_rows // WIN
    first = extended[:tok_rows].reshape((tile_count, WIN) + extended.shape[1:])
    second = extended[WIN:].reshape((tile_count, WIN) + extended.shape[1:])
    return jnp.concatenate([first, second], 1)


def local(queries, keys, values, feature_map, out_proj, teacher):
    tok_rows = queries.shape[0]
    kv_groups = keys.shape[1] // HEAD_DIM
    ctx_count = lax.axis_size("ctx")
    ctx_index = lax.axis_index("ctx")
    pieces = ring_gather(out_proj)
    query_heads = queries.reshape(tok_rows, kv_groups, GROUP, HEAD_DIM)
    key_heads = keys.reshape(tok_rows, kv_groups, HEAD_DIM)
    value_heads = values.reshape(tok_rows, kv_groups, HEAD_DIM)
    value_float = value_heads.astype(jnp.float32)
    query_features = jnp.einsum(
        "tgqe,gef->tgqf", query_heads, feature_map, preferred_element_type=jnp.float32
    )
    key_features = jnp.einsum(
        "tge,gef->tgf", key_heads, feature_map, preferred_element_type=jnp.float32
    )
    rim_rows = shifted(jnp.stack([keys[tok_rows - WIN :], values[tok_rows - WIN :]]), "ctx", 1)
    keys_ext = jnp.concatenate([rim_rows[0], keys], 0).reshape(tok_rows + WIN, kv_groups, HEAD_DIM)
    values_ext = jnp.concatenate([rim_rows[1], values], 0).reshape(
        tok_rows + WIN, kv_groups, HEAD_DIM
    )
    tile_count = tok_rows // WIN
    key_tiles = window_tiles(keys_ext, tok_rows)
    value_tiles = window_tiles(values_ext, tok_rows)
    query_tiles = query_heads.reshape(tile_count, WIN, kv_groups, GROUP, HEAD_DIM)
    causal = lax.broadcasted_iota(jnp.int32, (tok_rows, tok_rows), 0) >= lax.broadcasted_iota(
        jnp.int32, (tok_rows, tok_rows), 1
    )
    qk_inner = (
        jnp.einsum("tgqf,sgf->gqts", query_features, key_features, precision=exact_mode) / 4.0
    )
    kernel = jnp.where(causal, 1.0 + qk_inner + 0.5 * qk_inner * qk_inner, 0.0)
    numerator = jnp.einsum(
        "gqts,sge->tgqe", kernel.astype(jnp.bfloat16), value_heads, preferred_element_type=jnp.float32
    )
    denominator = jnp.transpose(jnp.sum(kernel, axis=-1), (2, 0, 1))
    query_tiles, numerator, denominator = after_hop(
        pieces, 1, query_tiles, numerator, denominator
    )
    scores = jnp.einsum(
        "ntgqe,nsge->ngqts", query_tiles, key_tiles, preferred_element_type=jnp.float32
    ) / math.sqrt(HEAD_DIM)
    tile_pos = lax.broadcasted_iota(jnp.int32, (tile_count, WIN, 2 * WIN), 0)
    query_pos = lax.broadcasted_iota(jnp.int32, (tile_count, WIN, 2 * WIN), 1)
    key_pos = lax.broadcasted_iota(jnp.int32, (tile_count, WIN, 2 * WIN), 2)
    distance = query_pos + WIN - key_pos
    allowed = (
        (distance >= 0)
        & (distance < WIN)
        & (ctx_index * tok_rows + tile_pos * WIN + key_pos - WIN >= 0)
    )
    allowed = allowed[:, None, None]
    scores = jnp.where(allowed, scores, -jnp.inf)
    row_max = jnp.max(scores, axis=-1, keepdims=True)
    weights = jnp.where(allowed, jnp.exp(scores - row_max), 0.0)
    attn_weights = (weights / jnp.sum(weights, axis=-1, keepdims=True)).astype(jnp.bfloat16)
    window_out = jnp.einsum(
        "ngqts,nsge->ntgqe", attn_weights, value_tiles, preferred_element_type=jnp.float32
    ).reshape(tok_rows, kv_groups, GROUP, HEAD_DIM)
    key_square = taylor_square(key_features)
    own_square_v = jnp.einsum("sgk,sge->gke", key_square, value_float, precision=exact_mode)
    own_linear_v = jnp.einsum("sgf,sge->gfe", key_features, value_float, precision=exact_mode)
    own_values = jnp.sum(value_float, axis=0)
    own_square_k = jnp.sum(key_square, axis=0)
    own_linear_k = jnp.sum(key_features, axis=0)
    no_row = jnp.zeros((8, HEAD_DIM), jnp.float32)
    packed = pack(own_square_v, own_linear_v, own_square_k, own_linear_k, own_values)
    earlier, window_out = after_hop(pieces, 2, sum_from(packed, 1), window_out)
    feature_count = feature_map.shape[2]
    past_square_v, past_linear_v, past_square_k, past_linear_k, past_values = unpack(
        earlier, kv_groups, feature_count
    )
    past_count = (ctx_index * tok_rows).astype(jnp.float32)
    query_square = taylor_square(query_features)
    numerator = (
        numerator
        + jnp.einsum("tgqk,gke->tgqe", query_square, past_square_v, precision=exact_mode) / 32.0
        + jnp.einsum("tgqf,gfe->tgqe", query_features, past_linear_v, precision=exact_mode) / 4.0
        + past_values[None, :, None, :]
    )
    denominator = (
        denominator
        + jnp.einsum("tgqk,gk->tgq", query_square, past_square_k, precision=exact_mode) / 32.0
        + jnp.einsum("tgqf,gf->tgq", query_features, past_linear_k, precision=exact_mode) / 4.0
        + past_count
    )
    linear_out = numerator / denominator[..., None]
    head_out = (
        (linear_out + window_out)
        .astype(jnp.bfloat16)
        .reshape(tok_rows, kv_groups * GROUP * HEAD_DIM)
    )
    head_out, zero = after_hop(pieces, 3, head_out, jnp.zeros((), jnp.bfloat16))
    all_heads = gather_heads(head_out)
    proj_full = assemble(pieces, zero, out_proj.shape[0])
    projected = jnp.dot(all_heads, proj_full, preferred_element_type=jnp.float32)
    student_out = projected.astype(jnp.bfloat16)
    residual = student_out.astype(jnp.float32) - teacher.astype(jnp.float32)
    total_rows = tok_rows * ctx_count
    squared = jnp.sum(residual * residual)
    d_student = (2.0 * residual / total_rows).astype(jnp.bfloat16)
    head_grad = scatter_heads(d_student, proj_full).reshape(
        tok_rows, kv_groups, GROUP, HEAD_DIM
    )
    numerator_grad = head_grad / denominator[..., None]
    denominator_grad = -jnp.sum(head_grad * linear_out, axis=-1) / denominator
    kernel_grad = (
        jnp.einsum(
            "tgqe,sge->gqts",
            two_terms(numerator_grad),
            jnp.concatenate([value_heads, value_heads], -1),
            preferred_element_type=jnp.float32,
        )
        + jnp.transpose(denominator_grad, (1, 2, 0))[..., None]
    )
    inner_grad = (jnp.where(causal, kernel_grad * (1.0 + qk_inner), 0.0) / 4.0).astype(
        jnp.bfloat16
    )
    query_grad = joined(
        jnp.einsum(
            "gqts,sgf->tgqf",
            inner_grad,
            two_terms(key_features),
            preferred_element_type=jnp.float32,
        )
    )
    key_grad = joined(
        jnp.einsum(
            "gqts,tgqf->sgf",
            inner_grad,
            two_terms(query_features),
            preferred_element_type=jnp.float32,
        )
    )
    query_square_grad = (
        jnp.einsum("tgqe,gke->tgqk", numerator_grad, past_square_v, precision=exact_mode)
        + denominator_grad[..., None] * past_square_k[None, :, None, :]
    ) / 32.0
    query_grad = (
        query_grad
        + (
            jnp.einsum("tgqe,gfe->tgqf", numerator_grad, past_linear_v, precision=exact_mode)
            + denominator_grad[..., None] * past_linear_k[None, :, None, :]
        )
        / 4.0
        + square_grad(query_square_grad, query_features)
    )
    own_back_square = jnp.einsum(
        "tgqk,tgqe->gke", query_square, numerator_grad, precision=exact_mode
    )
    own_back_linear = jnp.einsum(
        "tgqf,tgqe->gfe", query_features, numerator_grad, precision=exact_mode
    )
    own_den_square = jnp.einsum(
        "tgqk,tgq->gk", query_square, denominator_grad, precision=exact_mode
    )
    own_den_linear = jnp.einsum(
        "tgqf,tgq->gf", query_features, denominator_grad, precision=exact_mode
    )
    packed_back = pack(
        own_back_square,
        own_back_linear,
        own_den_square,
        own_den_linear,
        jnp.zeros((kv_groups, HEAD_DIM), jnp.float32),
    )
    later = sum_from(packed_back, -1)
    loss_row = sum_heads(jnp.full((8, HEAD_DIM), squared, jnp.float32))
    later_square, later_linear, later_den_square, later_den_linear, _ = unpack(
        later, kv_groups, feature_count
    )
    key_square_grad = (
        jnp.einsum("gke,sge->sgk", later_square, value_float, precision=exact_mode)
        + later_den_square[None]
    ) / 32.0
    key_grad = (
        key_grad
        + (
            jnp.einsum("gfe,sge->sgf", later_linear, value_float, precision=exact_mode)
            + later_den_linear[None]
        )
        / 4.0
        + square_grad(key_square_grad, key_features)
    )
    own_grad = jnp.einsum(
        "tgqe,tgqf->gef", query_heads.astype(jnp.float32), query_grad, precision=exact_mode
    ) + jnp.einsum("tge,tgf->gef", key_heads.astype(jnp.float32), key_grad, precision=exact_mode)
    packed_grad = jnp.concatenate([own_grad.reshape(-1, HEAD_DIM), loss_row], 0)
    summed, _ = exchange(packed_grad, no_row, "all", 0)
    feature_grad = summed[:-8].reshape(own_grad.shape)
    loss_value = summed[-8, 0] / (total_rows * D)
    return (student_out, loss_value, feature_grad)


FEATURE_PAIRS = 153
PAIR_ROWS = 160
CHUNKS = 8
STREAMS = 4


def pair_tables():
    j = np.arange(2 * HEAD_DIM)
    valid = j < FEATURE_PAIRS
    first = j % 17
    second = (first + j // 17) % 17
    select = np.zeros((2, 2 * HEAD_DIM, HEAD_DIM), np.float32)
    constant = np.zeros((2, 2 * HEAD_DIM), np.float32)
    for side, member in enumerate((first, second)):
        for row in np.nonzero(valid)[0]:
            if member[row] < 16:
                select[side, row, member[row]] = 1.0
            else:
                constant[side, row] = 1.0
    is_one = (first == 16).astype(int) + (second == 16).astype(int)
    coef = np.where(is_one == 2, 1.0, np.where(is_one == 1, 0.25, np.where(first == second, 1 / 32, 1 / 16)))
    coef = np.where(valid, coef, 0.0)
    bits = np.concatenate([select[0], select[1], np.eye(HEAD_DIM)], 0)
    rows = np.zeros((8, 2 * HEAD_DIM), np.float32)
    rows[0], rows[1], rows[2] = constant[0], constant[1], coef
    columns = np.zeros((2 * HEAD_DIM, HEAD_DIM), np.float32)
    columns[:, 0], columns[:, 1], columns[:, 2] = constant[0], constant[1], coef
    return bits, rows, columns


def mm(a, b):
    return lax.dot_general(a, b, (((1,), (0,)), ((), ())), preferred_element_type=jnp.float32)


def mm_t(a, b):
    return lax.dot_general(a, b, (((1,), (1,)), ((), ())), preferred_element_type=jnp.float32)


def split_terms(x):
    high = x.astype(jnp.bfloat16)
    return high, (x - high.astype(jnp.float32)).astype(jnp.bfloat16)


def fused_kernel(
    queries_ref, keys_ref, values_ref, map_ref, proj_ref, teacher_ref, bits_ref, rows_ref, columns_ref,
    student_ref, grad_ref, loss_ref,
    proj_buf, heads_buf, sums, first_factor, second_factor, pairs_t, queries_t, slope, lin, den_inv,
    d_student, acc, teacher_buf, keys_ext, values_ext, ones_values, wide_map, wide_map_t, kernel_map,
    past_high, past_low, key_features, key_factor_a, key_factor_b, keys_t,
    state_own, state_x, state_low, state_up,
    send_1, send_2, send_3, recv_1, recv_2, recv_3,
    cross, grad_a, grad_b, back, back_own, back_x, back_sum, back_later, back_in, final_own, final_in, loss_acc, loss_own, loss_in,
    ring_send, ring_recv, own_sem, teacher_sem, student_sem, rim_send, rim_recv, state_x_send, state_x_recv,
    state_up_send, state_up_recv, head_send, head_recv, s1_send, s1_recv, s2_send, s2_recv, s3_send, s3_recv,
    back_x_send, back_x_recv, back_send, back_recv, final_send, final_recv, loss_send, loss_recv,
):
    f32, bf16 = jnp.float32, jnp.bfloat16
    mesh_ids = pl.DeviceIdType.MESH
    ctx_count = 8
    tokens = queries_ref.shape[0]
    half = tokens // 2
    width = proj_buf.shape[2]
    E = HEAD_DIM
    c = lax.axis_index("ctx")
    h = lax.axis_index("head")
    z = c // 2
    x = c % 2
    pos = jnp.where(x == 0, z, 7 - z)

    def ring_at(p):
        p = lax.rem(p + 16, 8)
        return jnp.where(p < 4, 2 * p, 2 * (7 - p) + 1)

    up, down = ring_at(pos + 1), ring_at(pos - 1)
    near = h + 1 - 2 * (h % 2)
    far = (h + 2) % 4
    diagonal = 3 - h

    def remote(src, dst, send, recv, ctx, head):
        return pltpu.make_async_remote_copy(
            src_ref=src, dst_ref=dst, send_sem=send, recv_sem=recv, device_id=(ctx, head), device_id_type=mesh_ids
        )

    barrier = pltpu.get_barrier_semaphore()
    for d in range(1, ctx_count):
        pl.semaphore_signal(barrier, inc=1, device_id=((c + d) % ctx_count, h), device_id_type=mesh_ids)
    for d in range(1, 4):
        pl.semaphore_signal(barrier, inc=1, device_id=(c, (h + d) % 4), device_id_type=mesh_ids)
    pl.semaphore_wait(barrier, ctx_count + 2)

    def owner_rows(owner, d):
        return pl.ds(pl.multiple_of(owner * tokens + d * half, half), half)

    def hop(d, j, k):
        owner = ring_at(pos - k) if d == 0 else ring_at(pos + k)
        place = proj_buf.at[j, owner_rows(owner, d)]
        return remote(place, place, ring_send.at[d, j, k], ring_recv.at[d, j, k], up if d == 0 else down, h)

    def first_hop(d, j):
        place = proj_buf.at[j, owner_rows(c, d)]
        src = proj_ref.at[pl.ds(d * half, half), pl.ds(pl.multiple_of(j * width, width), width)]
        return remote(src, place, ring_send.at[d, j, 0], ring_recv.at[d, j, 0], up if d == 0 else down, h)

    def arrival(d, j, k):
        owner = ring_at(pos - 1 - k) if d == 0 else ring_at(pos + 1 + k)
        place = proj_buf.at[j, owner_rows(owner, d)]
        return remote(place, place, ring_send.at[d, j, k], ring_recv.at[d, j, k], up if d == 0 else down, h)

    def start_first(n):
        for d in (0, 1):
            first_hop(d, n).start()

    def service(group, n):
        k = n // STREAMS
        j = group * STREAMS + n % STREAMS
        for d in (0, 1):
            arrival(d, j, k - 1).wait_recv()
            hop(d, j, k).start()

    for n in range(STREAMS):
        start_first(n)

    for s, (src, dst) in enumerate(((keys_ref, keys_ext), (values_ref, values_ext))):

        @pl.when(c < ctx_count - 1)
        def _():
            remote(
                src.at[pl.ds(tokens - WIN, WIN)], dst.at[pl.ds(0, WIN)], rim_send.at[s], rim_recv.at[s],
                lax.rem(c + 1, ctx_count), h,
            ).start()

        @pl.when(c == 0)
        def _():
            dst[pl.ds(0, WIN), :] = jnp.zeros((WIN, E), bf16)

        dst[pl.ds(WIN, tokens), :] = src[...]
        dst[pl.ds(WIN + tokens, WIN), :] = jnp.zeros((WIN, E), bf16)

    teacher_copy = pltpu.make_async_copy(teacher_ref, teacher_buf, teacher_sem.at[0])
    teacher_copy.start()

    def own_copy(j):
        return pltpu.make_async_copy(
            proj_ref.at[:, pl.ds(pl.multiple_of(j * width, width), width)],
            proj_buf.at[j, pl.ds(pl.multiple_of(c * tokens, tokens), tokens)],
            own_sem.at[j],
        )

    for j in range(CHUNKS):
        own_copy(j).start()

    eye = bits_ref[pl.ds(4 * E, E), :]
    map_wide = mm(map_ref[...], eye[: map_ref.shape[1]]).astype(bf16)
    for s in range(2):
        select = bits_ref[pl.ds(s * 2 * E, 2 * E), :]
        wide_map[s] = mm_t(map_wide, select).astype(bf16)
        wide_map_t[s] = mm_t(select, map_wide).astype(bf16)
    keys = keys_ref[...]
    features = mm(keys, map_wide)
    feature_high, feature_low = split_terms(features)
    key_features[0] = feature_high
    key_features[1] = feature_low
    inner = (mm_t(map_wide, feature_high) + mm_t(map_wide, feature_low)) * 0.25
    inner_high, inner_low = split_terms(inner)
    kernel_map[pl.ds(0, E), :] = inner_high
    kernel_map[pl.ds(E, E), :] = inner_low
    keys_t[...] = mm_t(eye, keys).astype(bf16)
    key_a = mm(keys, wide_map[0]) + rows_ref[pl.ds(0, 1), :]
    key_b = mm(keys, wide_map[1]) + rows_ref[pl.ds(1, 1), :]
    key_factor_a[...] = (key_a * rows_ref[pl.ds(2, 1), :]).astype(bf16)
    key_factor_b[...] = (key_b * rows_ref[pl.ds(2, 1), :]).astype(bf16)
    ones_values[:, pl.ds(0, E)] = values_ref[...]
    ones_values[:, pl.ds(E, E)] = jnp.ones((tokens, E), bf16)
    key_a_t = mm_t(wide_map_t[0], keys) + columns_ref[:, 0:1]
    key_b_t = mm_t(wide_map_t[1], keys) + columns_ref[:, 1:2]
    key_high, key_low = split_terms(key_a_t * key_b_t * columns_ref[:, 2:3])
    state = mm(key_high, ones_values[...]) + mm(key_low, ones_values[...])

    def store_state(ref, value, den_row):
        ref[pl.ds(0, PAIR_ROWS), :] = value[:PAIR_ROWS]
        ref[pl.ds(PAIR_ROWS, 8), :] = den_row[:, :E]
        ref[pl.ds(PAIR_ROWS + 8, 8), :] = den_row[:, E:]

    store_state(state_own, state[:, :E], jnp.transpose(state[:, E:])[:8])
    state_x_copy = remote(state_own, state_x, state_x_send.at[0], state_x_recv.at[0], c + 1 - 2 * x, h)
    state_x_copy.start()

    def state_up_copy():
        return remote(state_up, state_low, state_up_send.at[0], state_up_recv.at[0], lax.rem(c + 2, ctx_count), h)

    def chain_step(level):
        if level == 0:
            state_x_copy.wait_recv()

            @pl.when(z == 0)
            def _():
                state_low[...] = jnp.zeros_like(state_low)

        else:

            @pl.when(z == level)
            def _():
                state_up_copy().wait_recv()

        if level < 3:

            @pl.when(z == level)
            def _():
                state_up[...] = state_low[...] + state_own[...] + state_x[...]
                state_up_copy().start()

    for s in range(2):

        @pl.when(c > 0)
        def _():
            dst = (keys_ext, values_ext)[s]
            remote(
                dst.at[pl.ds(0, WIN)], dst.at[pl.ds(0, WIN)], rim_send.at[s], rim_recv.at[s], c, h
            ).wait_recv()

    def query_tile(i, hp):
        token = pl.multiple_of(i * E, E)
        both = queries_ref[pl.ds(token, E), pl.ds(pl.multiple_of(hp * 2 * E, 2 * E), 2 * E)]
        return jnp.concatenate([both[:, :E], both[:, E:]], 0)

    for i in range(4):
        reach = (i + 1) * E

        def local_tile(hp, carry):
            tile = i * 4 + hp
            q = query_tile(i, hp)
            u = mm(jnp.concatenate([q, q], 1), kernel_map[:, pl.ds(0, reach)])
            row = lax.broadcasted_iota(jnp.int32, (2 * E, reach), 0) % E + i * E
            causal = row >= lax.broadcasted_iota(jnp.int32, (2 * E, reach), 1)
            kernel = jnp.where(causal, 1.0 + u + 0.5 * u * u, 0.0).astype(bf16)
            slope[tile, :, pl.ds(0, reach)] = jnp.where(causal, 0.25 + 0.25 * u, 0.0).astype(bf16)
            both = mm(kernel, ones_values[pl.ds(0, reach), :])
            lin[tile] = both[:, :E]
            den_inv[tile] = both[:, E:]
            scores = mm_t(q, keys_ext[pl.ds(i * E, 2 * E), :]) / math.sqrt(HEAD_DIM)
            token = lax.broadcasted_iota(jnp.int32, (2 * E, 2 * E), 0) % E
            place = lax.broadcasted_iota(jnp.int32, (2 * E, 2 * E), 1)
            distance = token + WIN - place
            allowed = (distance >= 0) & (distance < WIN) & (c * tokens + i * E + place - WIN >= 0)
            scores = jnp.where(allowed, scores, -jnp.inf)
            top = jnp.max(scores, axis=-1, keepdims=True)
            weights = jnp.where(allowed, jnp.exp(scores - top), 0.0)
            weights = (weights / jnp.sum(weights, axis=-1, keepdims=True)).astype(bf16)
            sums[tile, pl.ds(0, 2 * E), pl.ds(0, E)] = mm(weights, values_ext[pl.ds(i * E, 2 * E), :])
            first_factor[tile] = (mm(q, wide_map[0]) + rows_ref[pl.ds(0, 1), :]).astype(bf16)
            second_factor[tile] = (mm(q, wide_map[1]) + rows_ref[pl.ds(1, 1), :]).astype(bf16)
            pair_a = mm_t(wide_map_t[0], q) + columns_ref[:, 0:1]
            pair_b = mm_t(wide_map_t[1], q) + columns_ref[:, 1:2]
            pairs_t[tile] = (pair_a * pair_b).astype(bf16)[:PAIR_ROWS]
            queries_t[tile] = mm_t(eye, q).astype(bf16)
            service(0, STREAMS + tile)
            return carry

        lax.fori_loop(0, 4, local_tile, 0)
        chain_step(i)

    past = jnp.where(z > 0, state_low[...], 0.0) + jnp.where(x == 1, state_x[...], 0.0)
    past_rows = jnp.concatenate([past[PAIR_ROWS : PAIR_ROWS + 8], past[PAIR_ROWS + 8 :]], 1)
    past_den = jnp.transpose(jnp.broadcast_to(past_rows[:1], (E, 2 * E)))
    past_values = jnp.concatenate([past[:PAIR_ROWS], jnp.zeros((2 * E - PAIR_ROWS, E), f32)], 0)
    high, low = split_terms(jnp.concatenate([past_values, past_den], 1))
    past_high[...] = high
    past_low[...] = low

    def head_copy(i, d, source):
        piece = heads_buf.at[source, pl.ds(pl.multiple_of(i * E, E), E)]
        return remote(piece, piece, head_send.at[d, i], head_recv.at[source, i], c, (h + d) % 4)

    def past_tiles(i, carry):
        def past_tile(hp, carry):
            tile = i * 4 + hp
            q = query_tile(i, hp)
            pair = (mm(q, wide_map[0]) + rows_ref[pl.ds(0, 1), :]) * (mm(q, wide_map[1]) + rows_ref[pl.ds(1, 1), :])
            pair_high, pair_low = split_terms(pair)
            both = mm(pair_high, past_high[...]) + mm(pair_low, past_high[...]) + mm(pair_high, past_low[...])
            den = den_inv[tile] + both[:, E:]
            value = (lin[tile] + both[:, :E]) / den
            lin[tile] = value
            den_inv[tile] = 1.0 / den
            out = (value + sums[tile, pl.ds(0, 2 * E), pl.ds(0, E)]).astype(bf16)
            heads_buf[
                h, pl.ds(pl.multiple_of(i * E, E), E), pl.ds(pl.multiple_of(hp * 2 * E, 2 * E), 2 * E)
            ] = jnp.concatenate([out[:E], out[E:]], 1)
            return carry

        lax.fori_loop(0, 4, past_tile, 0)
        for d in range(1, 4):
            head_copy(i, d, h).start()
        service(0, STREAMS + 16 + 2 * i)
        service(0, STREAMS + 17 + 2 * i)
        return carry

    lax.fori_loop(0, 4, past_tiles, 0)
    for n in range(STREAMS):
        start_first(STREAMS + n)
    teacher_copy.wait()
    for j in range(CHUNKS):
        own_copy(j).wait()
    loss_acc[...] = jnp.zeros_like(loss_acc)
    for i in range(4):
        for d in range(1, 4):
            head_copy(i, d, (h + d) % 4).wait_recv()
    for j in range(STREAMS):
        for d in (0, 1):
            arrival(d, j, 6).wait_recv()

    def student_copy(j):
        return pltpu.make_async_copy(
            teacher_buf.at[:, pl.ds(pl.multiple_of(j * width, width), width)],
            student_ref.at[:, pl.ds(pl.multiple_of(j * width, width), width)],
            student_sem.at[j],
        )

    def finish_columns(j, product):
        student = product.astype(bf16)
        columns = pl.ds(pl.multiple_of(j * width, width), width)
        residual = student.astype(f32) - teacher_buf[:, columns].astype(f32)
        teacher_buf[:, columns] = student
        loss_acc[...] += jnp.sum((residual * residual).reshape(tokens // 8, 8, width), axis=0)
        d_student[j] = (residual * (2.0 / (tokens * ctx_count))).astype(bf16)
        student_copy(j).start()

    def first_columns(j, carry):
        product = mm(heads_buf[0], proj_buf[j, pl.ds(0, 8 * E), :])
        for s in range(1, 4):
            product += mm(heads_buf[s], proj_buf[j, pl.ds(s * 8 * E, 8 * E), :])
        finish_columns(j, product)
        service(1, STREAMS + j)
        return carry

    lax.fori_loop(0, STREAMS, first_columns, 0)

    def block_sum(group, r):
        rows = pl.ds(pl.multiple_of(r * width, width), width)
        total = mm_t(d_student[group * STREAMS], proj_buf[group * STREAMS, rows, :])
        for j in range(1, STREAMS):
            total += mm_t(d_student[group * STREAMS + j], proj_buf[group * STREAMS + j, rows, :])
        return total

    def first_sums(r, carry):
        sums[r] = block_sum(0, r)
        service(1, 2 * STREAMS + r)
        return carry

    lax.fori_loop(0, 16, first_sums, 0)

    def partial_product(owner, d, j):
        place = pl.multiple_of((owner % 2) * tokens + d * half, half)
        left = heads_buf[owner // 2, :, pl.ds(place, half)]
        return mm(left, proj_buf[j, owner_rows(owner, d), :])

    def second_early(s, carry):
        j = STREAMS + s
        total = partial_product(c, 0, j) + partial_product(c, 1, j)
        for k in range(5):
            total += partial_product(ring_at(pos - 1 - k), 0, j) + partial_product(ring_at(pos + 1 + k), 1, j)
        acc[s] = total
        service(1, 6 * STREAMS + s)
        return carry

    lax.fori_loop(0, STREAMS, second_early, 0)

    def second_middle(s, carry):
        j = STREAMS + s
        acc[s] += partial_product(ring_at(pos - 6), 0, j) + partial_product(ring_at(pos + 6), 1, j)
        return carry

    lax.fori_loop(0, STREAMS, second_middle, 0)

    def second_last(s, carry):
        j = STREAMS + s
        for d in (0, 1):
            arrival(d, j, 6).wait_recv()
        finish_columns(
            j, acc[s] + partial_product(ring_at(pos - 7), 0, j) + partial_product(ring_at(pos + 7), 1, j)
        )
        return carry

    lax.fori_loop(0, STREAMS, second_last, 0)

    def copy_1(p):
        return remote(send_1.at[p], recv_1.at[p], s1_send.at[p], s1_recv.at[p], c, near)

    def copy_2(p):
        return remote(send_2.at[p], recv_2.at[p], s2_send.at[p], s2_recv.at[p], c, near)

    def copy_3(p):
        return remote(send_3.at[p], recv_3.at[p], s3_send.at[p], s3_recv.at[p], c, far)

    def step_1(p):
        r = diagonal * 4 + p
        send_1[p] = (sums[r] + block_sum(1, r)).astype(bf16)
        copy_1(p).start()

    def step_2(p):
        r = far * 4 + p
        total = sums[r] + block_sum(1, r)
        copy_1(p).wait_recv()
        send_3[p] = (total + recv_1[p].astype(f32)).astype(bf16)
        copy_3(p).start()

    step_1(0)
    step_1(1)

    def step_both(p, carry):
        step_2(p)
        step_1(p + 2)
        return carry

    lax.fori_loop(0, 2, step_both, 0)
    step_2(2)
    step_2(3)

    def step_near(p, carry):
        r = near * 4 + p
        send_2[p] = (sums[r] + block_sum(1, r)).astype(bf16)
        copy_2(p).start()
        return carry

    lax.fori_loop(0, 4, step_near, 0)

    def step_own(p, carry):
        r = h * 4 + p
        sums[r] += block_sum(1, r)
        return carry

    lax.fori_loop(0, 4, step_own, 0)

    loss_own[...] = loss_acc[:, :E] + loss_acc[:, E:]

    def loss_copy(d, source):
        return remote(loss_own, loss_in.at[source], loss_send.at[d], loss_recv.at[source], c, (h + d) % 4)

    for d in range(1, 4):
        loss_copy(d, h).start()

    cross[...] = jnp.zeros_like(cross)
    grad_a[...] = jnp.zeros_like(grad_a)
    grad_b[...] = jnp.zeros_like(grad_b)
    back[...] = jnp.zeros_like(back)

    def grad_piece(p, carry):
        copy_2(p).wait_recv()
        copy_3(p).wait_recv()
        for i in range(4):
            reach = (i + 1) * E
            tile = i * 4 + p
            rows = pl.ds(i * E, E)
            g = sums[h * 4 + p, rows, :] + recv_2[p, rows, :].astype(f32) + recv_3[p, rows, :].astype(f32)
            g = jnp.concatenate([g[:, :E], g[:, E:]], 0)
            inverse = den_inv[tile]
            upper = (g * inverse).astype(bf16)
            lower = -jnp.sum(upper.astype(f32) * lin[tile], axis=-1, keepdims=True)
            lower = jnp.broadcast_to(lower, (2 * E, E))
            lower_high = lower.astype(bf16).astype(f32)
            lane = lax.broadcasted_iota(jnp.int32, (2 * E, E), 1)
            lower = (jnp.where(lane < E // 2, lower_high, lower - lower_high) * (2.0 / E)).astype(bf16)
            wide = jnp.concatenate([upper, lower], 1)
            weight = mm_t(wide, ones_values[pl.ds(0, reach), :]) * slope[tile, :, pl.ds(0, reach)].astype(f32)
            cross[:, pl.ds(0, reach)] += mm(queries_t[tile], weight.astype(bf16))
            pair_grad = mm_t(wide, past_high[...]) + mm_t(wide, past_low[...])
            grad_a[...] += mm(queries_t[tile], (pair_grad * second_factor[tile].astype(f32)).astype(bf16))
            grad_b[...] += mm(queries_t[tile], (pair_grad * first_factor[tile].astype(f32)).astype(bf16))
            back[...] += mm(pairs_t[tile], wide)
        return carry

    lax.fori_loop(0, 4, grad_piece, 0)

    back_den = jnp.transpose(
        jnp.concatenate([back[:, pl.ds(E, E)], jnp.zeros((2 * E - PAIR_ROWS, E), f32)], 0)
    )
    back_den = (back_den[:8] + back_den[E // 2 : E // 2 + 8]) * (E // 2)
    store_state(back_own, back[:, pl.ds(0, E)], back_den)
    back_x_copy = remote(back_own, back_x, back_x_send.at[0], back_x_recv.at[0], c + 1 - 2 * x, h)
    back_x_copy.start()

    def back_copy(level):
        return remote(back_sum, back_in.at[z], back_send.at[level], back_recv.at[z], 2 * level + x, h)

    def back_arrival(level):
        return remote(back_sum, back_in.at[level], back_send.at[level], back_recv.at[level], c, h)

    cross_high, cross_low = split_terms(cross[...])
    grad = mm(cross_high, key_features[0]) + mm(cross_high, key_features[1]) + mm(cross_low, key_features[0])
    mixed = jnp.transpose(mm(cross_high, keys_ref[...]) + mm(cross_low, keys_ref[...]))
    mixed_high, mixed_low = split_terms(mixed)
    map_wide = mm(map_ref[...], eye[: map_ref.shape[1]]).astype(bf16)
    grad += mm(mixed_high, map_wide) + mm(mixed_low, map_wide)

    back_x_copy.wait_recv()
    back_sum[...] = back_own[...] + back_x[...]
    for level in range(3):

        @pl.when(level < z)
        def _():
            back_copy(level).start()

    back_later[...] = jnp.where(x == 0, back_x[...], 0.0)
    for level in range(1, 4):

        @pl.when(level > z)
        def _():
            back_arrival(level).wait_recv()
            back_later[...] += back_in[level]

    later_values = jnp.concatenate([back_later[pl.ds(0, PAIR_ROWS), :], jnp.zeros((2 * E - PAIR_ROWS, E), f32)], 0)
    later_high, later_low = split_terms(later_values)
    pair_grad = mm_t(values_ref[...], later_high) + mm_t(values_ref[...], later_low)
    pair_grad += jnp.concatenate(
        [back_later[pl.ds(PAIR_ROWS, 1), :], back_later[pl.ds(PAIR_ROWS + 8, 1), :]], 1
    )
    total_a = grad_a[...] + mm(keys_t[...], (pair_grad * key_factor_b[...].astype(f32)).astype(bf16))
    total_b = grad_b[...] + mm(keys_t[...], (pair_grad * key_factor_a[...].astype(f32)).astype(bf16))
    for s, total in enumerate((total_a, total_b)):
        total_high, total_low = split_terms(total)
        select = bits_ref[pl.ds(s * 2 * E, 2 * E), :]
        grad += mm(total_high, select) + mm(total_low, select)
    final_own[pl.ds(0, 16), :] = jnp.transpose(grad)[:16]
    loss_sum = loss_own[...]
    for d in range(1, 4):
        loss_copy(d, (h + d) % 4).wait_recv()
        loss_sum += loss_in[(h + d) % 4]
    final_own[pl.ds(16, 8), :] = loss_sum

    def final_copy(d, source):
        return remote(final_own, final_in.at[source], final_send.at[d], final_recv.at[source], (c + d) % ctx_count, h)

    for d in range(1, ctx_count):
        final_copy(d, c).start()
    final_in[c] = final_own[...]
    for d in range(1, ctx_count):
        final_copy(d, (c + d) % ctx_count).wait_recv()
    final = final_in[0]
    for s in range(1, ctx_count):
        final += final_in[s]
    padded = jnp.concatenate([final[:16], jnp.zeros((E - 16, E), f32)], 0)
    grad_ref[...] = jnp.transpose(padded)
    loss_ref[...] = jnp.broadcast_to(jnp.sum(final[16:], keepdims=True), (8, E))

    for j in range(CHUNKS):
        student_copy(j).wait()
        for d in (0, 1):
            first_hop(d, j).wait_send()
            for k in range(1, 7):
                hop(d, j, k).wait_send()
    for s in range(2):

        @pl.when(c < ctx_count - 1)
        def _():
            dst = (keys_ext, values_ext)[s]
            src = (keys_ref, values_ref)[s]
            remote(
                src.at[pl.ds(tokens - WIN, WIN)], dst.at[pl.ds(0, WIN)], rim_send.at[s], rim_recv.at[s],
                lax.rem(c + 1, ctx_count), h,
            ).wait_send()

    state_x_copy.wait_send()

    @pl.when(z < 3)
    def _():
        state_up_copy().wait_send()

    back_x_copy.wait_send()
    for level in range(3):

        @pl.when(level < z)
        def _():
            back_copy(level).wait_send()

    for d in range(1, 4):
        loss_copy(d, h).wait_send()
        for i in range(4):
            head_copy(i, d, h).wait_send()
    for p in range(4):
        copy_1(p).wait_send()
        copy_2(p).wait_send()
        copy_3(p).wait_send()
    for d in range(1, ctx_count):
        final_copy(d, c).wait_send()


def fused_local(queries, keys, values, feature_map, out_proj, teacher):
    tokens = queries.shape[0]
    columns = out_proj.shape[1]
    rows = tokens * 8
    width = columns // CHUNKS
    E = HEAD_DIM
    bf16, f32 = jnp.bfloat16, jnp.float32
    bits, row_table, column_table = pair_tables()
    vmem = pl.BlockSpec(memory_space=pltpu.VMEM)
    anywhere = pl.BlockSpec(memory_space=pl.ANY)
    dma = pltpu.SemaphoreType.DMA
    state = (PAIR_ROWS + 16, E)
    scratch = [
        ((CHUNKS, rows, width), bf16),
        ((4, tokens, 8 * E), bf16),
        ((16, tokens, width), f32),
        ((16, 2 * E, 2 * E), bf16),
        ((16, 2 * E, 2 * E), bf16),
        ((16, PAIR_ROWS, 2 * E), bf16),
        ((16, E, 2 * E), bf16),
        ((16, 2 * E, tokens), bf16),
        ((16, 2 * E, E), f32),
        ((16, 2 * E, E), f32),
        ((CHUNKS, tokens, width), bf16),
        ((STREAMS, tokens, width), f32),
        ((tokens, columns), bf16),
        ((tokens + 2 * WIN, E), bf16),
        ((tokens + 2 * WIN, E), bf16),
        ((tokens, 2 * E), bf16),
        ((2, E, 2 * E), bf16),
        ((2, 2 * E, E), bf16),
        ((2 * E, tokens), bf16),
        ((2 * E, 2 * E), bf16),
        ((2 * E, 2 * E), bf16),
        ((2, tokens, E), bf16),
        ((tokens, 2 * E), bf16),
        ((tokens, 2 * E), bf16),
        ((E, tokens), bf16),
        (state, f32),
        (state, f32),
        (state, f32),
        (state, f32),
        ((4, tokens, width), bf16),
        ((4, tokens, width), bf16),
        ((4, tokens, width), bf16),
        ((4, tokens, width), bf16),
        ((4, tokens, width), bf16),
        ((4, tokens, width), bf16),
        ((E, tokens), f32),
        ((E, 2 * E), f32),
        ((E, 2 * E), f32),
        ((PAIR_ROWS, 2 * E), f32),
        (state, f32),
        (state, f32),
        (state, f32),
        (state, f32),
        ((4,) + state, f32),
        ((24, E), f32),
        ((8, 24, E), f32),
        ((8, width), f32),
        ((8, E), f32),
        ((4, 8, E), f32),
    ]
    semaphores = [
        (2, CHUNKS, 7), (2, CHUNKS, 7), (CHUNKS,), (1,), (CHUNKS,), (2,), (2,), (1,), (1,), (1,), (1,), (4, 4), (4, 4),
        (4,), (4,), (4,), (4,), (4,), (4,), (1,), (1,), (4,), (4,), (8,), (8,), (4,), (4,),
    ]
    student, grad, loss = pl.pallas_call(
        fused_kernel,
        out_shape=(
            jax.ShapeDtypeStruct((tokens, columns), bf16),
            jax.ShapeDtypeStruct((E, E), f32),
            jax.ShapeDtypeStruct((8, E), f32),
        ),
        in_specs=[vmem, vmem, vmem, vmem, anywhere, anywhere, vmem, vmem, vmem],
        out_specs=(anywhere, vmem, vmem),
        scratch_shapes=[pltpu.VMEM(shape, kind) for shape, kind in scratch] + [dma(shape) for shape in semaphores],
        compiler_params=pltpu.CompilerParams(
            collective_id=0, has_side_effects=True, vmem_limit_bytes=63 * 1024 * 1024
        ),
        cost_estimate=pl.CostEstimate(flops=30_000_000_000, bytes_accessed=40_000_000, transcendentals=2_000_000),
    )(
        queries, keys, values, feature_map[0], out_proj, teacher,
        jnp.asarray(bits, bf16), jnp.asarray(row_table, f32), jnp.asarray(column_table, f32),
    )
    return student, loss[0, 0] / (tokens * 8 * D), grad[None, :, : feature_map.shape[2]]


def fits_fused(mesh):
    return mesh.shape["ctx"] == 8 and mesh.shape["head"] == 4


def solution(mesh):
    return jax.shard_map(
        fused_local if fits_fused(mesh) else local,
        mesh=mesh,
        in_specs=(
            P("ctx", "head"),
            P("ctx", "head"),
            P("ctx", "head"),
            P("head", None, None),
            P("ctx", "head"),
            P("ctx", "head"),
        ),
        out_specs=(P("ctx", "head"), P(), P("head", None, None)),
        check_vma=False,
    )
```

```python
import functools
import math

import jax
import jax.numpy as jnp
import numpy as np
from jax import lax
from jax.experimental import pallas as pl
from jax.experimental.pallas import tpu as pltpu
from jax.sharding import PartitionSpec as P

D = 8192
HEAD_DIM = 128
GROUP = 8
WIN = 64


exact_mode = lax.Precision.HIGHEST


def shifted(block, axis, distance):
    devices = range(lax.axis_size(axis))
    route = [(i - distance, i) for i in devices if i - distance in devices]
    return lax.ppermute(block, axis, route)


def taylor_square(features):
    feature_count = features.shape[-1]
    outer = features[..., :, None] * features[..., None, :]
    return outer.reshape(features.shape[:-1] + (feature_count * feature_count,))


def two_terms(x):
    high = lax.reduce_precision(x, 8, 7)
    return jnp.concatenate([high.astype(jnp.bfloat16), (x - high).astype(jnp.bfloat16)], -1)


def joined(pair):
    half = pair.shape[-1] // 2
    return pair[..., :half] + pair[..., half:]


def square_grad(grad_square, features):
    feature_count = features.shape[-1]
    matrix = grad_square.reshape(features.shape + (feature_count,))
    return jnp.einsum("...fh,...h->...f", matrix, features, precision=exact_mode) + jnp.einsum(
        "...hf,...h->...f", matrix, features, precision=exact_mode
    )


def exchange_kernel(count, head_count, mode, x_ref, row_ref, out_ref, row_out, buf, row_buf, send, recv, row_send, row_recv):
    me = lax.axis_index("ctx")
    head = lax.axis_index("head")
    mesh_ids = pl.DeviceIdType.MESH
    barrier = pltpu.get_barrier_semaphore()
    for d in range(1, count):
        pl.semaphore_signal(
            barrier, inc=1, device_id=(lax.rem(me + d, count), head), device_id_type=mesh_ids
        )
    for d in range(1, head_count):
        pl.semaphore_signal(
            barrier, inc=1, device_id=(me, lax.rem(head + d, head_count)), device_id_type=mesh_ids
        )
    pl.semaphore_wait(barrier, count + head_count - 2)

    def wanted(source, target):
        return {"lower": source < target, "upper": source > target, "all": source != target}[mode]

    def ctx_copy(d):
        return pltpu.make_async_remote_copy(
            src_ref=x_ref,
            dst_ref=buf.at[me],
            send_sem=send.at[d],
            recv_sem=recv.at[me],
            device_id=(lax.rem(me + d, count), head),
            device_id_type=mesh_ids,
        )

    def row_copy(d):
        return pltpu.make_async_remote_copy(
            src_ref=row_ref,
            dst_ref=row_buf.at[head],
            send_sem=row_send.at[d],
            recv_sem=row_recv.at[head],
            device_id=(me, lax.rem(head + d, head_count)),
            device_id_type=mesh_ids,
        )

    def ctx_arrival(source):
        return pltpu.make_async_remote_copy(
            src_ref=x_ref,
            dst_ref=buf.at[source],
            send_sem=send.at[0],
            recv_sem=recv.at[source],
            device_id=(source, head),
            device_id_type=mesh_ids,
        )

    def row_arrival(source):
        return pltpu.make_async_remote_copy(
            src_ref=row_ref,
            dst_ref=row_buf.at[source],
            send_sem=row_send.at[0],
            recv_sem=row_recv.at[source],
            device_id=(me, source),
            device_id_type=mesh_ids,
        )

    for d in range(1, count):

        @pl.when(wanted(me, lax.rem(me + d, count)))
        def _():
            ctx_copy(d).start()

    for d in range(1, head_count):
        row_copy(d).start()

    row_out[...] = jnp.zeros_like(row_out)
    for source in range(head_count):

        @pl.when(source == head)
        def _():
            row_out[...] += row_ref[...]

        @pl.when(source != head)
        def _():
            row_arrival(source).wait_recv()
            row_out[...] += row_buf[source]

    out_ref[...] = jnp.zeros_like(out_ref)
    for source in range(count):
        if mode == "all":

            @pl.when(source == me)
            def _():
                out_ref[...] += x_ref[...].astype(jnp.float32)

        @pl.when(wanted(source, me))
        def _():
            ctx_arrival(source).wait_recv()
            out_ref[...] += buf[source].astype(jnp.float32)

    for d in range(1, count):

        @pl.when(wanted(me, lax.rem(me + d, count)))
        def _():
            ctx_copy(d).wait_send()

    for d in range(1, head_count):
        row_copy(d).wait_send()


def exchange(x, row, mode, collective_id):
    count = lax.axis_size("ctx")
    head_count = lax.axis_size("head")
    vmem = pl.BlockSpec(memory_space=pltpu.VMEM)
    return pl.pallas_call(
        functools.partial(exchange_kernel, count, head_count, mode),
        out_shape=(
            jax.ShapeDtypeStruct(x.shape, jnp.float32),
            jax.ShapeDtypeStruct(row.shape, jnp.float32),
        ),
        in_specs=[vmem, vmem],
        out_specs=(vmem, vmem),
        scratch_shapes=[
            pltpu.VMEM((count,) + x.shape, x.dtype),
            pltpu.VMEM((head_count,) + row.shape, jnp.float32),
            pltpu.SemaphoreType.DMA((count,)),
            pltpu.SemaphoreType.DMA((count,)),
            pltpu.SemaphoreType.DMA((head_count,)),
            pltpu.SemaphoreType.DMA((head_count,)),
        ],
        compiler_params=pltpu.CompilerParams(collective_id=collective_id, has_side_effects=True),
        cost_estimate=pl.CostEstimate(
            flops=count * x.size, bytes_accessed=40 * count * x.size, transcendentals=0
        ),
    )(x, row)


def pack(square, linear, square_den, linear_den, flat):
    groups, feature_count = linear_den.shape
    squares = feature_count * feature_count
    square_rows = square_den.reshape(groups, squares // HEAD_DIM, HEAD_DIM)
    linear_rows = jnp.pad(linear_den, ((0, 0), (0, HEAD_DIM - feature_count)))[:, None]
    small = jnp.concatenate([flat[:, None], linear_rows, square_rows], 1)
    small = jnp.pad(small, ((0, 0), (0, -small.shape[1] % 16), (0, 0)))
    return jnp.concatenate([square, linear, small], 1).reshape(-1, HEAD_DIM)


def unpack(packed, groups, feature_count):
    squares = feature_count * feature_count
    packed = packed.reshape(groups, -1, HEAD_DIM)
    top = squares + feature_count
    square_den = packed[:, top + 2 : top + 2 + squares // HEAD_DIM].reshape(groups, squares)
    return (
        packed[:, :squares],
        packed[:, squares:top],
        square_den,
        packed[:, top + 1, :feature_count],
        packed[:, top],
    )


def ring_gather(block):
    count = lax.axis_size("ctx")
    me = lax.axis_index("ctx")
    rows = block.shape[0]
    half = rows // 2
    ring = list(range(0, count, 2)) + list(range(1, count, 2))[::-1]
    place = [ring.index(i) for i in range(count)]
    position = jnp.array(place, jnp.int32)[me]
    ring_table = jnp.array(ring, jnp.int32)
    up_route = [(ring[p], ring[(p + 1) % count]) for p in range(count)]
    down_route = [(ring[(p + 1) % count], ring[p]) for p in range(count)]
    up, down = block[:half], block[half:]
    pieces = [(me, up, down, me)]
    for step in range(1, count):
        up = lax.ppermute(up, "ctx", up_route)
        down = lax.ppermute(down, "ctx", down_route)
        pieces.append(
            (
                ring_table[(position - step) % count],
                up,
                down,
                ring_table[(position + step) % count],
            )
        )
    return pieces


def after_hop(pieces, hop, *members):
    if hop >= len(pieces):
        return members
    up_owner, up, down, down_owner = pieces[hop]
    up, down, *members = lax.optimization_barrier((up, down, *members))
    pieces[hop] = (up_owner, up, down, down_owner)
    return members


def assemble(pieces, zero, rows):
    half = rows // 2
    count = len(pieces)
    full = jnp.broadcast_to(zero, (count * rows, pieces[0][1].shape[1]))
    for up_owner, up, down, down_owner in pieces:
        full = lax.dynamic_update_slice(full, up, (up_owner * rows, 0))
        full = lax.dynamic_update_slice(full, down, (down_owner * rows + half, 0))
    return full


def flipped(block, bit):
    return lax.ppermute(block, "head", [(i, i ^ bit) for i in range(4)])


def sum_heads(row):
    if lax.axis_size("head") != 4:
        return lax.psum(row, "head")
    row = row + flipped(row, 1)
    return row + flipped(row, 2)


def sum_from(block, sign):
    count = lax.axis_size("ctx")
    devices = range(count)
    total = jnp.zeros_like(block)
    for distance in range(1, count):
        route = [(i, i + sign * distance) for i in devices if i + sign * distance in devices]
        total = total + lax.ppermute(block, "ctx", route)
    return total


def gather_heads(block):
    if lax.axis_size("head") != 4:
        return lax.all_gather(block, "head", axis=1, tiled=True)
    head = lax.axis_index("head")
    rows, width = block.shape
    far = flipped(block, 2)
    near = flipped(block, 1)
    diagonal = flipped(far, 1)
    full = jnp.zeros((rows, 4 * width), block.dtype)
    for bit, member in ((0, block), (2, far), (1, near), (3, diagonal)):
        full = lax.dynamic_update_slice(full, member, (0, (head ^ bit) * width))
    return full


def scatter_heads(d_student, proj_full):
    def product(weights):
        return lax.dot_general(
            d_student, weights, (((1,), (1,)), ((), ())), preferred_element_type=jnp.float32
        ).astype(jnp.bfloat16)

    if lax.axis_size("head") != 4:
        terms = product(proj_full)
        return lax.psum_scatter(terms, "head", scatter_dimension=1, tiled=True).astype(jnp.float32)
    head = lax.axis_index("head")
    width = proj_full.shape[0] // 4

    def block(bit):
        return product(lax.dynamic_slice_in_dim(proj_full, (head ^ bit) * width, width, 0))

    diagonal = flipped(block(3), 1)
    far = block(2)
    pair = (far.astype(jnp.float32) + diagonal.astype(jnp.float32)).astype(jnp.bfloat16)
    far_sum = flipped(pair, 2)
    near = flipped(block(1), 1)
    own = block(0)
    return own.astype(jnp.float32) + near.astype(jnp.float32) + far_sum.astype(jnp.float32)


def window_tiles(extended, tok_rows):
    tile_count = tok_rows // WIN
    first = extended[:tok_rows].reshape((tile_count, WIN) + extended.shape[1:])
    second = extended[WIN:].reshape((tile_count, WIN) + extended.shape[1:])
    return jnp.concatenate([first, second], 1)


def local(queries, keys, values, feature_map, out_proj, teacher):
    tok_rows = queries.shape[0]
    kv_groups = keys.shape[1] // HEAD_DIM
    ctx_count = lax.axis_size("ctx")
    ctx_index = lax.axis_index("ctx")
    pieces = ring_gather(out_proj)
    query_heads = queries.reshape(tok_rows, kv_groups, GROUP, HEAD_DIM)
    key_heads = keys.reshape(tok_rows, kv_groups, HEAD_DIM)
    value_heads = values.reshape(tok_rows, kv_groups, HEAD_DIM)
    value_float = value_heads.astype(jnp.float32)
    query_features = jnp.einsum(
        "tgqe,gef->tgqf", query_heads, feature_map, preferred_element_type=jnp.float32
    )
    key_features = jnp.einsum(
        "tge,gef->tgf", key_heads, feature_map, preferred_element_type=jnp.float32
    )
    rim_rows = shifted(jnp.stack([keys[tok_rows - WIN :], values[tok_rows - WIN :]]), "ctx", 1)
    keys_ext = jnp.concatenate([rim_rows[0], keys], 0).reshape(tok_rows + WIN, kv_groups, HEAD_DIM)
    values_ext = jnp.concatenate([rim_rows[1], values], 0).reshape(
        tok_rows + WIN, kv_groups, HEAD_DIM
    )
    tile_count = tok_rows // WIN
    key_tiles = window_tiles(keys_ext, tok_rows)
    value_tiles = window_tiles(values_ext, tok_rows)
    query_tiles = query_heads.reshape(tile_count, WIN, kv_groups, GROUP, HEAD_DIM)
    causal = lax.broadcasted_iota(jnp.int32, (tok_rows, tok_rows), 0) >= lax.broadcasted_iota(
        jnp.int32, (tok_rows, tok_rows), 1
    )
    qk_inner = (
        jnp.einsum("tgqf,sgf->gqts", query_features, key_features, precision=exact_mode) / 4.0
    )
    kernel = jnp.where(causal, 1.0 + qk_inner + 0.5 * qk_inner * qk_inner, 0.0)
    numerator = jnp.einsum(
        "gqts,sge->tgqe", kernel.astype(jnp.bfloat16), value_heads, preferred_element_type=jnp.float32
    )
    denominator = jnp.transpose(jnp.sum(kernel, axis=-1), (2, 0, 1))
    query_tiles, numerator, denominator = after_hop(
        pieces, 1, query_tiles, numerator, denominator
    )
    scores = jnp.einsum(
        "ntgqe,nsge->ngqts", query_tiles, key_tiles, preferred_element_type=jnp.float32
    ) / math.sqrt(HEAD_DIM)
    tile_pos = lax.broadcasted_iota(jnp.int32, (tile_count, WIN, 2 * WIN), 0)
    query_pos = lax.broadcasted_iota(jnp.int32, (tile_count, WIN, 2 * WIN), 1)
    key_pos = lax.broadcasted_iota(jnp.int32, (tile_count, WIN, 2 * WIN), 2)
    distance = query_pos + WIN - key_pos
    allowed = (
        (distance >= 0)
        & (distance < WIN)
        & (ctx_index * tok_rows + tile_pos * WIN + key_pos - WIN >= 0)
    )
    allowed = allowed[:, None, None]
    scores = jnp.where(allowed, scores, -jnp.inf)
    row_max = jnp.max(scores, axis=-1, keepdims=True)
    weights = jnp.where(allowed, jnp.exp(scores - row_max), 0.0)
    attn_weights = (weights / jnp.sum(weights, axis=-1, keepdims=True)).astype(jnp.bfloat16)
    window_out = jnp.einsum(
        "ngqts,nsge->ntgqe", attn_weights, value_tiles, preferred_element_type=jnp.float32
    ).reshape(tok_rows, kv_groups, GROUP, HEAD_DIM)
    key_square = taylor_square(key_features)
    own_square_v = jnp.einsum("sgk,sge->gke", key_square, value_float, precision=exact_mode)
    own_linear_v = jnp.einsum("sgf,sge->gfe", key_features, value_float, precision=exact_mode)
    own_values = jnp.sum(value_float, axis=0)
    own_square_k = jnp.sum(key_square, axis=0)
    own_linear_k = jnp.sum(key_features, axis=0)
    no_row = jnp.zeros((8, HEAD_DIM), jnp.float32)
    packed = pack(own_square_v, own_linear_v, own_square_k, own_linear_k, own_values)
    earlier, window_out = after_hop(pieces, 2, sum_from(packed, 1), window_out)
    feature_count = feature_map.shape[2]
    past_square_v, past_linear_v, past_square_k, past_linear_k, past_values = unpack(
        earlier, kv_groups, feature_count
    )
    past_count = (ctx_index * tok_rows).astype(jnp.float32)
    query_square = taylor_square(query_features)
    numerator = (
        numerator
        + jnp.einsum("tgqk,gke->tgqe", query_square, past_square_v, precision=exact_mode) / 32.0
        + jnp.einsum("tgqf,gfe->tgqe", query_features, past_linear_v, precision=exact_mode) / 4.0
        + past_values[None, :, None, :]
    )
    denominator = (
        denominator
        + jnp.einsum("tgqk,gk->tgq", query_square, past_square_k, precision=exact_mode) / 32.0
        + jnp.einsum("tgqf,gf->tgq", query_features, past_linear_k, precision=exact_mode) / 4.0
        + past_count
    )
    linear_out = numerator / denominator[..., None]
    head_out = (
        (linear_out + window_out)
        .astype(jnp.bfloat16)
        .reshape(tok_rows, kv_groups * GROUP * HEAD_DIM)
    )
    head_out, zero = after_hop(pieces, 3, head_out, jnp.zeros((), jnp.bfloat16))
    all_heads = gather_heads(head_out)
    proj_full = assemble(pieces, zero, out_proj.shape[0])
    projected = jnp.dot(all_heads, proj_full, preferred_element_type=jnp.float32)
    student_out = projected.astype(jnp.bfloat16)
    residual = student_out.astype(jnp.float32) - teacher.astype(jnp.float32)
    total_rows = tok_rows * ctx_count
    squared = jnp.sum(residual * residual)
    d_student = (2.0 * residual / total_rows).astype(jnp.bfloat16)
    head_grad = scatter_heads(d_student, proj_full).reshape(
        tok_rows, kv_groups, GROUP, HEAD_DIM
    )
    numerator_grad = head_grad / denominator[..., None]
    denominator_grad = -jnp.sum(head_grad * linear_out, axis=-1) / denominator
    kernel_grad = (
        jnp.einsum(
            "tgqe,sge->gqts",
            two_terms(numerator_grad),
            jnp.concatenate([value_heads, value_heads], -1),
            preferred_element_type=jnp.float32,
        )
        + jnp.transpose(denominator_grad, (1, 2, 0))[..., None]
    )
    inner_grad = (jnp.where(causal, kernel_grad * (1.0 + qk_inner), 0.0) / 4.0).astype(
        jnp.bfloat16
    )
    query_grad = joined(
        jnp.einsum(
            "gqts,sgf->tgqf",
            inner_grad,
            two_terms(key_features),
            preferred_element_type=jnp.float32,
        )
    )
    key_grad = joined(
        jnp.einsum(
            "gqts,tgqf->sgf",
            inner_grad,
            two_terms(query_features),
            preferred_element_type=jnp.float32,
        )
    )
    query_square_grad = (
        jnp.einsum("tgqe,gke->tgqk", numerator_grad, past_square_v, precision=exact_mode)
        + denominator_grad[..., None] * past_square_k[None, :, None, :]
    ) / 32.0
    query_grad = (
        query_grad
        + (
            jnp.einsum("tgqe,gfe->tgqf", numerator_grad, past_linear_v, precision=exact_mode)
            + denominator_grad[..., None] * past_linear_k[None, :, None, :]
        )
        / 4.0
        + square_grad(query_square_grad, query_features)
    )
    own_back_square = jnp.einsum(
        "tgqk,tgqe->gke", query_square, numerator_grad, precision=exact_mode
    )
    own_back_linear = jnp.einsum(
        "tgqf,tgqe->gfe", query_features, numerator_grad, precision=exact_mode
    )
    own_den_square = jnp.einsum(
        "tgqk,tgq->gk", query_square, denominator_grad, precision=exact_mode
    )
    own_den_linear = jnp.einsum(
        "tgqf,tgq->gf", query_features, denominator_grad, precision=exact_mode
    )
    packed_back = pack(
        own_back_square,
        own_back_linear,
        own_den_square,
        own_den_linear,
        jnp.zeros((kv_groups, HEAD_DIM), jnp.float32),
    )
    later = sum_from(packed_back, -1)
    loss_row = sum_heads(jnp.full((8, HEAD_DIM), squared, jnp.float32))
    later_square, later_linear, later_den_square, later_den_linear, _ = unpack(
        later, kv_groups, feature_count
    )
    key_square_grad = (
        jnp.einsum("gke,sge->sgk", later_square, value_float, precision=exact_mode)
        + later_den_square[None]
    ) / 32.0
    key_grad = (
        key_grad
        + (
            jnp.einsum("gfe,sge->sgf", later_linear, value_float, precision=exact_mode)
            + later_den_linear[None]
        )
        / 4.0
        + square_grad(key_square_grad, key_features)
    )
    own_grad = jnp.einsum(
        "tgqe,tgqf->gef", query_heads.astype(jnp.float32), query_grad, precision=exact_mode
    ) + jnp.einsum("tge,tgf->gef", key_heads.astype(jnp.float32), key_grad, precision=exact_mode)
    packed_grad = jnp.concatenate([own_grad.reshape(-1, HEAD_DIM), loss_row], 0)
    summed, _ = exchange(packed_grad, no_row, "all", 0)
    feature_grad = summed[:-8].reshape(own_grad.shape)
    loss_value = summed[-8, 0] / (total_rows * D)
    return (student_out, loss_value, feature_grad)


FEATURE_PAIRS = 153
PAIR_ROWS = 160
CHUNKS = 8
STREAMS = 4


def pair_tables():
    j = np.arange(2 * HEAD_DIM)
    valid = j < FEATURE_PAIRS
    first = j % 17
    second = (first + j // 17) % 17
    select = np.zeros((2, 2 * HEAD_DIM, HEAD_DIM), np.float32)
    constant = np.zeros((2, 2 * HEAD_DIM), np.float32)
    for side, member in enumerate((first, second)):
        for row in np.nonzero(valid)[0]:
            if member[row] < 16:
                select[side, row, member[row]] = 1.0
            else:
                constant[side, row] = 1.0
    is_one = (first == 16).astype(int) + (second == 16).astype(int)
    coef = np.where(is_one == 2, 1.0, np.where(is_one == 1, 0.25, np.where(first == second, 1 / 32, 1 / 16)))
    coef = np.where(valid, coef, 0.0)
    bits = np.concatenate([select[0], select[1], np.eye(HEAD_DIM)], 0)
    rows = np.zeros((8, 2 * HEAD_DIM), np.float32)
    rows[0], rows[1], rows[2] = constant[0], constant[1], coef
    columns = np.zeros((2 * HEAD_DIM, HEAD_DIM), np.float32)
    columns[:, 0], columns[:, 1], columns[:, 2] = constant[0], constant[1], coef
    return bits, rows, columns


def mm(a, b):
    return lax.dot_general(a, b, (((1,), (0,)), ((), ())), preferred_element_type=jnp.float32)


def mm_t(a, b):
    return lax.dot_general(a, b, (((1,), (1,)), ((), ())), preferred_element_type=jnp.float32)


def split_terms(x):
    high = x.astype(jnp.bfloat16)
    return high, (x - high.astype(jnp.float32)).astype(jnp.bfloat16)


def fused_kernel(
    queries_in, keys_in, values_in, map_ref, proj_ref, teacher_ref, bits_ref, rows_ref, columns_ref,
    student_ref, grad_ref, loss_ref,
    proj_buf, heads_buf, sums, first_factor, second_factor, pairs_t, queries_t, slope, lin, den_inv,
    d_student, acc, queries_ref, teacher_buf, keys_ext, values_ext, ones_values, wide_map, wide_map_t, kernel_map,
    past_high, past_low, key_features, key_factor_a, key_factor_b, keys_t,
    state_own, state_x, state_low, state_up,
    send_1, send_2, send_3, recv_1, recv_2, recv_3,
    cross, grad_a, grad_b, back, back_own, back_x, back_sum, back_later, back_in, final_own, final_in, loss_acc, loss_own, loss_in,
    ring_send, ring_recv, own_sem, input_sem, teacher_sem, student_sem, rim_send, rim_recv, state_x_send, state_x_recv,
    state_up_send, state_up_recv, head_send, head_recv, s1_send, s1_recv, s2_send, s2_recv, s3_send, s3_recv,
    back_x_send, back_x_recv, back_send, back_recv, final_send, final_recv, loss_send, loss_recv,
):
    f32, bf16 = jnp.float32, jnp.bfloat16
    mesh_ids = pl.DeviceIdType.MESH
    ctx_count = 8
    tokens = queries_in.shape[0]
    half = tokens // 2
    width = proj_buf.shape[2]
    E = HEAD_DIM
    c = lax.axis_index("ctx")
    h = lax.axis_index("head")
    z = c // 2
    x = c % 2
    pos = jnp.where(x == 0, z, 7 - z)

    def ring_at(p):
        p = lax.rem(p + 16, 8)
        return jnp.where(p < 4, 2 * p, 2 * (7 - p) + 1)

    up, down = ring_at(pos + 1), ring_at(pos - 1)
    near = h + 1 - 2 * (h % 2)
    far = (h + 2) % 4
    diagonal = 3 - h

    def remote(src, dst, send, recv, ctx, head):
        return pltpu.make_async_remote_copy(
            src_ref=src, dst_ref=dst, send_sem=send, recv_sem=recv, device_id=(ctx, head), device_id_type=mesh_ids
        )

    inputs = [
        pltpu.make_async_copy(keys_in, keys_ext.at[pl.ds(WIN, tokens)], input_sem.at[0]),
        pltpu.make_async_copy(values_in, values_ext.at[pl.ds(WIN, tokens)], input_sem.at[1]),
        pltpu.make_async_copy(queries_in, queries_ref, input_sem.at[2]),
    ]
    barrier = pltpu.get_barrier_semaphore()
    for d in range(1, ctx_count):
        pl.semaphore_signal(barrier, inc=1, device_id=((c + d) % ctx_count, h), device_id_type=mesh_ids)
    for d in range(1, 4):
        pl.semaphore_signal(barrier, inc=1, device_id=(c, (h + d) % 4), device_id_type=mesh_ids)
    for copy in inputs:
        copy.start()
    pl.semaphore_wait(barrier, ctx_count + 2)

    def owner_rows(owner, d):
        return pl.ds(pl.multiple_of(owner * tokens + d * half, half), half)

    def hop(d, j, k):
        owner = ring_at(pos - k) if d == 0 else ring_at(pos + k)
        place = proj_buf.at[j, owner_rows(owner, d)]
        return remote(place, place, ring_send.at[d, j, k], ring_recv.at[d, j, k], up if d == 0 else down, h)

    def first_hop(d, j):
        place = proj_buf.at[j, owner_rows(c, d)]
        src = proj_ref.at[pl.ds(d * half, half), pl.ds(pl.multiple_of(j * width, width), width)]
        return remote(src, place, ring_send.at[d, j, 0], ring_recv.at[d, j, 0], up if d == 0 else down, h)

    def arrival(d, j, k):
        owner = ring_at(pos - 1 - k) if d == 0 else ring_at(pos + 1 + k)
        place = proj_buf.at[j, owner_rows(owner, d)]
        return remote(place, place, ring_send.at[d, j, k], ring_recv.at[d, j, k], up if d == 0 else down, h)

    def start_first(n):
        for d in (0, 1):
            first_hop(d, n).start()

    def service(group, n):
        k = n // STREAMS
        j = group * STREAMS + n % STREAMS
        for d in (0, 1):
            arrival(d, j, k - 1).wait_recv()
            hop(d, j, k).start()

    for s, (src, dst) in enumerate(((keys_in, keys_ext), (values_in, values_ext))):

        @pl.when(c < ctx_count - 1)
        def _():
            remote(
                src.at[pl.ds(tokens - WIN, WIN)], dst.at[pl.ds(0, WIN)], rim_send.at[s], rim_recv.at[s],
                lax.rem(c + 1, ctx_count), h,
            ).start()

        @pl.when(c == 0)
        def _():
            dst[pl.ds(0, WIN), :] = jnp.zeros((WIN, E), bf16)

        dst[pl.ds(WIN + tokens, WIN), :] = jnp.zeros((WIN, E), bf16)

    start_first(0)
    start_first(1)
    teacher_copy = pltpu.make_async_copy(teacher_ref, teacher_buf, teacher_sem.at[0])
    teacher_copy.start()

    def own_copy(j):
        return pltpu.make_async_copy(
            proj_ref.at[:, pl.ds(pl.multiple_of(j * width, width), width)],
            proj_buf.at[j, pl.ds(pl.multiple_of(c * tokens, tokens), tokens)],
            own_sem.at[j],
        )

    for j in range(CHUNKS):
        own_copy(j).start()

    eye = bits_ref[pl.ds(4 * E, E), :]
    map_rows = jnp.concatenate([map_ref[...], jnp.zeros((E - map_ref.shape[0], E), bf16)], 0)
    map_wide = mm_t(eye, map_rows).astype(bf16)
    for s in range(2):
        select = bits_ref[pl.ds(s * 2 * E, 2 * E), :]
        wide_map[s] = mm_t(map_wide, select).astype(bf16)
        wide_map_t[s] = mm_t(select, map_wide).astype(bf16)
    inputs[0].wait()
    inputs[1].wait()
    keys = keys_ext[pl.ds(WIN, tokens), :]
    features = mm(keys, map_wide)
    feature_high, feature_low = split_terms(features)
    key_features[0] = feature_high
    key_features[1] = feature_low
    inner = (mm_t(map_wide, feature_high) + mm_t(map_wide, feature_low)) * 0.25
    inner_high, inner_low = split_terms(inner)
    kernel_map[pl.ds(0, E), :] = inner_high
    kernel_map[pl.ds(E, E), :] = inner_low
    keys_t[...] = mm_t(eye, keys).astype(bf16)
    key_a = mm(keys, wide_map[0]) + rows_ref[pl.ds(0, 1), :]
    key_b = mm(keys, wide_map[1]) + rows_ref[pl.ds(1, 1), :]
    key_factor_a[...] = (key_a * rows_ref[pl.ds(2, 1), :]).astype(bf16)
    key_factor_b[...] = (key_b * rows_ref[pl.ds(2, 1), :]).astype(bf16)
    ones_values[:, pl.ds(0, E)] = values_ext[pl.ds(WIN, tokens), :]
    ones_values[:, pl.ds(E, E)] = jnp.ones((tokens, E), bf16)
    key_a_t = mm_t(wide_map_t[0], keys) + columns_ref[:, 0:1]
    key_b_t = mm_t(wide_map_t[1], keys) + columns_ref[:, 1:2]
    key_high, key_low = split_terms(key_a_t * key_b_t * columns_ref[:, 2:3])
    state = mm(key_high, ones_values[...]) + mm(key_low, ones_values[...])

    def store_state(ref, value, den_row):
        ref[pl.ds(0, PAIR_ROWS), :] = value[:PAIR_ROWS]
        ref[pl.ds(PAIR_ROWS, 8), :] = den_row[:, :E]
        ref[pl.ds(PAIR_ROWS + 8, 8), :] = den_row[:, E:]

    store_state(state_own, state[:, :E], jnp.transpose(state[:, E:])[:8])
    state_x_copy = remote(state_own, state_x, state_x_send.at[0], state_x_recv.at[0], c + 1 - 2 * x, h)
    state_x_copy.start()
    start_first(2)
    start_first(3)
    inputs[2].wait()

    def state_up_copy():
        return remote(state_up, state_low, state_up_send.at[0], state_up_recv.at[0], lax.rem(c + 2, ctx_count), h)

    def chain_step(level):
        if level == 0:
            state_x_copy.wait_recv()

            @pl.when(z == 0)
            def _():
                state_low[...] = jnp.zeros_like(state_low)

        else:

            @pl.when(z == level)
            def _():
                state_up_copy().wait_recv()

        if level < 3:

            @pl.when(z == level)
            def _():
                state_up[...] = state_low[...] + state_own[...] + state_x[...]
                state_up_copy().start()

    for s in range(2):

        @pl.when(c > 0)
        def _():
            dst = (keys_ext, values_ext)[s]
            remote(
                dst.at[pl.ds(0, WIN)], dst.at[pl.ds(0, WIN)], rim_send.at[s], rim_recv.at[s], c, h
            ).wait_recv()

    def query_tile(i, hp):
        token = pl.multiple_of(i * E, E)
        both = queries_ref[pl.ds(token, E), pl.ds(pl.multiple_of(hp * 2 * E, 2 * E), 2 * E)]
        return jnp.concatenate([both[:, :E], both[:, E:]], 0)

    for i in range(4):
        reach = (i + 1) * E

        def local_tile(hp, carry):
            tile = i * 4 + hp
            q = query_tile(i, hp)
            u = mm(jnp.concatenate([q, q], 1), kernel_map[:, pl.ds(0, reach)])
            row = lax.broadcasted_iota(jnp.int32, (2 * E, reach), 0) % E + i * E
            causal = row >= lax.broadcasted_iota(jnp.int32, (2 * E, reach), 1)
            kernel = jnp.where(causal, 1.0 + u + 0.5 * u * u, 0.0).astype(bf16)
            slope[tile, :, pl.ds(0, reach)] = jnp.where(causal, 0.25 + 0.25 * u, 0.0).astype(bf16)
            both = mm(kernel, ones_values[pl.ds(0, reach), :])
            lin[tile] = both[:, :E]
            den_inv[tile] = both[:, E:]
            scores = mm_t(q, keys_ext[pl.ds(i * E, 2 * E), :]) / math.sqrt(HEAD_DIM)
            token = lax.broadcasted_iota(jnp.int32, (2 * E, 2 * E), 0) % E
            place = lax.broadcasted_iota(jnp.int32, (2 * E, 2 * E), 1)
            distance = token + WIN - place
            allowed = (distance >= 0) & (distance < WIN) & (c * tokens + i * E + place - WIN >= 0)
            scores = jnp.where(allowed, scores, -jnp.inf)
            top = jnp.max(scores, axis=-1, keepdims=True)
            weights = jnp.where(allowed, jnp.exp(scores - top), 0.0)
            weights = (weights / jnp.sum(weights, axis=-1, keepdims=True)).astype(bf16)
            sums[tile, pl.ds(0, 2 * E), pl.ds(0, E)] = mm(weights, values_ext[pl.ds(i * E, 2 * E), :])
            first_factor[tile] = (mm(q, wide_map[0]) + rows_ref[pl.ds(0, 1), :]).astype(bf16)
            second_factor[tile] = (mm(q, wide_map[1]) + rows_ref[pl.ds(1, 1), :]).astype(bf16)
            pair_a = mm_t(wide_map_t[0], q) + columns_ref[:, 0:1]
            pair_b = mm_t(wide_map_t[1], q) + columns_ref[:, 1:2]
            pairs_t[tile] = (pair_a * pair_b).astype(bf16)[:PAIR_ROWS]
            queries_t[tile] = mm_t(eye, q).astype(bf16)
            service(0, STREAMS + tile)
            return carry

        lax.fori_loop(0, 4, local_tile, 0)
        chain_step(i)

    past = jnp.where(z > 0, state_low[...], 0.0) + jnp.where(x == 1, state_x[...], 0.0)
    past_rows = jnp.concatenate([past[PAIR_ROWS : PAIR_ROWS + 8], past[PAIR_ROWS + 8 :]], 1)
    past_den = jnp.transpose(jnp.broadcast_to(past_rows[:1], (E, 2 * E)))
    past_values = jnp.concatenate([past[:PAIR_ROWS], jnp.zeros((2 * E - PAIR_ROWS, E), f32)], 0)
    high, low = split_terms(jnp.concatenate([past_values, past_den], 1))
    past_high[...] = high
    past_low[...] = low

    def head_copy(i, d, source):
        piece = heads_buf.at[source, pl.ds(pl.multiple_of(i * E, E), E)]
        return remote(piece, piece, head_send.at[d, i], head_recv.at[source, i], c, (h + d) % 4)

    def past_tiles(i, carry):
        def past_tile(hp, carry):
            tile = i * 4 + hp
            q = query_tile(i, hp)
            pair = (mm(q, wide_map[0]) + rows_ref[pl.ds(0, 1), :]) * (mm(q, wide_map[1]) + rows_ref[pl.ds(1, 1), :])
            pair_high, pair_low = split_terms(pair)
            both = mm(pair_high, past_high[...]) + mm(pair_low, past_high[...]) + mm(pair_high, past_low[...])
            den = den_inv[tile] + both[:, E:]
            value = (lin[tile] + both[:, :E]) / den
            lin[tile] = value
            den_inv[tile] = 1.0 / den
            out = (value + sums[tile, pl.ds(0, 2 * E), pl.ds(0, E)]).astype(bf16)
            heads_buf[
                h, pl.ds(pl.multiple_of(i * E, E), E), pl.ds(pl.multiple_of(hp * 2 * E, 2 * E), 2 * E)
            ] = jnp.concatenate([out[:E], out[E:]], 1)
            return carry

        lax.fori_loop(0, 4, past_tile, 0)
        for d in range(1, 4):
            head_copy(i, d, h).start()
        service(0, STREAMS + 16 + 2 * i)
        service(0, STREAMS + 17 + 2 * i)
        return carry

    lax.fori_loop(0, 4, past_tiles, 0)
    for n in range(STREAMS):
        start_first(STREAMS + n)
    teacher_copy.wait()
    for j in range(CHUNKS):
        own_copy(j).wait()
    loss_acc[...] = jnp.zeros_like(loss_acc)
    for j in range(STREAMS):
        for d in (0, 1):
            arrival(d, j, 6).wait_recv()

    def second_service(n, carry):
        service(1, STREAMS + n)
        return carry

    lax.fori_loop(0, 3 * STREAMS, second_service, 0)
    for i in range(4):
        for d in range(1, 4):
            head_copy(i, d, (h + d) % 4).wait_recv()

    def student_copy(j):
        return pltpu.make_async_copy(
            teacher_buf.at[:, pl.ds(pl.multiple_of(j * width, width), width)],
            student_ref.at[:, pl.ds(pl.multiple_of(j * width, width), width)],
            student_sem.at[j],
        )

    def finish_columns(j, product):
        student = product.astype(bf16)
        columns = pl.ds(pl.multiple_of(j * width, width), width)
        residual = student.astype(f32) - teacher_buf[:, columns].astype(f32)
        teacher_buf[:, columns] = student
        loss_acc[...] += jnp.sum((residual * residual).reshape(tokens // 8, 8, width), axis=0)
        d_student[j] = (residual * (2.0 / (tokens * ctx_count))).astype(bf16)
        student_copy(j).start()

    def first_columns(j, carry):
        product = mm(heads_buf[0], proj_buf[j, pl.ds(0, 8 * E), :])
        for s in range(1, 4):
            product += mm(heads_buf[s], proj_buf[j, pl.ds(s * 8 * E, 8 * E), :])
        finish_columns(j, product)
        service(1, 4 * STREAMS + j)
        return carry

    lax.fori_loop(0, STREAMS, first_columns, 0)

    def block_sum(group, r):
        rows = pl.ds(pl.multiple_of(r * width, width), width)
        total = mm_t(d_student[group * STREAMS], proj_buf[group * STREAMS, rows, :])
        for j in range(1, STREAMS):
            total += mm_t(d_student[group * STREAMS + j], proj_buf[group * STREAMS + j, rows, :])
        return total

    def first_sums(n, carry):
        sums[2 * n] = block_sum(0, 2 * n)
        sums[2 * n + 1] = block_sum(0, 2 * n + 1)
        service(1, 5 * STREAMS + n)
        return carry

    lax.fori_loop(0, 8, first_sums, 0)

    def partial_product(owner, d, j):
        place = pl.multiple_of((owner % 2) * tokens + d * half, half)
        left = heads_buf[owner // 2, :, pl.ds(place, half)]
        return mm(left, proj_buf[j, owner_rows(owner, d), :])

    def second_early(s, carry):
        j = STREAMS + s
        total = partial_product(c, 0, j) + partial_product(c, 1, j)
        for k in range(6):
            total += partial_product(ring_at(pos - 1 - k), 0, j) + partial_product(ring_at(pos + 1 + k), 1, j)
        acc[s] = total
        return carry

    lax.fori_loop(0, STREAMS, second_early, 0)

    def second_last(s, carry):
        j = STREAMS + s
        for d in (0, 1):
            arrival(d, j, 6).wait_recv()
        finish_columns(
            j, acc[s] + partial_product(ring_at(pos - 7), 0, j) + partial_product(ring_at(pos + 7), 1, j)
        )
        return carry

    lax.fori_loop(0, STREAMS, second_last, 0)

    def copy_1(p):
        return remote(send_1.at[p], recv_1.at[p], s1_send.at[p], s1_recv.at[p], c, near)

    def copy_2(p):
        return remote(send_2.at[p], recv_2.at[p], s2_send.at[p], s2_recv.at[p], c, near)

    def copy_3(p):
        return remote(send_3.at[p], recv_3.at[p], s3_send.at[p], s3_recv.at[p], c, far)

    def step_1(p):
        r = diagonal * 4 + p
        send_1[p] = (sums[r] + block_sum(1, r)).astype(bf16)
        copy_1(p).start()

    def step_2(p):
        r = far * 4 + p
        total = sums[r] + block_sum(1, r)
        copy_1(p).wait_recv()
        send_3[p] = (total + recv_1[p].astype(f32)).astype(bf16)
        copy_3(p).start()

    step_1(0)
    step_1(1)

    def step_both(p, carry):
        step_2(p)
        step_1(p + 2)
        return carry

    lax.fori_loop(0, 2, step_both, 0)
    step_2(2)
    step_2(3)

    def step_near(p, carry):
        r = near * 4 + p
        send_2[p] = (sums[r] + block_sum(1, r)).astype(bf16)
        copy_2(p).start()
        return carry

    lax.fori_loop(0, 4, step_near, 0)

    def step_own(p, carry):
        r = h * 4 + p
        sums[r] += block_sum(1, r)
        return carry

    lax.fori_loop(0, 4, step_own, 0)

    loss_own[...] = loss_acc[:, :E] + loss_acc[:, E:]

    def loss_copy(d, source):
        return remote(loss_own, loss_in.at[source], loss_send.at[d], loss_recv.at[source], c, (h + d) % 4)

    for d in range(1, 4):
        loss_copy(d, h).start()

    cross[...] = jnp.zeros_like(cross)
    grad_a[...] = jnp.zeros_like(grad_a)
    grad_b[...] = jnp.zeros_like(grad_b)
    back[...] = jnp.zeros_like(back)

    def grad_piece(p, carry):
        copy_2(p).wait_recv()
        copy_3(p).wait_recv()
        for i in range(4):
            reach = (i + 1) * E
            tile = i * 4 + p
            rows = pl.ds(i * E, E)
            g = sums[h * 4 + p, rows, :] + recv_2[p, rows, :].astype(f32) + recv_3[p, rows, :].astype(f32)
            g = jnp.concatenate([g[:, :E], g[:, E:]], 0)
            inverse = den_inv[tile]
            upper = (g * inverse).astype(bf16)
            lower = -jnp.sum(upper.astype(f32) * lin[tile], axis=-1, keepdims=True)
            lower = jnp.broadcast_to(lower, (2 * E, E))
            lower_high = lower.astype(bf16).astype(f32)
            lane = lax.broadcasted_iota(jnp.int32, (2 * E, E), 1)
            lower = (jnp.where(lane < E // 2, lower_high, lower - lower_high) * (2.0 / E)).astype(bf16)
            wide = jnp.concatenate([upper, lower], 1)
            weight = mm_t(wide, ones_values[pl.ds(0, reach), :]) * slope[tile, :, pl.ds(0, reach)].astype(f32)
            cross[:, pl.ds(0, reach)] += mm(queries_t[tile], weight.astype(bf16))
            pair_grad = mm_t(wide, past_high[...]) + mm_t(wide, past_low[...])
            grad_a[...] += mm(queries_t[tile], (pair_grad * second_factor[tile].astype(f32)).astype(bf16))
            grad_b[...] += mm(queries_t[tile], (pair_grad * first_factor[tile].astype(f32)).astype(bf16))
            back[...] += mm(pairs_t[tile], wide)
        return carry

    lax.fori_loop(0, 4, grad_piece, 0)

    back_den = jnp.transpose(
        jnp.concatenate([back[:, pl.ds(E, E)], jnp.zeros((2 * E - PAIR_ROWS, E), f32)], 0)
    )
    back_den = (back_den[:8] + back_den[E // 2 : E // 2 + 8]) * (E // 2)
    store_state(back_own, back[:, pl.ds(0, E)], back_den)
    back_x_copy = remote(back_own, back_x, back_x_send.at[0], back_x_recv.at[0], c + 1 - 2 * x, h)
    back_x_copy.start()

    def back_copy(level):
        return remote(back_sum, back_in.at[z], back_send.at[level], back_recv.at[z], 2 * level + x, h)

    def back_arrival(level):
        return remote(back_sum, back_in.at[level], back_send.at[level], back_recv.at[level], c, h)

    cross_high, cross_low = split_terms(cross[...])
    grad = mm(cross_high, key_features[0]) + mm(cross_high, key_features[1]) + mm(cross_low, key_features[0])
    keys = keys_ext[pl.ds(WIN, tokens), :]
    mixed = jnp.transpose(mm(cross_high, keys) + mm(cross_low, keys))
    mixed_high, mixed_low = split_terms(mixed)
    map_rows = jnp.concatenate([map_ref[...], jnp.zeros((E - map_ref.shape[0], E), bf16)], 0)
    map_wide = mm_t(bits_ref[pl.ds(4 * E, E), :], map_rows).astype(bf16)
    grad += mm(mixed_high, map_wide) + mm(mixed_low, map_wide)

    back_x_copy.wait_recv()
    back_sum[...] = back_own[...] + back_x[...]
    for level in range(3):

        @pl.when(level < z)
        def _():
            back_copy(level).start()

    back_later[...] = jnp.where(x == 0, back_x[...], 0.0)
    for level in range(1, 4):

        @pl.when(level > z)
        def _():
            back_arrival(level).wait_recv()
            back_later[...] += back_in[level]

    later_values = jnp.concatenate([back_later[pl.ds(0, PAIR_ROWS), :], jnp.zeros((2 * E - PAIR_ROWS, E), f32)], 0)
    later_high, later_low = split_terms(later_values)
    pair_grad = mm_t(values_ext[pl.ds(WIN, tokens), :], later_high)
    pair_grad += mm_t(values_ext[pl.ds(WIN, tokens), :], later_low)
    pair_grad += jnp.concatenate(
        [back_later[pl.ds(PAIR_ROWS, 1), :], back_later[pl.ds(PAIR_ROWS + 8, 1), :]], 1
    )
    total_a = grad_a[...] + mm(keys_t[...], (pair_grad * key_factor_b[...].astype(f32)).astype(bf16))
    total_b = grad_b[...] + mm(keys_t[...], (pair_grad * key_factor_a[...].astype(f32)).astype(bf16))
    for s, total in enumerate((total_a, total_b)):
        total_high, total_low = split_terms(total)
        select = bits_ref[pl.ds(s * 2 * E, 2 * E), :]
        grad += mm(total_high, select) + mm(total_low, select)
    final_own[pl.ds(0, 16), :] = jnp.transpose(grad)[:16]
    loss_sum = loss_own[...]
    for d in range(1, 4):
        loss_copy(d, (h + d) % 4).wait_recv()
        loss_sum += loss_in[(h + d) % 4]
    final_own[pl.ds(16, 8), :] = loss_sum

    def final_copy(d, source):
        return remote(final_own, final_in.at[source], final_send.at[d], final_recv.at[source], (c + d) % ctx_count, h)

    for d in range(1, ctx_count):
        final_copy(d, c).start()
    final_in[c] = final_own[...]
    for d in range(1, ctx_count):
        final_copy(d, (c + d) % ctx_count).wait_recv()
    final = final_in[0]
    for s in range(1, ctx_count):
        final += final_in[s]
    grad_ref[...] = final[:16]
    loss_ref[...] = jnp.broadcast_to(jnp.sum(final[16:], keepdims=True) / (tokens * ctx_count * D), (8, E))

    for j in range(CHUNKS):
        student_copy(j).wait()
        for d in (0, 1):
            first_hop(d, j).wait_send()
            for k in range(1, 7):
                hop(d, j, k).wait_send()
    for s in range(2):

        @pl.when(c < ctx_count - 1)
        def _():
            dst = (keys_ext, values_ext)[s]
            src = (keys_in, values_in)[s]
            remote(
                src.at[pl.ds(tokens - WIN, WIN)], dst.at[pl.ds(0, WIN)], rim_send.at[s], rim_recv.at[s],
                lax.rem(c + 1, ctx_count), h,
            ).wait_send()

    state_x_copy.wait_send()

    @pl.when(z < 3)
    def _():
        state_up_copy().wait_send()

    back_x_copy.wait_send()
    for level in range(3):

        @pl.when(level < z)
        def _():
            back_copy(level).wait_send()

    for d in range(1, 4):
        loss_copy(d, h).wait_send()
        for i in range(4):
            head_copy(i, d, h).wait_send()
    for p in range(4):
        copy_1(p).wait_send()
        copy_2(p).wait_send()
        copy_3(p).wait_send()
    for d in range(1, ctx_count):
        final_copy(d, c).wait_send()


def deliver_kernel(student_ref, grad_ref, loss_ref, student_out, grad_out, loss_out, buffer, sem, out_sem):
    part = student_ref.shape[0] // 4
    rows = [pl.ds(s * part, part) for s in range(4)]
    reads = [pltpu.make_async_copy(student_ref.at[r], buffer.at[r], sem.at[s]) for s, r in enumerate(rows)]
    writes = [pltpu.make_async_copy(buffer.at[r], student_out.at[r], out_sem.at[s]) for s, r in enumerate(rows)]
    for copy in reads:
        copy.start()
    grad_out[...] = grad_ref[...]
    loss_out[0, 0] = jnp.max(loss_ref[...])
    for read, write in zip(reads, writes):
        read.wait()
        write.start()
    for copy in writes:
        copy.wait()


def fused_local(queries, keys, values, feature_map, out_proj, teacher):
    tokens = queries.shape[0]
    columns = out_proj.shape[1]
    rows = tokens * 8
    width = columns // CHUNKS
    E = HEAD_DIM
    bf16, f32 = jnp.bfloat16, jnp.float32
    bits, row_table, column_table = pair_tables()
    vmem = pl.BlockSpec(memory_space=pltpu.VMEM)
    anywhere = pl.BlockSpec(memory_space=pl.ANY)
    dma = pltpu.SemaphoreType.DMA
    state = (PAIR_ROWS + 16, E)
    scratch = [
        ((CHUNKS, rows, width), bf16),
        ((4, tokens, 8 * E), bf16),
        ((16, tokens, width), f32),
        ((16, 2 * E, 2 * E), bf16),
        ((16, 2 * E, 2 * E), bf16),
        ((16, PAIR_ROWS, 2 * E), bf16),
        ((16, E, 2 * E), bf16),
        ((16, 2 * E, tokens), bf16),
        ((16, 2 * E, E), f32),
        ((16, 2 * E, E), f32),
        ((CHUNKS, tokens, width), bf16),
        ((STREAMS, tokens, width), f32),
        ((tokens, 8 * E), bf16),
        ((tokens, columns), bf16),
        ((tokens + 2 * WIN, E), bf16),
        ((tokens + 2 * WIN, E), bf16),
        ((tokens, 2 * E), bf16),
        ((2, E, 2 * E), bf16),
        ((2, 2 * E, E), bf16),
        ((2 * E, tokens), bf16),
        ((2 * E, 2 * E), bf16),
        ((2 * E, 2 * E), bf16),
        ((2, tokens, E), bf16),
        ((tokens, 2 * E), bf16),
        ((tokens, 2 * E), bf16),
        ((E, tokens), bf16),
        (state, f32),
        (state, f32),
        (state, f32),
        (state, f32),
        ((4, tokens, width), bf16),
        ((4, tokens, width), bf16),
        ((4, tokens, width), bf16),
        ((4, tokens, width), bf16),
        ((4, tokens, width), bf16),
        ((4, tokens, width), bf16),
        ((E, tokens), f32),
        ((E, 2 * E), f32),
        ((E, 2 * E), f32),
        ((PAIR_ROWS, 2 * E), f32),
        (state, f32),
        (state, f32),
        (state, f32),
        (state, f32),
        ((4,) + state, f32),
        ((24, E), f32),
        ((8, 24, E), f32),
        ((8, width), f32),
        ((8, E), f32),
        ((4, 8, E), f32),
    ]
    semaphores = [
        (2, CHUNKS, 7), (2, CHUNKS, 7), (CHUNKS,), (3,), (1,), (CHUNKS,), (2,), (2,), (1,), (1,), (1,), (1,), (4, 4), (4, 4),
        (4,), (4,), (4,), (4,), (4,), (4,), (1,), (1,), (4,), (4,), (8,), (8,), (4,), (4,),
    ]
    student, grad, loss = pl.pallas_call(
        fused_kernel,
        out_shape=(
            jax.ShapeDtypeStruct((tokens, columns), bf16),
            jax.ShapeDtypeStruct((feature_map.shape[2], E), f32),
            jax.ShapeDtypeStruct((8, E), f32),
        ),
        in_specs=[anywhere, anywhere, anywhere, vmem, anywhere, anywhere, vmem, vmem, vmem],
        out_specs=(anywhere, vmem, vmem),
        scratch_shapes=[pltpu.VMEM(shape, kind) for shape, kind in scratch] + [dma(shape) for shape in semaphores],
        compiler_params=pltpu.CompilerParams(
            collective_id=0, has_side_effects=True, vmem_limit_bytes=63 * 1024 * 1024
        ),
        cost_estimate=pl.CostEstimate(flops=30_000_000_000, bytes_accessed=40_000_000, transcendentals=2_000_000),
    )(
        queries, keys, values, feature_map[0].T, out_proj, teacher,
        jnp.asarray(bits, bf16), jnp.asarray(row_table, f32), jnp.asarray(column_table, f32),
    )
    student, grad, loss = pl.pallas_call(
        deliver_kernel,
        out_shape=(
            jax.ShapeDtypeStruct(student.shape, bf16),
            jax.ShapeDtypeStruct(grad.shape, f32),
            jax.ShapeDtypeStruct((1, 1), f32),
        ),
        in_specs=[anywhere, vmem, vmem],
        out_specs=(anywhere, vmem, pl.BlockSpec(memory_space=pltpu.SMEM)),
        scratch_shapes=[pltpu.VMEM(student.shape, bf16), dma((4,)), dma((4,))],
        cost_estimate=pl.CostEstimate(flops=0, bytes_accessed=2 * student.size * 2, transcendentals=0),
    )(student, grad, loss)
    return student, loss.reshape(()), grad.T[None]


def fits_fused(mesh):
    return mesh.shape["ctx"] == 8 and mesh.shape["head"] == 4


def solution(mesh):
    return jax.shard_map(
        fused_local if fits_fused(mesh) else local,
        mesh=mesh,
        in_specs=(
            P("ctx", "head"),
            P("ctx", "head"),
            P("ctx", "head"),
            P("head", None, None),
            P("ctx", "head"),
            P("ctx", "head"),
        ),
        out_specs=(P("ctx", "head"), P(), P("head", None, None)),
        check_vma=False,
    )
```

```python
import functools
import math

import jax
import jax.numpy as jnp
import numpy as np
from jax import lax
from jax.experimental import pallas as pl
from jax.experimental.pallas import tpu as pltpu
from jax.sharding import PartitionSpec as P

D = 8192
HEAD_DIM = 128
GROUP = 8
WIN = 64


exact_mode = lax.Precision.HIGHEST


def shifted(block, axis, distance):
    devices = range(lax.axis_size(axis))
    route = [(i - distance, i) for i in devices if i - distance in devices]
    return lax.ppermute(block, axis, route)


def taylor_square(features):
    feature_count = features.shape[-1]
    outer = features[..., :, None] * features[..., None, :]
    return outer.reshape(features.shape[:-1] + (feature_count * feature_count,))


def two_terms(x):
    high = lax.reduce_precision(x, 8, 7)
    return jnp.concatenate([high.astype(jnp.bfloat16), (x - high).astype(jnp.bfloat16)], -1)


def joined(pair):
    half = pair.shape[-1] // 2
    return pair[..., :half] + pair[..., half:]


def square_grad(grad_square, features):
    feature_count = features.shape[-1]
    matrix = grad_square.reshape(features.shape + (feature_count,))
    return jnp.einsum("...fh,...h->...f", matrix, features, precision=exact_mode) + jnp.einsum(
        "...hf,...h->...f", matrix, features, precision=exact_mode
    )


def exchange_kernel(count, head_count, mode, x_ref, row_ref, out_ref, row_out, buf, row_buf, send, recv, row_send, row_recv):
    me = lax.axis_index("ctx")
    head = lax.axis_index("head")
    mesh_ids = pl.DeviceIdType.MESH
    barrier = pltpu.get_barrier_semaphore()
    for d in range(1, count):
        pl.semaphore_signal(
            barrier, inc=1, device_id=(lax.rem(me + d, count), head), device_id_type=mesh_ids
        )
    for d in range(1, head_count):
        pl.semaphore_signal(
            barrier, inc=1, device_id=(me, lax.rem(head + d, head_count)), device_id_type=mesh_ids
        )
    pl.semaphore_wait(barrier, count + head_count - 2)

    def wanted(source, target):
        return {"lower": source < target, "upper": source > target, "all": source != target}[mode]

    def ctx_copy(d):
        return pltpu.make_async_remote_copy(
            src_ref=x_ref,
            dst_ref=buf.at[me],
            send_sem=send.at[d],
            recv_sem=recv.at[me],
            device_id=(lax.rem(me + d, count), head),
            device_id_type=mesh_ids,
        )

    def row_copy(d):
        return pltpu.make_async_remote_copy(
            src_ref=row_ref,
            dst_ref=row_buf.at[head],
            send_sem=row_send.at[d],
            recv_sem=row_recv.at[head],
            device_id=(me, lax.rem(head + d, head_count)),
            device_id_type=mesh_ids,
        )

    def ctx_arrival(source):
        return pltpu.make_async_remote_copy(
            src_ref=x_ref,
            dst_ref=buf.at[source],
            send_sem=send.at[0],
            recv_sem=recv.at[source],
            device_id=(source, head),
            device_id_type=mesh_ids,
        )

    def row_arrival(source):
        return pltpu.make_async_remote_copy(
            src_ref=row_ref,
            dst_ref=row_buf.at[source],
            send_sem=row_send.at[0],
            recv_sem=row_recv.at[source],
            device_id=(me, source),
            device_id_type=mesh_ids,
        )

    for d in range(1, count):

        @pl.when(wanted(me, lax.rem(me + d, count)))
        def _():
            ctx_copy(d).start()

    for d in range(1, head_count):
        row_copy(d).start()

    row_out[...] = jnp.zeros_like(row_out)
    for source in range(head_count):

        @pl.when(source == head)
        def _():
            row_out[...] += row_ref[...]

        @pl.when(source != head)
        def _():
            row_arrival(source).wait_recv()
            row_out[...] += row_buf[source]

    out_ref[...] = jnp.zeros_like(out_ref)
    for source in range(count):
        if mode == "all":

            @pl.when(source == me)
            def _():
                out_ref[...] += x_ref[...].astype(jnp.float32)

        @pl.when(wanted(source, me))
        def _():
            ctx_arrival(source).wait_recv()
            out_ref[...] += buf[source].astype(jnp.float32)

    for d in range(1, count):

        @pl.when(wanted(me, lax.rem(me + d, count)))
        def _():
            ctx_copy(d).wait_send()

    for d in range(1, head_count):
        row_copy(d).wait_send()


def exchange(x, row, mode, collective_id):
    count = lax.axis_size("ctx")
    head_count = lax.axis_size("head")
    vmem = pl.BlockSpec(memory_space=pltpu.VMEM)
    return pl.pallas_call(
        functools.partial(exchange_kernel, count, head_count, mode),
        out_shape=(
            jax.ShapeDtypeStruct(x.shape, jnp.float32),
            jax.ShapeDtypeStruct(row.shape, jnp.float32),
        ),
        in_specs=[vmem, vmem],
        out_specs=(vmem, vmem),
        scratch_shapes=[
            pltpu.VMEM((count,) + x.shape, x.dtype),
            pltpu.VMEM((head_count,) + row.shape, jnp.float32),
            pltpu.SemaphoreType.DMA((count,)),
            pltpu.SemaphoreType.DMA((count,)),
            pltpu.SemaphoreType.DMA((head_count,)),
            pltpu.SemaphoreType.DMA((head_count,)),
        ],
        compiler_params=pltpu.CompilerParams(collective_id=collective_id, has_side_effects=True),
        cost_estimate=pl.CostEstimate(
            flops=count * x.size, bytes_accessed=40 * count * x.size, transcendentals=0
        ),
    )(x, row)


def pack(square, linear, square_den, linear_den, flat):
    groups, feature_count = linear_den.shape
    squares = feature_count * feature_count
    square_rows = square_den.reshape(groups, squares // HEAD_DIM, HEAD_DIM)
    linear_rows = jnp.pad(linear_den, ((0, 0), (0, HEAD_DIM - feature_count)))[:, None]
    small = jnp.concatenate([flat[:, None], linear_rows, square_rows], 1)
    small = jnp.pad(small, ((0, 0), (0, -small.shape[1] % 16), (0, 0)))
    return jnp.concatenate([square, linear, small], 1).reshape(-1, HEAD_DIM)


def unpack(packed, groups, feature_count):
    squares = feature_count * feature_count
    packed = packed.reshape(groups, -1, HEAD_DIM)
    top = squares + feature_count
    square_den = packed[:, top + 2 : top + 2 + squares // HEAD_DIM].reshape(groups, squares)
    return (
        packed[:, :squares],
        packed[:, squares:top],
        square_den,
        packed[:, top + 1, :feature_count],
        packed[:, top],
    )


def ring_gather(block):
    count = lax.axis_size("ctx")
    me = lax.axis_index("ctx")
    rows = block.shape[0]
    half = rows // 2
    ring = list(range(0, count, 2)) + list(range(1, count, 2))[::-1]
    place = [ring.index(i) for i in range(count)]
    position = jnp.array(place, jnp.int32)[me]
    ring_table = jnp.array(ring, jnp.int32)
    up_route = [(ring[p], ring[(p + 1) % count]) for p in range(count)]
    down_route = [(ring[(p + 1) % count], ring[p]) for p in range(count)]
    up, down = block[:half], block[half:]
    pieces = [(me, up, down, me)]
    for step in range(1, count):
        up = lax.ppermute(up, "ctx", up_route)
        down = lax.ppermute(down, "ctx", down_route)
        pieces.append(
            (
                ring_table[(position - step) % count],
                up,
                down,
                ring_table[(position + step) % count],
            )
        )
    return pieces


def after_hop(pieces, hop, *members):
    if hop >= len(pieces):
        return members
    up_owner, up, down, down_owner = pieces[hop]
    up, down, *members = lax.optimization_barrier((up, down, *members))
    pieces[hop] = (up_owner, up, down, down_owner)
    return members


def assemble(pieces, zero, rows):
    half = rows // 2
    count = len(pieces)
    full = jnp.broadcast_to(zero, (count * rows, pieces[0][1].shape[1]))
    for up_owner, up, down, down_owner in pieces:
        full = lax.dynamic_update_slice(full, up, (up_owner * rows, 0))
        full = lax.dynamic_update_slice(full, down, (down_owner * rows + half, 0))
    return full


def flipped(block, bit):
    return lax.ppermute(block, "head", [(i, i ^ bit) for i in range(4)])


def sum_heads(row):
    if lax.axis_size("head") != 4:
        return lax.psum(row, "head")
    row = row + flipped(row, 1)
    return row + flipped(row, 2)


def sum_from(block, sign):
    count = lax.axis_size("ctx")
    devices = range(count)
    total = jnp.zeros_like(block)
    for distance in range(1, count):
        route = [(i, i + sign * distance) for i in devices if i + sign * distance in devices]
        total = total + lax.ppermute(block, "ctx", route)
    return total


def gather_heads(block):
    if lax.axis_size("head") != 4:
        return lax.all_gather(block, "head", axis=1, tiled=True)
    head = lax.axis_index("head")
    rows, width = block.shape
    far = flipped(block, 2)
    near = flipped(block, 1)
    diagonal = flipped(far, 1)
    full = jnp.zeros((rows, 4 * width), block.dtype)
    for bit, member in ((0, block), (2, far), (1, near), (3, diagonal)):
        full = lax.dynamic_update_slice(full, member, (0, (head ^ bit) * width))
    return full


def scatter_heads(d_student, proj_full):
    def product(weights):
        return lax.dot_general(
            d_student, weights, (((1,), (1,)), ((), ())), preferred_element_type=jnp.float32
        ).astype(jnp.bfloat16)

    if lax.axis_size("head") != 4:
        terms = product(proj_full)
        return lax.psum_scatter(terms, "head", scatter_dimension=1, tiled=True).astype(jnp.float32)
    head = lax.axis_index("head")
    width = proj_full.shape[0] // 4

    def block(bit):
        return product(lax.dynamic_slice_in_dim(proj_full, (head ^ bit) * width, width, 0))

    diagonal = flipped(block(3), 1)
    far = block(2)
    pair = (far.astype(jnp.float32) + diagonal.astype(jnp.float32)).astype(jnp.bfloat16)
    far_sum = flipped(pair, 2)
    near = flipped(block(1), 1)
    own = block(0)
    return own.astype(jnp.float32) + near.astype(jnp.float32) + far_sum.astype(jnp.float32)


def window_tiles(extended, tok_rows):
    tile_count = tok_rows // WIN
    first = extended[:tok_rows].reshape((tile_count, WIN) + extended.shape[1:])
    second = extended[WIN:].reshape((tile_count, WIN) + extended.shape[1:])
    return jnp.concatenate([first, second], 1)


def local(queries, keys, values, feature_map, out_proj, teacher):
    tok_rows = queries.shape[0]
    kv_groups = keys.shape[1] // HEAD_DIM
    ctx_count = lax.axis_size("ctx")
    ctx_index = lax.axis_index("ctx")
    pieces = ring_gather(out_proj)
    query_heads = queries.reshape(tok_rows, kv_groups, GROUP, HEAD_DIM)
    key_heads = keys.reshape(tok_rows, kv_groups, HEAD_DIM)
    value_heads = values.reshape(tok_rows, kv_groups, HEAD_DIM)
    value_float = value_heads.astype(jnp.float32)
    query_features = jnp.einsum(
        "tgqe,gef->tgqf", query_heads, feature_map, preferred_element_type=jnp.float32
    )
    key_features = jnp.einsum(
        "tge,gef->tgf", key_heads, feature_map, preferred_element_type=jnp.float32
    )
    rim_rows = shifted(jnp.stack([keys[tok_rows - WIN :], values[tok_rows - WIN :]]), "ctx", 1)
    keys_ext = jnp.concatenate([rim_rows[0], keys], 0).reshape(tok_rows + WIN, kv_groups, HEAD_DIM)
    values_ext = jnp.concatenate([rim_rows[1], values], 0).reshape(
        tok_rows + WIN, kv_groups, HEAD_DIM
    )
    tile_count = tok_rows // WIN
    key_tiles = window_tiles(keys_ext, tok_rows)
    value_tiles = window_tiles(values_ext, tok_rows)
    query_tiles = query_heads.reshape(tile_count, WIN, kv_groups, GROUP, HEAD_DIM)
    causal = lax.broadcasted_iota(jnp.int32, (tok_rows, tok_rows), 0) >= lax.broadcasted_iota(
        jnp.int32, (tok_rows, tok_rows), 1
    )
    qk_inner = (
        jnp.einsum("tgqf,sgf->gqts", query_features, key_features, precision=exact_mode) / 4.0
    )
    kernel = jnp.where(causal, 1.0 + qk_inner + 0.5 * qk_inner * qk_inner, 0.0)
    numerator = jnp.einsum(
        "gqts,sge->tgqe", kernel.astype(jnp.bfloat16), value_heads, preferred_element_type=jnp.float32
    )
    denominator = jnp.transpose(jnp.sum(kernel, axis=-1), (2, 0, 1))
    query_tiles, numerator, denominator = after_hop(
        pieces, 1, query_tiles, numerator, denominator
    )
    scores = jnp.einsum(
        "ntgqe,nsge->ngqts", query_tiles, key_tiles, preferred_element_type=jnp.float32
    ) / math.sqrt(HEAD_DIM)
    tile_pos = lax.broadcasted_iota(jnp.int32, (tile_count, WIN, 2 * WIN), 0)
    query_pos = lax.broadcasted_iota(jnp.int32, (tile_count, WIN, 2 * WIN), 1)
    key_pos = lax.broadcasted_iota(jnp.int32, (tile_count, WIN, 2 * WIN), 2)
    distance = query_pos + WIN - key_pos
    allowed = (
        (distance >= 0)
        & (distance < WIN)
        & (ctx_index * tok_rows + tile_pos * WIN + key_pos - WIN >= 0)
    )
    allowed = allowed[:, None, None]
    scores = jnp.where(allowed, scores, -jnp.inf)
    row_max = jnp.max(scores, axis=-1, keepdims=True)
    weights = jnp.where(allowed, jnp.exp(scores - row_max), 0.0)
    attn_weights = (weights / jnp.sum(weights, axis=-1, keepdims=True)).astype(jnp.bfloat16)
    window_out = jnp.einsum(
        "ngqts,nsge->ntgqe", attn_weights, value_tiles, preferred_element_type=jnp.float32
    ).reshape(tok_rows, kv_groups, GROUP, HEAD_DIM)
    key_square = taylor_square(key_features)
    own_square_v = jnp.einsum("sgk,sge->gke", key_square, value_float, precision=exact_mode)
    own_linear_v = jnp.einsum("sgf,sge->gfe", key_features, value_float, precision=exact_mode)
    own_values = jnp.sum(value_float, axis=0)
    own_square_k = jnp.sum(key_square, axis=0)
    own_linear_k = jnp.sum(key_features, axis=0)
    no_row = jnp.zeros((8, HEAD_DIM), jnp.float32)
    packed = pack(own_square_v, own_linear_v, own_square_k, own_linear_k, own_values)
    earlier, window_out = after_hop(pieces, 2, sum_from(packed, 1), window_out)
    feature_count = feature_map.shape[2]
    past_square_v, past_linear_v, past_square_k, past_linear_k, past_values = unpack(
        earlier, kv_groups, feature_count
    )
    past_count = (ctx_index * tok_rows).astype(jnp.float32)
    query_square = taylor_square(query_features)
    numerator = (
        numerator
        + jnp.einsum("tgqk,gke->tgqe", query_square, past_square_v, precision=exact_mode) / 32.0
        + jnp.einsum("tgqf,gfe->tgqe", query_features, past_linear_v, precision=exact_mode) / 4.0
        + past_values[None, :, None, :]
    )
    denominator = (
        denominator
        + jnp.einsum("tgqk,gk->tgq", query_square, past_square_k, precision=exact_mode) / 32.0
        + jnp.einsum("tgqf,gf->tgq", query_features, past_linear_k, precision=exact_mode) / 4.0
        + past_count
    )
    linear_out = numerator / denominator[..., None]
    head_out = (
        (linear_out + window_out)
        .astype(jnp.bfloat16)
        .reshape(tok_rows, kv_groups * GROUP * HEAD_DIM)
    )
    head_out, zero = after_hop(pieces, 3, head_out, jnp.zeros((), jnp.bfloat16))
    all_heads = gather_heads(head_out)
    proj_full = assemble(pieces, zero, out_proj.shape[0])
    projected = jnp.dot(all_heads, proj_full, preferred_element_type=jnp.float32)
    student_out = projected.astype(jnp.bfloat16)
    residual = student_out.astype(jnp.float32) - teacher.astype(jnp.float32)
    total_rows = tok_rows * ctx_count
    squared = jnp.sum(residual * residual)
    d_student = (2.0 * residual / total_rows).astype(jnp.bfloat16)
    head_grad = scatter_heads(d_student, proj_full).reshape(
        tok_rows, kv_groups, GROUP, HEAD_DIM
    )
    numerator_grad = head_grad / denominator[..., None]
    denominator_grad = -jnp.sum(head_grad * linear_out, axis=-1) / denominator
    kernel_grad = (
        jnp.einsum(
            "tgqe,sge->gqts",
            two_terms(numerator_grad),
            jnp.concatenate([value_heads, value_heads], -1),
            preferred_element_type=jnp.float32,
        )
        + jnp.transpose(denominator_grad, (1, 2, 0))[..., None]
    )
    inner_grad = (jnp.where(causal, kernel_grad * (1.0 + qk_inner), 0.0) / 4.0).astype(
        jnp.bfloat16
    )
    query_grad = joined(
        jnp.einsum(
            "gqts,sgf->tgqf",
            inner_grad,
            two_terms(key_features),
            preferred_element_type=jnp.float32,
        )
    )
    key_grad = joined(
        jnp.einsum(
            "gqts,tgqf->sgf",
            inner_grad,
            two_terms(query_features),
            preferred_element_type=jnp.float32,
        )
    )
    query_square_grad = (
        jnp.einsum("tgqe,gke->tgqk", numerator_grad, past_square_v, precision=exact_mode)
        + denominator_grad[..., None] * past_square_k[None, :, None, :]
    ) / 32.0
    query_grad = (
        query_grad
        + (
            jnp.einsum("tgqe,gfe->tgqf", numerator_grad, past_linear_v, precision=exact_mode)
            + denominator_grad[..., None] * past_linear_k[None, :, None, :]
        )
        / 4.0
        + square_grad(query_square_grad, query_features)
    )
    own_back_square = jnp.einsum(
        "tgqk,tgqe->gke", query_square, numerator_grad, precision=exact_mode
    )
    own_back_linear = jnp.einsum(
        "tgqf,tgqe->gfe", query_features, numerator_grad, precision=exact_mode
    )
    own_den_square = jnp.einsum(
        "tgqk,tgq->gk", query_square, denominator_grad, precision=exact_mode
    )
    own_den_linear = jnp.einsum(
        "tgqf,tgq->gf", query_features, denominator_grad, precision=exact_mode
    )
    packed_back = pack(
        own_back_square,
        own_back_linear,
        own_den_square,
        own_den_linear,
        jnp.zeros((kv_groups, HEAD_DIM), jnp.float32),
    )
    later = sum_from(packed_back, -1)
    loss_row = sum_heads(jnp.full((8, HEAD_DIM), squared, jnp.float32))
    later_square, later_linear, later_den_square, later_den_linear, _ = unpack(
        later, kv_groups, feature_count
    )
    key_square_grad = (
        jnp.einsum("gke,sge->sgk", later_square, value_float, precision=exact_mode)
        + later_den_square[None]
    ) / 32.0
    key_grad = (
        key_grad
        + (
            jnp.einsum("gfe,sge->sgf", later_linear, value_float, precision=exact_mode)
            + later_den_linear[None]
        )
        / 4.0
        + square_grad(key_square_grad, key_features)
    )
    own_grad = jnp.einsum(
        "tgqe,tgqf->gef", query_heads.astype(jnp.float32), query_grad, precision=exact_mode
    ) + jnp.einsum("tge,tgf->gef", key_heads.astype(jnp.float32), key_grad, precision=exact_mode)
    packed_grad = jnp.concatenate([own_grad.reshape(-1, HEAD_DIM), loss_row], 0)
    summed, _ = exchange(packed_grad, no_row, "all", 0)
    feature_grad = summed[:-8].reshape(own_grad.shape)
    loss_value = summed[-8, 0] / (total_rows * D)
    return (student_out, loss_value, feature_grad)


FEATURE_PAIRS = 153
PAIR_ROWS = 160
CHUNKS = 8
STREAMS = 4


def pair_tables():
    j = np.arange(2 * HEAD_DIM)
    valid = j < FEATURE_PAIRS
    first = j % 17
    second = (first + j // 17) % 17
    select = np.zeros((2, 2 * HEAD_DIM, HEAD_DIM), np.float32)
    constant = np.zeros((2, 2 * HEAD_DIM), np.float32)
    for side, member in enumerate((first, second)):
        for row in np.nonzero(valid)[0]:
            if member[row] < 16:
                select[side, row, member[row]] = 1.0
            else:
                constant[side, row] = 1.0
    is_one = (first == 16).astype(int) + (second == 16).astype(int)
    coef = np.where(is_one == 2, 1.0, np.where(is_one == 1, 0.25, np.where(first == second, 1 / 32, 1 / 16)))
    coef = np.where(valid, coef, 0.0)
    bits = np.concatenate([select[0], select[1], np.eye(HEAD_DIM)], 0)
    rows = np.zeros((8, 2 * HEAD_DIM), np.float32)
    rows[0], rows[1], rows[2] = constant[0], constant[1], coef
    columns = np.zeros((2 * HEAD_DIM, HEAD_DIM), np.float32)
    columns[:, 0], columns[:, 1], columns[:, 2] = constant[0], constant[1], coef
    return bits, rows, columns


def mm(a, b):
    return lax.dot_general(a, b, (((1,), (0,)), ((), ())), preferred_element_type=jnp.float32)


def mm_t(a, b):
    return lax.dot_general(a, b, (((1,), (1,)), ((), ())), preferred_element_type=jnp.float32)


def split_terms(x):
    high = x.astype(jnp.bfloat16)
    return high, (x - high.astype(jnp.float32)).astype(jnp.bfloat16)


def fused_kernel(
    queries_in, keys_in, values_in, map_ref, proj_ref, teacher_ref, bits_ref, rows_ref, columns_ref,
    student_ref, grad_ref, loss_ref,
    proj_buf, heads_buf, sums, first_factor, second_factor, pairs_t, queries_t, slope, lin, den_inv,
    d_student, acc, queries_ref, teacher_buf, keys_ext, values_ext, ones_values, wide_map, wide_map_t, kernel_map,
    past_high, past_low, key_features, key_factor_a, key_factor_b, keys_t,
    state_own, state_x, state_low, state_up,
    send_1, send_2, send_3, recv_1, recv_2, recv_3,
    cross, grad_a, grad_b, back, back_own, back_x, back_sum, back_later, back_in, final_own, final_in, loss_acc, loss_own, loss_in,
    ring_send, ring_recv, own_sem, input_sem, teacher_sem, student_sem, rim_send, rim_recv, state_x_send, state_x_recv,
    state_up_send, state_up_recv, head_send, head_recv, s1_send, s1_recv, s2_send, s2_recv, s3_send, s3_recv,
    back_x_send, back_x_recv, back_send, back_recv, final_send, final_recv, loss_send, loss_recv,
):
    f32, bf16 = jnp.float32, jnp.bfloat16
    mesh_ids = pl.DeviceIdType.MESH
    ctx_count = 8
    tokens = queries_in.shape[0]
    half = tokens // 2
    width = proj_buf.shape[2]
    E = HEAD_DIM
    c = lax.axis_index("ctx")
    h = lax.axis_index("head")
    z = c // 2
    x = c % 2
    pos = jnp.where(x == 0, z, 7 - z)

    def ring_at(p):
        p = lax.rem(p + 16, 8)
        return jnp.where(p < 4, 2 * p, 2 * (7 - p) + 1)

    up, down = ring_at(pos + 1), ring_at(pos - 1)
    near = h + 1 - 2 * (h % 2)
    far = (h + 2) % 4
    diagonal = 3 - h

    def remote(src, dst, send, recv, ctx, head):
        return pltpu.make_async_remote_copy(
            src_ref=src, dst_ref=dst, send_sem=send, recv_sem=recv, device_id=(ctx, head), device_id_type=mesh_ids
        )

    inputs = [
        pltpu.make_async_copy(keys_in, keys_ext.at[pl.ds(WIN, tokens)], input_sem.at[0]),
        pltpu.make_async_copy(values_in, values_ext.at[pl.ds(WIN, tokens)], input_sem.at[1]),
        pltpu.make_async_copy(queries_in, queries_ref, input_sem.at[2]),
    ]
    barrier = pltpu.get_barrier_semaphore()
    for d in range(1, ctx_count):
        pl.semaphore_signal(barrier, inc=1, device_id=((c + d) % ctx_count, h), device_id_type=mesh_ids)
    for d in range(1, 4):
        pl.semaphore_signal(barrier, inc=1, device_id=(c, (h + d) % 4), device_id_type=mesh_ids)
    for copy in inputs:
        copy.start()
    pl.semaphore_wait(barrier, ctx_count + 2)

    def owner_rows(owner, d):
        return pl.ds(pl.multiple_of(owner * tokens + d * half, half), half)

    def hop(d, j, k):
        owner = ring_at(pos - k) if d == 0 else ring_at(pos + k)
        place = proj_buf.at[j, owner_rows(owner, d)]
        return remote(place, place, ring_send.at[d, j, k], ring_recv.at[d, j, k], up if d == 0 else down, h)

    def first_hop(d, j):
        place = proj_buf.at[j, owner_rows(c, d)]
        src = proj_ref.at[pl.ds(d * half, half), pl.ds(pl.multiple_of(j * width, width), width)]
        return remote(src, place, ring_send.at[d, j, 0], ring_recv.at[d, j, 0], up if d == 0 else down, h)

    def arrival(d, j, k):
        owner = ring_at(pos - 1 - k) if d == 0 else ring_at(pos + 1 + k)
        place = proj_buf.at[j, owner_rows(owner, d)]
        return remote(place, place, ring_send.at[d, j, k], ring_recv.at[d, j, k], up if d == 0 else down, h)

    def start_first(n):
        for d in (0, 1):
            first_hop(d, n).start()

    def service(group, n):
        k = n // STREAMS
        j = group * STREAMS + n % STREAMS
        for d in (0, 1):
            arrival(d, j, k - 1).wait_recv()
            hop(d, j, k).start()

    for s, (src, dst) in enumerate(((keys_in, keys_ext), (values_in, values_ext))):

        @pl.when(c < ctx_count - 1)
        def _():
            remote(
                src.at[pl.ds(tokens - WIN, WIN)], dst.at[pl.ds(0, WIN)], rim_send.at[s], rim_recv.at[s],
                lax.rem(c + 1, ctx_count), h,
            ).start()

        @pl.when(c == 0)
        def _():
            dst[pl.ds(0, WIN), :] = jnp.zeros((WIN, E), bf16)

        dst[pl.ds(WIN + tokens, WIN), :] = jnp.zeros((WIN, E), bf16)

    start_first(0)
    start_first(1)
    teacher_copy = pltpu.make_async_copy(teacher_ref, teacher_buf, teacher_sem.at[0])
    teacher_copy.start()

    def own_copy(j):
        return pltpu.make_async_copy(
            proj_ref.at[:, pl.ds(pl.multiple_of(j * width, width), width)],
            proj_buf.at[j, pl.ds(pl.multiple_of(c * tokens, tokens), tokens)],
            own_sem.at[j],
        )

    for j in range(CHUNKS):
        own_copy(j).start()

    eye = bits_ref[pl.ds(4 * E, E), :]
    map_rows = jnp.concatenate([map_ref[...], jnp.zeros((E - map_ref.shape[0], E), bf16)], 0)
    map_wide = mm_t(eye, map_rows).astype(bf16)
    for s in range(2):
        select = bits_ref[pl.ds(s * 2 * E, 2 * E), :]
        wide_map[s] = mm_t(map_wide, select).astype(bf16)
        wide_map_t[s] = mm_t(select, map_wide).astype(bf16)
    inputs[0].wait()
    inputs[1].wait()
    keys = keys_ext[pl.ds(WIN, tokens), :]
    features = mm(keys, map_wide)
    feature_high, feature_low = split_terms(features)
    key_features[0] = feature_high
    key_features[1] = feature_low
    inner = (mm_t(map_wide, feature_high) + mm_t(map_wide, feature_low)) * 0.25
    inner_high, inner_low = split_terms(inner)
    kernel_map[pl.ds(0, E), :] = inner_high
    kernel_map[pl.ds(E, E), :] = inner_low
    keys_t[...] = mm_t(eye, keys).astype(bf16)
    key_a = mm(keys, wide_map[0]) + rows_ref[pl.ds(0, 1), :]
    key_b = mm(keys, wide_map[1]) + rows_ref[pl.ds(1, 1), :]
    key_factor_a[...] = (key_a * rows_ref[pl.ds(2, 1), :]).astype(bf16)
    key_factor_b[...] = (key_b * rows_ref[pl.ds(2, 1), :]).astype(bf16)
    ones_values[:, pl.ds(0, E)] = values_ext[pl.ds(WIN, tokens), :]
    ones_values[:, pl.ds(E, E)] = jnp.ones((tokens, E), bf16)
    key_a_t = mm_t(wide_map_t[0], keys) + columns_ref[:, 0:1]
    key_b_t = mm_t(wide_map_t[1], keys) + columns_ref[:, 1:2]
    key_high, key_low = split_terms(key_a_t * key_b_t * columns_ref[:, 2:3])
    state = mm(key_high, ones_values[...]) + mm(key_low, ones_values[...])

    def store_state(ref, value, den_row):
        ref[pl.ds(0, PAIR_ROWS), :] = value[:PAIR_ROWS]
        ref[pl.ds(PAIR_ROWS, 8), :] = den_row[:, :E]
        ref[pl.ds(PAIR_ROWS + 8, 8), :] = den_row[:, E:]

    store_state(state_own, state[:, :E], jnp.transpose(state[:, E:])[:8])
    state_x_copy = remote(state_own, state_x, state_x_send.at[0], state_x_recv.at[0], c + 1 - 2 * x, h)
    state_x_copy.start()
    start_first(2)
    start_first(3)
    inputs[2].wait()

    def state_up_copy():
        return remote(state_up, state_low, state_up_send.at[0], state_up_recv.at[0], lax.rem(c + 2, ctx_count), h)

    def chain_step(level):
        if level == 0:
            state_x_copy.wait_recv()

            @pl.when(z == 0)
            def _():
                state_low[...] = jnp.zeros_like(state_low)

        else:

            @pl.when(z == level)
            def _():
                state_up_copy().wait_recv()

        if level < 3:

            @pl.when(z == level)
            def _():
                state_up[...] = state_low[...] + state_own[...] + state_x[...]
                state_up_copy().start()

    for s in range(2):

        @pl.when(c > 0)
        def _():
            dst = (keys_ext, values_ext)[s]
            remote(
                dst.at[pl.ds(0, WIN)], dst.at[pl.ds(0, WIN)], rim_send.at[s], rim_recv.at[s], c, h
            ).wait_recv()

    def query_tile(i, hp):
        token = pl.multiple_of(i * E, E)
        both = queries_ref[pl.ds(token, E), pl.ds(pl.multiple_of(hp * 2 * E, 2 * E), 2 * E)]
        return jnp.concatenate([both[:, :E], both[:, E:]], 0)

    for i in range(4):
        reach = (i + 1) * E

        def local_tile(hp, carry):
            tile = i * 4 + hp
            q = query_tile(i, hp)
            u = mm(jnp.concatenate([q, q], 1), kernel_map[:, pl.ds(0, reach)])
            row = lax.broadcasted_iota(jnp.int32, (2 * E, reach), 0) % E + i * E
            causal = row >= lax.broadcasted_iota(jnp.int32, (2 * E, reach), 1)
            kernel = jnp.where(causal, 1.0 + u + 0.5 * u * u, 0.0).astype(bf16)
            slope[tile, :, pl.ds(0, reach)] = jnp.where(causal, 0.25 + 0.25 * u, 0.0).astype(bf16)
            both = mm(kernel, ones_values[pl.ds(0, reach), :])
            lin[tile] = both[:, :E]
            den_inv[tile] = both[:, E:]
            scores = mm_t(q, keys_ext[pl.ds(i * E, 2 * E), :]) / math.sqrt(HEAD_DIM)
            token = lax.broadcasted_iota(jnp.int32, (2 * E, 2 * E), 0) % E
            place = lax.broadcasted_iota(jnp.int32, (2 * E, 2 * E), 1)
            distance = token + WIN - place
            allowed = (distance >= 0) & (distance < WIN) & (c * tokens + i * E + place - WIN >= 0)
            scores = jnp.where(allowed, scores, -jnp.inf)
            top = jnp.max(scores, axis=-1, keepdims=True)
            weights = jnp.where(allowed, jnp.exp(scores - top), 0.0)
            weights = (weights / jnp.sum(weights, axis=-1, keepdims=True)).astype(bf16)
            sums[tile, pl.ds(0, 2 * E), pl.ds(0, E)] = mm(weights, values_ext[pl.ds(i * E, 2 * E), :])
            first_factor[tile] = (mm(q, wide_map[0]) + rows_ref[pl.ds(0, 1), :]).astype(bf16)
            second_factor[tile] = (mm(q, wide_map[1]) + rows_ref[pl.ds(1, 1), :]).astype(bf16)
            pair_a = mm_t(wide_map_t[0], q) + columns_ref[:, 0:1]
            pair_b = mm_t(wide_map_t[1], q) + columns_ref[:, 1:2]
            pairs_t[tile] = (pair_a * pair_b).astype(bf16)[:PAIR_ROWS]
            queries_t[tile] = mm_t(eye, q).astype(bf16)
            service(0, STREAMS + tile)
            return carry

        lax.fori_loop(0, 4, local_tile, 0)
        chain_step(i)

    past = jnp.where(z > 0, state_low[...], 0.0) + jnp.where(x == 1, state_x[...], 0.0)
    past_rows = jnp.concatenate([past[PAIR_ROWS : PAIR_ROWS + 8], past[PAIR_ROWS + 8 :]], 1)
    past_den = jnp.transpose(jnp.broadcast_to(past_rows[:1], (E, 2 * E)))
    past_values = jnp.concatenate([past[:PAIR_ROWS], jnp.zeros((2 * E - PAIR_ROWS, E), f32)], 0)
    high, low = split_terms(jnp.concatenate([past_values, past_den], 1))
    past_high[...] = high
    past_low[...] = low

    def head_copy(i, d, source):
        piece = heads_buf.at[source, pl.ds(pl.multiple_of(i * E, E), E)]
        return remote(piece, piece, head_send.at[d, i], head_recv.at[source, i], c, (h + d) % 4)

    def past_tiles(i, carry):
        def past_tile(hp, carry):
            tile = i * 4 + hp
            q = query_tile(i, hp)
            pair = (mm(q, wide_map[0]) + rows_ref[pl.ds(0, 1), :]) * (mm(q, wide_map[1]) + rows_ref[pl.ds(1, 1), :])
            pair_high, pair_low = split_terms(pair)
            both = mm(pair_high, past_high[...]) + mm(pair_low, past_high[...]) + mm(pair_high, past_low[...])
            den = den_inv[tile] + both[:, E:]
            value = (lin[tile] + both[:, :E]) / den
            lin[tile] = value
            den_inv[tile] = 1.0 / den
            out = (value + sums[tile, pl.ds(0, 2 * E), pl.ds(0, E)]).astype(bf16)
            heads_buf[
                h, pl.ds(pl.multiple_of(i * E, E), E), pl.ds(pl.multiple_of(hp * 2 * E, 2 * E), 2 * E)
            ] = jnp.concatenate([out[:E], out[E:]], 1)
            return carry

        lax.fori_loop(0, 4, past_tile, 0)
        for d in range(1, 4):
            head_copy(i, d, h).start()
        service(0, STREAMS + 16 + 2 * i)
        service(0, STREAMS + 17 + 2 * i)
        return carry

    lax.fori_loop(0, 4, past_tiles, 0)
    for n in range(STREAMS):
        start_first(STREAMS + n)
    teacher_copy.wait()
    for j in range(CHUNKS):
        own_copy(j).wait()
    loss_acc[...] = jnp.zeros_like(loss_acc)
    for j in range(STREAMS):
        for d in (0, 1):
            arrival(d, j, 6).wait_recv()

    def second_service(n, carry):
        service(1, STREAMS + n)
        return carry

    lax.fori_loop(0, 3 * STREAMS, second_service, 0)
    for i in range(4):
        for d in range(1, 4):
            head_copy(i, d, (h + d) % 4).wait_recv()

    def student_copy(j):
        return pltpu.make_async_copy(
            teacher_buf.at[:, pl.ds(pl.multiple_of(j * width, width), width)],
            student_ref.at[:, pl.ds(pl.multiple_of(j * width, width), width)],
            student_sem.at[j],
        )

    def finish_columns(j, product):
        student = product.astype(bf16)
        columns = pl.ds(pl.multiple_of(j * width, width), width)
        residual = student.astype(f32) - teacher_buf[:, columns].astype(f32)
        teacher_buf[:, columns] = student
        loss_acc[...] += jnp.sum((residual * residual).reshape(tokens // 8, 8, width), axis=0)
        d_student[j] = (residual * (2.0 / (tokens * ctx_count))).astype(bf16)
        student_copy(j).start()

    def first_columns(j, carry):
        product = mm(heads_buf[0], proj_buf[j, pl.ds(0, 8 * E), :])
        for s in range(1, 4):
            product += mm(heads_buf[s], proj_buf[j, pl.ds(s * 8 * E, 8 * E), :])
        finish_columns(j, product)
        service(1, 4 * STREAMS + j)
        return carry

    lax.fori_loop(0, STREAMS, first_columns, 0)

    def block_sum(group, r):
        rows = pl.ds(pl.multiple_of(r * width, width), width)
        total = mm_t(d_student[group * STREAMS], proj_buf[group * STREAMS, rows, :])
        for j in range(1, STREAMS):
            total += mm_t(d_student[group * STREAMS + j], proj_buf[group * STREAMS + j, rows, :])
        return total

    def first_sums(n, carry):
        sums[2 * n] = block_sum(0, 2 * n)
        sums[2 * n + 1] = block_sum(0, 2 * n + 1)
        service(1, 5 * STREAMS + n)
        return carry

    lax.fori_loop(0, 8, first_sums, 0)

    def partial_product(owner, d, j):
        place = pl.multiple_of((owner % 2) * tokens + d * half, half)
        left = heads_buf[owner // 2, :, pl.ds(place, half)]
        return mm(left, proj_buf[j, owner_rows(owner, d), :])

    def second_early(s, carry):
        j = STREAMS + s
        total = partial_product(c, 0, j) + partial_product(c, 1, j)
        for k in range(6):
            total += partial_product(ring_at(pos - 1 - k), 0, j) + partial_product(ring_at(pos + 1 + k), 1, j)
        acc[s] = total
        return carry

    lax.fori_loop(0, STREAMS, second_early, 0)

    def second_last(s, carry):
        j = STREAMS + s
        for d in (0, 1):
            arrival(d, j, 6).wait_recv()
        finish_columns(
            j, acc[s] + partial_product(ring_at(pos - 7), 0, j) + partial_product(ring_at(pos + 7), 1, j)
        )
        return carry

    lax.fori_loop(0, STREAMS, second_last, 0)

    def unit_rows(u):
        return pl.ds(pl.multiple_of((u % 2) * half, half), half)

    def unit_sum(r, u):
        rows = pl.ds(pl.multiple_of(r * width, width), width)
        total = sums[r, unit_rows(u), :]
        for j in range(STREAMS, 2 * STREAMS):
            total += mm_t(d_student[j, unit_rows(u), :], proj_buf[j, rows, :])
        return total

    def copy_1(u):
        piece = (u // 2, unit_rows(u))
        return remote(send_1.at[piece], recv_1.at[piece], s1_send.at[u], s1_recv.at[u], c, near)

    def copy_2(p):
        return remote(send_2.at[p], recv_2.at[p], s2_send.at[p], s2_recv.at[p], c, near)

    def copy_3(u):
        piece = (u // 2, unit_rows(u))
        return remote(send_3.at[piece], recv_3.at[piece], s3_send.at[u], s3_recv.at[u], c, far)

    def step_1(u):
        send_1[u // 2, unit_rows(u), :] = unit_sum(diagonal * 4 + u // 2, u).astype(bf16)
        copy_1(u).start()

    def step_2(u):
        total = unit_sum(far * 4 + u // 2, u)
        copy_1(u).wait_recv()
        send_3[u // 2, unit_rows(u), :] = (total + recv_1[u // 2, unit_rows(u), :].astype(f32)).astype(bf16)
        copy_3(u).start()

    step_1(0)
    step_1(1)

    def step_both(u, carry):
        step_2(u)
        step_1(u + 2)
        return carry

    lax.fori_loop(0, 6, step_both, 0)
    step_2(6)
    step_2(7)

    def step_near(p, carry):
        r = near * 4 + p
        send_2[p] = (sums[r] + block_sum(1, r)).astype(bf16)
        copy_2(p).start()
        return carry

    lax.fori_loop(0, 4, step_near, 0)

    def step_own(p, carry):
        r = h * 4 + p
        sums[r] += block_sum(1, r)
        return carry

    lax.fori_loop(0, 4, step_own, 0)

    loss_own[...] = loss_acc[:, :E] + loss_acc[:, E:]

    def loss_copy(d, source):
        return remote(loss_own, loss_in.at[source], loss_send.at[d], loss_recv.at[source], c, (h + d) % 4)

    for d in range(1, 4):
        loss_copy(d, h).start()

    cross[...] = jnp.zeros_like(cross)
    grad_a[...] = jnp.zeros_like(grad_a)
    grad_b[...] = jnp.zeros_like(grad_b)
    back[...] = jnp.zeros_like(back)

    def grad_piece(p, carry):
        copy_2(p).wait_recv()
        for i in range(4):
            if i % 2 == 0:
                copy_3(2 * p + i // 2).wait_recv()
            reach = (i + 1) * E
            tile = i * 4 + p
            rows = pl.ds(i * E, E)
            g = sums[h * 4 + p, rows, :] + recv_2[p, rows, :].astype(f32) + recv_3[p, rows, :].astype(f32)
            g = jnp.concatenate([g[:, :E], g[:, E:]], 0)
            inverse = den_inv[tile]
            upper = (g * inverse).astype(bf16)
            lower = -jnp.sum(upper.astype(f32) * lin[tile], axis=-1, keepdims=True)
            lower = jnp.broadcast_to(lower, (2 * E, E))
            lower_high = lower.astype(bf16).astype(f32)
            lane = lax.broadcasted_iota(jnp.int32, (2 * E, E), 1)
            lower = (jnp.where(lane < E // 2, lower_high, lower - lower_high) * (2.0 / E)).astype(bf16)
            wide = jnp.concatenate([upper, lower], 1)
            weight = mm_t(wide, ones_values[pl.ds(0, reach), :]) * slope[tile, :, pl.ds(0, reach)].astype(f32)
            cross[:, pl.ds(0, reach)] += mm(queries_t[tile], weight.astype(bf16))
            pair_grad = mm_t(wide, past_high[...]) + mm_t(wide, past_low[...])
            grad_a[...] += mm(queries_t[tile], (pair_grad * second_factor[tile].astype(f32)).astype(bf16))
            grad_b[...] += mm(queries_t[tile], (pair_grad * first_factor[tile].astype(f32)).astype(bf16))
            back[...] += mm(pairs_t[tile], wide)
        return carry

    lax.fori_loop(0, 4, grad_piece, 0)

    back_den = jnp.transpose(
        jnp.concatenate([back[:, pl.ds(E, E)], jnp.zeros((2 * E - PAIR_ROWS, E), f32)], 0)
    )
    back_den = (back_den[:8] + back_den[E // 2 : E // 2 + 8]) * (E // 2)
    store_state(back_own, back[:, pl.ds(0, E)], back_den)
    back_x_copy = remote(back_own, back_x, back_x_send.at[0], back_x_recv.at[0], c + 1 - 2 * x, h)
    back_x_copy.start()

    def back_copy(level):
        return remote(back_sum, back_in.at[z], back_send.at[level], back_recv.at[z], 2 * level + x, h)

    def back_arrival(level):
        return remote(back_sum, back_in.at[level], back_send.at[level], back_recv.at[level], c, h)

    cross_high, cross_low = split_terms(cross[...])
    grad = mm(cross_high, key_features[0]) + mm(cross_high, key_features[1]) + mm(cross_low, key_features[0])
    keys = keys_ext[pl.ds(WIN, tokens), :]
    mixed = jnp.transpose(mm(cross_high, keys) + mm(cross_low, keys))
    mixed_high, mixed_low = split_terms(mixed)
    map_rows = jnp.concatenate([map_ref[...], jnp.zeros((E - map_ref.shape[0], E), bf16)], 0)
    map_wide = mm_t(bits_ref[pl.ds(4 * E, E), :], map_rows).astype(bf16)
    grad += mm(mixed_high, map_wide) + mm(mixed_low, map_wide)

    center = mm(jnp.ones((8, tokens), bf16), values_ext[pl.ds(WIN, tokens), :])
    center = (center / tokens).astype(bf16)
    back_x_copy.wait_recv()
    plane = back_own[...] + back_x[...]
    plane_values = plane[:PAIR_ROWS].astype(bf16)
    lost = (plane[:PAIR_ROWS] - plane_values.astype(f32)).astype(bf16)
    lost = jnp.concatenate([lost, jnp.zeros((2 * E - PAIR_ROWS, E), bf16)], 0)
    moved = mm_t(center, lost)
    plane_den = plane[PAIR_ROWS:] + jnp.concatenate([moved[:, :E], moved[:, E:]], 0)
    den_high, den_low = split_terms(plane_den)
    back_sum[pl.ds(0, PAIR_ROWS), :] = plane_values
    back_sum[pl.ds(PAIR_ROWS, 16), :] = den_high
    back_sum[pl.ds(PAIR_ROWS + 16, 16), :] = den_low
    for level in range(3):

        @pl.when(level < z)
        def _():
            back_copy(level).start()

    back_later[...] = jnp.where(x == 0, back_x[...], 0.0)
    for level in range(1, 4):

        @pl.when(level > z)
        def _():
            back_arrival(level).wait_recv()
            arrived = back_in[level].astype(f32)
            back_later[...] += arrived[: PAIR_ROWS + 16]
            back_later[pl.ds(PAIR_ROWS, 16), :] += arrived[PAIR_ROWS + 16 :]

    later_values = jnp.concatenate([back_later[pl.ds(0, PAIR_ROWS), :], jnp.zeros((2 * E - PAIR_ROWS, E), f32)], 0)
    later_high, later_low = split_terms(later_values)
    pair_grad = mm_t(values_ext[pl.ds(WIN, tokens), :], later_high)
    pair_grad += mm_t(values_ext[pl.ds(WIN, tokens), :], later_low)
    pair_grad += jnp.concatenate(
        [back_later[pl.ds(PAIR_ROWS, 1), :], back_later[pl.ds(PAIR_ROWS + 8, 1), :]], 1
    )
    total_a = grad_a[...] + mm(keys_t[...], (pair_grad * key_factor_b[...].astype(f32)).astype(bf16))
    total_b = grad_b[...] + mm(keys_t[...], (pair_grad * key_factor_a[...].astype(f32)).astype(bf16))
    for s, total in enumerate((total_a, total_b)):
        total_high, total_low = split_terms(total)
        select = bits_ref[pl.ds(s * 2 * E, 2 * E), :]
        grad += mm(total_high, select) + mm(total_low, select)
    final_own[pl.ds(0, 16), :] = jnp.transpose(grad)[:16]
    loss_sum = loss_own[...]
    for d in range(1, 4):
        loss_copy(d, (h + d) % 4).wait_recv()
        loss_sum += loss_in[(h + d) % 4]
    final_own[pl.ds(16, 8), :] = loss_sum

    def final_copy(d, source):
        return remote(final_own, final_in.at[source], final_send.at[d], final_recv.at[source], (c + d) % ctx_count, h)

    for d in range(1, ctx_count):
        final_copy(d, c).start()
    final_in[c] = final_own[...]
    for d in range(1, ctx_count):
        final_copy(d, (c + d) % ctx_count).wait_recv()
    final = final_in[0]
    for s in range(1, ctx_count):
        final += final_in[s]
    grad_ref[...] = final[:16]
    loss_ref[0, 0] = jnp.sum(final[16:]) / (tokens * ctx_count * D)

    for j in range(CHUNKS):
        student_copy(j).wait()
        for d in (0, 1):
            first_hop(d, j).wait_send()
            for k in range(1, 7):
                hop(d, j, k).wait_send()
    for s in range(2):

        @pl.when(c < ctx_count - 1)
        def _():
            dst = (keys_ext, values_ext)[s]
            src = (keys_in, values_in)[s]
            remote(
                src.at[pl.ds(tokens - WIN, WIN)], dst.at[pl.ds(0, WIN)], rim_send.at[s], rim_recv.at[s],
                lax.rem(c + 1, ctx_count), h,
            ).wait_send()

    state_x_copy.wait_send()

    @pl.when(z < 3)
    def _():
        state_up_copy().wait_send()

    back_x_copy.wait_send()
    for level in range(3):

        @pl.when(level < z)
        def _():
            back_copy(level).wait_send()

    for d in range(1, 4):
        loss_copy(d, h).wait_send()
        for i in range(4):
            head_copy(i, d, h).wait_send()
    for p in range(4):
        copy_2(p).wait_send()
    for u in range(8):
        copy_1(u).wait_send()
        copy_3(u).wait_send()
    for d in range(1, ctx_count):
        final_copy(d, c).wait_send()


def deliver_kernel(student_ref, grad_ref, loss_ref, student_out, grad_out, loss_out, buffer, grad_buffer, sem, out_sem):
    part = student_ref.shape[0] // 4
    moves = [(ref.at[pl.ds(s * part, part)], buffer.at[pl.ds(s * part, part)], student_out.at[pl.ds(s * part, part)])
             for s, ref in enumerate([student_ref] * 4)]
    moves.append((grad_ref, grad_buffer, grad_out))
    reads = [pltpu.make_async_copy(src, mid, sem.at[s]) for s, (src, mid, dst) in enumerate(moves)]
    writes = [pltpu.make_async_copy(mid, dst, out_sem.at[s]) for s, (src, mid, dst) in enumerate(moves)]
    for copy in reads:
        copy.start()
    loss_out[0, 0] = loss_ref[0, 0]
    for read, write in zip(reads, writes):
        read.wait()
        write.start()
    for copy in writes:
        copy.wait()


def fused_local(queries, keys, values, feature_map, out_proj, teacher):
    tokens = queries.shape[0]
    columns = out_proj.shape[1]
    rows = tokens * 8
    width = columns // CHUNKS
    E = HEAD_DIM
    bf16, f32 = jnp.bfloat16, jnp.float32
    bits, row_table, column_table = pair_tables()
    vmem = pl.BlockSpec(memory_space=pltpu.VMEM)
    anywhere = pl.BlockSpec(memory_space=pl.ANY)
    smem = pl.BlockSpec(memory_space=pltpu.SMEM)
    dma = pltpu.SemaphoreType.DMA
    state = (PAIR_ROWS + 16, E)
    scratch = [
        ((CHUNKS, rows, width), bf16),
        ((4, tokens, 8 * E), bf16),
        ((16, tokens, width), f32),
        ((16, 2 * E, 2 * E), bf16),
        ((16, 2 * E, 2 * E), bf16),
        ((16, PAIR_ROWS, 2 * E), bf16),
        ((16, E, 2 * E), bf16),
        ((16, 2 * E, tokens), bf16),
        ((16, 2 * E, E), f32),
        ((16, 2 * E, E), f32),
        ((CHUNKS, tokens, width), bf16),
        ((STREAMS, tokens, width), f32),
        ((tokens, 8 * E), bf16),
        ((tokens, columns), bf16),
        ((tokens + 2 * WIN, E), bf16),
        ((tokens + 2 * WIN, E), bf16),
        ((tokens, 2 * E), bf16),
        ((2, E, 2 * E), bf16),
        ((2, 2 * E, E), bf16),
        ((2 * E, tokens), bf16),
        ((2 * E, 2 * E), bf16),
        ((2 * E, 2 * E), bf16),
        ((2, tokens, E), bf16),
        ((tokens, 2 * E), bf16),
        ((tokens, 2 * E), bf16),
        ((E, tokens), bf16),
        (state, f32),
        (state, f32),
        (state, f32),
        (state, f32),
        ((4, tokens, width), bf16),
        ((4, tokens, width), bf16),
        ((4, tokens, width), bf16),
        ((4, tokens, width), bf16),
        ((4, tokens, width), bf16),
        ((4, tokens, width), bf16),
        ((E, tokens), f32),
        ((E, 2 * E), f32),
        ((E, 2 * E), f32),
        ((PAIR_ROWS, 2 * E), f32),
        (state, f32),
        (state, f32),
        ((PAIR_ROWS + 32, E), bf16),
        (state, f32),
        ((4, PAIR_ROWS + 32, E), bf16),
        ((24, E), f32),
        ((8, 24, E), f32),
        ((8, width), f32),
        ((8, E), f32),
        ((4, 8, E), f32),
    ]
    semaphores = [
        (2, CHUNKS, 7), (2, CHUNKS, 7), (CHUNKS,), (3,), (1,), (CHUNKS,), (2,), (2,), (1,), (1,), (1,), (1,), (4, 4), (4, 4),
        (8,), (8,), (4,), (4,), (8,), (8,), (1,), (1,), (4,), (4,), (8,), (8,), (4,), (4,),
    ]
    student, grad, loss = pl.pallas_call(
        fused_kernel,
        out_shape=(
            jax.ShapeDtypeStruct((tokens, columns), bf16),
            jax.ShapeDtypeStruct((feature_map.shape[2], E), f32),
            jax.ShapeDtypeStruct((1, 1), f32),
        ),
        in_specs=[anywhere, anywhere, anywhere, vmem, anywhere, anywhere, vmem, vmem, vmem],
        out_specs=(anywhere, vmem, smem),
        scratch_shapes=[pltpu.VMEM(shape, kind) for shape, kind in scratch] + [dma(shape) for shape in semaphores],
        compiler_params=pltpu.CompilerParams(
            collective_id=0, has_side_effects=True, vmem_limit_bytes=63 * 1024 * 1024
        ),
        cost_estimate=pl.CostEstimate(flops=30_000_000_000, bytes_accessed=40_000_000, transcendentals=2_000_000),
    )(
        queries, keys, values, feature_map[0].T, out_proj, teacher,
        jnp.asarray(bits, bf16), jnp.asarray(row_table, f32), jnp.asarray(column_table, f32),
    )
    student, grad, loss = pl.pallas_call(
        deliver_kernel,
        out_shape=(
            jax.ShapeDtypeStruct(student.shape, bf16),
            jax.ShapeDtypeStruct(grad.shape, f32),
            jax.ShapeDtypeStruct((1, 1), f32),
        ),
        in_specs=[anywhere, anywhere, smem],
        out_specs=(anywhere, anywhere, smem),
        scratch_shapes=[pltpu.VMEM(student.shape, bf16), pltpu.VMEM(grad.shape, f32), dma((5,)), dma((5,))],
        cost_estimate=pl.CostEstimate(flops=0, bytes_accessed=2 * student.size * 2, transcendentals=0),
    )(student, grad, loss)
    return student, loss.reshape(()), grad.T[None]


def fits_fused(mesh):
    return mesh.shape["ctx"] == 8 and mesh.shape["head"] == 4


def solution(mesh):
    return jax.shard_map(
        fused_local if fits_fused(mesh) else local,
        mesh=mesh,
        in_specs=(
            P("ctx", "head"),
            P("ctx", "head"),
            P("ctx", "head"),
            P("head", None, None),
            P("ctx", "head"),
            P("ctx", "head"),
        ),
        out_specs=(P("ctx", "head"), P(), P("head", None, None)),
        check_vma=False,
    )
```

```python
import functools
import math

import jax
import jax.numpy as jnp
import numpy as np
from jax import lax
from jax.experimental import pallas as pl
from jax.experimental.pallas import tpu as pltpu
from jax.sharding import PartitionSpec as P

D = 8192
HEAD_DIM = 128
GROUP = 8
WIN = 64


exact_mode = lax.Precision.HIGHEST


def shifted(block, axis, distance):
    devices = range(lax.axis_size(axis))
    route = [(i - distance, i) for i in devices if i - distance in devices]
    return lax.ppermute(block, axis, route)


def taylor_square(features):
    feature_count = features.shape[-1]
    outer = features[..., :, None] * features[..., None, :]
    return outer.reshape(features.shape[:-1] + (feature_count * feature_count,))


def two_terms(x):
    high = lax.reduce_precision(x, 8, 7)
    return jnp.concatenate([high.astype(jnp.bfloat16), (x - high).astype(jnp.bfloat16)], -1)


def joined(pair):
    half = pair.shape[-1] // 2
    return pair[..., :half] + pair[..., half:]


def square_grad(grad_square, features):
    feature_count = features.shape[-1]
    matrix = grad_square.reshape(features.shape + (feature_count,))
    return jnp.einsum("...fh,...h->...f", matrix, features, precision=exact_mode) + jnp.einsum(
        "...hf,...h->...f", matrix, features, precision=exact_mode
    )


def exchange_kernel(count, head_count, mode, x_ref, row_ref, out_ref, row_out, buf, row_buf, send, recv, row_send, row_recv):
    me = lax.axis_index("ctx")
    head = lax.axis_index("head")
    mesh_ids = pl.DeviceIdType.MESH
    barrier = pltpu.get_barrier_semaphore()
    for d in range(1, count):
        pl.semaphore_signal(
            barrier, inc=1, device_id=(lax.rem(me + d, count), head), device_id_type=mesh_ids
        )
    for d in range(1, head_count):
        pl.semaphore_signal(
            barrier, inc=1, device_id=(me, lax.rem(head + d, head_count)), device_id_type=mesh_ids
        )
    pl.semaphore_wait(barrier, count + head_count - 2)

    def wanted(source, target):
        return {"lower": source < target, "upper": source > target, "all": source != target}[mode]

    def ctx_copy(d):
        return pltpu.make_async_remote_copy(
            src_ref=x_ref,
            dst_ref=buf.at[me],
            send_sem=send.at[d],
            recv_sem=recv.at[me],
            device_id=(lax.rem(me + d, count), head),
            device_id_type=mesh_ids,
        )

    def row_copy(d):
        return pltpu.make_async_remote_copy(
            src_ref=row_ref,
            dst_ref=row_buf.at[head],
            send_sem=row_send.at[d],
            recv_sem=row_recv.at[head],
            device_id=(me, lax.rem(head + d, head_count)),
            device_id_type=mesh_ids,
        )

    def ctx_arrival(source):
        return pltpu.make_async_remote_copy(
            src_ref=x_ref,
            dst_ref=buf.at[source],
            send_sem=send.at[0],
            recv_sem=recv.at[source],
            device_id=(source, head),
            device_id_type=mesh_ids,
        )

    def row_arrival(source):
        return pltpu.make_async_remote_copy(
            src_ref=row_ref,
            dst_ref=row_buf.at[source],
            send_sem=row_send.at[0],
            recv_sem=row_recv.at[source],
            device_id=(me, source),
            device_id_type=mesh_ids,
        )

    for d in range(1, count):

        @pl.when(wanted(me, lax.rem(me + d, count)))
        def _():
            ctx_copy(d).start()

    for d in range(1, head_count):
        row_copy(d).start()

    row_out[...] = jnp.zeros_like(row_out)
    for source in range(head_count):

        @pl.when(source == head)
        def _():
            row_out[...] += row_ref[...]

        @pl.when(source != head)
        def _():
            row_arrival(source).wait_recv()
            row_out[...] += row_buf[source]

    out_ref[...] = jnp.zeros_like(out_ref)
    for source in range(count):
        if mode == "all":

            @pl.when(source == me)
            def _():
                out_ref[...] += x_ref[...].astype(jnp.float32)

        @pl.when(wanted(source, me))
        def _():
            ctx_arrival(source).wait_recv()
            out_ref[...] += buf[source].astype(jnp.float32)

    for d in range(1, count):

        @pl.when(wanted(me, lax.rem(me + d, count)))
        def _():
            ctx_copy(d).wait_send()

    for d in range(1, head_count):
        row_copy(d).wait_send()


def exchange(x, row, mode, collective_id):
    count = lax.axis_size("ctx")
    head_count = lax.axis_size("head")
    vmem = pl.BlockSpec(memory_space=pltpu.VMEM)
    return pl.pallas_call(
        functools.partial(exchange_kernel, count, head_count, mode),
        out_shape=(
            jax.ShapeDtypeStruct(x.shape, jnp.float32),
            jax.ShapeDtypeStruct(row.shape, jnp.float32),
        ),
        in_specs=[vmem, vmem],
        out_specs=(vmem, vmem),
        scratch_shapes=[
            pltpu.VMEM((count,) + x.shape, x.dtype),
            pltpu.VMEM((head_count,) + row.shape, jnp.float32),
            pltpu.SemaphoreType.DMA((count,)),
            pltpu.SemaphoreType.DMA((count,)),
            pltpu.SemaphoreType.DMA((head_count,)),
            pltpu.SemaphoreType.DMA((head_count,)),
        ],
        compiler_params=pltpu.CompilerParams(collective_id=collective_id, has_side_effects=True),
        cost_estimate=pl.CostEstimate(
            flops=count * x.size, bytes_accessed=40 * count * x.size, transcendentals=0
        ),
    )(x, row)


def pack(square, linear, square_den, linear_den, flat):
    groups, feature_count = linear_den.shape
    squares = feature_count * feature_count
    square_rows = square_den.reshape(groups, squares // HEAD_DIM, HEAD_DIM)
    linear_rows = jnp.pad(linear_den, ((0, 0), (0, HEAD_DIM - feature_count)))[:, None]
    small = jnp.concatenate([flat[:, None], linear_rows, square_rows], 1)
    small = jnp.pad(small, ((0, 0), (0, -small.shape[1] % 16), (0, 0)))
    return jnp.concatenate([square, linear, small], 1).reshape(-1, HEAD_DIM)


def unpack(packed, groups, feature_count):
    squares = feature_count * feature_count
    packed = packed.reshape(groups, -1, HEAD_DIM)
    top = squares + feature_count
    square_den = packed[:, top + 2 : top + 2 + squares // HEAD_DIM].reshape(groups, squares)
    return (
        packed[:, :squares],
        packed[:, squares:top],
        square_den,
        packed[:, top + 1, :feature_count],
        packed[:, top],
    )


def ring_gather(block):
    count = lax.axis_size("ctx")
    me = lax.axis_index("ctx")
    rows = block.shape[0]
    half = rows // 2
    ring = list(range(0, count, 2)) + list(range(1, count, 2))[::-1]
    place = [ring.index(i) for i in range(count)]
    position = jnp.array(place, jnp.int32)[me]
    ring_table = jnp.array(ring, jnp.int32)
    up_route = [(ring[p], ring[(p + 1) % count]) for p in range(count)]
    down_route = [(ring[(p + 1) % count], ring[p]) for p in range(count)]
    up, down = block[:half], block[half:]
    pieces = [(me, up, down, me)]
    for step in range(1, count):
        up = lax.ppermute(up, "ctx", up_route)
        down = lax.ppermute(down, "ctx", down_route)
        pieces.append(
            (
                ring_table[(position - step) % count],
                up,
                down,
                ring_table[(position + step) % count],
            )
        )
    return pieces


def after_hop(pieces, hop, *members):
    if hop >= len(pieces):
        return members
    up_owner, up, down, down_owner = pieces[hop]
    up, down, *members = lax.optimization_barrier((up, down, *members))
    pieces[hop] = (up_owner, up, down, down_owner)
    return members


def assemble(pieces, zero, rows):
    half = rows // 2
    count = len(pieces)
    full = jnp.broadcast_to(zero, (count * rows, pieces[0][1].shape[1]))
    for up_owner, up, down, down_owner in pieces:
        full = lax.dynamic_update_slice(full, up, (up_owner * rows, 0))
        full = lax.dynamic_update_slice(full, down, (down_owner * rows + half, 0))
    return full


def flipped(block, bit):
    return lax.ppermute(block, "head", [(i, i ^ bit) for i in range(4)])


def sum_heads(row):
    if lax.axis_size("head") != 4:
        return lax.psum(row, "head")
    row = row + flipped(row, 1)
    return row + flipped(row, 2)


def sum_from(block, sign):
    count = lax.axis_size("ctx")
    devices = range(count)
    total = jnp.zeros_like(block)
    for distance in range(1, count):
        route = [(i, i + sign * distance) for i in devices if i + sign * distance in devices]
        total = total + lax.ppermute(block, "ctx", route)
    return total


def gather_heads(block):
    if lax.axis_size("head") != 4:
        return lax.all_gather(block, "head", axis=1, tiled=True)
    head = lax.axis_index("head")
    rows, width = block.shape
    far = flipped(block, 2)
    near = flipped(block, 1)
    diagonal = flipped(far, 1)
    full = jnp.zeros((rows, 4 * width), block.dtype)
    for bit, member in ((0, block), (2, far), (1, near), (3, diagonal)):
        full = lax.dynamic_update_slice(full, member, (0, (head ^ bit) * width))
    return full


def scatter_heads(d_student, proj_full):
    def product(weights):
        return lax.dot_general(
            d_student, weights, (((1,), (1,)), ((), ())), preferred_element_type=jnp.float32
        ).astype(jnp.bfloat16)

    if lax.axis_size("head") != 4:
        terms = product(proj_full)
        return lax.psum_scatter(terms, "head", scatter_dimension=1, tiled=True).astype(jnp.float32)
    head = lax.axis_index("head")
    width = proj_full.shape[0] // 4

    def block(bit):
        return product(lax.dynamic_slice_in_dim(proj_full, (head ^ bit) * width, width, 0))

    diagonal = flipped(block(3), 1)
    far = block(2)
    pair = (far.astype(jnp.float32) + diagonal.astype(jnp.float32)).astype(jnp.bfloat16)
    far_sum = flipped(pair, 2)
    near = flipped(block(1), 1)
    own = block(0)
    return own.astype(jnp.float32) + near.astype(jnp.float32) + far_sum.astype(jnp.float32)


def window_tiles(extended, tok_rows):
    tile_count = tok_rows // WIN
    first = extended[:tok_rows].reshape((tile_count, WIN) + extended.shape[1:])
    second = extended[WIN:].reshape((tile_count, WIN) + extended.shape[1:])
    return jnp.concatenate([first, second], 1)


def local(queries, keys, values, feature_map, out_proj, teacher):
    tok_rows = queries.shape[0]
    kv_groups = keys.shape[1] // HEAD_DIM
    ctx_count = lax.axis_size("ctx")
    ctx_index = lax.axis_index("ctx")
    pieces = ring_gather(out_proj)
    query_heads = queries.reshape(tok_rows, kv_groups, GROUP, HEAD_DIM)
    key_heads = keys.reshape(tok_rows, kv_groups, HEAD_DIM)
    value_heads = values.reshape(tok_rows, kv_groups, HEAD_DIM)
    value_float = value_heads.astype(jnp.float32)
    query_features = jnp.einsum(
        "tgqe,gef->tgqf", query_heads, feature_map, preferred_element_type=jnp.float32
    )
    key_features = jnp.einsum(
        "tge,gef->tgf", key_heads, feature_map, preferred_element_type=jnp.float32
    )
    rim_rows = shifted(jnp.stack([keys[tok_rows - WIN :], values[tok_rows - WIN :]]), "ctx", 1)
    keys_ext = jnp.concatenate([rim_rows[0], keys], 0).reshape(tok_rows + WIN, kv_groups, HEAD_DIM)
    values_ext = jnp.concatenate([rim_rows[1], values], 0).reshape(
        tok_rows + WIN, kv_groups, HEAD_DIM
    )
    tile_count = tok_rows // WIN
    key_tiles = window_tiles(keys_ext, tok_rows)
    value_tiles = window_tiles(values_ext, tok_rows)
    query_tiles = query_heads.reshape(tile_count, WIN, kv_groups, GROUP, HEAD_DIM)
    causal = lax.broadcasted_iota(jnp.int32, (tok_rows, tok_rows), 0) >= lax.broadcasted_iota(
        jnp.int32, (tok_rows, tok_rows), 1
    )
    qk_inner = (
        jnp.einsum("tgqf,sgf->gqts", query_features, key_features, precision=exact_mode) / 4.0
    )
    kernel = jnp.where(causal, 1.0 + qk_inner + 0.5 * qk_inner * qk_inner, 0.0)
    numerator = jnp.einsum(
        "gqts,sge->tgqe", kernel.astype(jnp.bfloat16), value_heads, preferred_element_type=jnp.float32
    )
    denominator = jnp.transpose(jnp.sum(kernel, axis=-1), (2, 0, 1))
    query_tiles, numerator, denominator = after_hop(
        pieces, 1, query_tiles, numerator, denominator
    )
    scores = jnp.einsum(
        "ntgqe,nsge->ngqts", query_tiles, key_tiles, preferred_element_type=jnp.float32
    ) / math.sqrt(HEAD_DIM)
    tile_pos = lax.broadcasted_iota(jnp.int32, (tile_count, WIN, 2 * WIN), 0)
    query_pos = lax.broadcasted_iota(jnp.int32, (tile_count, WIN, 2 * WIN), 1)
    key_pos = lax.broadcasted_iota(jnp.int32, (tile_count, WIN, 2 * WIN), 2)
    distance = query_pos + WIN - key_pos
    allowed = (
        (distance >= 0)
        & (distance < WIN)
        & (ctx_index * tok_rows + tile_pos * WIN + key_pos - WIN >= 0)
    )
    allowed = allowed[:, None, None]
    scores = jnp.where(allowed, scores, -jnp.inf)
    row_max = jnp.max(scores, axis=-1, keepdims=True)
    weights = jnp.where(allowed, jnp.exp(scores - row_max), 0.0)
    attn_weights = (weights / jnp.sum(weights, axis=-1, keepdims=True)).astype(jnp.bfloat16)
    window_out = jnp.einsum(
        "ngqts,nsge->ntgqe", attn_weights, value_tiles, preferred_element_type=jnp.float32
    ).reshape(tok_rows, kv_groups, GROUP, HEAD_DIM)
    key_square = taylor_square(key_features)
    own_square_v = jnp.einsum("sgk,sge->gke", key_square, value_float, precision=exact_mode)
    own_linear_v = jnp.einsum("sgf,sge->gfe", key_features, value_float, precision=exact_mode)
    own_values = jnp.sum(value_float, axis=0)
    own_square_k = jnp.sum(key_square, axis=0)
    own_linear_k = jnp.sum(key_features, axis=0)
    no_row = jnp.zeros((8, HEAD_DIM), jnp.float32)
    packed = pack(own_square_v, own_linear_v, own_square_k, own_linear_k, own_values)
    earlier, window_out = after_hop(pieces, 2, sum_from(packed, 1), window_out)
    feature_count = feature_map.shape[2]
    past_square_v, past_linear_v, past_square_k, past_linear_k, past_values = unpack(
        earlier, kv_groups, feature_count
    )
    past_count = (ctx_index * tok_rows).astype(jnp.float32)
    query_square = taylor_square(query_features)
    numerator = (
        numerator
        + jnp.einsum("tgqk,gke->tgqe", query_square, past_square_v, precision=exact_mode) / 32.0
        + jnp.einsum("tgqf,gfe->tgqe", query_features, past_linear_v, precision=exact_mode) / 4.0
        + past_values[None, :, None, :]
    )
    denominator = (
        denominator
        + jnp.einsum("tgqk,gk->tgq", query_square, past_square_k, precision=exact_mode) / 32.0
        + jnp.einsum("tgqf,gf->tgq", query_features, past_linear_k, precision=exact_mode) / 4.0
        + past_count
    )
    linear_out = numerator / denominator[..., None]
    head_out = (
        (linear_out + window_out)
        .astype(jnp.bfloat16)
        .reshape(tok_rows, kv_groups * GROUP * HEAD_DIM)
    )
    head_out, zero = after_hop(pieces, 3, head_out, jnp.zeros((), jnp.bfloat16))
    all_heads = gather_heads(head_out)
    proj_full = assemble(pieces, zero, out_proj.shape[0])
    projected = jnp.dot(all_heads, proj_full, preferred_element_type=jnp.float32)
    student_out = projected.astype(jnp.bfloat16)
    residual = student_out.astype(jnp.float32) - teacher.astype(jnp.float32)
    total_rows = tok_rows * ctx_count
    squared = jnp.sum(residual * residual)
    d_student = (2.0 * residual / total_rows).astype(jnp.bfloat16)
    head_grad = scatter_heads(d_student, proj_full).reshape(
        tok_rows, kv_groups, GROUP, HEAD_DIM
    )
    numerator_grad = head_grad / denominator[..., None]
    denominator_grad = -jnp.sum(head_grad * linear_out, axis=-1) / denominator
    kernel_grad = (
        jnp.einsum(
            "tgqe,sge->gqts",
            two_terms(numerator_grad),
            jnp.concatenate([value_heads, value_heads], -1),
            preferred_element_type=jnp.float32,
        )
        + jnp.transpose(denominator_grad, (1, 2, 0))[..., None]
    )
    inner_grad = (jnp.where(causal, kernel_grad * (1.0 + qk_inner), 0.0) / 4.0).astype(
        jnp.bfloat16
    )
    query_grad = joined(
        jnp.einsum(
            "gqts,sgf->tgqf",
            inner_grad,
            two_terms(key_features),
            preferred_element_type=jnp.float32,
        )
    )
    key_grad = joined(
        jnp.einsum(
            "gqts,tgqf->sgf",
            inner_grad,
            two_terms(query_features),
            preferred_element_type=jnp.float32,
        )
    )
    query_square_grad = (
        jnp.einsum("tgqe,gke->tgqk", numerator_grad, past_square_v, precision=exact_mode)
        + denominator_grad[..., None] * past_square_k[None, :, None, :]
    ) / 32.0
    query_grad = (
        query_grad
        + (
            jnp.einsum("tgqe,gfe->tgqf", numerator_grad, past_linear_v, precision=exact_mode)
            + denominator_grad[..., None] * past_linear_k[None, :, None, :]
        )
        / 4.0
        + square_grad(query_square_grad, query_features)
    )
    own_back_square = jnp.einsum(
        "tgqk,tgqe->gke", query_square, numerator_grad, precision=exact_mode
    )
    own_back_linear = jnp.einsum(
        "tgqf,tgqe->gfe", query_features, numerator_grad, precision=exact_mode
    )
    own_den_square = jnp.einsum(
        "tgqk,tgq->gk", query_square, denominator_grad, precision=exact_mode
    )
    own_den_linear = jnp.einsum(
        "tgqf,tgq->gf", query_features, denominator_grad, precision=exact_mode
    )
    packed_back = pack(
        own_back_square,
        own_back_linear,
        own_den_square,
        own_den_linear,
        jnp.zeros((kv_groups, HEAD_DIM), jnp.float32),
    )
    later = sum_from(packed_back, -1)
    loss_row = sum_heads(jnp.full((8, HEAD_DIM), squared, jnp.float32))
    later_square, later_linear, later_den_square, later_den_linear, _ = unpack(
        later, kv_groups, feature_count
    )
    key_square_grad = (
        jnp.einsum("gke,sge->sgk", later_square, value_float, precision=exact_mode)
        + later_den_square[None]
    ) / 32.0
    key_grad = (
        key_grad
        + (
            jnp.einsum("gfe,sge->sgf", later_linear, value_float, precision=exact_mode)
            + later_den_linear[None]
        )
        / 4.0
        + square_grad(key_square_grad, key_features)
    )
    own_grad = jnp.einsum(
        "tgqe,tgqf->gef", query_heads.astype(jnp.float32), query_grad, precision=exact_mode
    ) + jnp.einsum("tge,tgf->gef", key_heads.astype(jnp.float32), key_grad, precision=exact_mode)
    packed_grad = jnp.concatenate([own_grad.reshape(-1, HEAD_DIM), loss_row], 0)
    summed, _ = exchange(packed_grad, no_row, "all", 0)
    feature_grad = summed[:-8].reshape(own_grad.shape)
    loss_value = summed[-8, 0] / (total_rows * D)
    return (student_out, loss_value, feature_grad)


FEATURE_PAIRS = 153
PAIR_ROWS = 160
CHUNKS = 4
STREAMS = 2


def pair_tables():
    j = np.arange(2 * HEAD_DIM)
    valid = j < FEATURE_PAIRS
    first = j % 17
    second = (first + j // 17) % 17
    select = np.zeros((2, 2 * HEAD_DIM, HEAD_DIM), np.float32)
    constant = np.zeros((2, 2 * HEAD_DIM), np.float32)
    for side, member in enumerate((first, second)):
        for row in np.nonzero(valid)[0]:
            if member[row] < 16:
                select[side, row, member[row]] = 1.0
            else:
                constant[side, row] = 1.0
    is_one = (first == 16).astype(int) + (second == 16).astype(int)
    coef = np.where(is_one == 2, 1.0, np.where(is_one == 1, 0.25, np.where(first == second, 1 / 32, 1 / 16)))
    coef = np.where(valid, coef, 0.0)
    bits = np.concatenate([select[0], select[1], np.eye(HEAD_DIM)], 0)
    rows = np.zeros((8, 2 * HEAD_DIM), np.float32)
    rows[0], rows[1], rows[2] = constant[0], constant[1], coef
    columns = np.zeros((2 * HEAD_DIM, HEAD_DIM), np.float32)
    columns[:, 0], columns[:, 1], columns[:, 2] = constant[0], constant[1], coef
    return bits, rows, columns


def mm(a, b):
    return lax.dot_general(a, b, (((1,), (0,)), ((), ())), preferred_element_type=jnp.float32)


def mm_t(a, b):
    return lax.dot_general(a, b, (((1,), (1,)), ((), ())), preferred_element_type=jnp.float32)


def split_terms(x):
    high = x.astype(jnp.bfloat16)
    return high, (x - high.astype(jnp.float32)).astype(jnp.bfloat16)


def fused_kernel(
    queries_in, keys_in, values_in, map_ref, proj_ref, teacher_ref, bits_ref, rows_ref, columns_ref,
    student_ref, grad_ref, loss_ref,
    proj_buf, heads_buf, window, own_sum, first_factor, second_factor, pairs_t, queries_t, slope, lin, den_inv,
    d_student, acc, queries_ref, teacher_buf, keys_ext, values_ext, ones_values, wide_map, wide_map_t, kernel_map,
    past_high, past_low, key_features, key_factor_a, key_factor_b, keys_t,
    state_own, state_x, state_low, state_up,
    send_n, recv_n, send_d, recv_d, send_a, recv_a, send_b, recv_b,
    cross, grad_a, grad_b, back, back_own, back_x, back_sum, back_later, back_in, final_own, final_in, loss_acc, loss_own, loss_in,
    ring_send, ring_recv, own_sem, input_sem, teacher_sem, teacher_send, teacher_recv, student_sem, student_send,
    student_recv, part_send, part_recv, rim_send, rim_recv, state_x_send, state_x_recv,
    state_up_send, state_up_recv, side_send, side_recv, near_send, near_recv, far_send, far_recv,
    n_send, n_recv, d_send, d_recv, a_send, a_recv, b_send, b_recv,
    back_x_send, back_x_recv, back_send, back_recv, final_send, final_recv, loss_send, loss_recv,
):
    f32, bf16 = jnp.float32, jnp.bfloat16
    mesh_ids = pl.DeviceIdType.MESH
    ctx_count = 8
    tokens = queries_in.shape[0]
    half = tokens // 2
    width = proj_buf.shape[2]
    E = HEAD_DIM
    c = lax.axis_index("ctx")
    h = lax.axis_index("head")
    z = c // 2
    x = c % 2
    side = c + 1 - 2 * x
    columns_here = x * (proj_ref.shape[1] // 2)
    columns_there = (1 - x) * (proj_ref.shape[1] // 2)

    near = h + 1 - 2 * (h % 2)
    far = (h + 2) % 4
    diagonal = 3 - h

    def remote(src, dst, send, recv, ctx, head):
        return pltpu.make_async_remote_copy(
            src_ref=src, dst_ref=dst, send_sem=send, recv_sem=recv, device_id=(ctx, head), device_id_type=mesh_ids
        )

    inputs = [
        pltpu.make_async_copy(keys_in, keys_ext.at[pl.ds(WIN, tokens)], input_sem.at[0]),
        pltpu.make_async_copy(values_in, values_ext.at[pl.ds(WIN, tokens)], input_sem.at[1]),
        pltpu.make_async_copy(queries_in, queries_ref, input_sem.at[2]),
    ]
    barrier = pltpu.get_barrier_semaphore()
    for d in range(1, ctx_count):
        pl.semaphore_signal(barrier, inc=1, device_id=((c + d) % ctx_count, h), device_id_type=mesh_ids)
    for d in range(1, 4):
        pl.semaphore_signal(barrier, inc=1, device_id=(c, (h + d) % 4), device_id_type=mesh_ids)
    for copy in inputs:
        copy.start()
    pl.semaphore_wait(barrier, ctx_count + 2)

    def plane_rows(plane, q):
        return pl.ds(pl.multiple_of(plane * 2 * tokens + q * half, half), half)

    def chunk_columns(start, j):
        return pl.ds(pl.multiple_of(start + j * width, width), width)

    def part_copy(j, d, ctx):
        place = proj_buf.at[j, pl.ds(pl.multiple_of(ctx * tokens + d * half, half), half)]
        src = proj_ref.at[pl.ds(d * half, half), chunk_columns(columns_there, j)]
        return remote(src, place, part_send.at[j, d], part_recv.at[j, d], side, h)

    def target(d):
        return lax.rem(c + 2, ctx_count) if d == 0 else lax.rem(c + ctx_count - 2, ctx_count)

    def has_target(d):
        return z < 3 if d == 0 else z > 0

    def has_owner(d, k):
        return z >= k if d == 0 else z + k <= 3

    def hop(d, j, k, q):
        place = proj_buf.at[j, plane_rows(jnp.clip(z - k if d == 0 else z + k, 0, 3), q)]
        return remote(place, place, ring_send.at[d, j, k * 4 + q], ring_recv.at[d, j, k * 4 + q], target(d), h)

    def first_hop(d, j, q, m):
        place = proj_buf.at[j, plane_rows(z, q)]
        src = proj_ref.at[pl.ds(m * half, half), chunk_columns(columns_here, j)] if m < 2 else place
        return remote(src, place, ring_send.at[d, j, q], ring_recv.at[d, j, q], target(d), h)

    def arrival(d, j, k, q):
        plane = jnp.clip(z - 1 - k if d == 0 else z + 1 + k, 0, 3)
        place = proj_buf.at[j, plane_rows(plane, q)]
        return remote(place, place, ring_send.at[d, j, k * 4 + q], ring_recv.at[d, j, k * 4 + q], target(d), h)

    def quarter(m):
        return lax.rem(2 * x + m, 4)

    def start_first(group, r):
        m = r // STREAMS
        j = group * STREAMS + r % STREAMS
        if m >= 2:
            part_copy(j, m - 2, side).wait_recv()
        for d in (0, 1):

            @pl.when(has_target(d))
            def _():
                first_hop(d, j, quarter(m), m).start()

    def service(group, n):
        k = n // 8
        j = group * STREAMS + n % STREAMS
        q = quarter((n % 8) // STREAMS)
        for d in (0, 1):

            @pl.when(has_owner(d, k))
            def _():
                arrival(d, j, k - 1, q).wait_recv()

            @pl.when(has_owner(d, k) & has_target(d))
            def _():
                hop(d, j, k, q).start()

    def last_arrival(group, r):
        for d in (0, 1):

            @pl.when(has_owner(d, 3))
            def _():
                arrival(d, group * STREAMS + r % STREAMS, 2, quarter(r // STREAMS)).wait_recv()

    for s, (src, dst) in enumerate(((keys_in, keys_ext), (values_in, values_ext))):

        @pl.when(c < ctx_count - 1)
        def _():
            remote(
                src.at[pl.ds(tokens - WIN, WIN)], dst.at[pl.ds(0, WIN)], rim_send.at[s], rim_recv.at[s],
                lax.rem(c + 1, ctx_count), h,
            ).start()

        @pl.when(c == 0)
        def _():
            dst[pl.ds(0, WIN), :] = jnp.zeros((WIN, E), bf16)

        dst[pl.ds(WIN + tokens, WIN), :] = jnp.zeros((WIN, E), bf16)

    for r in range(4):
        start_first(0, r)
    for j in range(STREAMS):
        for d in (0, 1):
            part_copy(j, d, c).start()
    teacher_copy = pltpu.make_async_copy(
        teacher_ref.at[:, pl.ds(pl.multiple_of(columns_here, width), CHUNKS * width)], teacher_buf.at[x], teacher_sem.at[0]
    )
    teacher_copy.start()

    def teacher_part(ctx_half):
        return remote(
            teacher_ref.at[:, pl.ds(pl.multiple_of(columns_there, width), CHUNKS * width)],
            teacher_buf.at[ctx_half], teacher_send.at[0], teacher_recv.at[0], side, h,
        )

    def own_copy(j):
        return pltpu.make_async_copy(
            proj_ref.at[:, chunk_columns(columns_here, j)],
            proj_buf.at[j, pl.ds(pl.multiple_of(c * tokens, tokens), tokens)],
            own_sem.at[j],
        )

    for j in range(CHUNKS):
        own_copy(j).start()

    eye = bits_ref[pl.ds(4 * E, E), :]
    map_rows = jnp.concatenate([map_ref[...], jnp.zeros((E - map_ref.shape[0], E), bf16)], 0)
    map_wide = mm_t(eye, map_rows).astype(bf16)
    for s in range(2):
        select = bits_ref[pl.ds(s * 2 * E, 2 * E), :]
        wide_map[s] = mm_t(map_wide, select).astype(bf16)
        wide_map_t[s] = mm_t(select, map_wide).astype(bf16)
    inputs[0].wait()
    inputs[1].wait()
    keys = keys_ext[pl.ds(WIN, tokens), :]
    features = mm(keys, map_wide)
    feature_high, feature_low = split_terms(features)
    key_features[0] = feature_high
    key_features[1] = feature_low
    inner = (mm_t(map_wide, feature_high) + mm_t(map_wide, feature_low)) * 0.25
    inner_high, inner_low = split_terms(inner)
    kernel_map[pl.ds(0, E), :] = inner_high
    kernel_map[pl.ds(E, E), :] = inner_low
    keys_t[...] = mm_t(eye, keys).astype(bf16)
    key_a = mm(keys, wide_map[0]) + rows_ref[pl.ds(0, 1), :]
    key_b = mm(keys, wide_map[1]) + rows_ref[pl.ds(1, 1), :]
    key_factor_a[...] = (key_a * rows_ref[pl.ds(2, 1), :]).astype(bf16)
    key_factor_b[...] = (key_b * rows_ref[pl.ds(2, 1), :]).astype(bf16)
    ones_values[:, pl.ds(0, E)] = values_ext[pl.ds(WIN, tokens), :]
    ones_values[:, pl.ds(E, E)] = jnp.ones((tokens, E), bf16)
    key_a_t = mm_t(wide_map_t[0], keys) + columns_ref[:, 0:1]
    key_b_t = mm_t(wide_map_t[1], keys) + columns_ref[:, 1:2]
    key_high, key_low = split_terms(key_a_t * key_b_t * columns_ref[:, 2:3])
    state = mm(key_high, ones_values[...]) + mm(key_low, ones_values[...])

    def store_state(ref, value, den_row):
        ref[pl.ds(0, PAIR_ROWS), :] = value[:PAIR_ROWS]
        ref[pl.ds(PAIR_ROWS, 8), :] = den_row[:, :E]
        ref[pl.ds(PAIR_ROWS + 8, 8), :] = den_row[:, E:]

    store_state(state_own, state[:, :E], jnp.transpose(state[:, E:])[:8])
    state_x_copy = remote(state_own, state_x, state_x_send.at[0], state_x_recv.at[0], side, h)
    state_x_copy.start()
    for r in range(4, 8):
        start_first(0, r)
    for j in range(STREAMS, CHUNKS):
        for d in (0, 1):
            part_copy(j, d, c).start()
    teacher_part(x).start()
    inputs[2].wait()

    def state_up_copy():
        return remote(state_up, state_low, state_up_send.at[0], state_up_recv.at[0], lax.rem(c + 2, ctx_count), h)

    def chain_step(level):
        if level == 0:
            state_x_copy.wait_recv()

            @pl.when(z == 0)
            def _():
                state_low[...] = jnp.zeros_like(state_low)

        else:

            @pl.when(z == level)
            def _():
                state_up_copy().wait_recv()

        if level < 3:

            @pl.when(z == level)
            def _():
                state_up[...] = state_low[...] + state_own[...] + state_x[...]
                state_up_copy().start()

    for s in range(2):

        @pl.when(c > 0)
        def _():
            dst = (keys_ext, values_ext)[s]
            remote(
                dst.at[pl.ds(0, WIN)], dst.at[pl.ds(0, WIN)], rim_send.at[s], rim_recv.at[s], c, h
            ).wait_recv()

    def query_tile(i, hp):
        token = pl.multiple_of(i * E, E)
        both = queries_ref[pl.ds(token, E), pl.ds(pl.multiple_of(hp * 2 * E, 2 * E), 2 * E)]
        return jnp.concatenate([both[:, :E], both[:, E:]], 0)

    for i in range(4):
        reach = (i + 1) * E

        def local_tile(hp, carry):
            tile = i * 4 + hp
            q = query_tile(i, hp)
            u = mm(jnp.concatenate([q, q], 1), kernel_map[:, pl.ds(0, reach)])
            row = lax.broadcasted_iota(jnp.int32, (2 * E, reach), 0) % E + i * E
            causal = row >= lax.broadcasted_iota(jnp.int32, (2 * E, reach), 1)
            kernel = jnp.where(causal, 1.0 + u + 0.5 * u * u, 0.0).astype(bf16)
            slope[tile, :, pl.ds(0, reach)] = jnp.where(causal, 0.25 + 0.25 * u, 0.0).astype(bf16)
            both = mm(kernel, ones_values[pl.ds(0, reach), :])
            lin[tile] = both[:, :E]
            den_inv[tile] = both[:, E:]
            scores = mm_t(q, keys_ext[pl.ds(i * E, 2 * E), :]) / math.sqrt(HEAD_DIM)
            token = lax.broadcasted_iota(jnp.int32, (2 * E, 2 * E), 0) % E
            place = lax.broadcasted_iota(jnp.int32, (2 * E, 2 * E), 1)
            distance = token + WIN - place
            allowed = (distance >= 0) & (distance < WIN) & (c * tokens + i * E + place - WIN >= 0)
            scores = jnp.where(allowed, scores, -jnp.inf)
            top = jnp.max(scores, axis=-1, keepdims=True)
            weights = jnp.where(allowed, jnp.exp(scores - top), 0.0)
            weights = (weights / jnp.sum(weights, axis=-1, keepdims=True)).astype(bf16)
            window[tile] = mm(weights, values_ext[pl.ds(i * E, 2 * E), :])
            first_factor[tile] = (mm(q, wide_map[0]) + rows_ref[pl.ds(0, 1), :]).astype(bf16)
            second_factor[tile] = (mm(q, wide_map[1]) + rows_ref[pl.ds(1, 1), :]).astype(bf16)
            pair_a = mm_t(wide_map_t[0], q) + columns_ref[:, 0:1]
            pair_b = mm_t(wide_map_t[1], q) + columns_ref[:, 1:2]
            pairs_t[tile] = (pair_a * pair_b).astype(bf16)[:PAIR_ROWS]
            queries_t[tile] = mm_t(eye, q).astype(bf16)
            service(0, 8 + tile)
            return carry

        lax.fori_loop(0, 4, local_tile, 0)
        chain_step(i)

    past = jnp.where(z > 0, state_low[...], 0.0) + jnp.where(x == 1, state_x[...], 0.0)
    past_rows = jnp.concatenate([past[PAIR_ROWS : PAIR_ROWS + 8], past[PAIR_ROWS + 8 :]], 1)
    past_den = jnp.transpose(jnp.broadcast_to(past_rows[:1], (E, 2 * E)))
    past_values = jnp.concatenate([past[:PAIR_ROWS], jnp.zeros((2 * E - PAIR_ROWS, E), f32)], 0)
    high, low = split_terms(jnp.concatenate([past_values, past_den], 1))
    past_high[...] = high
    past_low[...] = low

    def head_piece(i, ctx_half, head):
        return heads_buf.at[ctx_half * 4 + head, pl.ds(pl.multiple_of(i * E, E), E)]

    def side_copy(i, ctx_half):
        piece = head_piece(i, ctx_half, h)
        return remote(piece, piece, side_send.at[i], side_recv.at[i], side, h)

    def near_copy(i, s, head):
        ctx_half = x if s % 2 == 0 else 1 - x
        piece = head_piece(i, ctx_half, head)
        return remote(piece, piece, near_send.at[s, i], near_recv.at[s, i], c, near)

    def far_copy(i, s, head):
        ctx_half = x if s == 0 else 1 - x
        piece = head_piece(i, ctx_half, head)
        return remote(piece, piece, far_send.at[s, i], far_recv.at[s, i], c, far)

    def past_tiles(i, carry):
        def past_tile(hp, carry):
            tile = i * 4 + hp
            q = query_tile(i, hp)
            pair = (mm(q, wide_map[0]) + rows_ref[pl.ds(0, 1), :]) * (mm(q, wide_map[1]) + rows_ref[pl.ds(1, 1), :])
            pair_high, pair_low = split_terms(pair)
            both = mm(pair_high, past_high[...]) + mm(pair_low, past_high[...]) + mm(pair_high, past_low[...])
            den = den_inv[tile] + both[:, E:]
            value = (lin[tile] + both[:, :E]) / den
            lin[tile] = value
            den_inv[tile] = 1.0 / den
            out = (value + window[tile]).astype(bf16)
            heads_buf[
                x * 4 + h, pl.ds(pl.multiple_of(i * E, E), E), pl.ds(pl.multiple_of(hp * 2 * E, 2 * E), 2 * E)
            ] = jnp.concatenate([out[:E], out[E:]], 1)
            return carry

        lax.fori_loop(0, 4, past_tile, 0)
        side_copy(i, x).start()
        far_copy(i, 0, h).start()
        near_copy(i, 0, h).start()
        return carry

    lax.fori_loop(0, 4, past_tiles, 0)
    for r in range(8):
        start_first(1, r)

    def relay_side(i, carry):
        side_copy(i, 1 - x).wait_recv()
        far_copy(i, 1, h).start()
        near_copy(i, 1, h).start()
        return carry

    lax.fori_loop(0, 4, relay_side, 0)

    def relay_far(i, carry):
        service(1, 8 + i)
        far_copy(i, 0, far).wait_recv()
        near_copy(i, 2, far).start()
        return carry

    lax.fori_loop(0, 4, relay_far, 0)

    def relay_last(i, carry):
        service(1, 12 + i)
        far_copy(i, 1, far).wait_recv()
        near_copy(i, 3, far).start()
        return carry

    lax.fori_loop(0, 4, relay_last, 0)
    teacher_copy.wait()
    teacher_part(1 - x).wait_recv()
    for j in range(CHUNKS):
        own_copy(j).wait()
    loss_acc[...] = jnp.zeros_like(loss_acc)
    for i in range(4):
        for s in range(4):
            near_copy(i, s, near if s < 2 else diagonal).wait_recv()
    for r in range(8):
        last_arrival(0, r)

    def student_copy(j):
        return pltpu.make_async_copy(
            teacher_buf.at[x, :, chunk_columns(0, j)], student_ref.at[:, chunk_columns(columns_here, j)], student_sem.at[j]
        )

    def student_part(j, start):
        return remote(
            teacher_buf.at[1 - x, :, chunk_columns(0, j)], student_ref.at[:, chunk_columns(start, j)],
            student_send.at[j], student_recv.at[j], side, h,
        )

    def finish_columns(j, ctx_half, product):
        student = product.astype(bf16)
        columns = chunk_columns(0, j)
        residual = student.astype(f32) - teacher_buf[ctx_half, :, columns].astype(f32)
        teacher_buf[ctx_half, :, columns] = student
        loss_acc[...] += jnp.sum((residual * residual).reshape(tokens // 8, 8, width), axis=0)
        d_student[j, ctx_half] = (residual * (2.0 / (tokens * ctx_count))).astype(bf16)

    def finish_both(j, products):
        finish_columns(j, 1 - x, products[1])
        student_part(j, columns_here).start()
        finish_columns(j, x, products[0])
        student_copy(j).start()

    def plane_product(ctx_half, plane, j):
        rows = pl.ds(pl.multiple_of(plane * 2 * tokens, 2 * tokens), 2 * tokens)
        return mm(heads_buf[ctx_half * 4 + plane], proj_buf[j, rows, :])

    def first_columns(j, carry):
        products = []
        for ctx_half in (x, 1 - x):
            product = plane_product(ctx_half, 0, j)
            for plane in range(1, 4):
                product += plane_product(ctx_half, plane, j)
            products.append(product)
        finish_both(j, products)
        for n in range(4):
            service(1, 16 + 4 * j + n)
        return carry

    lax.fori_loop(0, STREAMS, first_columns, 0)
    last_plane = jnp.where(z >= 2, 0, 3)

    def second_early(s, carry):
        j = STREAMS + s
        for t, ctx_half in enumerate((x, 1 - x)):
            product = plane_product(ctx_half, (last_plane + 1) % 4, j)
            for b in (2, 3):
                product += plane_product(ctx_half, (last_plane + b) % 4, j)
            acc[s * 2 + t] = product
        return carry

    lax.fori_loop(0, STREAMS, second_early, 0)
    for r in range(8):
        last_arrival(1, r)
        m, s = r // STREAMS, r % STREAMS
        j = STREAMS + s
        q = quarter(m)
        products = []
        for t, ctx_half in enumerate((x, 1 - x)):
            left = heads_buf[ctx_half * 4 + last_plane, :, pl.ds(pl.multiple_of(q * half, half), half)]
            products.append(acc[s * 2 + t] + mm(left, proj_buf[j, plane_rows(last_plane, q), :]))
            if m < 3:
                acc[s * 2 + t] = products[t]
        if m == 3:
            finish_both(j, products)

    def block_sum(ctx_half, head, p):
        rows = pl.ds(pl.multiple_of((head * 4 + p) * width, width), width)
        total = mm_t(d_student[0, ctx_half], proj_buf[0, rows, :])
        for j in range(1, CHUNKS):
            total += mm_t(d_student[j, ctx_half], proj_buf[j, rows, :])
        return total

    def copy_n(s):
        return remote(send_n.at[s], recv_n.at[s], n_send.at[s], n_recv.at[s], c, near)

    def copy_d(p):
        ctx, head = (side, h) if p < 2 else (c, far)
        return remote(send_d.at[p], recv_d.at[p], d_send.at[p], d_recv.at[p], ctx, head)

    def copy_a(p):
        return remote(send_a.at[p], recv_a.at[p], a_send.at[p], a_recv.at[p], side, h)

    def copy_b(p):
        return remote(send_b.at[p], recv_b.at[p], b_send.at[p], b_recv.at[p], c, far)

    kinds = {"d": (1, 1), "a": (1, 0), "b": (0, 1), "own": (0, 0)}

    def slot(kind, p):
        return (kinds[kind][0] * 2 + kinds[kind][1]) * 4 + p

    def give(kind, p):
        other, distant = kinds[kind]
        ctx_half = 1 - x if other else x
        send_n[slot(kind, p)] = block_sum(ctx_half, diagonal if distant else near, p).astype(bf16)
        copy_n(slot(kind, p)).start()

    def take(kind, p):
        other, distant = kinds[kind]
        ctx_half = 1 - x if other else x
        total = block_sum(ctx_half, far if distant else h, p)
        copy_n(slot(kind, p)).wait_recv()
        return total + recv_n[slot(kind, p)].astype(f32)

    def send_corner(p):
        send_d[p] = take("d", p).astype(bf16)
        copy_d(p).start()

    def send_side(kind, p, corner):
        total = take(kind, p)
        if corner:
            copy_d(p).wait_recv()
            total += recv_d[p].astype(f32)
        if kind == "a":
            send_a[p] = total.astype(bf16)
            copy_a(p).start()
        else:
            send_b[p] = total.astype(bf16)
            copy_b(p).start()

    for p in (0, 1):
        give("d", p)
        give("d", p + 2)
        send_corner(p)
        send_corner(p + 2)
    for p in (0, 1):
        give("a", p)
        give("b", p + 2)
        send_side("a", p, False)
        send_side("b", p + 2, False)
    for p in (0, 1):
        give("a", p + 2)
        give("b", p)
        send_side("a", p + 2, True)
        send_side("b", p, True)
    for p in range(4):
        give("own", p)
    for p in range(4):
        own_sum[p] = take("own", p)

    loss_own[...] = loss_acc[:, :E] + loss_acc[:, E:]

    def loss_copy(d, source):
        return remote(loss_own, loss_in.at[source], loss_send.at[d], loss_recv.at[source], c, (h + d) % 4)

    for d in range(1, 4):
        loss_copy(d, h).start()

    cross[...] = jnp.zeros_like(cross)
    grad_a[...] = jnp.zeros_like(grad_a)
    grad_b[...] = jnp.zeros_like(grad_b)
    back[...] = jnp.zeros_like(back)

    def grad_piece(p, carry):
        copy_a(p).wait_recv()
        copy_b(p).wait_recv()
        for i in range(4):
            reach = (i + 1) * E
            tile = i * 4 + p
            rows = pl.ds(i * E, E)
            g = own_sum[p, rows, :] + recv_a[p, rows, :].astype(f32) + recv_b[p, rows, :].astype(f32)
            g = jnp.concatenate([g[:, :E], g[:, E:]], 0)
            inverse = den_inv[tile]
            upper = (g * inverse).astype(bf16)
            lower = -jnp.sum(upper.astype(f32) * lin[tile], axis=-1, keepdims=True)
            lower = jnp.broadcast_to(lower, (2 * E, E))
            lower_high = lower.astype(bf16).astype(f32)
            lane = lax.broadcasted_iota(jnp.int32, (2 * E, E), 1)
            lower = (jnp.where(lane < E // 2, lower_high, lower - lower_high) * (2.0 / E)).astype(bf16)
            wide = jnp.concatenate([upper, lower], 1)
            weight = mm_t(wide, ones_values[pl.ds(0, reach), :]) * slope[tile, :, pl.ds(0, reach)].astype(f32)
            cross[:, pl.ds(0, reach)] += mm(queries_t[tile], weight.astype(bf16))
            pair_grad = mm_t(wide, past_high[...]) + mm_t(wide, past_low[...])
            grad_a[...] += mm(queries_t[tile], (pair_grad * second_factor[tile].astype(f32)).astype(bf16))
            grad_b[...] += mm(queries_t[tile], (pair_grad * first_factor[tile].astype(f32)).astype(bf16))
            back[...] += mm(pairs_t[tile], wide)
        return carry

    def grad_pieces(n, carry):
        return grad_piece((n % 2) * 2 + n // 2, carry)

    lax.fori_loop(0, 4, grad_pieces, 0)

    back_den = jnp.transpose(
        jnp.concatenate([back[:, pl.ds(E, E)], jnp.zeros((2 * E - PAIR_ROWS, E), f32)], 0)
    )
    back_den = (back_den[:8] + back_den[E // 2 : E // 2 + 8]) * (E // 2)
    store_state(back_own, back[:, pl.ds(0, E)], back_den)
    back_x_copy = remote(back_own, back_x, back_x_send.at[0], back_x_recv.at[0], side, h)
    back_x_copy.start()

    def back_copy(level):
        return remote(back_sum, back_in.at[z], back_send.at[level], back_recv.at[z], 2 * level + x, h)

    def back_arrival(level):
        return remote(back_sum, back_in.at[level], back_send.at[level], back_recv.at[level], c, h)

    cross_high, cross_low = split_terms(cross[...])
    grad = mm(cross_high, key_features[0]) + mm(cross_high, key_features[1]) + mm(cross_low, key_features[0])
    keys = keys_ext[pl.ds(WIN, tokens), :]
    mixed = jnp.transpose(mm(cross_high, keys) + mm(cross_low, keys))
    mixed_high, mixed_low = split_terms(mixed)
    map_rows = jnp.concatenate([map_ref[...], jnp.zeros((E - map_ref.shape[0], E), bf16)], 0)
    map_wide = mm_t(bits_ref[pl.ds(4 * E, E), :], map_rows).astype(bf16)
    grad += mm(mixed_high, map_wide) + mm(mixed_low, map_wide)

    center = mm(jnp.ones((8, tokens), bf16), values_ext[pl.ds(WIN, tokens), :])
    center = (center / tokens).astype(bf16)
    back_x_copy.wait_recv()
    plane = back_own[...] + back_x[...]
    plane_values = plane[:PAIR_ROWS].astype(bf16)
    lost = (plane[:PAIR_ROWS] - plane_values.astype(f32)).astype(bf16)
    lost = jnp.concatenate([lost, jnp.zeros((2 * E - PAIR_ROWS, E), bf16)], 0)
    moved = mm_t(center, lost)
    plane_den = plane[PAIR_ROWS:] + jnp.concatenate([moved[:, :E], moved[:, E:]], 0)
    den_high, den_low = split_terms(plane_den)
    back_sum[pl.ds(0, PAIR_ROWS), :] = plane_values
    back_sum[pl.ds(PAIR_ROWS, 16), :] = den_high
    back_sum[pl.ds(PAIR_ROWS + 16, 16), :] = den_low
    for level in range(3):

        @pl.when(level < z)
        def _():
            back_copy(level).start()

    back_later[...] = jnp.where(x == 0, back_x[...], 0.0)
    for level in range(1, 4):

        @pl.when(level > z)
        def _():
            back_arrival(level).wait_recv()
            arrived = back_in[level].astype(f32)
            back_later[...] += arrived[: PAIR_ROWS + 16]
            back_later[pl.ds(PAIR_ROWS, 16), :] += arrived[PAIR_ROWS + 16 :]

    later_values = jnp.concatenate([back_later[pl.ds(0, PAIR_ROWS), :], jnp.zeros((2 * E - PAIR_ROWS, E), f32)], 0)
    later_high, later_low = split_terms(later_values)
    pair_grad = mm_t(values_ext[pl.ds(WIN, tokens), :], later_high)
    pair_grad += mm_t(values_ext[pl.ds(WIN, tokens), :], later_low)
    pair_grad += jnp.concatenate(
        [back_later[pl.ds(PAIR_ROWS, 1), :], back_later[pl.ds(PAIR_ROWS + 8, 1), :]], 1
    )
    total_a = grad_a[...] + mm(keys_t[...], (pair_grad * key_factor_b[...].astype(f32)).astype(bf16))
    total_b = grad_b[...] + mm(keys_t[...], (pair_grad * key_factor_a[...].astype(f32)).astype(bf16))
    for s, total in enumerate((total_a, total_b)):
        total_high, total_low = split_terms(total)
        select = bits_ref[pl.ds(s * 2 * E, 2 * E), :]
        grad += mm(total_high, select) + mm(total_low, select)
    final_own[pl.ds(0, 16), :] = jnp.transpose(grad)[:16]
    loss_sum = loss_own[...]
    for d in range(1, 4):
        loss_copy(d, (h + d) % 4).wait_recv()
        loss_sum += loss_in[(h + d) % 4]
    final_own[pl.ds(16, 8), :] = loss_sum

    def final_copy(d, source):
        return remote(final_own, final_in.at[source], final_send.at[d], final_recv.at[source], (c + d) % ctx_count, h)

    for d in range(1, ctx_count):
        final_copy(d, c).start()
    final_in[c] = final_own[...]
    for d in range(1, ctx_count):
        final_copy(d, (c + d) % ctx_count).wait_recv()
    final = final_in[0]
    for s in range(1, ctx_count):
        final += final_in[s]
    grad_ref[...] = final[:16]
    loss_ref[0, 0] = jnp.sum(final[16:]) / (tokens * ctx_count * D)

    for j in range(CHUNKS):
        student_copy(j).wait()
        student_part(j, columns_here).wait_send()
        student_part(j, columns_there).wait_recv()
        for d in (0, 1):
            part_copy(j, d, c).wait_send()
            for m in range(4):
                for k in range(3):

                    @pl.when(has_target(d) & has_owner(d, k))
                    def _():
                        hop(d, j, k, quarter(m)).wait_send()

    teacher_part(x).wait_send()
    for s in range(2):

        @pl.when(c < ctx_count - 1)
        def _():
            dst = (keys_ext, values_ext)[s]
            src = (keys_in, values_in)[s]
            remote(
                src.at[pl.ds(tokens - WIN, WIN)], dst.at[pl.ds(0, WIN)], rim_send.at[s], rim_recv.at[s],
                lax.rem(c + 1, ctx_count), h,
            ).wait_send()

    state_x_copy.wait_send()

    @pl.when(z < 3)
    def _():
        state_up_copy().wait_send()

    back_x_copy.wait_send()
    for level in range(3):

        @pl.when(level < z)
        def _():
            back_copy(level).wait_send()

    for d in range(1, 4):
        loss_copy(d, h).wait_send()
    for i in range(4):
        side_copy(i, x).wait_send()
        for s in range(2):
            far_copy(i, s, h).wait_send()
        for s in range(4):
            near_copy(i, s, h if s < 2 else far).wait_send()
    for p in range(4):
        copy_d(p).wait_send()
        copy_a(p).wait_send()
        copy_b(p).wait_send()
    for s in range(16):
        copy_n(s).wait_send()
    for d in range(1, ctx_count):
        final_copy(d, c).wait_send()


def deliver_kernel(student_ref, grad_ref, loss_ref, student_out, grad_out, loss_out, buffer, grad_buffer, sem, out_sem):
    part = student_ref.shape[0] // 4
    moves = [(ref.at[pl.ds(s * part, part)], buffer.at[pl.ds(s * part, part)], student_out.at[pl.ds(s * part, part)])
             for s, ref in enumerate([student_ref] * 4)]
    moves.append((grad_ref, grad_buffer, grad_out))
    reads = [pltpu.make_async_copy(src, mid, sem.at[s]) for s, (src, mid, dst) in enumerate(moves)]
    writes = [pltpu.make_async_copy(mid, dst, out_sem.at[s]) for s, (src, mid, dst) in enumerate(moves)]
    for copy in reads:
        copy.start()
    loss_out[0, 0] = loss_ref[0, 0]
    for read, write in zip(reads, writes):
        read.wait()
        write.start()
    for copy in writes:
        copy.wait()


def fused_local(queries, keys, values, feature_map, out_proj, teacher):
    tokens = queries.shape[0]
    columns = out_proj.shape[1]
    rows = tokens * 8
    width = columns // 2 // CHUNKS
    E = HEAD_DIM
    bf16, f32 = jnp.bfloat16, jnp.float32
    bits, row_table, column_table = pair_tables()
    vmem = pl.BlockSpec(memory_space=pltpu.VMEM)
    anywhere = pl.BlockSpec(memory_space=pl.ANY)
    smem = pl.BlockSpec(memory_space=pltpu.SMEM)
    dma = pltpu.SemaphoreType.DMA
    state = (PAIR_ROWS + 16, E)
    scratch = [
        ((CHUNKS, rows, width), bf16),
        ((8, tokens, 8 * E), bf16),
        ((16, 2 * E, E), f32),
        ((4, tokens, width), f32),
        ((16, 2 * E, 2 * E), bf16),
        ((16, 2 * E, 2 * E), bf16),
        ((16, PAIR_ROWS, 2 * E), bf16),
        ((16, E, 2 * E), bf16),
        ((16, 2 * E, tokens), bf16),
        ((16, 2 * E, E), f32),
        ((16, 2 * E, E), f32),
        ((CHUNKS, 2, tokens, width), bf16),
        ((2 * STREAMS, tokens, width), f32),
        ((tokens, 8 * E), bf16),
        ((2, tokens, columns // 2), bf16),
        ((tokens + 2 * WIN, E), bf16),
        ((tokens + 2 * WIN, E), bf16),
        ((tokens, 2 * E), bf16),
        ((2, E, 2 * E), bf16),
        ((2, 2 * E, E), bf16),
        ((2 * E, tokens), bf16),
        ((2 * E, 2 * E), bf16),
        ((2 * E, 2 * E), bf16),
        ((2, tokens, E), bf16),
        ((tokens, 2 * E), bf16),
        ((tokens, 2 * E), bf16),
        ((E, tokens), bf16),
        (state, f32),
        (state, f32),
        (state, f32),
        (state, f32),
        ((16, tokens, width), bf16),
        ((16, tokens, width), bf16),
        ((4, tokens, width), bf16),
        ((4, tokens, width), bf16),
        ((4, tokens, width), bf16),
        ((4, tokens, width), bf16),
        ((4, tokens, width), bf16),
        ((4, tokens, width), bf16),
        ((E, tokens), f32),
        ((E, 2 * E), f32),
        ((E, 2 * E), f32),
        ((PAIR_ROWS, 2 * E), f32),
        (state, f32),
        (state, f32),
        ((PAIR_ROWS + 32, E), bf16),
        (state, f32),
        ((4, PAIR_ROWS + 32, E), bf16),
        ((24, E), f32),
        ((8, 24, E), f32),
        ((8, width), f32),
        ((8, E), f32),
        ((4, 8, E), f32),
    ]
    semaphores = [
        (2, CHUNKS, 12), (2, CHUNKS, 12), (CHUNKS,), (3,), (1,), (1,), (1,), (CHUNKS,), (CHUNKS,), (CHUNKS,), (CHUNKS, 2),
        (CHUNKS, 2), (2,), (2,), (1,), (1,), (1,), (1,), (4,), (4,), (4, 4), (4, 4), (2, 4), (2, 4), (16,), (16,), (4,), (4,),
        (4,), (4,), (4,), (4,), (1,), (1,), (4,), (4,), (8,), (8,), (4,), (4,),
    ]
    student, grad, loss = pl.pallas_call(
        fused_kernel,
        out_shape=(
            jax.ShapeDtypeStruct((tokens, columns), bf16),
            jax.ShapeDtypeStruct((feature_map.shape[2], E), f32),
            jax.ShapeDtypeStruct((1, 1), f32),
        ),
        in_specs=[anywhere, anywhere, anywhere, vmem, anywhere, anywhere, vmem, vmem, vmem],
        out_specs=(anywhere, vmem, smem),
        scratch_shapes=[pltpu.VMEM(shape, kind) for shape, kind in scratch] + [dma(shape) for shape in semaphores],
        compiler_params=pltpu.CompilerParams(
            collective_id=0, has_side_effects=True, vmem_limit_bytes=63 * 1024 * 1024
        ),
        cost_estimate=pl.CostEstimate(flops=30_000_000_000, bytes_accessed=40_000_000, transcendentals=2_000_000),
    )(
        queries, keys, values, feature_map[0].T, out_proj, teacher,
        jnp.asarray(bits, bf16), jnp.asarray(row_table, f32), jnp.asarray(column_table, f32),
    )
    student, grad, loss = pl.pallas_call(
        deliver_kernel,
        out_shape=(
            jax.ShapeDtypeStruct(student.shape, bf16),
            jax.ShapeDtypeStruct(grad.shape, f32),
            jax.ShapeDtypeStruct((1, 1), f32),
        ),
        in_specs=[anywhere, anywhere, smem],
        out_specs=(anywhere, anywhere, smem),
        scratch_shapes=[pltpu.VMEM(student.shape, bf16), pltpu.VMEM(grad.shape, f32), dma((5,)), dma((5,))],
        cost_estimate=pl.CostEstimate(flops=0, bytes_accessed=2 * student.size * 2, transcendentals=0),
    )(student, grad, loss)
    return student, loss.reshape(()), grad.T[None]


def fits_fused(mesh):
    return mesh.shape["ctx"] == 8 and mesh.shape["head"] == 4


def solution(mesh):
    return jax.shard_map(
        fused_local if fits_fused(mesh) else local,
        mesh=mesh,
        in_specs=(
            P("ctx", "head"),
            P("ctx", "head"),
            P("ctx", "head"),
            P("head", None, None),
            P("ctx", "head"),
            P("ctx", "head"),
        ),
        out_specs=(P("ctx", "head"), P(), P("head", None, None)),
        check_vma=False,
    )
```

```python
import functools
import math

import jax
import jax.numpy as jnp
import numpy as np
from jax import lax
from jax.experimental import pallas as pl
from jax.experimental.pallas import tpu as pltpu
from jax.sharding import PartitionSpec as P

D = 8192
HEAD_DIM = 128
GROUP = 8
WIN = 64


exact_mode = lax.Precision.HIGHEST


def shifted(block, axis, distance):
    devices = range(lax.axis_size(axis))
    route = [(i - distance, i) for i in devices if i - distance in devices]
    return lax.ppermute(block, axis, route)


def taylor_square(features):
    feature_count = features.shape[-1]
    outer = features[..., :, None] * features[..., None, :]
    return outer.reshape(features.shape[:-1] + (feature_count * feature_count,))


def two_terms(x):
    high = lax.reduce_precision(x, 8, 7)
    return jnp.concatenate([high.astype(jnp.bfloat16), (x - high).astype(jnp.bfloat16)], -1)


def joined(pair):
    half = pair.shape[-1] // 2
    return pair[..., :half] + pair[..., half:]


def square_grad(grad_square, features):
    feature_count = features.shape[-1]
    matrix = grad_square.reshape(features.shape + (feature_count,))
    return jnp.einsum("...fh,...h->...f", matrix, features, precision=exact_mode) + jnp.einsum(
        "...hf,...h->...f", matrix, features, precision=exact_mode
    )


def exchange_kernel(count, head_count, mode, x_ref, row_ref, out_ref, row_out, buf, row_buf, send, recv, row_send, row_recv):
    me = lax.axis_index("ctx")
    head = lax.axis_index("head")
    mesh_ids = pl.DeviceIdType.MESH
    barrier = pltpu.get_barrier_semaphore()
    for d in range(1, count):
        pl.semaphore_signal(
            barrier, inc=1, device_id=(lax.rem(me + d, count), head), device_id_type=mesh_ids
        )
    for d in range(1, head_count):
        pl.semaphore_signal(
            barrier, inc=1, device_id=(me, lax.rem(head + d, head_count)), device_id_type=mesh_ids
        )
    pl.semaphore_wait(barrier, count + head_count - 2)

    def wanted(source, target):
        return {"lower": source < target, "upper": source > target, "all": source != target}[mode]

    def ctx_copy(d):
        return pltpu.make_async_remote_copy(
            src_ref=x_ref,
            dst_ref=buf.at[me],
            send_sem=send.at[d],
            recv_sem=recv.at[me],
            device_id=(lax.rem(me + d, count), head),
            device_id_type=mesh_ids,
        )

    def row_copy(d):
        return pltpu.make_async_remote_copy(
            src_ref=row_ref,
            dst_ref=row_buf.at[head],
            send_sem=row_send.at[d],
            recv_sem=row_recv.at[head],
            device_id=(me, lax.rem(head + d, head_count)),
            device_id_type=mesh_ids,
        )

    def ctx_arrival(source):
        return pltpu.make_async_remote_copy(
            src_ref=x_ref,
            dst_ref=buf.at[source],
            send_sem=send.at[0],
            recv_sem=recv.at[source],
            device_id=(source, head),
            device_id_type=mesh_ids,
        )

    def row_arrival(source):
        return pltpu.make_async_remote_copy(
            src_ref=row_ref,
            dst_ref=row_buf.at[source],
            send_sem=row_send.at[0],
            recv_sem=row_recv.at[source],
            device_id=(me, source),
            device_id_type=mesh_ids,
        )

    for d in range(1, count):

        @pl.when(wanted(me, lax.rem(me + d, count)))
        def _():
            ctx_copy(d).start()

    for d in range(1, head_count):
        row_copy(d).start()

    row_out[...] = jnp.zeros_like(row_out)
    for source in range(head_count):

        @pl.when(source == head)
        def _():
            row_out[...] += row_ref[...]

        @pl.when(source != head)
        def _():
            row_arrival(source).wait_recv()
            row_out[...] += row_buf[source]

    out_ref[...] = jnp.zeros_like(out_ref)
    for source in range(count):
        if mode == "all":

            @pl.when(source == me)
            def _():
                out_ref[...] += x_ref[...].astype(jnp.float32)

        @pl.when(wanted(source, me))
        def _():
            ctx_arrival(source).wait_recv()
            out_ref[...] += buf[source].astype(jnp.float32)

    for d in range(1, count):

        @pl.when(wanted(me, lax.rem(me + d, count)))
        def _():
            ctx_copy(d).wait_send()

    for d in range(1, head_count):
        row_copy(d).wait_send()


def exchange(x, row, mode, collective_id):
    count = lax.axis_size("ctx")
    head_count = lax.axis_size("head")
    vmem = pl.BlockSpec(memory_space=pltpu.VMEM)
    return pl.pallas_call(
        functools.partial(exchange_kernel, count, head_count, mode),
        out_shape=(
            jax.ShapeDtypeStruct(x.shape, jnp.float32),
            jax.ShapeDtypeStruct(row.shape, jnp.float32),
        ),
        in_specs=[vmem, vmem],
        out_specs=(vmem, vmem),
        scratch_shapes=[
            pltpu.VMEM((count,) + x.shape, x.dtype),
            pltpu.VMEM((head_count,) + row.shape, jnp.float32),
            pltpu.SemaphoreType.DMA((count,)),
            pltpu.SemaphoreType.DMA((count,)),
            pltpu.SemaphoreType.DMA((head_count,)),
            pltpu.SemaphoreType.DMA((head_count,)),
        ],
        compiler_params=pltpu.CompilerParams(collective_id=collective_id, has_side_effects=True),
        cost_estimate=pl.CostEstimate(
            flops=count * x.size, bytes_accessed=40 * count * x.size, transcendentals=0
        ),
    )(x, row)


def pack(square, linear, square_den, linear_den, flat):
    groups, feature_count = linear_den.shape
    squares = feature_count * feature_count
    square_rows = square_den.reshape(groups, squares // HEAD_DIM, HEAD_DIM)
    linear_rows = jnp.pad(linear_den, ((0, 0), (0, HEAD_DIM - feature_count)))[:, None]
    small = jnp.concatenate([flat[:, None], linear_rows, square_rows], 1)
    small = jnp.pad(small, ((0, 0), (0, -small.shape[1] % 16), (0, 0)))
    return jnp.concatenate([square, linear, small], 1).reshape(-1, HEAD_DIM)


def unpack(packed, groups, feature_count):
    squares = feature_count * feature_count
    packed = packed.reshape(groups, -1, HEAD_DIM)
    top = squares + feature_count
    square_den = packed[:, top + 2 : top + 2 + squares // HEAD_DIM].reshape(groups, squares)
    return (
        packed[:, :squares],
        packed[:, squares:top],
        square_den,
        packed[:, top + 1, :feature_count],
        packed[:, top],
    )


def ring_gather(block):
    count = lax.axis_size("ctx")
    me = lax.axis_index("ctx")
    rows = block.shape[0]
    half = rows // 2
    ring = list(range(0, count, 2)) + list(range(1, count, 2))[::-1]
    place = [ring.index(i) for i in range(count)]
    position = jnp.array(place, jnp.int32)[me]
    ring_table = jnp.array(ring, jnp.int32)
    up_route = [(ring[p], ring[(p + 1) % count]) for p in range(count)]
    down_route = [(ring[(p + 1) % count], ring[p]) for p in range(count)]
    up, down = block[:half], block[half:]
    pieces = [(me, up, down, me)]
    for step in range(1, count):
        up = lax.ppermute(up, "ctx", up_route)
        down = lax.ppermute(down, "ctx", down_route)
        pieces.append(
            (
                ring_table[(position - step) % count],
                up,
                down,
                ring_table[(position + step) % count],
            )
        )
    return pieces


def after_hop(pieces, hop, *members):
    if hop >= len(pieces):
        return members
    up_owner, up, down, down_owner = pieces[hop]
    up, down, *members = lax.optimization_barrier((up, down, *members))
    pieces[hop] = (up_owner, up, down, down_owner)
    return members


def assemble(pieces, zero, rows):
    half = rows // 2
    count = len(pieces)
    full = jnp.broadcast_to(zero, (count * rows, pieces[0][1].shape[1]))
    for up_owner, up, down, down_owner in pieces:
        full = lax.dynamic_update_slice(full, up, (up_owner * rows, 0))
        full = lax.dynamic_update_slice(full, down, (down_owner * rows + half, 0))
    return full


def flipped(block, bit):
    return lax.ppermute(block, "head", [(i, i ^ bit) for i in range(4)])


def sum_heads(row):
    if lax.axis_size("head") != 4:
        return lax.psum(row, "head")
    row = row + flipped(row, 1)
    return row + flipped(row, 2)


def sum_from(block, sign):
    count = lax.axis_size("ctx")
    devices = range(count)
    total = jnp.zeros_like(block)
    for distance in range(1, count):
        route = [(i, i + sign * distance) for i in devices if i + sign * distance in devices]
        total = total + lax.ppermute(block, "ctx", route)
    return total


def gather_heads(block):
    if lax.axis_size("head") != 4:
        return lax.all_gather(block, "head", axis=1, tiled=True)
    head = lax.axis_index("head")
    rows, width = block.shape
    far = flipped(block, 2)
    near = flipped(block, 1)
    diagonal = flipped(far, 1)
    full = jnp.zeros((rows, 4 * width), block.dtype)
    for bit, member in ((0, block), (2, far), (1, near), (3, diagonal)):
        full = lax.dynamic_update_slice(full, member, (0, (head ^ bit) * width))
    return full


def scatter_heads(d_student, proj_full):
    def product(weights):
        return lax.dot_general(
            d_student, weights, (((1,), (1,)), ((), ())), preferred_element_type=jnp.float32
        ).astype(jnp.bfloat16)

    if lax.axis_size("head") != 4:
        terms = product(proj_full)
        return lax.psum_scatter(terms, "head", scatter_dimension=1, tiled=True).astype(jnp.float32)
    head = lax.axis_index("head")
    width = proj_full.shape[0] // 4

    def block(bit):
        return product(lax.dynamic_slice_in_dim(proj_full, (head ^ bit) * width, width, 0))

    diagonal = flipped(block(3), 1)
    far = block(2)
    pair = (far.astype(jnp.float32) + diagonal.astype(jnp.float32)).astype(jnp.bfloat16)
    far_sum = flipped(pair, 2)
    near = flipped(block(1), 1)
    own = block(0)
    return own.astype(jnp.float32) + near.astype(jnp.float32) + far_sum.astype(jnp.float32)


def window_tiles(extended, tok_rows):
    tile_count = tok_rows // WIN
    first = extended[:tok_rows].reshape((tile_count, WIN) + extended.shape[1:])
    second = extended[WIN:].reshape((tile_count, WIN) + extended.shape[1:])
    return jnp.concatenate([first, second], 1)


def local(queries, keys, values, feature_map, out_proj, teacher):
    tok_rows = queries.shape[0]
    kv_groups = keys.shape[1] // HEAD_DIM
    ctx_count = lax.axis_size("ctx")
    ctx_index = lax.axis_index("ctx")
    pieces = ring_gather(out_proj)
    query_heads = queries.reshape(tok_rows, kv_groups, GROUP, HEAD_DIM)
    key_heads = keys.reshape(tok_rows, kv_groups, HEAD_DIM)
    value_heads = values.reshape(tok_rows, kv_groups, HEAD_DIM)
    value_float = value_heads.astype(jnp.float32)
    query_features = jnp.einsum(
        "tgqe,gef->tgqf", query_heads, feature_map, preferred_element_type=jnp.float32
    )
    key_features = jnp.einsum(
        "tge,gef->tgf", key_heads, feature_map, preferred_element_type=jnp.float32
    )
    rim_rows = shifted(jnp.stack([keys[tok_rows - WIN :], values[tok_rows - WIN :]]), "ctx", 1)
    keys_ext = jnp.concatenate([rim_rows[0], keys], 0).reshape(tok_rows + WIN, kv_groups, HEAD_DIM)
    values_ext = jnp.concatenate([rim_rows[1], values], 0).reshape(
        tok_rows + WIN, kv_groups, HEAD_DIM
    )
    tile_count = tok_rows // WIN
    key_tiles = window_tiles(keys_ext, tok_rows)
    value_tiles = window_tiles(values_ext, tok_rows)
    query_tiles = query_heads.reshape(tile_count, WIN, kv_groups, GROUP, HEAD_DIM)
    causal = lax.broadcasted_iota(jnp.int32, (tok_rows, tok_rows), 0) >= lax.broadcasted_iota(
        jnp.int32, (tok_rows, tok_rows), 1
    )
    qk_inner = (
        jnp.einsum("tgqf,sgf->gqts", query_features, key_features, precision=exact_mode) / 4.0
    )
    kernel = jnp.where(causal, 1.0 + qk_inner + 0.5 * qk_inner * qk_inner, 0.0)
    numerator = jnp.einsum(
        "gqts,sge->tgqe", kernel.astype(jnp.bfloat16), value_heads, preferred_element_type=jnp.float32
    )
    denominator = jnp.transpose(jnp.sum(kernel, axis=-1), (2, 0, 1))
    query_tiles, numerator, denominator = after_hop(
        pieces, 1, query_tiles, numerator, denominator
    )
    scores = jnp.einsum(
        "ntgqe,nsge->ngqts", query_tiles, key_tiles, preferred_element_type=jnp.float32
    ) / math.sqrt(HEAD_DIM)
    tile_pos = lax.broadcasted_iota(jnp.int32, (tile_count, WIN, 2 * WIN), 0)
    query_pos = lax.broadcasted_iota(jnp.int32, (tile_count, WIN, 2 * WIN), 1)
    key_pos = lax.broadcasted_iota(jnp.int32, (tile_count, WIN, 2 * WIN), 2)
    distance = query_pos + WIN - key_pos
    allowed = (
        (distance >= 0)
        & (distance < WIN)
        & (ctx_index * tok_rows + tile_pos * WIN + key_pos - WIN >= 0)
    )
    allowed = allowed[:, None, None]
    scores = jnp.where(allowed, scores, -jnp.inf)
    row_max = jnp.max(scores, axis=-1, keepdims=True)
    weights = jnp.where(allowed, jnp.exp(scores - row_max), 0.0)
    attn_weights = (weights / jnp.sum(weights, axis=-1, keepdims=True)).astype(jnp.bfloat16)
    window_out = jnp.einsum(
        "ngqts,nsge->ntgqe", attn_weights, value_tiles, preferred_element_type=jnp.float32
    ).reshape(tok_rows, kv_groups, GROUP, HEAD_DIM)
    key_square = taylor_square(key_features)
    own_square_v = jnp.einsum("sgk,sge->gke", key_square, value_float, precision=exact_mode)
    own_linear_v = jnp.einsum("sgf,sge->gfe", key_features, value_float, precision=exact_mode)
    own_values = jnp.sum(value_float, axis=0)
    own_square_k = jnp.sum(key_square, axis=0)
    own_linear_k = jnp.sum(key_features, axis=0)
    no_row = jnp.zeros((8, HEAD_DIM), jnp.float32)
    packed = pack(own_square_v, own_linear_v, own_square_k, own_linear_k, own_values)
    earlier, window_out = after_hop(pieces, 2, sum_from(packed, 1), window_out)
    feature_count = feature_map.shape[2]
    past_square_v, past_linear_v, past_square_k, past_linear_k, past_values = unpack(
        earlier, kv_groups, feature_count
    )
    past_count = (ctx_index * tok_rows).astype(jnp.float32)
    query_square = taylor_square(query_features)
    numerator = (
        numerator
        + jnp.einsum("tgqk,gke->tgqe", query_square, past_square_v, precision=exact_mode) / 32.0
        + jnp.einsum("tgqf,gfe->tgqe", query_features, past_linear_v, precision=exact_mode) / 4.0
        + past_values[None, :, None, :]
    )
    denominator = (
        denominator
        + jnp.einsum("tgqk,gk->tgq", query_square, past_square_k, precision=exact_mode) / 32.0
        + jnp.einsum("tgqf,gf->tgq", query_features, past_linear_k, precision=exact_mode) / 4.0
        + past_count
    )
    linear_out = numerator / denominator[..., None]
    head_out = (
        (linear_out + window_out)
        .astype(jnp.bfloat16)
        .reshape(tok_rows, kv_groups * GROUP * HEAD_DIM)
    )
    head_out, zero = after_hop(pieces, 3, head_out, jnp.zeros((), jnp.bfloat16))
    all_heads = gather_heads(head_out)
    proj_full = assemble(pieces, zero, out_proj.shape[0])
    projected = jnp.dot(all_heads, proj_full, preferred_element_type=jnp.float32)
    student_out = projected.astype(jnp.bfloat16)
    residual = student_out.astype(jnp.float32) - teacher.astype(jnp.float32)
    total_rows = tok_rows * ctx_count
    squared = jnp.sum(residual * residual)
    d_student = (2.0 * residual / total_rows).astype(jnp.bfloat16)
    head_grad = scatter_heads(d_student, proj_full).reshape(
        tok_rows, kv_groups, GROUP, HEAD_DIM
    )
    numerator_grad = head_grad / denominator[..., None]
    denominator_grad = -jnp.sum(head_grad * linear_out, axis=-1) / denominator
    kernel_grad = (
        jnp.einsum(
            "tgqe,sge->gqts",
            two_terms(numerator_grad),
            jnp.concatenate([value_heads, value_heads], -1),
            preferred_element_type=jnp.float32,
        )
        + jnp.transpose(denominator_grad, (1, 2, 0))[..., None]
    )
    inner_grad = (jnp.where(causal, kernel_grad * (1.0 + qk_inner), 0.0) / 4.0).astype(
        jnp.bfloat16
    )
    query_grad = joined(
        jnp.einsum(
            "gqts,sgf->tgqf",
            inner_grad,
            two_terms(key_features),
            preferred_element_type=jnp.float32,
        )
    )
    key_grad = joined(
        jnp.einsum(
            "gqts,tgqf->sgf",
            inner_grad,
            two_terms(query_features),
            preferred_element_type=jnp.float32,
        )
    )
    query_square_grad = (
        jnp.einsum("tgqe,gke->tgqk", numerator_grad, past_square_v, precision=exact_mode)
        + denominator_grad[..., None] * past_square_k[None, :, None, :]
    ) / 32.0
    query_grad = (
        query_grad
        + (
            jnp.einsum("tgqe,gfe->tgqf", numerator_grad, past_linear_v, precision=exact_mode)
            + denominator_grad[..., None] * past_linear_k[None, :, None, :]
        )
        / 4.0
        + square_grad(query_square_grad, query_features)
    )
    own_back_square = jnp.einsum(
        "tgqk,tgqe->gke", query_square, numerator_grad, precision=exact_mode
    )
    own_back_linear = jnp.einsum(
        "tgqf,tgqe->gfe", query_features, numerator_grad, precision=exact_mode
    )
    own_den_square = jnp.einsum(
        "tgqk,tgq->gk", query_square, denominator_grad, precision=exact_mode
    )
    own_den_linear = jnp.einsum(
        "tgqf,tgq->gf", query_features, denominator_grad, precision=exact_mode
    )
    packed_back = pack(
        own_back_square,
        own_back_linear,
        own_den_square,
        own_den_linear,
        jnp.zeros((kv_groups, HEAD_DIM), jnp.float32),
    )
    later = sum_from(packed_back, -1)
    loss_row = sum_heads(jnp.full((8, HEAD_DIM), squared, jnp.float32))
    later_square, later_linear, later_den_square, later_den_linear, _ = unpack(
        later, kv_groups, feature_count
    )
    key_square_grad = (
        jnp.einsum("gke,sge->sgk", later_square, value_float, precision=exact_mode)
        + later_den_square[None]
    ) / 32.0
    key_grad = (
        key_grad
        + (
            jnp.einsum("gfe,sge->sgf", later_linear, value_float, precision=exact_mode)
            + later_den_linear[None]
        )
        / 4.0
        + square_grad(key_square_grad, key_features)
    )
    own_grad = jnp.einsum(
        "tgqe,tgqf->gef", query_heads.astype(jnp.float32), query_grad, precision=exact_mode
    ) + jnp.einsum("tge,tgf->gef", key_heads.astype(jnp.float32), key_grad, precision=exact_mode)
    packed_grad = jnp.concatenate([own_grad.reshape(-1, HEAD_DIM), loss_row], 0)
    summed, _ = exchange(packed_grad, no_row, "all", 0)
    feature_grad = summed[:-8].reshape(own_grad.shape)
    loss_value = summed[-8, 0] / (total_rows * D)
    return (student_out, loss_value, feature_grad)


FEATURE_PAIRS = 153
PAIR_ROWS = 160
CHUNKS = 4


def pair_tables():
    j = np.arange(2 * HEAD_DIM)
    valid = j < FEATURE_PAIRS
    first = j % 17
    second = (first + j // 17) % 17
    select = np.zeros((2, 2 * HEAD_DIM, HEAD_DIM), np.float32)
    constant = np.zeros((2, 2 * HEAD_DIM), np.float32)
    for side, member in enumerate((first, second)):
        for row in np.nonzero(valid)[0]:
            if member[row] < 16:
                select[side, row, member[row]] = 1.0
            else:
                constant[side, row] = 1.0
    is_one = (first == 16).astype(int) + (second == 16).astype(int)
    coef = np.where(is_one == 2, 1.0, np.where(is_one == 1, 0.25, np.where(first == second, 1 / 32, 1 / 16)))
    coef = np.where(valid, coef, 0.0)
    bits = np.concatenate([select[0], select[1], np.eye(HEAD_DIM)], 0)
    rows = np.zeros((8, 2 * HEAD_DIM), np.float32)
    rows[0], rows[1], rows[2] = constant[0], constant[1], coef
    columns = np.zeros((2 * HEAD_DIM, HEAD_DIM), np.float32)
    columns[:, 0], columns[:, 1], columns[:, 2] = constant[0], constant[1], coef
    return bits, rows, columns


def mm(a, b):
    return lax.dot_general(a, b, (((1,), (0,)), ((), ())), preferred_element_type=jnp.float32)


def mm_t(a, b):
    return lax.dot_general(a, b, (((1,), (1,)), ((), ())), preferred_element_type=jnp.float32)


def split_terms(x):
    high = x.astype(jnp.bfloat16)
    return high, (x - high.astype(jnp.float32)).astype(jnp.bfloat16)


def fused_kernel(
    queries_in, keys_in, values_in, map_ref, proj_ref, teacher_ref, bits_ref, rows_ref, columns_ref,
    student_ref, grad_ref, loss_ref,
    proj_buf, heads_buf, window, own_sum, first_factor, second_factor, pairs_t, queries_t, slope, lin, den_inv,
    d_student, acc, queries_ref, teacher_buf, keys_ext, values_ext, ones_values, wide_map, wide_map_t, kernel_map,
    past_high, past_low, key_features, key_factor_a, key_factor_b, keys_t,
    state_own, state_x, state_low, state_up,
    send_n, recv_n, send_d, recv_d, send_a, recv_a, send_b, recv_b,
    cross, grad_a, grad_b, back, back_own, back_x, back_sum, back_later, back_in, final_own, final_in, loss_acc, loss_own, loss_in,
    ring_send, ring_recv, own_sem, input_sem, teacher_sem, teacher_send, teacher_recv, student_sem, student_send,
    student_recv, part_send, part_recv, rim_send, rim_recv, state_x_send, state_x_recv,
    state_up_send, state_up_recv, side_send, side_recv, near_send, near_recv, far_send, far_recv,
    n_send, n_recv, d_send, d_recv, a_send, a_recv, b_send, b_recv,
    back_x_send, back_x_recv, back_send, back_recv, final_send, final_recv, loss_send, loss_recv,
):
    f32, bf16 = jnp.float32, jnp.bfloat16
    mesh_ids = pl.DeviceIdType.MESH
    ctx_count = 8
    tokens = queries_in.shape[0]
    half = tokens // 2
    width = proj_buf.shape[2]
    E = HEAD_DIM
    c = lax.axis_index("ctx")
    h = lax.axis_index("head")
    z = c // 2
    x = c % 2
    side = c + 1 - 2 * x
    columns_here = x * (proj_ref.shape[1] // 2)
    columns_there = (1 - x) * (proj_ref.shape[1] // 2)

    near = h + 1 - 2 * (h % 2)
    far = (h + 2) % 4
    diagonal = 3 - h

    def remote(src, dst, send, recv, ctx, head):
        return pltpu.make_async_remote_copy(
            src_ref=src, dst_ref=dst, send_sem=send, recv_sem=recv, device_id=(ctx, head), device_id_type=mesh_ids
        )

    inputs = [
        pltpu.make_async_copy(keys_in, keys_ext.at[pl.ds(WIN, tokens)], input_sem.at[0]),
        pltpu.make_async_copy(values_in, values_ext.at[pl.ds(WIN, tokens)], input_sem.at[1]),
        pltpu.make_async_copy(queries_in, queries_ref, input_sem.at[2]),
    ]
    barrier = pltpu.get_barrier_semaphore()
    for d in range(1, ctx_count):
        pl.semaphore_signal(barrier, inc=1, device_id=((c + d) % ctx_count, h), device_id_type=mesh_ids)
    for d in range(1, 4):
        pl.semaphore_signal(barrier, inc=1, device_id=(c, (h + d) % 4), device_id_type=mesh_ids)
    for copy in inputs:
        copy.start()
    pl.semaphore_wait(barrier, ctx_count + 2)

    def plane_rows(plane, q):
        return pl.ds(pl.multiple_of(plane * 2 * tokens + q * half, half), half)

    def chunk_columns(start, j):
        return pl.ds(pl.multiple_of(start + j * width, width), width)

    def part_copy(j, d, ctx):
        place = proj_buf.at[j, pl.ds(pl.multiple_of(ctx * tokens + d * half, half), half)]
        src = proj_ref.at[pl.ds(d * half, half), chunk_columns(columns_there, j)]
        return remote(src, place, part_send.at[j, d], part_recv.at[j, d], side, h)

    def target(d):
        return lax.rem(c + 2, ctx_count) if d == 0 else lax.rem(c + ctx_count - 2, ctx_count)

    def has_target(d):
        return z < 3 if d == 0 else z > 0

    def has_owner(d, k):
        return z >= k if d == 0 else z + k <= 3

    def hop(d, j, k, q):
        place = proj_buf.at[j, plane_rows(jnp.clip(z - k if d == 0 else z + k, 0, 3), q)]
        return remote(place, place, ring_send.at[d, j, k * 4 + q], ring_recv.at[d, j, k * 4 + q], target(d), h)

    def first_hop(d, j, q, m):
        place = proj_buf.at[j, plane_rows(z, q)]
        src = proj_ref.at[pl.ds(m * half, half), chunk_columns(columns_here, j)] if m < 2 else place
        return remote(src, place, ring_send.at[d, j, q], ring_recv.at[d, j, q], target(d), h)

    def arrival(d, j, k, q):
        plane = jnp.clip(z - 1 - k if d == 0 else z + 1 + k, 0, 3)
        place = proj_buf.at[j, plane_rows(plane, q)]
        return remote(place, place, ring_send.at[d, j, k * 4 + q], ring_recv.at[d, j, k * 4 + q], target(d), h)

    def quarter(m):
        return lax.rem(2 * x + m, 4)

    def start_first(j, m):
        if m >= 2:
            part_copy(j, m - 2, side).wait_recv()
        for d in (0, 1):

            @pl.when(has_target(d))
            def _():
                first_hop(d, j, quarter(m), m).start()

    def service(j, k, m):
        for d in (0, 1):

            @pl.when(has_owner(d, k))
            def _():
                arrival(d, j, k - 1, quarter(m)).wait_recv()

            @pl.when(has_owner(d, k) & has_target(d))
            def _():
                hop(d, j, k, quarter(m)).start()

    def last_arrival(j, m):
        for d in (0, 1):

            @pl.when(has_owner(d, 3))
            def _():
                arrival(d, j, 2, quarter(m)).wait_recv()

    for s, (src, dst) in enumerate(((keys_in, keys_ext), (values_in, values_ext))):

        @pl.when(c < ctx_count - 1)
        def _():
            remote(
                src.at[pl.ds(tokens - WIN, WIN)], dst.at[pl.ds(0, WIN)], rim_send.at[s], rim_recv.at[s],
                lax.rem(c + 1, ctx_count), h,
            ).start()

        @pl.when(c == 0)
        def _():
            dst[pl.ds(0, WIN), :] = jnp.zeros((WIN, E), bf16)

        dst[pl.ds(WIN + tokens, WIN), :] = jnp.zeros((WIN, E), bf16)

    for j in (0, 1):
        for m in (0, 1):
            start_first(j, m)
            part_copy(j, m, c).start()
    teacher_copy = pltpu.make_async_copy(
        teacher_ref.at[:, pl.ds(pl.multiple_of(columns_here, width), CHUNKS * width)], teacher_buf.at[x], teacher_sem.at[0]
    )
    teacher_copy.start()

    def teacher_part(ctx_half):
        return remote(
            teacher_ref.at[:, pl.ds(pl.multiple_of(columns_there, width), CHUNKS * width)],
            teacher_buf.at[ctx_half], teacher_send.at[0], teacher_recv.at[0], side, h,
        )

    def own_copy(j):
        return pltpu.make_async_copy(
            proj_ref.at[:, chunk_columns(columns_here, j)],
            proj_buf.at[j, pl.ds(pl.multiple_of(c * tokens, tokens), tokens)],
            own_sem.at[j],
        )

    for j in range(CHUNKS):
        own_copy(j).start()

    eye = bits_ref[pl.ds(4 * E, E), :]
    map_rows = jnp.concatenate([map_ref[...], jnp.zeros((E - map_ref.shape[0], E), bf16)], 0)
    map_wide = mm_t(eye, map_rows).astype(bf16)
    for s in range(2):
        select = bits_ref[pl.ds(s * 2 * E, 2 * E), :]
        wide_map[s] = mm_t(map_wide, select).astype(bf16)
        wide_map_t[s] = mm_t(select, map_wide).astype(bf16)
    inputs[0].wait()
    inputs[1].wait()
    keys = keys_ext[pl.ds(WIN, tokens), :]
    features = mm(keys, map_wide)
    feature_high, feature_low = split_terms(features)
    key_features[0] = feature_high
    key_features[1] = feature_low
    inner = (mm_t(map_wide, feature_high) + mm_t(map_wide, feature_low)) * 0.25
    inner_high, inner_low = split_terms(inner)
    kernel_map[pl.ds(0, E), :] = inner_high
    kernel_map[pl.ds(E, E), :] = inner_low
    keys_t[...] = mm_t(eye, keys).astype(bf16)
    key_a = mm(keys, wide_map[0]) + rows_ref[pl.ds(0, 1), :]
    key_b = mm(keys, wide_map[1]) + rows_ref[pl.ds(1, 1), :]
    key_factor_a[...] = (key_a * rows_ref[pl.ds(2, 1), :]).astype(bf16)
    key_factor_b[...] = (key_b * rows_ref[pl.ds(2, 1), :]).astype(bf16)
    ones_values[:, pl.ds(0, E)] = values_ext[pl.ds(WIN, tokens), :]
    ones_values[:, pl.ds(E, E)] = jnp.ones((tokens, E), bf16)
    key_a_t = mm_t(wide_map_t[0], keys) + columns_ref[:, 0:1]
    key_b_t = mm_t(wide_map_t[1], keys) + columns_ref[:, 1:2]
    key_high, key_low = split_terms(key_a_t * key_b_t * columns_ref[:, 2:3])
    state = mm(key_high, ones_values[...]) + mm(key_low, ones_values[...])

    def store_state(ref, value, den_row):
        ref[pl.ds(0, PAIR_ROWS), :] = value[:PAIR_ROWS]
        ref[pl.ds(PAIR_ROWS, 8), :] = den_row[:, :E]
        ref[pl.ds(PAIR_ROWS + 8, 8), :] = den_row[:, E:]

    store_state(state_own, state[:, :E], jnp.transpose(state[:, E:])[:8])
    state_x_copy = remote(state_own, state_x, state_x_send.at[0], state_x_recv.at[0], side, h)
    state_x_copy.start()
    for m in (2, 3):
        start_first(0, m)
    for j in (2, 3):
        for d in (0, 1):
            part_copy(j, d, c).start()
    teacher_part(x).start()
    inputs[2].wait()

    def state_up_copy():
        return remote(state_up, state_low, state_up_send.at[0], state_up_recv.at[0], lax.rem(c + 2, ctx_count), h)

    def chain_step(level):
        if level == 0:
            state_x_copy.wait_recv()

            @pl.when(z == 0)
            def _():
                state_low[...] = jnp.zeros_like(state_low)

        else:

            @pl.when(z == level)
            def _():
                state_up_copy().wait_recv()

        if level < 3:

            @pl.when(z == level)
            def _():
                state_up[...] = state_low[...] + state_own[...] + state_x[...]
                state_up_copy().start()

    for s in range(2):

        @pl.when(c > 0)
        def _():
            dst = (keys_ext, values_ext)[s]
            remote(
                dst.at[pl.ds(0, WIN)], dst.at[pl.ds(0, WIN)], rim_send.at[s], rim_recv.at[s], c, h
            ).wait_recv()

    def query_tile(i, hp):
        token = pl.multiple_of(i * E, E)
        both = queries_ref[pl.ds(token, E), pl.ds(pl.multiple_of(hp * 2 * E, 2 * E), 2 * E)]
        return jnp.concatenate([both[:, :E], both[:, E:]], 0)

    def window_rows(hp):
        return pl.ds(pl.multiple_of((hp % 2) * 2 * E, 2 * E), 2 * E)

    def window_columns(hp):
        return pl.ds(pl.multiple_of((hp // 2) * E, E), E)

    for i in range(4):
        reach = (i + 1) * E

        def local_tile(hp, carry):
            tile = i * 4 + hp
            q = query_tile(i, hp)
            u = mm(jnp.concatenate([q, q], 1), kernel_map[:, pl.ds(0, reach)])
            row = lax.broadcasted_iota(jnp.int32, (2 * E, reach), 0) % E + i * E
            causal = row >= lax.broadcasted_iota(jnp.int32, (2 * E, reach), 1)
            kernel = jnp.where(causal, 1.0 + u + 0.5 * u * u, 0.0).astype(bf16)
            slope[tile, :, pl.ds(0, reach)] = jnp.where(causal, 0.25 + 0.25 * u, 0.0).astype(bf16)
            both = mm(kernel, ones_values[pl.ds(0, reach), :])
            lin[tile] = both[:, :E]
            den_inv[tile] = both[:, E:]
            scores = mm_t(q, keys_ext[pl.ds(i * E, 2 * E), :]) / math.sqrt(HEAD_DIM)
            token = lax.broadcasted_iota(jnp.int32, (2 * E, 2 * E), 0) % E
            place = lax.broadcasted_iota(jnp.int32, (2 * E, 2 * E), 1)
            distance = token + WIN - place
            allowed = (distance >= 0) & (distance < WIN) & (c * tokens + i * E + place - WIN >= 0)
            scores = jnp.where(allowed, scores, -jnp.inf)
            top = jnp.max(scores, axis=-1, keepdims=True)
            weights = jnp.where(allowed, jnp.exp(scores - top), 0.0)
            weights = (weights / jnp.sum(weights, axis=-1, keepdims=True)).astype(bf16)
            window[i, window_rows(hp), window_columns(hp)] = mm(weights, values_ext[pl.ds(i * E, 2 * E), :])
            first_factor[tile] = (mm(q, wide_map[0]) + rows_ref[pl.ds(0, 1), :]).astype(bf16)
            second_factor[tile] = (mm(q, wide_map[1]) + rows_ref[pl.ds(1, 1), :]).astype(bf16)
            pair_a = mm_t(wide_map_t[0], q) + columns_ref[:, 0:1]
            pair_b = mm_t(wide_map_t[1], q) + columns_ref[:, 1:2]
            pairs_t[tile] = (pair_a * pair_b).astype(bf16)[:PAIR_ROWS]
            queries_t[tile] = mm_t(eye, q).astype(bf16)
            service(i // 2, 1 + i % 2, hp)
            return carry

        lax.fori_loop(0, 4, local_tile, 0)
        chain_step(i)
        if i == 1:
            for m in (2, 3):
                start_first(1, m)

    past = jnp.where(z > 0, state_low[...], 0.0) + jnp.where(x == 1, state_x[...], 0.0)
    past_rows = jnp.concatenate([past[PAIR_ROWS : PAIR_ROWS + 8], past[PAIR_ROWS + 8 :]], 1)
    past_den = jnp.transpose(jnp.broadcast_to(past_rows[:1], (E, 2 * E)))
    past_values = jnp.concatenate([past[:PAIR_ROWS], jnp.zeros((2 * E - PAIR_ROWS, E), f32)], 0)
    high, low = split_terms(jnp.concatenate([past_values, past_den], 1))
    past_high[...] = high
    past_low[...] = low

    def head_piece(i, ctx_half, head):
        return heads_buf.at[ctx_half * 4 + head, pl.ds(pl.multiple_of(i * E, E), E)]

    def side_copy(i, ctx_half):
        piece = head_piece(i, ctx_half, h)
        return remote(piece, piece, side_send.at[i], side_recv.at[i], side, h)

    def near_copy(i, s, head):
        ctx_half = x if s % 2 == 0 else 1 - x
        piece = head_piece(i, ctx_half, head)
        return remote(piece, piece, near_send.at[s, i], near_recv.at[s, i], c, near)

    def far_copy(i, s, head):
        ctx_half = x if s == 0 else 1 - x
        piece = head_piece(i, ctx_half, head)
        return remote(piece, piece, far_send.at[s, i], far_recv.at[s, i], c, far)

    def past_tiles(i, carry):
        def past_tile(hp, carry):
            tile = i * 4 + hp
            q = query_tile(i, hp)
            pair = (mm(q, wide_map[0]) + rows_ref[pl.ds(0, 1), :]) * (mm(q, wide_map[1]) + rows_ref[pl.ds(1, 1), :])
            pair_high, pair_low = split_terms(pair)
            both = mm(pair_high, past_high[...]) + mm(pair_low, past_high[...]) + mm(pair_high, past_low[...])
            den = den_inv[tile] + both[:, E:]
            value = (lin[tile] + both[:, :E]) / den
            lin[tile] = value
            den_inv[tile] = 1.0 / den
            out = (value + window[i, window_rows(hp), window_columns(hp)]).astype(bf16)
            heads_buf[
                x * 4 + h, pl.ds(pl.multiple_of(i * E, E), E), pl.ds(pl.multiple_of(hp * 2 * E, 2 * E), 2 * E)
            ] = jnp.concatenate([out[:E], out[E:]], 1)
            return carry

        lax.fori_loop(0, 4, past_tile, 0)
        side_copy(i, x).start()
        far_copy(i, 0, h).start()
        near_copy(i, 0, h).start()
        return carry

    lax.fori_loop(0, 4, past_tiles, 0)
    for m in range(4):
        start_first(2, m)

    def relay_side(i, carry):
        service(2, 1, i)
        side_copy(i, 1 - x).wait_recv()
        far_copy(i, 1, h).start()
        near_copy(i, 1, h).start()
        return carry

    lax.fori_loop(0, 4, relay_side, 0)

    def relay_far(i, carry):
        service(2, 2, i)
        far_copy(i, 0, far).wait_recv()
        near_copy(i, 2, far).start()
        return carry

    lax.fori_loop(0, 4, relay_far, 0)

    for m in range(4):
        start_first(3, m)

    def relay_last(i, carry):
        service(3, 1, i)
        far_copy(i, 1, far).wait_recv()
        near_copy(i, 3, far).start()
        return carry

    lax.fori_loop(0, 4, relay_last, 0)
    teacher_copy.wait()
    teacher_part(1 - x).wait_recv()
    for j in range(CHUNKS):
        own_copy(j).wait()
    loss_acc[...] = jnp.zeros_like(loss_acc)
    for i in range(4):
        for s in range(4):
            near_copy(i, s, near if s < 2 else diagonal).wait_recv()
    def student_copy(j):
        return pltpu.make_async_copy(
            teacher_buf.at[x, :, chunk_columns(0, j)], student_ref.at[:, chunk_columns(columns_here, j)], student_sem.at[j]
        )

    def student_part(j, start):
        return remote(
            teacher_buf.at[1 - x, :, chunk_columns(0, j)], student_ref.at[:, chunk_columns(start, j)],
            student_send.at[j], student_recv.at[j], side, h,
        )

    def finish_columns(j, ctx_half, product):
        student = product.astype(bf16)
        columns = chunk_columns(0, j)
        residual = student.astype(f32) - teacher_buf[ctx_half, :, columns].astype(f32)
        teacher_buf[ctx_half, :, columns] = student
        loss_acc[...] += jnp.sum((residual * residual).reshape(tokens // 8, 8, width), axis=0)
        d_student[j, ctx_half] = (residual * (2.0 / (tokens * ctx_count))).astype(bf16)

    def finish_both(j, products):
        for product, ctx_half in zip(products, (x, 1 - x)):
            finish_columns(j, ctx_half, product)
        student_copy(j).start()

    def plane_product(ctx_half, plane, j):
        rows = pl.ds(pl.multiple_of(plane * 2 * tokens, 2 * tokens), 2 * tokens)
        return mm(heads_buf[ctx_half * 4 + plane], proj_buf[j, rows, :])

    def first_columns(j, carry):
        for m in range(4):
            last_arrival(j, m)
        products = []
        for ctx_half in (x, 1 - x):
            product = plane_product(ctx_half, 0, j)
            for plane in range(1, 4):
                product += plane_product(ctx_half, plane, j)
            products.append(product)
        finish_both(j, products)
        student_part(j, columns_here).start()
        for m in range(2):

            @pl.when(j < 2)
            def _():
                service(3, 2, j * 2 + m)

        return carry

    lax.fori_loop(0, 3, first_columns, 0)
    last_plane = jnp.where(z >= 2, 0, 3)

    for t, ctx_half in enumerate((x, 1 - x)):
        product = plane_product(ctx_half, (last_plane + 1) % 4, 3)
        for b in (2, 3):
            product += plane_product(ctx_half, (last_plane + b) % 4, 3)
        acc[t] = product

    def block_sum(chunks, ctx_half, head, p):
        rows = pl.ds(pl.multiple_of((head * 4 + p) * width, width), width)
        total = mm_t(d_student[chunks[0], ctx_half], proj_buf[chunks[0], rows, :])
        for j in chunks[1:]:
            total += mm_t(d_student[j, ctx_half], proj_buf[j, rows, :])
        return total

    for s, (head, p) in enumerate(((diagonal, 0), (diagonal, 2), (far, 0), (far, 2))):
        window[s] = block_sum((0, 1, 2), 1 - x, head, p)

    for m in range(4):
        last_arrival(3, m)
        products = []
        for t, ctx_half in enumerate((x, 1 - x)):
            left = heads_buf[ctx_half * 4 + last_plane, :, pl.ds(pl.multiple_of(quarter(m) * half, half), half)]
            products.append(acc[t] + mm(left, proj_buf[3, plane_rows(last_plane, quarter(m)), :]))
            if m < 3:
                acc[t] = products[t]
        if m == 3:
            finish_both(3, products)

    def copy_n(s):
        return remote(send_n.at[s], recv_n.at[s], n_send.at[s], n_recv.at[s], c, near)

    def copy_d(p):
        ctx, head = (side, h) if p < 2 else (c, far)
        return remote(send_d.at[p], recv_d.at[p], d_send.at[p], d_recv.at[p], ctx, head)

    def copy_a(p):
        return remote(send_a.at[p], recv_a.at[p], a_send.at[p], a_recv.at[p], side, h)

    def copy_b(p):
        return remote(send_b.at[p], recv_b.at[p], b_send.at[p], b_recv.at[p], c, far)

    kinds = {"d": (1, 1), "a": (1, 0), "b": (0, 1), "own": (0, 0)}

    def slot(kind, p):
        return (kinds[kind][0] * 2 + kinds[kind][1]) * 4 + p

    def give(kind, p):
        other, distant = kinds[kind]
        ctx_half = 1 - x if other else x
        head = diagonal if distant else near
        if kind == "d" and p % 2 == 0:
            total = window[p // 2] + block_sum((3,), ctx_half, head, p)
        else:
            total = block_sum(range(CHUNKS), ctx_half, head, p)
        send_n[slot(kind, p)] = total.astype(bf16)
        copy_n(slot(kind, p)).start()

    def take(kind, p):
        other, distant = kinds[kind]
        ctx_half = 1 - x if other else x
        head = far if distant else h
        if kind == "d" and p % 2 == 0:
            total = window[2 + p // 2] + block_sum((3,), ctx_half, head, p)
        else:
            total = block_sum(range(CHUNKS), ctx_half, head, p)
        copy_n(slot(kind, p)).wait_recv()
        return total + recv_n[slot(kind, p)].astype(f32)

    def send_corner(p):
        send_d[p] = take("d", p).astype(bf16)
        copy_d(p).start()

    def send_side(kind, p, corner):
        total = take(kind, p)
        if corner:
            copy_d(p).wait_recv()
            total += recv_d[p].astype(f32)
        if kind == "a":
            send_a[p] = total.astype(bf16)
            copy_a(p).start()
        else:
            send_b[p] = total.astype(bf16)
            copy_b(p).start()

    give("d", 0)
    give("d", 2)
    send_corner(0)
    send_corner(2)
    give("d", 1)
    give("d", 3)
    send_corner(1)
    send_corner(3)
    for p in (0, 1):
        give("a", p)
        give("b", p + 2)
        send_side("a", p, False)
        send_side("b", p + 2, False)
    for p in (0, 1):
        give("a", p + 2)
        give("b", p)
        send_side("a", p + 2, True)
        send_side("b", p, True)
    for p in range(4):
        give("own", p)
    for p in range(4):
        own_sum[p] = take("own", p)

    loss_own[...] = loss_acc[:, :E] + loss_acc[:, E:]

    def loss_copy(d, source):
        return remote(loss_own, loss_in.at[source], loss_send.at[d], loss_recv.at[source], c, (h + d) % 4)

    for d in range(1, 4):
        loss_copy(d, h).start()

    cross[...] = jnp.zeros_like(cross)
    grad_a[...] = jnp.zeros_like(grad_a)
    grad_b[...] = jnp.zeros_like(grad_b)
    back[...] = jnp.zeros_like(back)

    def grad_piece(p, carry):
        copy_a(p).wait_recv()
        copy_b(p).wait_recv()
        for i in range(4):
            reach = (i + 1) * E
            tile = i * 4 + p
            rows = pl.ds(i * E, E)
            g = own_sum[p, rows, :] + recv_a[p, rows, :].astype(f32) + recv_b[p, rows, :].astype(f32)
            g = jnp.concatenate([g[:, :E], g[:, E:]], 0)
            inverse = den_inv[tile]
            upper = (g * inverse).astype(bf16)
            lower = -jnp.sum(upper.astype(f32) * lin[tile], axis=-1, keepdims=True)
            lower = jnp.broadcast_to(lower, (2 * E, E))
            lower_high = lower.astype(bf16).astype(f32)
            lane = lax.broadcasted_iota(jnp.int32, (2 * E, E), 1)
            lower = (jnp.where(lane < E // 2, lower_high, lower - lower_high) * (2.0 / E)).astype(bf16)
            wide = jnp.concatenate([upper, lower], 1)
            weight = mm_t(wide, ones_values[pl.ds(0, reach), :]) * slope[tile, :, pl.ds(0, reach)].astype(f32)
            cross[:, pl.ds(0, reach)] += mm(queries_t[tile], weight.astype(bf16))
            pair_grad = mm_t(wide, past_high[...]) + mm_t(wide, past_low[...])
            grad_a[...] += mm(queries_t[tile], (pair_grad * second_factor[tile].astype(f32)).astype(bf16))
            grad_b[...] += mm(queries_t[tile], (pair_grad * first_factor[tile].astype(f32)).astype(bf16))
            back[...] += mm(pairs_t[tile], wide)
        return carry

    def grad_pieces(n, carry):
        return grad_piece((n % 2) * 2 + n // 2, carry)

    lax.fori_loop(0, 4, grad_pieces, 0)

    back_den = jnp.transpose(
        jnp.concatenate([back[:, pl.ds(E, E)], jnp.zeros((2 * E - PAIR_ROWS, E), f32)], 0)
    )
    back_den = (back_den[:8] + back_den[E // 2 : E // 2 + 8]) * (E // 2)
    store_state(back_own, back[:, pl.ds(0, E)], back_den)
    back_x_copy = remote(back_own, back_x, back_x_send.at[0], back_x_recv.at[0], side, h)
    back_x_copy.start()
    student_part(3, columns_here).start()

    def back_copy(level):
        return remote(back_sum, back_in.at[z], back_send.at[level], back_recv.at[z], 2 * level + x, h)

    def back_arrival(level):
        return remote(back_sum, back_in.at[level], back_send.at[level], back_recv.at[level], c, h)

    cross_high, cross_low = split_terms(cross[...])
    grad = mm(cross_high, key_features[0]) + mm(cross_high, key_features[1]) + mm(cross_low, key_features[0])
    keys = keys_ext[pl.ds(WIN, tokens), :]
    mixed = jnp.transpose(mm(cross_high, keys) + mm(cross_low, keys))
    mixed_high, mixed_low = split_terms(mixed)
    map_rows = jnp.concatenate([map_ref[...], jnp.zeros((E - map_ref.shape[0], E), bf16)], 0)
    map_wide = mm_t(bits_ref[pl.ds(4 * E, E), :], map_rows).astype(bf16)
    grad += mm(mixed_high, map_wide) + mm(mixed_low, map_wide)

    center = mm(jnp.ones((8, tokens), bf16), values_ext[pl.ds(WIN, tokens), :])
    center = (center / tokens).astype(bf16)
    back_x_copy.wait_recv()
    plane = back_own[...] + back_x[...]
    plane_values = plane[:PAIR_ROWS].astype(bf16)
    lost = (plane[:PAIR_ROWS] - plane_values.astype(f32)).astype(bf16)
    lost = jnp.concatenate([lost, jnp.zeros((2 * E - PAIR_ROWS, E), bf16)], 0)
    moved = mm_t(center, lost)
    plane_den = plane[PAIR_ROWS:] + jnp.concatenate([moved[:, :E], moved[:, E:]], 0)
    den_high, den_low = split_terms(plane_den)
    back_sum[pl.ds(0, PAIR_ROWS), :] = plane_values
    back_sum[pl.ds(PAIR_ROWS, 16), :] = den_high
    back_sum[pl.ds(PAIR_ROWS + 16, 16), :] = den_low
    for level in range(3):

        @pl.when(level < z)
        def _():
            back_copy(level).start()

    back_later[...] = jnp.where(x == 0, back_x[...], 0.0)
    for level in range(1, 4):

        @pl.when(level > z)
        def _():
            back_arrival(level).wait_recv()
            arrived = back_in[level].astype(f32)
            back_later[...] += arrived[: PAIR_ROWS + 16]
            back_later[pl.ds(PAIR_ROWS, 16), :] += arrived[PAIR_ROWS + 16 :]

    later_values = jnp.concatenate([back_later[pl.ds(0, PAIR_ROWS), :], jnp.zeros((2 * E - PAIR_ROWS, E), f32)], 0)
    later_high, later_low = split_terms(later_values)
    pair_grad = mm_t(values_ext[pl.ds(WIN, tokens), :], later_high)
    pair_grad += mm_t(values_ext[pl.ds(WIN, tokens), :], later_low)
    pair_grad += jnp.concatenate(
        [back_later[pl.ds(PAIR_ROWS, 1), :], back_later[pl.ds(PAIR_ROWS + 8, 1), :]], 1
    )
    total_a = grad_a[...] + mm(keys_t[...], (pair_grad * key_factor_b[...].astype(f32)).astype(bf16))
    total_b = grad_b[...] + mm(keys_t[...], (pair_grad * key_factor_a[...].astype(f32)).astype(bf16))
    for s, total in enumerate((total_a, total_b)):
        total_high, total_low = split_terms(total)
        select = bits_ref[pl.ds(s * 2 * E, 2 * E), :]
        grad += mm(total_high, select) + mm(total_low, select)
    final_own[pl.ds(0, 16), :] = jnp.transpose(grad)[:16]
    loss_sum = loss_own[...]
    for d in range(1, 4):
        loss_copy(d, (h + d) % 4).wait_recv()
        loss_sum += loss_in[(h + d) % 4]
    final_own[pl.ds(16, 8), :] = loss_sum

    def final_copy(d, source):
        return remote(final_own, final_in.at[source], final_send.at[d], final_recv.at[source], (c + d) % ctx_count, h)

    for d in range(1, ctx_count):
        final_copy(d, c).start()
    final_in[c] = final_own[...]
    for d in range(1, ctx_count):
        final_copy(d, (c + d) % ctx_count).wait_recv()
    final = final_in[0]
    for s in range(1, ctx_count):
        final += final_in[s]
    grad_ref[...] = final[:16]
    loss_ref[0, 0] = jnp.sum(final[16:]) / (tokens * ctx_count * D)

    for j in range(CHUNKS):
        student_copy(j).wait()
        student_part(j, columns_here).wait_send()
        student_part(j, columns_there).wait_recv()
        for d in (0, 1):
            part_copy(j, d, c).wait_send()
            for m in range(4):
                for k in range(3):

                    @pl.when(has_target(d) & has_owner(d, k))
                    def _():
                        hop(d, j, k, quarter(m)).wait_send()

    teacher_part(x).wait_send()
    for s in range(2):

        @pl.when(c < ctx_count - 1)
        def _():
            dst = (keys_ext, values_ext)[s]
            src = (keys_in, values_in)[s]
            remote(
                src.at[pl.ds(tokens - WIN, WIN)], dst.at[pl.ds(0, WIN)], rim_send.at[s], rim_recv.at[s],
                lax.rem(c + 1, ctx_count), h,
            ).wait_send()

    state_x_copy.wait_send()

    @pl.when(z < 3)
    def _():
        state_up_copy().wait_send()

    back_x_copy.wait_send()
    for level in range(3):

        @pl.when(level < z)
        def _():
            back_copy(level).wait_send()

    for d in range(1, 4):
        loss_copy(d, h).wait_send()
    for i in range(4):
        side_copy(i, x).wait_send()
        for s in range(2):
            far_copy(i, s, h).wait_send()
        for s in range(4):
            near_copy(i, s, h if s < 2 else far).wait_send()
    for p in range(4):
        copy_d(p).wait_send()
        copy_a(p).wait_send()
        copy_b(p).wait_send()
    for s in range(16):
        copy_n(s).wait_send()
    for d in range(1, ctx_count):
        final_copy(d, c).wait_send()


def deliver_kernel(student_ref, grad_ref, loss_ref, student_out, grad_out, loss_out, buffer, grad_buffer, sem, out_sem):
    part = student_ref.shape[0] // 4
    moves = [(ref.at[pl.ds(s * part, part)], buffer.at[pl.ds(s * part, part)], student_out.at[pl.ds(s * part, part)])
             for s, ref in enumerate([student_ref] * 4)]
    moves.append((grad_ref, grad_buffer, grad_out))
    reads = [pltpu.make_async_copy(src, mid, sem.at[s]) for s, (src, mid, dst) in enumerate(moves)]
    writes = [pltpu.make_async_copy(mid, dst, out_sem.at[s]) for s, (src, mid, dst) in enumerate(moves)]
    for copy in reads:
        copy.start()
    loss_out[0, 0] = loss_ref[0, 0]
    for read, write in zip(reads, writes):
        read.wait()
        write.start()
    for copy in writes:
        copy.wait()


def fused_local(queries, keys, values, feature_map, out_proj, teacher):
    tokens = queries.shape[0]
    columns = out_proj.shape[1]
    rows = tokens * 8
    width = columns // 2 // CHUNKS
    E = HEAD_DIM
    bf16, f32 = jnp.bfloat16, jnp.float32
    bits, row_table, column_table = pair_tables()
    vmem = pl.BlockSpec(memory_space=pltpu.VMEM)
    anywhere = pl.BlockSpec(memory_space=pl.ANY)
    smem = pl.BlockSpec(memory_space=pltpu.SMEM)
    dma = pltpu.SemaphoreType.DMA
    state = (PAIR_ROWS + 16, E)
    scratch = [
        ((CHUNKS, rows, width), bf16),
        ((8, tokens, 8 * E), bf16),
        ((4, tokens, width), f32),
        ((4, tokens, width), f32),
        ((16, 2 * E, 2 * E), bf16),
        ((16, 2 * E, 2 * E), bf16),
        ((16, PAIR_ROWS, 2 * E), bf16),
        ((16, E, 2 * E), bf16),
        ((16, 2 * E, tokens), bf16),
        ((16, 2 * E, E), f32),
        ((16, 2 * E, E), f32),
        ((CHUNKS, 2, tokens, width), bf16),
        ((2, tokens, width), f32),
        ((tokens, 8 * E), bf16),
        ((2, tokens, columns // 2), bf16),
        ((tokens + 2 * WIN, E), bf16),
        ((tokens + 2 * WIN, E), bf16),
        ((tokens, 2 * E), bf16),
        ((2, E, 2 * E), bf16),
        ((2, 2 * E, E), bf16),
        ((2 * E, tokens), bf16),
        ((2 * E, 2 * E), bf16),
        ((2 * E, 2 * E), bf16),
        ((2, tokens, E), bf16),
        ((tokens, 2 * E), bf16),
        ((tokens, 2 * E), bf16),
        ((E, tokens), bf16),
        (state, f32),
        (state, f32),
        (state, f32),
        (state, f32),
        ((16, tokens, width), bf16),
        ((16, tokens, width), bf16),
        ((4, tokens, width), bf16),
        ((4, tokens, width), bf16),
        ((4, tokens, width), bf16),
        ((4, tokens, width), bf16),
        ((4, tokens, width), bf16),
        ((4, tokens, width), bf16),
        ((E, tokens), f32),
        ((E, 2 * E), f32),
        ((E, 2 * E), f32),
        ((PAIR_ROWS, 2 * E), f32),
        (state, f32),
        (state, f32),
        ((PAIR_ROWS + 32, E), bf16),
        (state, f32),
        ((4, PAIR_ROWS + 32, E), bf16),
        ((24, E), f32),
        ((8, 24, E), f32),
        ((8, width), f32),
        ((8, E), f32),
        ((4, 8, E), f32),
    ]
    semaphores = [
        (2, CHUNKS, 12), (2, CHUNKS, 12), (CHUNKS,), (3,), (1,), (1,), (1,), (CHUNKS,), (CHUNKS,), (CHUNKS,), (CHUNKS, 2),
        (CHUNKS, 2), (2,), (2,), (1,), (1,), (1,), (1,), (4,), (4,), (4, 4), (4, 4), (2, 4), (2, 4), (16,), (16,), (4,), (4,),
        (4,), (4,), (4,), (4,), (1,), (1,), (4,), (4,), (8,), (8,), (4,), (4,),
    ]
    student, grad, loss = pl.pallas_call(
        fused_kernel,
        out_shape=(
            jax.ShapeDtypeStruct((tokens, columns), bf16),
            jax.ShapeDtypeStruct((feature_map.shape[2], E), f32),
            jax.ShapeDtypeStruct((1, 1), f32),
        ),
        in_specs=[anywhere, anywhere, anywhere, vmem, anywhere, anywhere, vmem, vmem, vmem],
        out_specs=(anywhere, vmem, smem),
        scratch_shapes=[pltpu.VMEM(shape, kind) for shape, kind in scratch] + [dma(shape) for shape in semaphores],
        compiler_params=pltpu.CompilerParams(
            collective_id=0, has_side_effects=True, vmem_limit_bytes=63 * 1024 * 1024
        ),
        cost_estimate=pl.CostEstimate(flops=30_000_000_000, bytes_accessed=40_000_000, transcendentals=2_000_000),
    )(
        queries, keys, values, feature_map[0].T, out_proj, teacher,
        jnp.asarray(bits, bf16), jnp.asarray(row_table, f32), jnp.asarray(column_table, f32),
    )
    student, grad, loss = pl.pallas_call(
        deliver_kernel,
        out_shape=(
            jax.ShapeDtypeStruct(student.shape, bf16),
            jax.ShapeDtypeStruct(grad.shape, f32),
            jax.ShapeDtypeStruct((1, 1), f32),
        ),
        in_specs=[anywhere, anywhere, smem],
        out_specs=(anywhere, anywhere, smem),
        scratch_shapes=[pltpu.VMEM(student.shape, bf16), pltpu.VMEM(grad.shape, f32), dma((5,)), dma((5,))],
        cost_estimate=pl.CostEstimate(flops=0, bytes_accessed=2 * student.size * 2, transcendentals=0),
    )(student, grad, loss)
    return student, loss.reshape(()), grad.T[None]


def fits_fused(mesh):
    return mesh.shape["ctx"] == 8 and mesh.shape["head"] == 4


def solution(mesh):
    return jax.shard_map(
        fused_local if fits_fused(mesh) else local,
        mesh=mesh,
        in_specs=(
            P("ctx", "head"),
            P("ctx", "head"),
            P("ctx", "head"),
            P("head", None, None),
            P("ctx", "head"),
            P("ctx", "head"),
        ),
        out_specs=(P("ctx", "head"), P(), P("head", None, None)),
        check_vma=False,
    )
```

```python
import functools
import math

import jax
import jax.numpy as jnp
import numpy as np
from jax import lax
from jax.experimental import pallas as pl
from jax.experimental.pallas import tpu as pltpu
from jax.sharding import PartitionSpec as P

D = 8192
HEAD_DIM = 128
GROUP = 8
WIN = 64


exact_mode = lax.Precision.HIGHEST


def shifted(block, axis, distance):
    devices = range(lax.axis_size(axis))
    route = [(i - distance, i) for i in devices if i - distance in devices]
    return lax.ppermute(block, axis, route)


def taylor_square(features):
    feature_count = features.shape[-1]
    outer = features[..., :, None] * features[..., None, :]
    return outer.reshape(features.shape[:-1] + (feature_count * feature_count,))


def two_terms(x):
    high = lax.reduce_precision(x, 8, 7)
    return jnp.concatenate([high.astype(jnp.bfloat16), (x - high).astype(jnp.bfloat16)], -1)


def joined(pair):
    half = pair.shape[-1] // 2
    return pair[..., :half] + pair[..., half:]


def square_grad(grad_square, features):
    feature_count = features.shape[-1]
    matrix = grad_square.reshape(features.shape + (feature_count,))
    return jnp.einsum("...fh,...h->...f", matrix, features, precision=exact_mode) + jnp.einsum(
        "...hf,...h->...f", matrix, features, precision=exact_mode
    )


def exchange_kernel(count, head_count, mode, x_ref, row_ref, out_ref, row_out, buf, row_buf, send, recv, row_send, row_recv):
    me = lax.axis_index("ctx")
    head = lax.axis_index("head")
    mesh_ids = pl.DeviceIdType.MESH
    barrier = pltpu.get_barrier_semaphore()
    for d in range(1, count):
        pl.semaphore_signal(
            barrier, inc=1, device_id=(lax.rem(me + d, count), head), device_id_type=mesh_ids
        )
    for d in range(1, head_count):
        pl.semaphore_signal(
            barrier, inc=1, device_id=(me, lax.rem(head + d, head_count)), device_id_type=mesh_ids
        )
    pl.semaphore_wait(barrier, count + head_count - 2)

    def wanted(source, target):
        return {"lower": source < target, "upper": source > target, "all": source != target}[mode]

    def ctx_copy(d):
        return pltpu.make_async_remote_copy(
            src_ref=x_ref,
            dst_ref=buf.at[me],
            send_sem=send.at[d],
            recv_sem=recv.at[me],
            device_id=(lax.rem(me + d, count), head),
            device_id_type=mesh_ids,
        )

    def row_copy(d):
        return pltpu.make_async_remote_copy(
            src_ref=row_ref,
            dst_ref=row_buf.at[head],
            send_sem=row_send.at[d],
            recv_sem=row_recv.at[head],
            device_id=(me, lax.rem(head + d, head_count)),
            device_id_type=mesh_ids,
        )

    def ctx_arrival(source):
        return pltpu.make_async_remote_copy(
            src_ref=x_ref,
            dst_ref=buf.at[source],
            send_sem=send.at[0],
            recv_sem=recv.at[source],
            device_id=(source, head),
            device_id_type=mesh_ids,
        )

    def row_arrival(source):
        return pltpu.make_async_remote_copy(
            src_ref=row_ref,
            dst_ref=row_buf.at[source],
            send_sem=row_send.at[0],
            recv_sem=row_recv.at[source],
            device_id=(me, source),
            device_id_type=mesh_ids,
        )

    for d in range(1, count):

        @pl.when(wanted(me, lax.rem(me + d, count)))
        def _():
            ctx_copy(d).start()

    for d in range(1, head_count):
        row_copy(d).start()

    row_out[...] = jnp.zeros_like(row_out)
    for source in range(head_count):

        @pl.when(source == head)
        def _():
            row_out[...] += row_ref[...]

        @pl.when(source != head)
        def _():
            row_arrival(source).wait_recv()
            row_out[...] += row_buf[source]

    out_ref[...] = jnp.zeros_like(out_ref)
    for source in range(count):
        if mode == "all":

            @pl.when(source == me)
            def _():
                out_ref[...] += x_ref[...].astype(jnp.float32)

        @pl.when(wanted(source, me))
        def _():
            ctx_arrival(source).wait_recv()
            out_ref[...] += buf[source].astype(jnp.float32)

    for d in range(1, count):

        @pl.when(wanted(me, lax.rem(me + d, count)))
        def _():
            ctx_copy(d).wait_send()

    for d in range(1, head_count):
        row_copy(d).wait_send()


def exchange(x, row, mode, collective_id):
    count = lax.axis_size("ctx")
    head_count = lax.axis_size("head")
    vmem = pl.BlockSpec(memory_space=pltpu.VMEM)
    return pl.pallas_call(
        functools.partial(exchange_kernel, count, head_count, mode),
        out_shape=(
            jax.ShapeDtypeStruct(x.shape, jnp.float32),
            jax.ShapeDtypeStruct(row.shape, jnp.float32),
        ),
        in_specs=[vmem, vmem],
        out_specs=(vmem, vmem),
        scratch_shapes=[
            pltpu.VMEM((count,) + x.shape, x.dtype),
            pltpu.VMEM((head_count,) + row.shape, jnp.float32),
            pltpu.SemaphoreType.DMA((count,)),
            pltpu.SemaphoreType.DMA((count,)),
            pltpu.SemaphoreType.DMA((head_count,)),
            pltpu.SemaphoreType.DMA((head_count,)),
        ],
        compiler_params=pltpu.CompilerParams(collective_id=collective_id, has_side_effects=True),
        cost_estimate=pl.CostEstimate(
            flops=count * x.size, bytes_accessed=40 * count * x.size, transcendentals=0
        ),
    )(x, row)


def pack(square, linear, square_den, linear_den, flat):
    groups, feature_count = linear_den.shape
    squares = feature_count * feature_count
    square_rows = square_den.reshape(groups, squares // HEAD_DIM, HEAD_DIM)
    linear_rows = jnp.pad(linear_den, ((0, 0), (0, HEAD_DIM - feature_count)))[:, None]
    small = jnp.concatenate([flat[:, None], linear_rows, square_rows], 1)
    small = jnp.pad(small, ((0, 0), (0, -small.shape[1] % 16), (0, 0)))
    return jnp.concatenate([square, linear, small], 1).reshape(-1, HEAD_DIM)


def unpack(packed, groups, feature_count):
    squares = feature_count * feature_count
    packed = packed.reshape(groups, -1, HEAD_DIM)
    top = squares + feature_count
    square_den = packed[:, top + 2 : top + 2 + squares // HEAD_DIM].reshape(groups, squares)
    return (
        packed[:, :squares],
        packed[:, squares:top],
        square_den,
        packed[:, top + 1, :feature_count],
        packed[:, top],
    )


def ring_gather(block):
    count = lax.axis_size("ctx")
    me = lax.axis_index("ctx")
    rows = block.shape[0]
    half = rows // 2
    ring = list(range(0, count, 2)) + list(range(1, count, 2))[::-1]
    place = [ring.index(i) for i in range(count)]
    position = jnp.array(place, jnp.int32)[me]
    ring_table = jnp.array(ring, jnp.int32)
    up_route = [(ring[p], ring[(p + 1) % count]) for p in range(count)]
    down_route = [(ring[(p + 1) % count], ring[p]) for p in range(count)]
    up, down = block[:half], block[half:]
    pieces = [(me, up, down, me)]
    for step in range(1, count):
        up = lax.ppermute(up, "ctx", up_route)
        down = lax.ppermute(down, "ctx", down_route)
        pieces.append(
            (
                ring_table[(position - step) % count],
                up,
                down,
                ring_table[(position + step) % count],
            )
        )
    return pieces


def after_hop(pieces, hop, *members):
    if hop >= len(pieces):
        return members
    up_owner, up, down, down_owner = pieces[hop]
    up, down, *members = lax.optimization_barrier((up, down, *members))
    pieces[hop] = (up_owner, up, down, down_owner)
    return members


def assemble(pieces, zero, rows):
    half = rows // 2
    count = len(pieces)
    full = jnp.broadcast_to(zero, (count * rows, pieces[0][1].shape[1]))
    for up_owner, up, down, down_owner in pieces:
        full = lax.dynamic_update_slice(full, up, (up_owner * rows, 0))
        full = lax.dynamic_update_slice(full, down, (down_owner * rows + half, 0))
    return full


def flipped(block, bit):
    return lax.ppermute(block, "head", [(i, i ^ bit) for i in range(4)])


def sum_heads(row):
    if lax.axis_size("head") != 4:
        return lax.psum(row, "head")
    row = row + flipped(row, 1)
    return row + flipped(row, 2)


def sum_from(block, sign):
    count = lax.axis_size("ctx")
    devices = range(count)
    total = jnp.zeros_like(block)
    for distance in range(1, count):
        route = [(i, i + sign * distance) for i in devices if i + sign * distance in devices]
        total = total + lax.ppermute(block, "ctx", route)
    return total


def gather_heads(block):
    if lax.axis_size("head") != 4:
        return lax.all_gather(block, "head", axis=1, tiled=True)
    head = lax.axis_index("head")
    rows, width = block.shape
    far = flipped(block, 2)
    near = flipped(block, 1)
    diagonal = flipped(far, 1)
    full = jnp.zeros((rows, 4 * width), block.dtype)
    for bit, member in ((0, block), (2, far), (1, near), (3, diagonal)):
        full = lax.dynamic_update_slice(full, member, (0, (head ^ bit) * width))
    return full


def scatter_heads(d_student, proj_full):
    def product(weights):
        return lax.dot_general(
            d_student, weights, (((1,), (1,)), ((), ())), preferred_element_type=jnp.float32
        ).astype(jnp.bfloat16)

    if lax.axis_size("head") != 4:
        terms = product(proj_full)
        return lax.psum_scatter(terms, "head", scatter_dimension=1, tiled=True).astype(jnp.float32)
    head = lax.axis_index("head")
    width = proj_full.shape[0] // 4

    def block(bit):
        return product(lax.dynamic_slice_in_dim(proj_full, (head ^ bit) * width, width, 0))

    diagonal = flipped(block(3), 1)
    far = block(2)
    pair = (far.astype(jnp.float32) + diagonal.astype(jnp.float32)).astype(jnp.bfloat16)
    far_sum = flipped(pair, 2)
    near = flipped(block(1), 1)
    own = block(0)
    return own.astype(jnp.float32) + near.astype(jnp.float32) + far_sum.astype(jnp.float32)


def window_tiles(extended, tok_rows):
    tile_count = tok_rows // WIN
    first = extended[:tok_rows].reshape((tile_count, WIN) + extended.shape[1:])
    second = extended[WIN:].reshape((tile_count, WIN) + extended.shape[1:])
    return jnp.concatenate([first, second], 1)


def local(queries, keys, values, feature_map, out_proj, teacher):
    tok_rows = queries.shape[0]
    kv_groups = keys.shape[1] // HEAD_DIM
    ctx_count = lax.axis_size("ctx")
    ctx_index = lax.axis_index("ctx")
    pieces = ring_gather(out_proj)
    query_heads = queries.reshape(tok_rows, kv_groups, GROUP, HEAD_DIM)
    key_heads = keys.reshape(tok_rows, kv_groups, HEAD_DIM)
    value_heads = values.reshape(tok_rows, kv_groups, HEAD_DIM)
    value_float = value_heads.astype(jnp.float32)
    query_features = jnp.einsum(
        "tgqe,gef->tgqf", query_heads, feature_map, preferred_element_type=jnp.float32
    )
    key_features = jnp.einsum(
        "tge,gef->tgf", key_heads, feature_map, preferred_element_type=jnp.float32
    )
    rim_rows = shifted(jnp.stack([keys[tok_rows - WIN :], values[tok_rows - WIN :]]), "ctx", 1)
    keys_ext = jnp.concatenate([rim_rows[0], keys], 0).reshape(tok_rows + WIN, kv_groups, HEAD_DIM)
    values_ext = jnp.concatenate([rim_rows[1], values], 0).reshape(
        tok_rows + WIN, kv_groups, HEAD_DIM
    )
    tile_count = tok_rows // WIN
    key_tiles = window_tiles(keys_ext, tok_rows)
    value_tiles = window_tiles(values_ext, tok_rows)
    query_tiles = query_heads.reshape(tile_count, WIN, kv_groups, GROUP, HEAD_DIM)
    causal = lax.broadcasted_iota(jnp.int32, (tok_rows, tok_rows), 0) >= lax.broadcasted_iota(
        jnp.int32, (tok_rows, tok_rows), 1
    )
    qk_inner = (
        jnp.einsum("tgqf,sgf->gqts", query_features, key_features, precision=exact_mode) / 4.0
    )
    kernel = jnp.where(causal, 1.0 + qk_inner + 0.5 * qk_inner * qk_inner, 0.0)
    numerator = jnp.einsum(
        "gqts,sge->tgqe", kernel.astype(jnp.bfloat16), value_heads, preferred_element_type=jnp.float32
    )
    denominator = jnp.transpose(jnp.sum(kernel, axis=-1), (2, 0, 1))
    query_tiles, numerator, denominator = after_hop(
        pieces, 1, query_tiles, numerator, denominator
    )
    scores = jnp.einsum(
        "ntgqe,nsge->ngqts", query_tiles, key_tiles, preferred_element_type=jnp.float32
    ) / math.sqrt(HEAD_DIM)
    tile_pos = lax.broadcasted_iota(jnp.int32, (tile_count, WIN, 2 * WIN), 0)
    query_pos = lax.broadcasted_iota(jnp.int32, (tile_count, WIN, 2 * WIN), 1)
    key_pos = lax.broadcasted_iota(jnp.int32, (tile_count, WIN, 2 * WIN), 2)
    distance = query_pos + WIN - key_pos
    allowed = (
        (distance >= 0)
        & (distance < WIN)
        & (ctx_index * tok_rows + tile_pos * WIN + key_pos - WIN >= 0)
    )
    allowed = allowed[:, None, None]
    scores = jnp.where(allowed, scores, -jnp.inf)
    row_max = jnp.max(scores, axis=-1, keepdims=True)
    weights = jnp.where(allowed, jnp.exp(scores - row_max), 0.0)
    attn_weights = (weights / jnp.sum(weights, axis=-1, keepdims=True)).astype(jnp.bfloat16)
    window_out = jnp.einsum(
        "ngqts,nsge->ntgqe", attn_weights, value_tiles, preferred_element_type=jnp.float32
    ).reshape(tok_rows, kv_groups, GROUP, HEAD_DIM)
    key_square = taylor_square(key_features)
    own_square_v = jnp.einsum("sgk,sge->gke", key_square, value_float, precision=exact_mode)
    own_linear_v = jnp.einsum("sgf,sge->gfe", key_features, value_float, precision=exact_mode)
    own_values = jnp.sum(value_float, axis=0)
    own_square_k = jnp.sum(key_square, axis=0)
    own_linear_k = jnp.sum(key_features, axis=0)
    no_row = jnp.zeros((8, HEAD_DIM), jnp.float32)
    packed = pack(own_square_v, own_linear_v, own_square_k, own_linear_k, own_values)
    earlier, window_out = after_hop(pieces, 2, sum_from(packed, 1), window_out)
    feature_count = feature_map.shape[2]
    past_square_v, past_linear_v, past_square_k, past_linear_k, past_values = unpack(
        earlier, kv_groups, feature_count
    )
    past_count = (ctx_index * tok_rows).astype(jnp.float32)
    query_square = taylor_square(query_features)
    numerator = (
        numerator
        + jnp.einsum("tgqk,gke->tgqe", query_square, past_square_v, precision=exact_mode) / 32.0
        + jnp.einsum("tgqf,gfe->tgqe", query_features, past_linear_v, precision=exact_mode) / 4.0
        + past_values[None, :, None, :]
    )
    denominator = (
        denominator
        + jnp.einsum("tgqk,gk->tgq", query_square, past_square_k, precision=exact_mode) / 32.0
        + jnp.einsum("tgqf,gf->tgq", query_features, past_linear_k, precision=exact_mode) / 4.0
        + past_count
    )
    linear_out = numerator / denominator[..., None]
    head_out = (
        (linear_out + window_out)
        .astype(jnp.bfloat16)
        .reshape(tok_rows, kv_groups * GROUP * HEAD_DIM)
    )
    head_out, zero = after_hop(pieces, 3, head_out, jnp.zeros((), jnp.bfloat16))
    all_heads = gather_heads(head_out)
    proj_full = assemble(pieces, zero, out_proj.shape[0])
    projected = jnp.dot(all_heads, proj_full, preferred_element_type=jnp.float32)
    student_out = projected.astype(jnp.bfloat16)
    residual = student_out.astype(jnp.float32) - teacher.astype(jnp.float32)
    total_rows = tok_rows * ctx_count
    squared = jnp.sum(residual * residual)
    d_student = (2.0 * residual / total_rows).astype(jnp.bfloat16)
    head_grad = scatter_heads(d_student, proj_full).reshape(
        tok_rows, kv_groups, GROUP, HEAD_DIM
    )
    numerator_grad = head_grad / denominator[..., None]
    denominator_grad = -jnp.sum(head_grad * linear_out, axis=-1) / denominator
    kernel_grad = (
        jnp.einsum(
            "tgqe,sge->gqts",
            two_terms(numerator_grad),
            jnp.concatenate([value_heads, value_heads], -1),
            preferred_element_type=jnp.float32,
        )
        + jnp.transpose(denominator_grad, (1, 2, 0))[..., None]
    )
    inner_grad = (jnp.where(causal, kernel_grad * (1.0 + qk_inner), 0.0) / 4.0).astype(
        jnp.bfloat16
    )
    query_grad = joined(
        jnp.einsum(
            "gqts,sgf->tgqf",
            inner_grad,
            two_terms(key_features),
            preferred_element_type=jnp.float32,
        )
    )
    key_grad = joined(
        jnp.einsum(
            "gqts,tgqf->sgf",
            inner_grad,
            two_terms(query_features),
            preferred_element_type=jnp.float32,
        )
    )
    query_square_grad = (
        jnp.einsum("tgqe,gke->tgqk", numerator_grad, past_square_v, precision=exact_mode)
        + denominator_grad[..., None] * past_square_k[None, :, None, :]
    ) / 32.0
    query_grad = (
        query_grad
        + (
            jnp.einsum("tgqe,gfe->tgqf", numerator_grad, past_linear_v, precision=exact_mode)
            + denominator_grad[..., None] * past_linear_k[None, :, None, :]
        )
        / 4.0
        + square_grad(query_square_grad, query_features)
    )
    own_back_square = jnp.einsum(
        "tgqk,tgqe->gke", query_square, numerator_grad, precision=exact_mode
    )
    own_back_linear = jnp.einsum(
        "tgqf,tgqe->gfe", query_features, numerator_grad, precision=exact_mode
    )
    own_den_square = jnp.einsum(
        "tgqk,tgq->gk", query_square, denominator_grad, precision=exact_mode
    )
    own_den_linear = jnp.einsum(
        "tgqf,tgq->gf", query_features, denominator_grad, precision=exact_mode
    )
    packed_back = pack(
        own_back_square,
        own_back_linear,
        own_den_square,
        own_den_linear,
        jnp.zeros((kv_groups, HEAD_DIM), jnp.float32),
    )
    later = sum_from(packed_back, -1)
    loss_row = sum_heads(jnp.full((8, HEAD_DIM), squared, jnp.float32))
    later_square, later_linear, later_den_square, later_den_linear, _ = unpack(
        later, kv_groups, feature_count
    )
    key_square_grad = (
        jnp.einsum("gke,sge->sgk", later_square, value_float, precision=exact_mode)
        + later_den_square[None]
    ) / 32.0
    key_grad = (
        key_grad
        + (
            jnp.einsum("gfe,sge->sgf", later_linear, value_float, precision=exact_mode)
            + later_den_linear[None]
        )
        / 4.0
        + square_grad(key_square_grad, key_features)
    )
    own_grad = jnp.einsum(
        "tgqe,tgqf->gef", query_heads.astype(jnp.float32), query_grad, precision=exact_mode
    ) + jnp.einsum("tge,tgf->gef", key_heads.astype(jnp.float32), key_grad, precision=exact_mode)
    packed_grad = jnp.concatenate([own_grad.reshape(-1, HEAD_DIM), loss_row], 0)
    summed, _ = exchange(packed_grad, no_row, "all", 0)
    feature_grad = summed[:-8].reshape(own_grad.shape)
    loss_value = summed[-8, 0] / (total_rows * D)
    return (student_out, loss_value, feature_grad)


FEATURE_PAIRS = 153
PAIR_ROWS = 160
CHUNKS = 4


def pair_tables():
    j = np.arange(2 * HEAD_DIM)
    valid = j < FEATURE_PAIRS
    first = j % 17
    second = (first + j // 17) % 17
    select = np.zeros((2, 2 * HEAD_DIM, HEAD_DIM), np.float32)
    constant = np.zeros((2, 2 * HEAD_DIM), np.float32)
    for side, member in enumerate((first, second)):
        for row in np.nonzero(valid)[0]:
            if member[row] < 16:
                select[side, row, member[row]] = 1.0
            else:
                constant[side, row] = 1.0
    is_one = (first == 16).astype(int) + (second == 16).astype(int)
    coef = np.where(is_one == 2, 1.0, np.where(is_one == 1, 0.25, np.where(first == second, 1 / 32, 1 / 16)))
    coef = np.where(valid, coef, 0.0)
    bits = np.concatenate([select[0], select[1], np.eye(HEAD_DIM)], 0)
    rows = np.zeros((8, 2 * HEAD_DIM), np.float32)
    rows[0], rows[1], rows[2] = constant[0], constant[1], coef
    columns = np.zeros((2 * HEAD_DIM, HEAD_DIM), np.float32)
    columns[:, 0], columns[:, 1], columns[:, 2] = constant[0], constant[1], coef
    return bits, rows, columns


def mm(a, b):
    return lax.dot_general(a, b, (((1,), (0,)), ((), ())), preferred_element_type=jnp.float32)


def mm_t(a, b):
    return lax.dot_general(a, b, (((1,), (1,)), ((), ())), preferred_element_type=jnp.float32)


def split_terms(x):
    high = x.astype(jnp.bfloat16)
    return high, (x - high.astype(jnp.float32)).astype(jnp.bfloat16)


def fused_kernel(
    queries_in, keys_in, values_in, map_ref, proj_ref, teacher_ref, bits_ref, rows_ref, columns_ref,
    student_ref, grad_ref, loss_ref,
    proj_buf, heads_buf, window, own_sum, first_factor, second_factor, pairs_t, queries_t, slope, lin, den_inv,
    d_student, acc, queries_ref, teacher_buf, keys_ext, values_ext, ones_values, wide_map, wide_map_t, kernel_map,
    past_high, past_low, key_features, key_factor_a, key_factor_b, keys_t,
    state_own, state_x, state_low, state_up,
    send_n, recv_n, send_d, recv_d, send_a, recv_a, send_b, recv_b,
    cross, grad_a, grad_b, back, back_own, back_x, back_sum, back_later, back_in, final_own, final_in, loss_acc, loss_own, loss_in,
    ring_send, ring_recv, own_sem, input_sem, teacher_sem, teacher_send, teacher_recv, student_sem, student_send,
    student_recv, part_send, part_recv, rim_send, rim_recv, state_x_send, state_x_recv,
    state_up_send, state_up_recv, side_send, side_recv, near_send, near_recv, far_send, far_recv,
    n_send, n_recv, d_send, d_recv, a_send, a_recv, b_send, b_recv,
    back_x_send, back_x_recv, back_send, back_recv, final_send, final_recv, loss_send, loss_recv,
):
    f32, bf16 = jnp.float32, jnp.bfloat16
    mesh_ids = pl.DeviceIdType.MESH
    ctx_count = 8
    tokens = queries_in.shape[0]
    half = tokens // 2
    width = proj_buf.shape[2]
    E = HEAD_DIM
    c = lax.axis_index("ctx")
    h = lax.axis_index("head")
    z = c // 2
    x = c % 2
    side = c + 1 - 2 * x
    columns_here = x * (proj_ref.shape[1] // 2)
    columns_there = (1 - x) * (proj_ref.shape[1] // 2)

    near = h + 1 - 2 * (h % 2)
    far = (h + 2) % 4
    diagonal = 3 - h

    def remote(src, dst, send, recv, ctx, head):
        return pltpu.make_async_remote_copy(
            src_ref=src, dst_ref=dst, send_sem=send, recv_sem=recv, device_id=(ctx, head), device_id_type=mesh_ids
        )

    inputs = [
        pltpu.make_async_copy(keys_in, keys_ext.at[pl.ds(WIN, tokens)], input_sem.at[0]),
        pltpu.make_async_copy(values_in, values_ext.at[pl.ds(WIN, tokens)], input_sem.at[1]),
        pltpu.make_async_copy(queries_in, queries_ref, input_sem.at[2]),
    ]
    barrier = pltpu.get_barrier_semaphore()
    for d in range(1, ctx_count):
        pl.semaphore_signal(barrier, inc=1, device_id=((c + d) % ctx_count, h), device_id_type=mesh_ids)
    for d in range(1, 4):
        pl.semaphore_signal(barrier, inc=1, device_id=(c, (h + d) % 4), device_id_type=mesh_ids)
    for copy in inputs:
        copy.start()
    pl.semaphore_wait(barrier, ctx_count + 2)

    def plane_rows(plane, q):
        return pl.ds(pl.multiple_of(plane * 2 * tokens + q * half, half), half)

    def chunk_columns(start, j):
        return pl.ds(pl.multiple_of(start + j * width, width), width)

    def part_copy(j, d, ctx):
        place = proj_buf.at[j, pl.ds(pl.multiple_of(ctx * tokens + d * half, half), half)]
        src = proj_ref.at[pl.ds(d * half, half), chunk_columns(columns_there, j)]
        return remote(src, place, part_send.at[j, d], part_recv.at[j, d], side, h)

    def target(d):
        return lax.rem(c + 2, ctx_count) if d == 0 else lax.rem(c + ctx_count - 2, ctx_count)

    def has_target(d):
        return z < 3 if d == 0 else z > 0

    def has_owner(d, k):
        return z >= k if d == 0 else z + k <= 3

    def hop(d, j, k, q):
        place = proj_buf.at[j, plane_rows(jnp.clip(z - k if d == 0 else z + k, 0, 3), q)]
        return remote(place, place, ring_send.at[d, j, k * 4 + q], ring_recv.at[d, j, k * 4 + q], target(d), h)

    def first_hop(d, j, q, m):
        place = proj_buf.at[j, plane_rows(z, q)]
        src = proj_ref.at[pl.ds(m * half, half), chunk_columns(columns_here, j)] if m < 2 else place
        return remote(src, place, ring_send.at[d, j, q], ring_recv.at[d, j, q], target(d), h)

    def arrival(d, j, k, q):
        plane = jnp.clip(z - 1 - k if d == 0 else z + 1 + k, 0, 3)
        place = proj_buf.at[j, plane_rows(plane, q)]
        return remote(place, place, ring_send.at[d, j, k * 4 + q], ring_recv.at[d, j, k * 4 + q], target(d), h)

    def quarter(m):
        return lax.rem(2 * x + m, 4)

    def start_first(j, m):
        if m >= 2:
            part_copy(j, m - 2, side).wait_recv()
        for d in (0, 1):

            @pl.when(has_target(d))
            def _():
                first_hop(d, j, quarter(m), m).start()

    def service(j, k, m):
        for d in (0, 1):

            @pl.when(has_owner(d, k))
            def _():
                arrival(d, j, k - 1, quarter(m)).wait_recv()

            @pl.when(has_owner(d, k) & has_target(d))
            def _():
                hop(d, j, k, quarter(m)).start()

    def last_arrival(j, m):
        for d in (0, 1):

            @pl.when(has_owner(d, 3))
            def _():
                arrival(d, j, 2, quarter(m)).wait_recv()

    for s, (src, dst) in enumerate(((keys_in, keys_ext), (values_in, values_ext))):

        @pl.when(c < ctx_count - 1)
        def _():
            remote(
                src.at[pl.ds(tokens - WIN, WIN)], dst.at[pl.ds(0, WIN)], rim_send.at[s], rim_recv.at[s],
                lax.rem(c + 1, ctx_count), h,
            ).start()

        @pl.when(c == 0)
        def _():
            dst[pl.ds(0, WIN), :] = jnp.zeros((WIN, E), bf16)

        dst[pl.ds(WIN + tokens, WIN), :] = jnp.zeros((WIN, E), bf16)

    for j in (0, 1):
        for m in (0, 1):
            start_first(j, m)
            part_copy(j, m, c).start()
    teacher_copy = pltpu.make_async_copy(
        teacher_ref.at[:, pl.ds(pl.multiple_of(columns_here, width), CHUNKS * width)], teacher_buf.at[x], teacher_sem.at[0]
    )
    teacher_copy.start()

    def teacher_part(ctx_half):
        return remote(
            teacher_ref.at[:, pl.ds(pl.multiple_of(columns_there, width), CHUNKS * width)],
            teacher_buf.at[ctx_half], teacher_send.at[0], teacher_recv.at[0], side, h,
        )

    def own_copy(j):
        return pltpu.make_async_copy(
            proj_ref.at[:, chunk_columns(columns_here, j)],
            proj_buf.at[j, pl.ds(pl.multiple_of(c * tokens, tokens), tokens)],
            own_sem.at[j],
        )

    for j in range(CHUNKS):
        own_copy(j).start()

    eye = bits_ref[pl.ds(4 * E, E), :]
    map_rows = jnp.concatenate([map_ref[...], jnp.zeros((E - map_ref.shape[0], E), bf16)], 0)
    map_wide = mm_t(eye, map_rows).astype(bf16)
    for s in range(2):
        select = bits_ref[pl.ds(s * 2 * E, 2 * E), :]
        wide_map[s] = mm_t(map_wide, select).astype(bf16)
        wide_map_t[s] = mm_t(select, map_wide).astype(bf16)
    inputs[0].wait()
    inputs[1].wait()
    keys = keys_ext[pl.ds(WIN, tokens), :]
    features = mm(keys, map_wide)
    feature_high, feature_low = split_terms(features)
    key_features[0] = feature_high
    key_features[1] = feature_low
    inner = (mm_t(map_wide, feature_high) + mm_t(map_wide, feature_low)) * 0.25
    inner_high, inner_low = split_terms(inner)
    kernel_map[pl.ds(0, E), :] = inner_high
    kernel_map[pl.ds(E, E), :] = inner_low
    keys_t[...] = mm_t(eye, keys).astype(bf16)
    key_a = mm(keys, wide_map[0]) + rows_ref[pl.ds(0, 1), :]
    key_b = mm(keys, wide_map[1]) + rows_ref[pl.ds(1, 1), :]
    key_factor_a[...] = (key_a * rows_ref[pl.ds(2, 1), :]).astype(bf16)
    key_factor_b[...] = (key_b * rows_ref[pl.ds(2, 1), :]).astype(bf16)
    ones_values[:, pl.ds(0, E)] = values_ext[pl.ds(WIN, tokens), :]
    ones_values[:, pl.ds(E, E)] = jnp.ones((tokens, E), bf16)
    key_a_t = mm_t(wide_map_t[0], keys) + columns_ref[:, 0:1]
    key_b_t = mm_t(wide_map_t[1], keys) + columns_ref[:, 1:2]
    key_high, key_low = split_terms(key_a_t * key_b_t * columns_ref[:, 2:3])
    state = mm(key_high, ones_values[...]) + mm(key_low, ones_values[...])

    def store_state(ref, value, den_row):
        ref[pl.ds(0, PAIR_ROWS), :] = value[:PAIR_ROWS]
        ref[pl.ds(PAIR_ROWS, 8), :] = den_row[:, :E]
        ref[pl.ds(PAIR_ROWS + 8, 8), :] = den_row[:, E:]

    store_state(state_own, state[:, :E], jnp.transpose(state[:, E:])[:8])
    state_x_copy = remote(state_own, state_x, state_x_send.at[0], state_x_recv.at[0], side, h)
    state_x_copy.start()
    for m in (2, 3):
        start_first(0, m)
    for j in (2, 3):
        for d in (0, 1):
            part_copy(j, d, c).start()
    teacher_part(x).start()
    inputs[2].wait()

    def state_up_copy():
        return remote(state_up, state_low, state_up_send.at[0], state_up_recv.at[0], lax.rem(c + 2, ctx_count), h)

    def chain_step(level):
        if level == 0:
            state_x_copy.wait_recv()

            @pl.when(z == 0)
            def _():
                state_low[...] = jnp.zeros_like(state_low)

        else:

            @pl.when(z == level)
            def _():
                state_up_copy().wait_recv()

        if level < 3:

            @pl.when(z == level)
            def _():
                state_up[...] = state_low[...] + state_own[...] + state_x[...]
                state_up_copy().start()

    for s in range(2):

        @pl.when(c > 0)
        def _():
            dst = (keys_ext, values_ext)[s]
            remote(
                dst.at[pl.ds(0, WIN)], dst.at[pl.ds(0, WIN)], rim_send.at[s], rim_recv.at[s], c, h
            ).wait_recv()

    def query_tile(i, hp):
        token = pl.multiple_of(i * E, E)
        both = queries_ref[pl.ds(token, E), pl.ds(pl.multiple_of(hp * 2 * E, 2 * E), 2 * E)]
        return jnp.concatenate([both[:, :E], both[:, E:]], 0)

    def window_rows(hp):
        return pl.ds(pl.multiple_of((hp % 2) * 2 * E, 2 * E), 2 * E)

    def window_columns(hp):
        return pl.ds(pl.multiple_of((hp // 2) * E, E), E)

    for i in range(4):
        reach = (i + 1) * E

        def local_tile(hp, carry):
            tile = i * 4 + hp
            q = query_tile(i, hp)
            u = mm(jnp.concatenate([q, q], 1), kernel_map[:, pl.ds(0, reach)])
            row = lax.broadcasted_iota(jnp.int32, (2 * E, reach), 0) % E + i * E
            causal = row >= lax.broadcasted_iota(jnp.int32, (2 * E, reach), 1)
            kernel = jnp.where(causal, 1.0 + u + 0.5 * u * u, 0.0).astype(bf16)
            slope[tile, :, pl.ds(0, reach)] = jnp.where(causal, 0.25 + 0.25 * u, 0.0).astype(bf16)
            both = mm(kernel, ones_values[pl.ds(0, reach), :])
            lin[tile] = both[:, :E]
            den_inv[tile] = both[:, E:]
            scores = mm_t(q, keys_ext[pl.ds(i * E, 2 * E), :]) / math.sqrt(HEAD_DIM)
            token = lax.broadcasted_iota(jnp.int32, (2 * E, 2 * E), 0) % E
            place = lax.broadcasted_iota(jnp.int32, (2 * E, 2 * E), 1)
            distance = token + WIN - place
            allowed = (distance >= 0) & (distance < WIN) & (c * tokens + i * E + place - WIN >= 0)
            scores = jnp.where(allowed, scores, -jnp.inf)
            top = jnp.max(scores, axis=-1, keepdims=True)
            weights = jnp.where(allowed, jnp.exp(scores - top), 0.0)
            weights = (weights / jnp.sum(weights, axis=-1, keepdims=True)).astype(bf16)
            window[i, window_rows(hp), window_columns(hp)] = mm(weights, values_ext[pl.ds(i * E, 2 * E), :])
            first_factor[tile] = (mm(q, wide_map[0]) + rows_ref[pl.ds(0, 1), :]).astype(bf16)
            second_factor[tile] = (mm(q, wide_map[1]) + rows_ref[pl.ds(1, 1), :]).astype(bf16)
            pair_a = mm_t(wide_map_t[0], q) + columns_ref[:, 0:1]
            pair_b = mm_t(wide_map_t[1], q) + columns_ref[:, 1:2]
            pairs_t[tile] = (pair_a * pair_b).astype(bf16)[:PAIR_ROWS]
            queries_t[tile] = mm_t(eye, q).astype(bf16)
            service(i // 2, 1 + i % 2, hp)
            return carry

        lax.fori_loop(0, 4, local_tile, 0)
        chain_step(i)
        if i == 1:
            for m in (2, 3):
                start_first(1, m)

    past = jnp.where(z > 0, state_low[...], 0.0) + jnp.where(x == 1, state_x[...], 0.0)
    past_rows = jnp.concatenate([past[PAIR_ROWS : PAIR_ROWS + 8], past[PAIR_ROWS + 8 :]], 1)
    past_den = jnp.transpose(jnp.broadcast_to(past_rows[:1], (E, 2 * E)))
    past_values = jnp.concatenate([past[:PAIR_ROWS], jnp.zeros((2 * E - PAIR_ROWS, E), f32)], 0)
    high, low = split_terms(jnp.concatenate([past_values, past_den], 1))
    past_high[...] = high
    past_low[...] = low

    def head_piece(i, ctx_half, head):
        return heads_buf.at[ctx_half * 4 + head, pl.ds(pl.multiple_of(i * E, E), E)]

    def side_copy(i, ctx_half):
        piece = head_piece(i, ctx_half, h)
        return remote(piece, piece, side_send.at[i], side_recv.at[i], side, h)

    def near_copy(i, s, head):
        ctx_half = x if s % 2 == 0 else 1 - x
        piece = head_piece(i, ctx_half, head)
        return remote(piece, piece, near_send.at[s, i], near_recv.at[s, i], c, near)

    def far_copy(i, s, head):
        ctx_half = x if s == 0 else 1 - x
        piece = head_piece(i, ctx_half, head)
        return remote(piece, piece, far_send.at[s, i], far_recv.at[s, i], c, far)

    def past_tiles(i, carry):
        def past_tile(hp, carry):
            tile = i * 4 + hp
            q = query_tile(i, hp)
            pair = (mm(q, wide_map[0]) + rows_ref[pl.ds(0, 1), :]) * (mm(q, wide_map[1]) + rows_ref[pl.ds(1, 1), :])
            pair_high, pair_low = split_terms(pair)
            both = mm(pair_high, past_high[...]) + mm(pair_low, past_high[...]) + mm(pair_high, past_low[...])
            den = den_inv[tile] + both[:, E:]
            value = (lin[tile] + both[:, :E]) / den
            lin[tile] = value
            den_inv[tile] = 1.0 / den
            out = (value + window[i, window_rows(hp), window_columns(hp)]).astype(bf16)
            heads_buf[
                x * 4 + h, pl.ds(pl.multiple_of(i * E, E), E), pl.ds(pl.multiple_of(hp * 2 * E, 2 * E), 2 * E)
            ] = jnp.concatenate([out[:E], out[E:]], 1)
            return carry

        lax.fori_loop(0, 4, past_tile, 0)
        side_copy(i, x).start()
        far_copy(i, 0, h).start()
        near_copy(i, 0, h).start()
        return carry

    lax.fori_loop(0, 4, past_tiles, 0)
    for m in range(4):
        start_first(2, m)

    def relay_side(i, carry):
        service(2, 1, i)
        side_copy(i, 1 - x).wait_recv()
        far_copy(i, 1, h).start()
        near_copy(i, 1, h).start()
        return carry

    lax.fori_loop(0, 4, relay_side, 0)

    def relay_far(i, carry):
        service(2, 2, i)
        far_copy(i, 0, far).wait_recv()
        near_copy(i, 2, far).start()
        return carry

    lax.fori_loop(0, 4, relay_far, 0)

    for m in range(4):
        start_first(3, m)

    def relay_last(i, carry):
        service(3, 1, i)
        far_copy(i, 1, far).wait_recv()
        near_copy(i, 3, far).start()
        return carry

    lax.fori_loop(0, 4, relay_last, 0)
    teacher_copy.wait()
    teacher_part(1 - x).wait_recv()
    for j in range(CHUNKS):
        own_copy(j).wait()
    loss_acc[...] = jnp.zeros_like(loss_acc)
    for i in range(4):
        for s in range(4):
            near_copy(i, s, near if s < 2 else diagonal).wait_recv()
    def student_copy(j):
        return pltpu.make_async_copy(
            teacher_buf.at[x, :, chunk_columns(0, j)], student_ref.at[:, chunk_columns(columns_here, j)], student_sem.at[j]
        )

    def student_part(j, start):
        return remote(
            teacher_buf.at[1 - x, :, chunk_columns(0, j)], student_ref.at[:, chunk_columns(start, j)],
            student_send.at[j], student_recv.at[j], side, h,
        )

    def finish_columns(j, ctx_half, product):
        student = product.astype(bf16)
        columns = chunk_columns(0, j)
        residual = student.astype(f32) - teacher_buf[ctx_half, :, columns].astype(f32)
        teacher_buf[ctx_half, :, columns] = student
        loss_acc[...] += jnp.sum((residual * residual).reshape(tokens // 8, 8, width), axis=0)
        d_student[j, ctx_half] = (residual * (2.0 / (tokens * ctx_count))).astype(bf16)

    def finish_both(j, products):
        for product, ctx_half in zip(products, (x, 1 - x)):
            finish_columns(j, ctx_half, product)
        student_copy(j).start()

    def plane_product(ctx_half, plane, j):
        rows = pl.ds(pl.multiple_of(plane * 2 * tokens, 2 * tokens), 2 * tokens)
        return mm(heads_buf[ctx_half * 4 + plane], proj_buf[j, rows, :])

    def first_columns(j, carry):
        for m in range(4):
            last_arrival(j, m)
        products = []
        for ctx_half in (x, 1 - x):
            product = plane_product(ctx_half, 0, j)
            for plane in range(1, 4):
                product += plane_product(ctx_half, plane, j)
            products.append(product)
        finish_both(j, products)
        student_part(j, columns_here).start()
        for m in range(2):

            @pl.when(j < 2)
            def _():
                service(3, 2, j * 2 + m)

        return carry

    lax.fori_loop(0, 3, first_columns, 0)
    last_plane = jnp.where(z >= 2, 0, 3)

    for t, ctx_half in enumerate((x, 1 - x)):
        product = plane_product(ctx_half, (last_plane + 1) % 4, 3)
        for b in (2, 3):
            product += plane_product(ctx_half, (last_plane + b) % 4, 3)
        acc[t] = product

    def block_sum(chunks, ctx_half, head, p):
        rows = pl.ds(pl.multiple_of((head * 4 + p) * width, width), width)
        total = mm_t(d_student[chunks[0], ctx_half], proj_buf[chunks[0], rows, :])
        for j in chunks[1:]:
            total += mm_t(d_student[j, ctx_half], proj_buf[j, rows, :])
        return total

    for s, (head, p) in enumerate(((diagonal, 0), (diagonal, 2), (far, 0), (far, 2))):
        window[s] = block_sum((0, 1, 2), 1 - x, head, p)

    for m in range(4):
        last_arrival(3, m)
        products = []
        for t, ctx_half in enumerate((x, 1 - x)):
            left = heads_buf[ctx_half * 4 + last_plane, :, pl.ds(pl.multiple_of(quarter(m) * half, half), half)]
            products.append(acc[t] + mm(left, proj_buf[3, plane_rows(last_plane, quarter(m)), :]))
            if m < 3:
                acc[t] = products[t]
        if m == 3:
            finish_both(3, products)

    def copy_n(s):
        return remote(send_n.at[s], recv_n.at[s], n_send.at[s], n_recv.at[s], c, near)

    def copy_d(p):
        ctx, head = (side, h) if p < 2 else (c, far)
        return remote(send_d.at[p], recv_d.at[p], d_send.at[p], d_recv.at[p], ctx, head)

    def copy_a(p):
        return remote(send_a.at[p], recv_a.at[p], a_send.at[p], a_recv.at[p], side, h)

    def copy_b(p):
        return remote(send_b.at[p], recv_b.at[p], b_send.at[p], b_recv.at[p], c, far)

    kinds = {"d": (1, 1), "a": (1, 0), "b": (0, 1), "own": (0, 0)}

    def slot(kind, p):
        return (kinds[kind][0] * 2 + kinds[kind][1]) * 4 + p

    def give(kind, p):
        other, distant = kinds[kind]
        ctx_half = 1 - x if other else x
        head = diagonal if distant else near
        if kind == "d" and p % 2 == 0:
            total = window[p // 2] + block_sum((3,), ctx_half, head, p)
        else:
            total = block_sum(range(CHUNKS), ctx_half, head, p)
        send_n[slot(kind, p)] = total.astype(bf16)
        copy_n(slot(kind, p)).start()

    def take(kind, p):
        other, distant = kinds[kind]
        ctx_half = 1 - x if other else x
        head = far if distant else h
        if kind == "d" and p % 2 == 0:
            total = window[2 + p // 2] + block_sum((3,), ctx_half, head, p)
        else:
            total = block_sum(range(CHUNKS), ctx_half, head, p)
        copy_n(slot(kind, p)).wait_recv()
        return total + recv_n[slot(kind, p)].astype(f32)

    def send_corner(p):
        send_d[p] = take("d", p).astype(bf16)
        copy_d(p).start()

    def send_side(kind, p, corner):
        total = take(kind, p)
        if corner:
            copy_d(p).wait_recv()
            total += recv_d[p].astype(f32)
        if kind == "a":
            send_a[p] = total.astype(bf16)
            copy_a(p).start()
        else:
            send_b[p] = total.astype(bf16)
            copy_b(p).start()

    give("d", 0)
    give("d", 2)
    send_corner(0)
    send_corner(2)
    give("d", 1)
    give("d", 3)
    send_corner(1)
    send_corner(3)
    for a, b in ((0, 2), (1, 0), (2, 1), (3, 3)):
        give("a", a)
        give("b", b)
        send_side("a", a, a >= 2)
        send_side("b", b, b < 2)
    for p in range(4):
        give("own", p)
    for p in range(4):
        own_sum[p] = take("own", p)

    loss_own[...] = loss_acc[:, :E] + loss_acc[:, E:]

    def loss_copy(d, source):
        return remote(loss_own, loss_in.at[source], loss_send.at[d], loss_recv.at[source], c, (h + d) % 4)

    for d in range(1, 4):
        loss_copy(d, h).start()

    cross[...] = jnp.zeros_like(cross)
    grad_a[...] = jnp.zeros_like(grad_a)
    grad_b[...] = jnp.zeros_like(grad_b)
    back[...] = jnp.zeros_like(back)

    def grad_piece(p, carry):
        copy_a(p).wait_recv()
        copy_b(p).wait_recv()
        for i in range(4):
            reach = (i + 1) * E
            tile = i * 4 + p
            rows = pl.ds(i * E, E)
            g = own_sum[p, rows, :] + recv_a[p, rows, :].astype(f32) + recv_b[p, rows, :].astype(f32)
            g = jnp.concatenate([g[:, :E], g[:, E:]], 0)
            inverse = den_inv[tile]
            upper = (g * inverse).astype(bf16)
            lower = -jnp.sum(upper.astype(f32) * lin[tile], axis=-1, keepdims=True)
            lower = jnp.broadcast_to(lower, (2 * E, E))
            lower_high = lower.astype(bf16).astype(f32)
            lane = lax.broadcasted_iota(jnp.int32, (2 * E, E), 1)
            lower = (jnp.where(lane < E // 2, lower_high, lower - lower_high) * (2.0 / E)).astype(bf16)
            wide = jnp.concatenate([upper, lower], 1)
            weight = mm_t(wide, ones_values[pl.ds(0, reach), :]) * slope[tile, :, pl.ds(0, reach)].astype(f32)
            cross[:, pl.ds(0, reach)] += mm(queries_t[tile], weight.astype(bf16))
            pair_grad = mm_t(wide, past_high[...]) + mm_t(wide, past_low[...])
            grad_a[...] += mm(queries_t[tile], (pair_grad * second_factor[tile].astype(f32)).astype(bf16))
            grad_b[...] += mm(queries_t[tile], (pair_grad * first_factor[tile].astype(f32)).astype(bf16))
            back[...] += mm(pairs_t[tile], wide)
        return carry

    lax.fori_loop(0, 4, grad_piece, 0)

    back_den = jnp.transpose(
        jnp.concatenate([back[:, pl.ds(E, E)], jnp.zeros((2 * E - PAIR_ROWS, E), f32)], 0)
    )
    back_den = (back_den[:8] + back_den[E // 2 : E // 2 + 8]) * (E // 2)
    store_state(back_own, back[:, pl.ds(0, E)], back_den)
    back_x_copy = remote(back_own, back_x, back_x_send.at[0], back_x_recv.at[0], side, h)
    back_x_copy.start()
    student_part(3, columns_here).start()

    def back_copy(level):
        return remote(back_sum, back_in.at[z], back_send.at[level], back_recv.at[z], 2 * level + x, h)

    def back_arrival(level):
        return remote(back_sum, back_in.at[level], back_send.at[level], back_recv.at[level], c, h)

    cross_high, cross_low = split_terms(cross[...])
    grad = mm(cross_high, key_features[0]) + mm(cross_high, key_features[1]) + mm(cross_low, key_features[0])
    keys = keys_ext[pl.ds(WIN, tokens), :]
    mixed = jnp.transpose(mm(cross_high, keys) + mm(cross_low, keys))
    mixed_high, mixed_low = split_terms(mixed)
    map_rows = jnp.concatenate([map_ref[...], jnp.zeros((E - map_ref.shape[0], E), bf16)], 0)
    map_wide = mm_t(bits_ref[pl.ds(4 * E, E), :], map_rows).astype(bf16)
    grad += mm(mixed_high, map_wide) + mm(mixed_low, map_wide)

    center = mm(jnp.ones((8, tokens), bf16), values_ext[pl.ds(WIN, tokens), :])
    center = (center / tokens).astype(bf16)
    back_x_copy.wait_recv()
    plane = back_own[...] + back_x[...]
    plane_values = plane[:PAIR_ROWS].astype(bf16)
    lost = (plane[:PAIR_ROWS] - plane_values.astype(f32)).astype(bf16)
    lost = jnp.concatenate([lost, jnp.zeros((2 * E - PAIR_ROWS, E), bf16)], 0)
    moved = mm_t(center, lost)
    plane_den = plane[PAIR_ROWS:] + jnp.concatenate([moved[:, :E], moved[:, E:]], 0)
    den_high, den_low = split_terms(plane_den)
    back_sum[pl.ds(0, PAIR_ROWS), :] = plane_values
    back_sum[pl.ds(PAIR_ROWS, 16), :] = den_high
    back_sum[pl.ds(PAIR_ROWS + 16, 16), :] = den_low
    for level in range(3):

        @pl.when(level < z)
        def _():
            back_copy(level).start()

    back_later[...] = jnp.where(x == 0, back_x[...], 0.0)
    for level in range(1, 4):

        @pl.when(level > z)
        def _():
            back_arrival(level).wait_recv()
            arrived = back_in[level].astype(f32)
            back_later[...] += arrived[: PAIR_ROWS + 16]
            back_later[pl.ds(PAIR_ROWS, 16), :] += arrived[PAIR_ROWS + 16 :]

    later_values = jnp.concatenate([back_later[pl.ds(0, PAIR_ROWS), :], jnp.zeros((2 * E - PAIR_ROWS, E), f32)], 0)
    later_high, later_low = split_terms(later_values)
    pair_grad = mm_t(values_ext[pl.ds(WIN, tokens), :], later_high)
    pair_grad += mm_t(values_ext[pl.ds(WIN, tokens), :], later_low)
    pair_grad += jnp.concatenate(
        [back_later[pl.ds(PAIR_ROWS, 1), :], back_later[pl.ds(PAIR_ROWS + 8, 1), :]], 1
    )
    total_a = grad_a[...] + mm(keys_t[...], (pair_grad * key_factor_b[...].astype(f32)).astype(bf16))
    total_b = grad_b[...] + mm(keys_t[...], (pair_grad * key_factor_a[...].astype(f32)).astype(bf16))
    for s, total in enumerate((total_a, total_b)):
        total_high, total_low = split_terms(total)
        select = bits_ref[pl.ds(s * 2 * E, 2 * E), :]
        grad += mm(total_high, select) + mm(total_low, select)
    final_own[pl.ds(0, 16), :] = jnp.transpose(grad)[:16]
    loss_sum = loss_own[...]
    for d in range(1, 4):
        loss_copy(d, (h + d) % 4).wait_recv()
        loss_sum += loss_in[(h + d) % 4]
    final_own[pl.ds(16, 8), :] = loss_sum

    def final_copy(d, source):
        return remote(final_own, final_in.at[source], final_send.at[d], final_recv.at[source], (c + d) % ctx_count, h)

    for d in range(1, ctx_count):
        final_copy(d, c).start()
    final_in[c] = final_own[...]
    for d in range(1, ctx_count):
        final_copy(d, (c + d) % ctx_count).wait_recv()
    final = final_in[0]
    for s in range(1, ctx_count):
        final += final_in[s]
    grad_ref[...] = final[:16]
    loss_ref[0, 0] = jnp.sum(final[16:]) / (tokens * ctx_count * D)

    for j in range(CHUNKS):
        student_copy(j).wait()
        student_part(j, columns_here).wait_send()
        student_part(j, columns_there).wait_recv()
        for d in (0, 1):
            part_copy(j, d, c).wait_send()
            for m in range(4):
                for k in range(3):

                    @pl.when(has_target(d) & has_owner(d, k))
                    def _():
                        hop(d, j, k, quarter(m)).wait_send()

    teacher_part(x).wait_send()
    for s in range(2):

        @pl.when(c < ctx_count - 1)
        def _():
            dst = (keys_ext, values_ext)[s]
            src = (keys_in, values_in)[s]
            remote(
                src.at[pl.ds(tokens - WIN, WIN)], dst.at[pl.ds(0, WIN)], rim_send.at[s], rim_recv.at[s],
                lax.rem(c + 1, ctx_count), h,
            ).wait_send()

    state_x_copy.wait_send()

    @pl.when(z < 3)
    def _():
        state_up_copy().wait_send()

    back_x_copy.wait_send()
    for level in range(3):

        @pl.when(level < z)
        def _():
            back_copy(level).wait_send()

    for d in range(1, 4):
        loss_copy(d, h).wait_send()
    for i in range(4):
        side_copy(i, x).wait_send()
        for s in range(2):
            far_copy(i, s, h).wait_send()
        for s in range(4):
            near_copy(i, s, h if s < 2 else far).wait_send()
    for p in range(4):
        copy_d(p).wait_send()
        copy_a(p).wait_send()
        copy_b(p).wait_send()
    for s in range(16):
        copy_n(s).wait_send()
    for d in range(1, ctx_count):
        final_copy(d, c).wait_send()


def deliver_kernel(student_ref, grad_ref, loss_ref, student_out, grad_out, loss_out, buffer, grad_buffer, sem, out_sem):
    part = student_ref.shape[0] // 4
    moves = [(ref.at[pl.ds(s * part, part)], buffer.at[pl.ds(s * part, part)], student_out.at[pl.ds(s * part, part)])
             for s, ref in enumerate([student_ref] * 4)]
    moves.append((grad_ref, grad_buffer, grad_out))
    reads = [pltpu.make_async_copy(src, mid, sem.at[s]) for s, (src, mid, dst) in enumerate(moves)]
    writes = [pltpu.make_async_copy(mid, dst, out_sem.at[s]) for s, (src, mid, dst) in enumerate(moves)]
    for copy in reads:
        copy.start()
    loss_out[0, 0] = loss_ref[0, 0]
    for read, write in zip(reads, writes):
        read.wait()
        write.start()
    for copy in writes:
        copy.wait()


def fused_local(queries, keys, values, feature_map, out_proj, teacher):
    tokens = queries.shape[0]
    columns = out_proj.shape[1]
    rows = tokens * 8
    width = columns // 2 // CHUNKS
    E = HEAD_DIM
    bf16, f32 = jnp.bfloat16, jnp.float32
    bits, row_table, column_table = pair_tables()
    vmem = pl.BlockSpec(memory_space=pltpu.VMEM)
    anywhere = pl.BlockSpec(memory_space=pl.ANY)
    smem = pl.BlockSpec(memory_space=pltpu.SMEM)
    dma = pltpu.SemaphoreType.DMA
    state = (PAIR_ROWS + 16, E)
    scratch = [
        ((CHUNKS, rows, width), bf16),
        ((8, tokens, 8 * E), bf16),
        ((4, tokens, width), f32),
        ((4, tokens, width), f32),
        ((16, 2 * E, 2 * E), bf16),
        ((16, 2 * E, 2 * E), bf16),
        ((16, PAIR_ROWS, 2 * E), bf16),
        ((16, E, 2 * E), bf16),
        ((16, 2 * E, tokens), bf16),
        ((16, 2 * E, E), f32),
        ((16, 2 * E, E), f32),
        ((CHUNKS, 2, tokens, width), bf16),
        ((2, tokens, width), f32),
        ((tokens, 8 * E), bf16),
        ((2, tokens, columns // 2), bf16),
        ((tokens + 2 * WIN, E), bf16),
        ((tokens + 2 * WIN, E), bf16),
        ((tokens, 2 * E), bf16),
        ((2, E, 2 * E), bf16),
        ((2, 2 * E, E), bf16),
        ((2 * E, tokens), bf16),
        ((2 * E, 2 * E), bf16),
        ((2 * E, 2 * E), bf16),
        ((2, tokens, E), bf16),
        ((tokens, 2 * E), bf16),
        ((tokens, 2 * E), bf16),
        ((E, tokens), bf16),
        (state, f32),
        (state, f32),
        (state, f32),
        (state, f32),
        ((16, tokens, width), bf16),
        ((16, tokens, width), bf16),
        ((4, tokens, width), bf16),
        ((4, tokens, width), bf16),
        ((4, tokens, width), bf16),
        ((4, tokens, width), bf16),
        ((4, tokens, width), bf16),
        ((4, tokens, width), bf16),
        ((E, tokens), f32),
        ((E, 2 * E), f32),
        ((E, 2 * E), f32),
        ((PAIR_ROWS, 2 * E), f32),
        (state, f32),
        (state, f32),
        ((PAIR_ROWS + 32, E), bf16),
        (state, f32),
        ((4, PAIR_ROWS + 32, E), bf16),
        ((24, E), f32),
        ((8, 24, E), f32),
        ((8, width), f32),
        ((8, E), f32),
        ((4, 8, E), f32),
    ]
    semaphores = [
        (2, CHUNKS, 12), (2, CHUNKS, 12), (CHUNKS,), (3,), (1,), (1,), (1,), (CHUNKS,), (CHUNKS,), (CHUNKS,), (CHUNKS, 2),
        (CHUNKS, 2), (2,), (2,), (1,), (1,), (1,), (1,), (4,), (4,), (4, 4), (4, 4), (2, 4), (2, 4), (16,), (16,), (4,), (4,),
        (4,), (4,), (4,), (4,), (1,), (1,), (4,), (4,), (8,), (8,), (4,), (4,),
    ]
    student, grad, loss = pl.pallas_call(
        fused_kernel,
        out_shape=(
            jax.ShapeDtypeStruct((tokens, columns), bf16),
            jax.ShapeDtypeStruct((feature_map.shape[2], E), f32),
            jax.ShapeDtypeStruct((1, 1), f32),
        ),
        in_specs=[anywhere, anywhere, anywhere, vmem, anywhere, anywhere, vmem, vmem, vmem],
        out_specs=(anywhere, vmem, smem),
        scratch_shapes=[pltpu.VMEM(shape, kind) for shape, kind in scratch] + [dma(shape) for shape in semaphores],
        compiler_params=pltpu.CompilerParams(
            collective_id=0, has_side_effects=True, vmem_limit_bytes=63 * 1024 * 1024
        ),
        cost_estimate=pl.CostEstimate(flops=30_000_000_000, bytes_accessed=40_000_000, transcendentals=2_000_000),
    )(
        queries, keys, values, feature_map[0].T, out_proj, teacher,
        jnp.asarray(bits, bf16), jnp.asarray(row_table, f32), jnp.asarray(column_table, f32),
    )
    student, grad, loss = pl.pallas_call(
        deliver_kernel,
        out_shape=(
            jax.ShapeDtypeStruct(student.shape, bf16),
            jax.ShapeDtypeStruct(grad.shape, f32),
            jax.ShapeDtypeStruct((1, 1), f32),
        ),
        in_specs=[anywhere, anywhere, smem],
        out_specs=(anywhere, anywhere, smem),
        scratch_shapes=[pltpu.VMEM(student.shape, bf16), pltpu.VMEM(grad.shape, f32), dma((5,)), dma((5,))],
        cost_estimate=pl.CostEstimate(flops=0, bytes_accessed=2 * student.size * 2, transcendentals=0),
    )(student, grad, loss)
    return student, loss.reshape(()), grad.T[None]


def fits_fused(mesh):
    return mesh.shape["ctx"] == 8 and mesh.shape["head"] == 4


def solution(mesh):
    return jax.shard_map(
        fused_local if fits_fused(mesh) else local,
        mesh=mesh,
        in_specs=(
            P("ctx", "head"),
            P("ctx", "head"),
            P("ctx", "head"),
            P("head", None, None),
            P("ctx", "head"),
            P("ctx", "head"),
        ),
        out_specs=(P("ctx", "head"), P(), P("head", None, None)),
        check_vma=False,
    )
```

```python
import functools
import math

import jax
import jax.numpy as jnp
import numpy as np
from jax import lax
from jax.experimental import pallas as pl
from jax.experimental.pallas import tpu as pltpu
from jax.sharding import PartitionSpec as P

D = 8192
HEAD_DIM = 128
GROUP = 8
WIN = 64


exact_mode = lax.Precision.HIGHEST


def shifted(block, axis, distance):
    devices = range(lax.axis_size(axis))
    route = [(i - distance, i) for i in devices if i - distance in devices]
    return lax.ppermute(block, axis, route)


def taylor_square(features):
    feature_count = features.shape[-1]
    outer = features[..., :, None] * features[..., None, :]
    return outer.reshape(features.shape[:-1] + (feature_count * feature_count,))


def two_terms(x):
    high = lax.reduce_precision(x, 8, 7)
    return jnp.concatenate([high.astype(jnp.bfloat16), (x - high).astype(jnp.bfloat16)], -1)


def joined(pair):
    half = pair.shape[-1] // 2
    return pair[..., :half] + pair[..., half:]


def square_grad(grad_square, features):
    feature_count = features.shape[-1]
    matrix = grad_square.reshape(features.shape + (feature_count,))
    return jnp.einsum("...fh,...h->...f", matrix, features, precision=exact_mode) + jnp.einsum(
        "...hf,...h->...f", matrix, features, precision=exact_mode
    )


def exchange_kernel(count, head_count, mode, x_ref, row_ref, out_ref, row_out, buf, row_buf, send, recv, row_send, row_recv):
    me = lax.axis_index("ctx")
    head = lax.axis_index("head")
    mesh_ids = pl.DeviceIdType.MESH
    barrier = pltpu.get_barrier_semaphore()
    for d in range(1, count):
        pl.semaphore_signal(
            barrier, inc=1, device_id=(lax.rem(me + d, count), head), device_id_type=mesh_ids
        )
    for d in range(1, head_count):
        pl.semaphore_signal(
            barrier, inc=1, device_id=(me, lax.rem(head + d, head_count)), device_id_type=mesh_ids
        )
    pl.semaphore_wait(barrier, count + head_count - 2)

    def wanted(source, target):
        return {"lower": source < target, "upper": source > target, "all": source != target}[mode]

    def ctx_copy(d):
        return pltpu.make_async_remote_copy(
            src_ref=x_ref,
            dst_ref=buf.at[me],
            send_sem=send.at[d],
            recv_sem=recv.at[me],
            device_id=(lax.rem(me + d, count), head),
            device_id_type=mesh_ids,
        )

    def row_copy(d):
        return pltpu.make_async_remote_copy(
            src_ref=row_ref,
            dst_ref=row_buf.at[head],
            send_sem=row_send.at[d],
            recv_sem=row_recv.at[head],
            device_id=(me, lax.rem(head + d, head_count)),
            device_id_type=mesh_ids,
        )

    def ctx_arrival(source):
        return pltpu.make_async_remote_copy(
            src_ref=x_ref,
            dst_ref=buf.at[source],
            send_sem=send.at[0],
            recv_sem=recv.at[source],
            device_id=(source, head),
            device_id_type=mesh_ids,
        )

    def row_arrival(source):
        return pltpu.make_async_remote_copy(
            src_ref=row_ref,
            dst_ref=row_buf.at[source],
            send_sem=row_send.at[0],
            recv_sem=row_recv.at[source],
            device_id=(me, source),
            device_id_type=mesh_ids,
        )

    for d in range(1, count):

        @pl.when(wanted(me, lax.rem(me + d, count)))
        def _():
            ctx_copy(d).start()

    for d in range(1, head_count):
        row_copy(d).start()

    row_out[...] = jnp.zeros_like(row_out)
    for source in range(head_count):

        @pl.when(source == head)
        def _():
            row_out[...] += row_ref[...]

        @pl.when(source != head)
        def _():
            row_arrival(source).wait_recv()
            row_out[...] += row_buf[source]

    out_ref[...] = jnp.zeros_like(out_ref)
    for source in range(count):
        if mode == "all":

            @pl.when(source == me)
            def _():
                out_ref[...] += x_ref[...].astype(jnp.float32)

        @pl.when(wanted(source, me))
        def _():
            ctx_arrival(source).wait_recv()
            out_ref[...] += buf[source].astype(jnp.float32)

    for d in range(1, count):

        @pl.when(wanted(me, lax.rem(me + d, count)))
        def _():
            ctx_copy(d).wait_send()

    for d in range(1, head_count):
        row_copy(d).wait_send()


def exchange(x, row, mode, collective_id):
    count = lax.axis_size("ctx")
    head_count = lax.axis_size("head")
    vmem = pl.BlockSpec(memory_space=pltpu.VMEM)
    return pl.pallas_call(
        functools.partial(exchange_kernel, count, head_count, mode),
        out_shape=(
            jax.ShapeDtypeStruct(x.shape, jnp.float32),
            jax.ShapeDtypeStruct(row.shape, jnp.float32),
        ),
        in_specs=[vmem, vmem],
        out_specs=(vmem, vmem),
        scratch_shapes=[
            pltpu.VMEM((count,) + x.shape, x.dtype),
            pltpu.VMEM((head_count,) + row.shape, jnp.float32),
            pltpu.SemaphoreType.DMA((count,)),
            pltpu.SemaphoreType.DMA((count,)),
            pltpu.SemaphoreType.DMA((head_count,)),
            pltpu.SemaphoreType.DMA((head_count,)),
        ],
        compiler_params=pltpu.CompilerParams(collective_id=collective_id, has_side_effects=True),
        cost_estimate=pl.CostEstimate(
            flops=count * x.size, bytes_accessed=40 * count * x.size, transcendentals=0
        ),
    )(x, row)


def pack(square, linear, square_den, linear_den, flat):
    groups, feature_count = linear_den.shape
    squares = feature_count * feature_count
    square_rows = square_den.reshape(groups, squares // HEAD_DIM, HEAD_DIM)
    linear_rows = jnp.pad(linear_den, ((0, 0), (0, HEAD_DIM - feature_count)))[:, None]
    small = jnp.concatenate([flat[:, None], linear_rows, square_rows], 1)
    small = jnp.pad(small, ((0, 0), (0, -small.shape[1] % 16), (0, 0)))
    return jnp.concatenate([square, linear, small], 1).reshape(-1, HEAD_DIM)


def unpack(packed, groups, feature_count):
    squares = feature_count * feature_count
    packed = packed.reshape(groups, -1, HEAD_DIM)
    top = squares + feature_count
    square_den = packed[:, top + 2 : top + 2 + squares // HEAD_DIM].reshape(groups, squares)
    return (
        packed[:, :squares],
        packed[:, squares:top],
        square_den,
        packed[:, top + 1, :feature_count],
        packed[:, top],
    )


def ring_gather(block):
    count = lax.axis_size("ctx")
    me = lax.axis_index("ctx")
    rows = block.shape[0]
    half = rows // 2
    ring = list(range(0, count, 2)) + list(range(1, count, 2))[::-1]
    place = [ring.index(i) for i in range(count)]
    position = jnp.array(place, jnp.int32)[me]
    ring_table = jnp.array(ring, jnp.int32)
    up_route = [(ring[p], ring[(p + 1) % count]) for p in range(count)]
    down_route = [(ring[(p + 1) % count], ring[p]) for p in range(count)]
    up, down = block[:half], block[half:]
    pieces = [(me, up, down, me)]
    for step in range(1, count):
        up = lax.ppermute(up, "ctx", up_route)
        down = lax.ppermute(down, "ctx", down_route)
        pieces.append(
            (
                ring_table[(position - step) % count],
                up,
                down,
                ring_table[(position + step) % count],
            )
        )
    return pieces


def after_hop(pieces, hop, *members):
    if hop >= len(pieces):
        return members
    up_owner, up, down, down_owner = pieces[hop]
    up, down, *members = lax.optimization_barrier((up, down, *members))
    pieces[hop] = (up_owner, up, down, down_owner)
    return members


def assemble(pieces, zero, rows):
    half = rows // 2
    count = len(pieces)
    full = jnp.broadcast_to(zero, (count * rows, pieces[0][1].shape[1]))
    for up_owner, up, down, down_owner in pieces:
        full = lax.dynamic_update_slice(full, up, (up_owner * rows, 0))
        full = lax.dynamic_update_slice(full, down, (down_owner * rows + half, 0))
    return full


def flipped(block, bit):
    return lax.ppermute(block, "head", [(i, i ^ bit) for i in range(4)])


def sum_heads(row):
    if lax.axis_size("head") != 4:
        return lax.psum(row, "head")
    row = row + flipped(row, 1)
    return row + flipped(row, 2)


def sum_from(block, sign):
    count = lax.axis_size("ctx")
    devices = range(count)
    total = jnp.zeros_like(block)
    for distance in range(1, count):
        route = [(i, i + sign * distance) for i in devices if i + sign * distance in devices]
        total = total + lax.ppermute(block, "ctx", route)
    return total


def gather_heads(block):
    if lax.axis_size("head") != 4:
        return lax.all_gather(block, "head", axis=1, tiled=True)
    head = lax.axis_index("head")
    rows, width = block.shape
    far = flipped(block, 2)
    near = flipped(block, 1)
    diagonal = flipped(far, 1)
    full = jnp.zeros((rows, 4 * width), block.dtype)
    for bit, member in ((0, block), (2, far), (1, near), (3, diagonal)):
        full = lax.dynamic_update_slice(full, member, (0, (head ^ bit) * width))
    return full


def scatter_heads(d_student, proj_full):
    def product(weights):
        return lax.dot_general(
            d_student, weights, (((1,), (1,)), ((), ())), preferred_element_type=jnp.float32
        ).astype(jnp.bfloat16)

    if lax.axis_size("head") != 4:
        terms = product(proj_full)
        return lax.psum_scatter(terms, "head", scatter_dimension=1, tiled=True).astype(jnp.float32)
    head = lax.axis_index("head")
    width = proj_full.shape[0] // 4

    def block(bit):
        return product(lax.dynamic_slice_in_dim(proj_full, (head ^ bit) * width, width, 0))

    diagonal = flipped(block(3), 1)
    far = block(2)
    pair = (far.astype(jnp.float32) + diagonal.astype(jnp.float32)).astype(jnp.bfloat16)
    far_sum = flipped(pair, 2)
    near = flipped(block(1), 1)
    own = block(0)
    return own.astype(jnp.float32) + near.astype(jnp.float32) + far_sum.astype(jnp.float32)


def window_tiles(extended, tok_rows):
    tile_count = tok_rows // WIN
    first = extended[:tok_rows].reshape((tile_count, WIN) + extended.shape[1:])
    second = extended[WIN:].reshape((tile_count, WIN) + extended.shape[1:])
    return jnp.concatenate([first, second], 1)


def local(queries, keys, values, feature_map, out_proj, teacher):
    tok_rows = queries.shape[0]
    kv_groups = keys.shape[1] // HEAD_DIM
    ctx_count = lax.axis_size("ctx")
    ctx_index = lax.axis_index("ctx")
    pieces = ring_gather(out_proj)
    query_heads = queries.reshape(tok_rows, kv_groups, GROUP, HEAD_DIM)
    key_heads = keys.reshape(tok_rows, kv_groups, HEAD_DIM)
    value_heads = values.reshape(tok_rows, kv_groups, HEAD_DIM)
    value_float = value_heads.astype(jnp.float32)
    query_features = jnp.einsum(
        "tgqe,gef->tgqf", query_heads, feature_map, preferred_element_type=jnp.float32
    )
    key_features = jnp.einsum(
        "tge,gef->tgf", key_heads, feature_map, preferred_element_type=jnp.float32
    )
    rim_rows = shifted(jnp.stack([keys[tok_rows - WIN :], values[tok_rows - WIN :]]), "ctx", 1)
    keys_ext = jnp.concatenate([rim_rows[0], keys], 0).reshape(tok_rows + WIN, kv_groups, HEAD_DIM)
    values_ext = jnp.concatenate([rim_rows[1], values], 0).reshape(
        tok_rows + WIN, kv_groups, HEAD_DIM
    )
    tile_count = tok_rows // WIN
    key_tiles = window_tiles(keys_ext, tok_rows)
    value_tiles = window_tiles(values_ext, tok_rows)
    query_tiles = query_heads.reshape(tile_count, WIN, kv_groups, GROUP, HEAD_DIM)
    causal = lax.broadcasted_iota(jnp.int32, (tok_rows, tok_rows), 0) >= lax.broadcasted_iota(
        jnp.int32, (tok_rows, tok_rows), 1
    )
    qk_inner = (
        jnp.einsum("tgqf,sgf->gqts", query_features, key_features, precision=exact_mode) / 4.0
    )
    kernel = jnp.where(causal, 1.0 + qk_inner + 0.5 * qk_inner * qk_inner, 0.0)
    numerator = jnp.einsum(
        "gqts,sge->tgqe", kernel.astype(jnp.bfloat16), value_heads, preferred_element_type=jnp.float32
    )
    denominator = jnp.transpose(jnp.sum(kernel, axis=-1), (2, 0, 1))
    query_tiles, numerator, denominator = after_hop(
        pieces, 1, query_tiles, numerator, denominator
    )
    scores = jnp.einsum(
        "ntgqe,nsge->ngqts", query_tiles, key_tiles, preferred_element_type=jnp.float32
    ) / math.sqrt(HEAD_DIM)
    tile_pos = lax.broadcasted_iota(jnp.int32, (tile_count, WIN, 2 * WIN), 0)
    query_pos = lax.broadcasted_iota(jnp.int32, (tile_count, WIN, 2 * WIN), 1)
    key_pos = lax.broadcasted_iota(jnp.int32, (tile_count, WIN, 2 * WIN), 2)
    distance = query_pos + WIN - key_pos
    allowed = (
        (distance >= 0)
        & (distance < WIN)
        & (ctx_index * tok_rows + tile_pos * WIN + key_pos - WIN >= 0)
    )
    allowed = allowed[:, None, None]
    scores = jnp.where(allowed, scores, -jnp.inf)
    row_max = jnp.max(scores, axis=-1, keepdims=True)
    weights = jnp.where(allowed, jnp.exp(scores - row_max), 0.0)
    attn_weights = (weights / jnp.sum(weights, axis=-1, keepdims=True)).astype(jnp.bfloat16)
    window_out = jnp.einsum(
        "ngqts,nsge->ntgqe", attn_weights, value_tiles, preferred_element_type=jnp.float32
    ).reshape(tok_rows, kv_groups, GROUP, HEAD_DIM)
    key_square = taylor_square(key_features)
    own_square_v = jnp.einsum("sgk,sge->gke", key_square, value_float, precision=exact_mode)
    own_linear_v = jnp.einsum("sgf,sge->gfe", key_features, value_float, precision=exact_mode)
    own_values = jnp.sum(value_float, axis=0)
    own_square_k = jnp.sum(key_square, axis=0)
    own_linear_k = jnp.sum(key_features, axis=0)
    no_row = jnp.zeros((8, HEAD_DIM), jnp.float32)
    packed = pack(own_square_v, own_linear_v, own_square_k, own_linear_k, own_values)
    earlier, window_out = after_hop(pieces, 2, sum_from(packed, 1), window_out)
    feature_count = feature_map.shape[2]
    past_square_v, past_linear_v, past_square_k, past_linear_k, past_values = unpack(
        earlier, kv_groups, feature_count
    )
    past_count = (ctx_index * tok_rows).astype(jnp.float32)
    query_square = taylor_square(query_features)
    numerator = (
        numerator
        + jnp.einsum("tgqk,gke->tgqe", query_square, past_square_v, precision=exact_mode) / 32.0
        + jnp.einsum("tgqf,gfe->tgqe", query_features, past_linear_v, precision=exact_mode) / 4.0
        + past_values[None, :, None, :]
    )
    denominator = (
        denominator
        + jnp.einsum("tgqk,gk->tgq", query_square, past_square_k, precision=exact_mode) / 32.0
        + jnp.einsum("tgqf,gf->tgq", query_features, past_linear_k, precision=exact_mode) / 4.0
        + past_count
    )
    linear_out = numerator / denominator[..., None]
    head_out = (
        (linear_out + window_out)
        .astype(jnp.bfloat16)
        .reshape(tok_rows, kv_groups * GROUP * HEAD_DIM)
    )
    head_out, zero = after_hop(pieces, 3, head_out, jnp.zeros((), jnp.bfloat16))
    all_heads = gather_heads(head_out)
    proj_full = assemble(pieces, zero, out_proj.shape[0])
    projected = jnp.dot(all_heads, proj_full, preferred_element_type=jnp.float32)
    student_out = projected.astype(jnp.bfloat16)
    residual = student_out.astype(jnp.float32) - teacher.astype(jnp.float32)
    total_rows = tok_rows * ctx_count
    squared = jnp.sum(residual * residual)
    d_student = (2.0 * residual / total_rows).astype(jnp.bfloat16)
    head_grad = scatter_heads(d_student, proj_full).reshape(
        tok_rows, kv_groups, GROUP, HEAD_DIM
    )
    numerator_grad = head_grad / denominator[..., None]
    denominator_grad = -jnp.sum(head_grad * linear_out, axis=-1) / denominator
    kernel_grad = (
        jnp.einsum(
            "tgqe,sge->gqts",
            two_terms(numerator_grad),
            jnp.concatenate([value_heads, value_heads], -1),
            preferred_element_type=jnp.float32,
        )
        + jnp.transpose(denominator_grad, (1, 2, 0))[..., None]
    )
    inner_grad = (jnp.where(causal, kernel_grad * (1.0 + qk_inner), 0.0) / 4.0).astype(
        jnp.bfloat16
    )
    query_grad = joined(
        jnp.einsum(
            "gqts,sgf->tgqf",
            inner_grad,
            two_terms(key_features),
            preferred_element_type=jnp.float32,
        )
    )
    key_grad = joined(
        jnp.einsum(
            "gqts,tgqf->sgf",
            inner_grad,
            two_terms(query_features),
            preferred_element_type=jnp.float32,
        )
    )
    query_square_grad = (
        jnp.einsum("tgqe,gke->tgqk", numerator_grad, past_square_v, precision=exact_mode)
        + denominator_grad[..., None] * past_square_k[None, :, None, :]
    ) / 32.0
    query_grad = (
        query_grad
        + (
            jnp.einsum("tgqe,gfe->tgqf", numerator_grad, past_linear_v, precision=exact_mode)
            + denominator_grad[..., None] * past_linear_k[None, :, None, :]
        )
        / 4.0
        + square_grad(query_square_grad, query_features)
    )
    own_back_square = jnp.einsum(
        "tgqk,tgqe->gke", query_square, numerator_grad, precision=exact_mode
    )
    own_back_linear = jnp.einsum(
        "tgqf,tgqe->gfe", query_features, numerator_grad, precision=exact_mode
    )
    own_den_square = jnp.einsum(
        "tgqk,tgq->gk", query_square, denominator_grad, precision=exact_mode
    )
    own_den_linear = jnp.einsum(
        "tgqf,tgq->gf", query_features, denominator_grad, precision=exact_mode
    )
    packed_back = pack(
        own_back_square,
        own_back_linear,
        own_den_square,
        own_den_linear,
        jnp.zeros((kv_groups, HEAD_DIM), jnp.float32),
    )
    later = sum_from(packed_back, -1)
    loss_row = sum_heads(jnp.full((8, HEAD_DIM), squared, jnp.float32))
    later_square, later_linear, later_den_square, later_den_linear, _ = unpack(
        later, kv_groups, feature_count
    )
    key_square_grad = (
        jnp.einsum("gke,sge->sgk", later_square, value_float, precision=exact_mode)
        + later_den_square[None]
    ) / 32.0
    key_grad = (
        key_grad
        + (
            jnp.einsum("gfe,sge->sgf", later_linear, value_float, precision=exact_mode)
            + later_den_linear[None]
        )
        / 4.0
        + square_grad(key_square_grad, key_features)
    )
    own_grad = jnp.einsum(
        "tgqe,tgqf->gef", query_heads.astype(jnp.float32), query_grad, precision=exact_mode
    ) + jnp.einsum("tge,tgf->gef", key_heads.astype(jnp.float32), key_grad, precision=exact_mode)
    packed_grad = jnp.concatenate([own_grad.reshape(-1, HEAD_DIM), loss_row], 0)
    summed, _ = exchange(packed_grad, no_row, "all", 0)
    feature_grad = summed[:-8].reshape(own_grad.shape)
    loss_value = summed[-8, 0] / (total_rows * D)
    return (student_out, loss_value, feature_grad)


FEATURE_PAIRS = 153
PAIR_ROWS = 160
CHUNKS = 4


def pair_tables():
    j = np.arange(2 * HEAD_DIM)
    valid = j < FEATURE_PAIRS
    first = j % 17
    second = (first + j // 17) % 17
    select = np.zeros((2, 2 * HEAD_DIM, HEAD_DIM), np.float32)
    constant = np.zeros((2, 2 * HEAD_DIM), np.float32)
    for side, member in enumerate((first, second)):
        for row in np.nonzero(valid)[0]:
            if member[row] < 16:
                select[side, row, member[row]] = 1.0
            else:
                constant[side, row] = 1.0
    is_one = (first == 16).astype(int) + (second == 16).astype(int)
    coef = np.where(is_one == 2, 1.0, np.where(is_one == 1, 0.25, np.where(first == second, 1 / 32, 1 / 16)))
    coef = np.where(valid, coef, 0.0)
    bits = np.concatenate([select[0], select[1], np.eye(HEAD_DIM)], 0)
    rows = np.zeros((8, 2 * HEAD_DIM), np.float32)
    rows[0], rows[1], rows[2] = constant[0], constant[1], coef
    columns = np.zeros((2 * HEAD_DIM, HEAD_DIM), np.float32)
    columns[:, 0], columns[:, 1], columns[:, 2] = constant[0], constant[1], coef
    return bits, rows, columns


def mm(a, b):
    return lax.dot_general(a, b, (((1,), (0,)), ((), ())), preferred_element_type=jnp.float32)


def mm_t(a, b):
    return lax.dot_general(a, b, (((1,), (1,)), ((), ())), preferred_element_type=jnp.float32)


def split_terms(x):
    high = x.astype(jnp.bfloat16)
    return high, (x - high.astype(jnp.float32)).astype(jnp.bfloat16)


def fused_kernel(
    queries_in, keys_in, values_in, map_ref, proj_ref, teacher_ref, bits_ref, rows_ref, columns_ref,
    student_ref, grad_ref, loss_ref,
    proj_buf, heads_buf, window, own_sum, first_factor, second_factor, pairs_t, queries_t, slope, lin, den_inv,
    d_student, acc, queries_ref, teacher_buf, keys_ext, values_ext, ones_values, wide_map, wide_map_t, kernel_map,
    past_high, past_low, key_features, key_factor_a, key_factor_b, keys_t,
    state_own, state_x, state_low, state_up,
    send_n, recv_n, send_d, recv_d, send_a, recv_a, send_b, recv_b,
    cross, grad_a, grad_b, back, back_own, back_x, back_sum, back_later, back_in, final_own, final_in, loss_acc, loss_own, loss_in,
    ring_send, ring_recv, own_sem, input_sem, teacher_sem, teacher_send, teacher_recv, student_sem, student_send,
    student_recv, part_send, part_recv, rim_send, rim_recv, state_x_send, state_x_recv,
    state_up_send, state_up_recv, side_send, side_recv, near_send, near_recv, far_send, far_recv,
    n_send, n_recv, d_send, d_recv, a_send, a_recv, b_send, b_recv,
    back_x_send, back_x_recv, back_send, back_recv, final_send, final_recv, loss_send, loss_recv,
):
    f32, bf16 = jnp.float32, jnp.bfloat16
    mesh_ids = pl.DeviceIdType.MESH
    ctx_count = 8
    tokens = queries_in.shape[0]
    half = tokens // 2
    width = proj_buf.shape[2]
    E = HEAD_DIM
    c = lax.axis_index("ctx")
    h = lax.axis_index("head")
    z = c // 2
    x = c % 2
    side = c + 1 - 2 * x
    columns_here = x * (proj_ref.shape[1] // 2)
    columns_there = (1 - x) * (proj_ref.shape[1] // 2)

    near = h + 1 - 2 * (h % 2)
    far = (h + 2) % 4
    diagonal = 3 - h

    def remote(src, dst, send, recv, ctx, head):
        return pltpu.make_async_remote_copy(
            src_ref=src, dst_ref=dst, send_sem=send, recv_sem=recv, device_id=(ctx, head), device_id_type=mesh_ids
        )

    inputs = [
        pltpu.make_async_copy(keys_in, keys_ext.at[pl.ds(WIN, tokens)], input_sem.at[0]),
        pltpu.make_async_copy(values_in, values_ext.at[pl.ds(WIN, tokens)], input_sem.at[1]),
        pltpu.make_async_copy(queries_in, queries_ref, input_sem.at[2]),
    ]
    barrier = pltpu.get_barrier_semaphore()
    for d in range(1, ctx_count):
        pl.semaphore_signal(barrier, inc=1, device_id=((c + d) % ctx_count, h), device_id_type=mesh_ids)
    for d in range(1, 4):
        pl.semaphore_signal(barrier, inc=1, device_id=(c, (h + d) % 4), device_id_type=mesh_ids)
    for copy in inputs:
        copy.start()
    pl.semaphore_wait(barrier, ctx_count + 2)

    def plane_rows(plane, q):
        return pl.ds(pl.multiple_of(plane * 2 * tokens + q * half, half), half)

    def chunk_columns(start, j):
        return pl.ds(pl.multiple_of(start + j * width, width), width)

    def part_copy(j, d, ctx):
        place = proj_buf.at[j, pl.ds(pl.multiple_of(ctx * tokens + d * half, half), half)]
        src = proj_ref.at[pl.ds(d * half, half), chunk_columns(columns_there, j)]
        return remote(src, place, part_send.at[j, d], part_recv.at[j, d], side, h)

    def target(d):
        return lax.rem(c + 2, ctx_count) if d == 0 else lax.rem(c + ctx_count - 2, ctx_count)

    def has_target(d):
        return z < 3 if d == 0 else z > 0

    def has_owner(d, k):
        return z >= k if d == 0 else z + k <= 3

    def hop(d, j, k, q):
        place = proj_buf.at[j, plane_rows(jnp.clip(z - k if d == 0 else z + k, 0, 3), q)]
        return remote(place, place, ring_send.at[d, j, k * 4 + q], ring_recv.at[d, j, k * 4 + q], target(d), h)

    def first_hop(d, j, q, m):
        place = proj_buf.at[j, plane_rows(z, q)]
        src = proj_ref.at[pl.ds(m * half, half), chunk_columns(columns_here, j)] if m < 2 else place
        return remote(src, place, ring_send.at[d, j, q], ring_recv.at[d, j, q], target(d), h)

    def arrival(d, j, k, q):
        plane = jnp.clip(z - 1 - k if d == 0 else z + 1 + k, 0, 3)
        place = proj_buf.at[j, plane_rows(plane, q)]
        return remote(place, place, ring_send.at[d, j, k * 4 + q], ring_recv.at[d, j, k * 4 + q], target(d), h)

    def quarter(m):
        return lax.rem(2 * x + m, 4)

    def start_first(j, m):
        if m >= 2:
            part_copy(j, m - 2, side).wait_recv()
        for d in (0, 1):

            @pl.when(has_target(d))
            def _():
                first_hop(d, j, quarter(m), m).start()

    def service(j, k, m):
        for d in (0, 1):

            @pl.when(has_owner(d, k))
            def _():
                arrival(d, j, k - 1, quarter(m)).wait_recv()

            @pl.when(has_owner(d, k) & has_target(d))
            def _():
                hop(d, j, k, quarter(m)).start()

    def last_arrival(j, m):
        for d in (0, 1):

            @pl.when(has_owner(d, 3))
            def _():
                arrival(d, j, 2, quarter(m)).wait_recv()

    for s, (src, dst) in enumerate(((keys_in, keys_ext), (values_in, values_ext))):

        @pl.when(c < ctx_count - 1)
        def _():
            remote(
                src.at[pl.ds(tokens - WIN, WIN)], dst.at[pl.ds(0, WIN)], rim_send.at[s], rim_recv.at[s],
                lax.rem(c + 1, ctx_count), h,
            ).start()

        @pl.when(c == 0)
        def _():
            dst[pl.ds(0, WIN), :] = jnp.zeros((WIN, E), bf16)

        dst[pl.ds(WIN + tokens, WIN), :] = jnp.zeros((WIN, E), bf16)

    for j in (0, 1):
        for m in (0, 1):
            start_first(j, m)
            part_copy(j, m, c).start()
    teacher_copy = pltpu.make_async_copy(
        teacher_ref.at[:, pl.ds(pl.multiple_of(columns_here, width), CHUNKS * width)], teacher_buf.at[x], teacher_sem.at[0]
    )
    teacher_copy.start()

    def teacher_part(ctx_half):
        return remote(
            teacher_ref.at[:, pl.ds(pl.multiple_of(columns_there, width), CHUNKS * width)],
            teacher_buf.at[ctx_half], teacher_send.at[0], teacher_recv.at[0], side, h,
        )

    def own_copy(j):
        return pltpu.make_async_copy(
            proj_ref.at[:, chunk_columns(columns_here, j)],
            proj_buf.at[j, pl.ds(pl.multiple_of(c * tokens, tokens), tokens)],
            own_sem.at[j],
        )

    for j in range(CHUNKS):
        own_copy(j).start()

    eye = bits_ref[pl.ds(4 * E, E), :]
    map_rows = jnp.concatenate([map_ref[...], jnp.zeros((E - map_ref.shape[0], E), bf16)], 0)
    map_wide = mm_t(eye, map_rows).astype(bf16)
    for s in range(2):
        select = bits_ref[pl.ds(s * 2 * E, 2 * E), :]
        wide_map[s] = mm_t(map_wide, select).astype(bf16)
        wide_map_t[s] = mm_t(select, map_wide).astype(bf16)
    inputs[0].wait()
    inputs[1].wait()
    keys = keys_ext[pl.ds(WIN, tokens), :]
    features = mm(keys, map_wide)
    feature_high, feature_low = split_terms(features)
    key_features[0] = feature_high
    key_features[1] = feature_low
    inner = (mm_t(map_wide, feature_high) + mm_t(map_wide, feature_low)) * 0.25
    inner_high, inner_low = split_terms(inner)
    kernel_map[pl.ds(0, E), :] = inner_high
    kernel_map[pl.ds(E, E), :] = inner_low
    keys_t[...] = mm_t(eye, keys).astype(bf16)
    key_a = mm(keys, wide_map[0]) + rows_ref[pl.ds(0, 1), :]
    key_b = mm(keys, wide_map[1]) + rows_ref[pl.ds(1, 1), :]
    key_factor_a[...] = (key_a * rows_ref[pl.ds(2, 1), :]).astype(bf16)
    key_factor_b[...] = (key_b * rows_ref[pl.ds(2, 1), :]).astype(bf16)
    ones_values[:, pl.ds(0, E)] = values_ext[pl.ds(WIN, tokens), :]
    ones_values[:, pl.ds(E, E)] = jnp.ones((tokens, E), bf16)
    key_a_t = mm_t(wide_map_t[0], keys) + columns_ref[:, 0:1]
    key_b_t = mm_t(wide_map_t[1], keys) + columns_ref[:, 1:2]
    key_high, key_low = split_terms(key_a_t * key_b_t * columns_ref[:, 2:3])
    state = mm(key_high, ones_values[...]) + mm(key_low, ones_values[...])

    def store_state(ref, value, den_row):
        ref[pl.ds(0, PAIR_ROWS), :] = value[:PAIR_ROWS]
        ref[pl.ds(PAIR_ROWS, 8), :] = den_row[:, :E]
        ref[pl.ds(PAIR_ROWS + 8, 8), :] = den_row[:, E:]

    store_state(state_own, state[:, :E], jnp.transpose(state[:, E:])[:8])
    state_x_copy = remote(state_own, state_x, state_x_send.at[0], state_x_recv.at[0], side, h)
    state_x_copy.start()
    for m in (2, 3):
        start_first(0, m)
    for j in (2, 3):
        for d in (0, 1):
            part_copy(j, d, c).start()
    teacher_part(x).start()
    inputs[2].wait()

    def state_up_copy():
        return remote(state_up, state_low, state_up_send.at[0], state_up_recv.at[0], lax.rem(c + 2, ctx_count), h)

    def chain_step(level):
        if level == 0:
            state_x_copy.wait_recv()

            @pl.when(z == 0)
            def _():
                state_low[...] = jnp.zeros_like(state_low)

        else:

            @pl.when(z == level)
            def _():
                state_up_copy().wait_recv()

        if level < 3:

            @pl.when(z == level)
            def _():
                state_up[...] = state_low[...] + state_own[...] + state_x[...]
                state_up_copy().start()

    for s in range(2):

        @pl.when(c > 0)
        def _():
            dst = (keys_ext, values_ext)[s]
            remote(
                dst.at[pl.ds(0, WIN)], dst.at[pl.ds(0, WIN)], rim_send.at[s], rim_recv.at[s], c, h
            ).wait_recv()

    def query_tile(i, hp):
        token = pl.multiple_of(i * E, E)
        both = queries_ref[pl.ds(token, E), pl.ds(pl.multiple_of(hp * 2 * E, 2 * E), 2 * E)]
        return jnp.concatenate([both[:, :E], both[:, E:]], 0)

    def window_rows(hp):
        return pl.ds(pl.multiple_of((hp % 2) * 2 * E, 2 * E), 2 * E)

    def window_columns(hp):
        return pl.ds(pl.multiple_of((hp // 2) * E, E), E)

    for i in range(4):
        reach = (i + 1) * E

        def local_tile(hp, carry):
            tile = i * 4 + hp
            q = query_tile(i, hp)
            u = mm(jnp.concatenate([q, q], 1), kernel_map[:, pl.ds(0, reach)])
            row = lax.broadcasted_iota(jnp.int32, (2 * E, reach), 0) % E + i * E
            causal = row >= lax.broadcasted_iota(jnp.int32, (2 * E, reach), 1)
            kernel = jnp.where(causal, 1.0 + u + 0.5 * u * u, 0.0).astype(bf16)
            slope[tile, :, pl.ds(0, reach)] = jnp.where(causal, 0.25 + 0.25 * u, 0.0).astype(bf16)
            both = mm(kernel, ones_values[pl.ds(0, reach), :])
            lin[tile] = both[:, :E]
            den_inv[tile] = both[:, E:]
            scores = mm_t(q, keys_ext[pl.ds(i * E, 2 * E), :]) / math.sqrt(HEAD_DIM)
            token = lax.broadcasted_iota(jnp.int32, (2 * E, 2 * E), 0) % E
            place = lax.broadcasted_iota(jnp.int32, (2 * E, 2 * E), 1)
            distance = token + WIN - place
            allowed = (distance >= 0) & (distance < WIN) & (c * tokens + i * E + place - WIN >= 0)
            scores = jnp.where(allowed, scores, -jnp.inf)
            top = jnp.max(scores, axis=-1, keepdims=True)
            weights = jnp.where(allowed, jnp.exp(scores - top), 0.0)
            weights = (weights / jnp.sum(weights, axis=-1, keepdims=True)).astype(bf16)
            window[i, window_rows(hp), window_columns(hp)] = mm(weights, values_ext[pl.ds(i * E, 2 * E), :])
            first_factor[tile] = (mm(q, wide_map[0]) + rows_ref[pl.ds(0, 1), :]).astype(bf16)
            second_factor[tile] = (mm(q, wide_map[1]) + rows_ref[pl.ds(1, 1), :]).astype(bf16)
            pair_a = mm_t(wide_map_t[0], q) + columns_ref[:, 0:1]
            pair_b = mm_t(wide_map_t[1], q) + columns_ref[:, 1:2]
            pairs_t[tile] = (pair_a * pair_b).astype(bf16)[:PAIR_ROWS]
            queries_t[tile] = mm_t(eye, q).astype(bf16)
            service(i // 2, 1 + i % 2, hp)
            return carry

        lax.fori_loop(0, 4, local_tile, 0)
        chain_step(i)
        if i == 1:
            for m in (2, 3):
                start_first(1, m)

    past = jnp.where(z > 0, state_low[...], 0.0) + jnp.where(x == 1, state_x[...], 0.0)
    past_rows = jnp.concatenate([past[PAIR_ROWS : PAIR_ROWS + 8], past[PAIR_ROWS + 8 :]], 1)
    past_den = jnp.transpose(jnp.broadcast_to(past_rows[:1], (E, 2 * E)))
    past_values = jnp.concatenate([past[:PAIR_ROWS], jnp.zeros((2 * E - PAIR_ROWS, E), f32)], 0)
    high, low = split_terms(jnp.concatenate([past_values, past_den], 1))
    past_high[...] = high
    past_low[...] = low

    def head_piece(i, ctx_half, head):
        return heads_buf.at[ctx_half * 4 + head, pl.ds(pl.multiple_of(i * E, E), E)]

    def side_copy(i, ctx_half):
        piece = head_piece(i, ctx_half, h)
        return remote(piece, piece, side_send.at[i], side_recv.at[i], side, h)

    def near_copy(i, s, head):
        ctx_half = x if s % 2 == 0 else 1 - x
        piece = head_piece(i, ctx_half, head)
        return remote(piece, piece, near_send.at[s, i], near_recv.at[s, i], c, near)

    def far_copy(i, s, head):
        ctx_half = x if s == 0 else 1 - x
        piece = head_piece(i, ctx_half, head)
        return remote(piece, piece, far_send.at[s, i], far_recv.at[s, i], c, far)

    def past_tiles(i, carry):
        def past_tile(hp, carry):
            tile = i * 4 + hp
            q = query_tile(i, hp)
            pair = (mm(q, wide_map[0]) + rows_ref[pl.ds(0, 1), :]) * (mm(q, wide_map[1]) + rows_ref[pl.ds(1, 1), :])
            pair_high, pair_low = split_terms(pair)
            both = mm(pair_high, past_high[...]) + mm(pair_low, past_high[...]) + mm(pair_high, past_low[...])
            den = den_inv[tile] + both[:, E:]
            value = (lin[tile] + both[:, :E]) / den
            lin[tile] = value
            den_inv[tile] = 1.0 / den
            out = (value + window[i, window_rows(hp), window_columns(hp)]).astype(bf16)
            heads_buf[
                x * 4 + h, pl.ds(pl.multiple_of(i * E, E), E), pl.ds(pl.multiple_of(hp * 2 * E, 2 * E), 2 * E)
            ] = jnp.concatenate([out[:E], out[E:]], 1)
            return carry

        lax.fori_loop(0, 4, past_tile, 0)
        side_copy(i, x).start()
        far_copy(i, 0, h).start()
        near_copy(i, 0, h).start()
        return carry

    lax.fori_loop(0, 4, past_tiles, 0)
    for m in range(4):
        start_first(2, m)

    def relay_side(i, carry):
        service(2, 1, i)
        side_copy(i, 1 - x).wait_recv()
        far_copy(i, 1, h).start()
        near_copy(i, 1, h).start()
        return carry

    lax.fori_loop(0, 4, relay_side, 0)

    def relay_far(i, carry):
        service(2, 2, i)
        far_copy(i, 0, far).wait_recv()
        near_copy(i, 2, far).start()
        return carry

    lax.fori_loop(0, 4, relay_far, 0)

    for m in range(4):
        start_first(3, m)

    def relay_last(i, carry):
        service(3, 1, i)
        far_copy(i, 1, far).wait_recv()
        near_copy(i, 3, far).start()
        return carry

    lax.fori_loop(0, 4, relay_last, 0)
    teacher_copy.wait()
    teacher_part(1 - x).wait_recv()
    for j in range(CHUNKS):
        own_copy(j).wait()
    loss_acc[...] = jnp.zeros_like(loss_acc)
    for i in range(4):
        for s in range(4):
            near_copy(i, s, near if s < 2 else diagonal).wait_recv()
    def student_copy(j):
        return pltpu.make_async_copy(
            teacher_buf.at[x, :, chunk_columns(0, j)], student_ref.at[:, chunk_columns(columns_here, j)], student_sem.at[j]
        )

    def student_part(j, start):
        return remote(
            teacher_buf.at[1 - x, :, chunk_columns(0, j)], student_ref.at[:, chunk_columns(start, j)],
            student_send.at[j], student_recv.at[j], side, h,
        )

    def finish_columns(j, ctx_half, product):
        student = product.astype(bf16)
        columns = chunk_columns(0, j)
        residual = student.astype(f32) - teacher_buf[ctx_half, :, columns].astype(f32)
        teacher_buf[ctx_half, :, columns] = student
        loss_acc[...] += jnp.sum((residual * residual).reshape(tokens // 8, 8, width), axis=0)
        d_student[j, ctx_half] = (residual * (2.0 / (tokens * ctx_count))).astype(bf16)

    def finish_both(j, products):
        for product, ctx_half in zip(products, (x, 1 - x)):
            finish_columns(j, ctx_half, product)
        student_copy(j).start()

    def plane_product(ctx_half, plane, j):
        rows = pl.ds(pl.multiple_of(plane * 2 * tokens, 2 * tokens), 2 * tokens)
        return mm(heads_buf[ctx_half * 4 + plane], proj_buf[j, rows, :])

    def first_columns(j, carry):
        for m in range(4):
            last_arrival(j, m)
        products = []
        for ctx_half in (x, 1 - x):
            product = plane_product(ctx_half, 0, j)
            for plane in range(1, 4):
                product += plane_product(ctx_half, plane, j)
            products.append(product)
        finish_both(j, products)
        student_part(j, columns_here).start()
        for m in range(2):

            @pl.when(j < 2)
            def _():
                service(3, 2, j * 2 + m)

        return carry

    lax.fori_loop(0, 3, first_columns, 0)
    last_plane = jnp.where(z >= 2, 0, 3)

    for t, ctx_half in enumerate((x, 1 - x)):
        product = plane_product(ctx_half, (last_plane + 1) % 4, 3)
        for b in (2, 3):
            product += plane_product(ctx_half, (last_plane + b) % 4, 3)
        acc[t] = product

    def block_sum(chunks, ctx_half, head, p):
        rows = pl.ds(pl.multiple_of((head * 4 + p) * width, width), width)
        total = mm_t(d_student[chunks[0], ctx_half], proj_buf[chunks[0], rows, :])
        for j in chunks[1:]:
            total += mm_t(d_student[j, ctx_half], proj_buf[j, rows, :])
        return total

    for s, (head, p) in enumerate(((diagonal, 0), (diagonal, 2), (far, 0), (far, 2))):
        window[s] = block_sum((0, 1, 2), 1 - x, head, p)

    for m in range(4):
        last_arrival(3, m)
        products = []
        for t, ctx_half in enumerate((x, 1 - x)):
            left = heads_buf[ctx_half * 4 + last_plane, :, pl.ds(pl.multiple_of(quarter(m) * half, half), half)]
            products.append(acc[t] + mm(left, proj_buf[3, plane_rows(last_plane, quarter(m)), :]))
            if m < 3:
                acc[t] = products[t]
        if m == 3:
            finish_both(3, products)

    def copy_n(s):
        return remote(send_n.at[s], recv_n.at[s], n_send.at[s], n_recv.at[s], c, near)

    def copy_d(p):
        ctx, head = (side, h) if p < 2 else (c, far)
        return remote(send_d.at[p], recv_d.at[p], d_send.at[p], d_recv.at[p], ctx, head)

    def copy_a(p):
        return remote(send_a.at[p], recv_a.at[p], a_send.at[p], a_recv.at[p], side, h)

    def copy_b(p):
        return remote(send_b.at[p], recv_b.at[p], b_send.at[p], b_recv.at[p], c, far)

    kinds = {"d": (1, 1), "a": (1, 0), "b": (0, 1), "own": (0, 0)}

    def slot(kind, p):
        return (kinds[kind][0] * 2 + kinds[kind][1]) * 4 + p

    def give(kind, p):
        other, distant = kinds[kind]
        ctx_half = 1 - x if other else x
        head = diagonal if distant else near
        if kind == "d" and p % 2 == 0:
            total = window[p // 2] + block_sum((3,), ctx_half, head, p)
        else:
            total = block_sum(range(CHUNKS), ctx_half, head, p)
        send_n[slot(kind, p)] = total.astype(bf16)
        copy_n(slot(kind, p)).start()

    def take(kind, p):
        other, distant = kinds[kind]
        ctx_half = 1 - x if other else x
        head = far if distant else h
        if kind == "d" and p % 2 == 0:
            total = window[2 + p // 2] + block_sum((3,), ctx_half, head, p)
        else:
            total = block_sum(range(CHUNKS), ctx_half, head, p)
        copy_n(slot(kind, p)).wait_recv()
        return total + recv_n[slot(kind, p)].astype(f32)

    def send_corner(p):
        send_d[p] = take("d", p).astype(bf16)
        copy_d(p).start()

    def send_side(kind, p, corner):
        total = take(kind, p)
        if corner:
            copy_d(p).wait_recv()
            total += recv_d[p].astype(f32)
        if kind == "a":
            send_a[p] = total.astype(bf16)
            copy_a(p).start()
        else:
            send_b[p] = total.astype(bf16)
            copy_b(p).start()

    give("d", 0)
    give("d", 2)
    send_corner(0)
    send_corner(2)
    give("d", 1)
    give("d", 3)
    send_corner(1)
    send_corner(3)
    for a, b in ((0, 2), (1, 0), (2, 1), (3, 3)):
        give("a", a)
        give("b", b)
        send_side("a", a, a >= 2)
        send_side("b", b, b < 2)
    for p in range(4):
        give("own", p)
    for p in range(4):
        own_sum[p] = take("own", p)

    loss_own[...] = loss_acc[:, :E] + loss_acc[:, E:]

    def loss_copy(d, source):
        return remote(loss_own, loss_in.at[source], loss_send.at[d], loss_recv.at[source], c, (h + d) % 4)

    for d in range(1, 4):
        loss_copy(d, h).start()

    cross[...] = jnp.zeros_like(cross)
    grad_a[...] = jnp.zeros_like(grad_a)
    grad_b[...] = jnp.zeros_like(grad_b)
    back[...] = jnp.zeros_like(back)

    def grad_piece(p, carry):
        copy_a(p).wait_recv()
        copy_b(p).wait_recv()
        for i in range(4):
            reach = (i + 1) * E
            tile = i * 4 + p
            rows = pl.ds(i * E, E)
            g = own_sum[p, rows, :] + recv_a[p, rows, :].astype(f32) + recv_b[p, rows, :].astype(f32)
            g = jnp.concatenate([g[:, :E], g[:, E:]], 0)
            inverse = den_inv[tile]
            upper = (g * inverse).astype(bf16)
            lower = -jnp.sum(upper.astype(f32) * lin[tile], axis=-1, keepdims=True)
            lower = jnp.broadcast_to(lower, (2 * E, E))
            lower_high = lower.astype(bf16).astype(f32)
            lane = lax.broadcasted_iota(jnp.int32, (2 * E, E), 1)
            lower = (jnp.where(lane < E // 2, lower_high, lower - lower_high) * (2.0 / E)).astype(bf16)
            wide = jnp.concatenate([upper, lower], 1)
            weight = mm_t(wide, ones_values[pl.ds(0, reach), :]) * slope[tile, :, pl.ds(0, reach)].astype(f32)
            cross[:, pl.ds(0, reach)] += mm(queries_t[tile], weight.astype(bf16))
            pair_grad = mm_t(wide, past_high[...]) + mm_t(wide, past_low[...])
            grad_a[...] += mm(queries_t[tile], (pair_grad * second_factor[tile].astype(f32)).astype(bf16))
            grad_b[...] += mm(queries_t[tile], (pair_grad * first_factor[tile].astype(f32)).astype(bf16))
            back[...] += mm(pairs_t[tile], wide)
        return carry

    lax.fori_loop(0, 4, grad_piece, 0)

    back_den = jnp.transpose(
        jnp.concatenate([back[:, pl.ds(E, E)], jnp.zeros((2 * E - PAIR_ROWS, E), f32)], 0)
    )
    back_den = (back_den[:8] + back_den[E // 2 : E // 2 + 8]) * (E // 2)
    store_state(back_own, back[:, pl.ds(0, E)], back_den)
    back_x_copy = remote(back_own, back_x, back_x_send.at[0], back_x_recv.at[0], side, h)
    back_x_copy.start()

    def back_copy(level):
        return remote(back_sum, back_in.at[z], back_send.at[level], back_recv.at[z], 2 * level + x, h)

    def back_arrival(level):
        return remote(back_sum, back_in.at[level], back_send.at[level], back_recv.at[level], c, h)

    cross_high, cross_low = split_terms(cross[...])
    grad = mm(cross_high, key_features[0]) + mm(cross_high, key_features[1]) + mm(cross_low, key_features[0])
    keys = keys_ext[pl.ds(WIN, tokens), :]
    mixed = jnp.transpose(mm(cross_high, keys) + mm(cross_low, keys))
    mixed_high, mixed_low = split_terms(mixed)
    map_rows = jnp.concatenate([map_ref[...], jnp.zeros((E - map_ref.shape[0], E), bf16)], 0)
    map_wide = mm_t(bits_ref[pl.ds(4 * E, E), :], map_rows).astype(bf16)
    grad += mm(mixed_high, map_wide) + mm(mixed_low, map_wide)

    center = mm(jnp.ones((8, tokens), bf16), values_ext[pl.ds(WIN, tokens), :])
    center = (center / tokens).astype(bf16)
    back_x_copy.wait_recv()
    plane = back_own[...] + back_x[...]
    plane_values = plane[:PAIR_ROWS].astype(bf16)
    lost = (plane[:PAIR_ROWS] - plane_values.astype(f32)).astype(bf16)
    lost = jnp.concatenate([lost, jnp.zeros((2 * E - PAIR_ROWS, E), bf16)], 0)
    moved = mm_t(center, lost)
    plane_den = plane[PAIR_ROWS:] + jnp.concatenate([moved[:, :E], moved[:, E:]], 0)
    den_high, den_low = split_terms(plane_den)
    back_sum[pl.ds(0, PAIR_ROWS), :] = plane_values
    back_sum[pl.ds(PAIR_ROWS, 16), :] = den_high
    back_sum[pl.ds(PAIR_ROWS + 16, 16), :] = den_low
    for level in range(3):

        @pl.when(level < z)
        def _():
            back_copy(level).start()

    student_part(3, columns_here).start()
    back_later[...] = jnp.where(x == 0, back_x[...], 0.0)
    for level in range(1, 4):

        @pl.when(level > z)
        def _():
            back_arrival(level).wait_recv()
            arrived = back_in[level].astype(f32)
            back_later[...] += arrived[: PAIR_ROWS + 16]
            back_later[pl.ds(PAIR_ROWS, 16), :] += arrived[PAIR_ROWS + 16 :]

    later_values = jnp.concatenate([back_later[pl.ds(0, PAIR_ROWS), :], jnp.zeros((2 * E - PAIR_ROWS, E), f32)], 0)
    later_high, later_low = split_terms(later_values)
    pair_grad = mm_t(values_ext[pl.ds(WIN, tokens), :], later_high)
    pair_grad += mm_t(values_ext[pl.ds(WIN, tokens), :], later_low)
    pair_grad += jnp.concatenate(
        [back_later[pl.ds(PAIR_ROWS, 1), :], back_later[pl.ds(PAIR_ROWS + 8, 1), :]], 1
    )
    total_a = grad_a[...] + mm(keys_t[...], (pair_grad * key_factor_b[...].astype(f32)).astype(bf16))
    total_b = grad_b[...] + mm(keys_t[...], (pair_grad * key_factor_a[...].astype(f32)).astype(bf16))
    for s, total in enumerate((total_a, total_b)):
        total_high, total_low = split_terms(total)
        select = bits_ref[pl.ds(s * 2 * E, 2 * E), :]
        grad += mm(total_high, select) + mm(total_low, select)
    final_own[pl.ds(0, 16), :] = jnp.transpose(grad)[:16]
    loss_sum = loss_own[...]
    for d in range(1, 4):
        loss_copy(d, (h + d) % 4).wait_recv()
        loss_sum += loss_in[(h + d) % 4]
    final_own[pl.ds(16, 8), :] = loss_sum

    def final_copy(d, source):
        return remote(final_own, final_in.at[source], final_send.at[d], final_recv.at[source], (c + d) % ctx_count, h)

    for d in range(1, ctx_count):
        final_copy(d, c).start()
    final_in[c] = final_own[...]
    for d in range(1, ctx_count):
        final_copy(d, (c + d) % ctx_count).wait_recv()
    final = final_in[0]
    for s in range(1, ctx_count):
        final += final_in[s]
    grad_ref[...] = final[:16]
    loss_ref[0, 0] = jnp.sum(final[16:]) / (tokens * ctx_count * D)

    for j in range(CHUNKS):
        student_copy(j).wait()
        student_part(j, columns_here).wait_send()
        student_part(j, columns_there).wait_recv()
        for d in (0, 1):
            part_copy(j, d, c).wait_send()
            for m in range(4):
                for k in range(3):

                    @pl.when(has_target(d) & has_owner(d, k))
                    def _():
                        hop(d, j, k, quarter(m)).wait_send()

    teacher_part(x).wait_send()
    for s in range(2):

        @pl.when(c < ctx_count - 1)
        def _():
            dst = (keys_ext, values_ext)[s]
            src = (keys_in, values_in)[s]
            remote(
                src.at[pl.ds(tokens - WIN, WIN)], dst.at[pl.ds(0, WIN)], rim_send.at[s], rim_recv.at[s],
                lax.rem(c + 1, ctx_count), h,
            ).wait_send()

    state_x_copy.wait_send()

    @pl.when(z < 3)
    def _():
        state_up_copy().wait_send()

    back_x_copy.wait_send()
    for level in range(3):

        @pl.when(level < z)
        def _():
            back_copy(level).wait_send()

    for d in range(1, 4):
        loss_copy(d, h).wait_send()
    for i in range(4):
        side_copy(i, x).wait_send()
        for s in range(2):
            far_copy(i, s, h).wait_send()
        for s in range(4):
            near_copy(i, s, h if s < 2 else far).wait_send()
    for p in range(4):
        copy_d(p).wait_send()
        copy_a(p).wait_send()
        copy_b(p).wait_send()
    for s in range(16):
        copy_n(s).wait_send()
    for d in range(1, ctx_count):
        final_copy(d, c).wait_send()


def deliver_kernel(student_ref, grad_ref, loss_ref, student_out, grad_out, loss_out, buffer, grad_buffer, sem, out_sem):
    part = student_ref.shape[0] // 4
    moves = [(ref.at[pl.ds(s * part, part)], buffer.at[pl.ds(s * part, part)], student_out.at[pl.ds(s * part, part)])
             for s, ref in enumerate([student_ref] * 4)]
    moves.append((grad_ref, grad_buffer, grad_out))
    reads = [pltpu.make_async_copy(src, mid, sem.at[s]) for s, (src, mid, dst) in enumerate(moves)]
    writes = [pltpu.make_async_copy(mid, dst, out_sem.at[s]) for s, (src, mid, dst) in enumerate(moves)]
    for copy in reads:
        copy.start()
    loss_out[0, 0] = loss_ref[0, 0]
    for read, write in zip(reads, writes):
        read.wait()
        write.start()
    for copy in writes:
        copy.wait()


def fused_local(queries, keys, values, feature_map, out_proj, teacher):
    tokens = queries.shape[0]
    columns = out_proj.shape[1]
    rows = tokens * 8
    width = columns // 2 // CHUNKS
    E = HEAD_DIM
    bf16, f32 = jnp.bfloat16, jnp.float32
    bits, row_table, column_table = pair_tables()
    vmem = pl.BlockSpec(memory_space=pltpu.VMEM)
    anywhere = pl.BlockSpec(memory_space=pl.ANY)
    smem = pl.BlockSpec(memory_space=pltpu.SMEM)
    dma = pltpu.SemaphoreType.DMA
    state = (PAIR_ROWS + 16, E)
    scratch = [
        ((CHUNKS, rows, width), bf16),
        ((8, tokens, 8 * E), bf16),
        ((4, tokens, width), f32),
        ((4, tokens, width), f32),
        ((16, 2 * E, 2 * E), bf16),
        ((16, 2 * E, 2 * E), bf16),
        ((16, PAIR_ROWS, 2 * E), bf16),
        ((16, E, 2 * E), bf16),
        ((16, 2 * E, tokens), bf16),
        ((16, 2 * E, E), f32),
        ((16, 2 * E, E), f32),
        ((CHUNKS, 2, tokens, width), bf16),
        ((2, tokens, width), f32),
        ((tokens, 8 * E), bf16),
        ((2, tokens, columns // 2), bf16),
        ((tokens + 2 * WIN, E), bf16),
        ((tokens + 2 * WIN, E), bf16),
        ((tokens, 2 * E), bf16),
        ((2, E, 2 * E), bf16),
        ((2, 2 * E, E), bf16),
        ((2 * E, tokens), bf16),
        ((2 * E, 2 * E), bf16),
        ((2 * E, 2 * E), bf16),
        ((2, tokens, E), bf16),
        ((tokens, 2 * E), bf16),
        ((tokens, 2 * E), bf16),
        ((E, tokens), bf16),
        (state, f32),
        (state, f32),
        (state, f32),
        (state, f32),
        ((16, tokens, width), bf16),
        ((16, tokens, width), bf16),
        ((4, tokens, width), bf16),
        ((4, tokens, width), bf16),
        ((4, tokens, width), bf16),
        ((4, tokens, width), bf16),
        ((4, tokens, width), bf16),
        ((4, tokens, width), bf16),
        ((E, tokens), f32),
        ((E, 2 * E), f32),
        ((E, 2 * E), f32),
        ((PAIR_ROWS, 2 * E), f32),
        (state, f32),
        (state, f32),
        ((PAIR_ROWS + 32, E), bf16),
        (state, f32),
        ((4, PAIR_ROWS + 32, E), bf16),
        ((24, E), f32),
        ((8, 24, E), f32),
        ((8, width), f32),
        ((8, E), f32),
        ((4, 8, E), f32),
    ]
    semaphores = [
        (2, CHUNKS, 12), (2, CHUNKS, 12), (CHUNKS,), (3,), (1,), (1,), (1,), (CHUNKS,), (CHUNKS,), (CHUNKS,), (CHUNKS, 2),
        (CHUNKS, 2), (2,), (2,), (1,), (1,), (1,), (1,), (4,), (4,), (4, 4), (4, 4), (2, 4), (2, 4), (16,), (16,), (4,), (4,),
        (4,), (4,), (4,), (4,), (1,), (1,), (4,), (4,), (8,), (8,), (4,), (4,),
    ]
    student, grad, loss = pl.pallas_call(
        fused_kernel,
        out_shape=(
            jax.ShapeDtypeStruct((tokens, columns), bf16),
            jax.ShapeDtypeStruct((feature_map.shape[2], E), f32),
            jax.ShapeDtypeStruct((1, 1), f32),
        ),
        in_specs=[anywhere, anywhere, anywhere, vmem, anywhere, anywhere, vmem, vmem, vmem],
        out_specs=(anywhere, vmem, smem),
        scratch_shapes=[pltpu.VMEM(shape, kind) for shape, kind in scratch] + [dma(shape) for shape in semaphores],
        compiler_params=pltpu.CompilerParams(
            collective_id=0, has_side_effects=True, vmem_limit_bytes=63 * 1024 * 1024
        ),
        cost_estimate=pl.CostEstimate(flops=30_000_000_000, bytes_accessed=40_000_000, transcendentals=2_000_000),
    )(
        queries, keys, values, feature_map[0].T, out_proj, teacher,
        jnp.asarray(bits, bf16), jnp.asarray(row_table, f32), jnp.asarray(column_table, f32),
    )
    student, grad, loss = pl.pallas_call(
        deliver_kernel,
        out_shape=(
            jax.ShapeDtypeStruct(student.shape, bf16),
            jax.ShapeDtypeStruct(grad.shape, f32),
            jax.ShapeDtypeStruct((1, 1), f32),
        ),
        in_specs=[anywhere, anywhere, smem],
        out_specs=(anywhere, anywhere, smem),
        scratch_shapes=[pltpu.VMEM(student.shape, bf16), pltpu.VMEM(grad.shape, f32), dma((5,)), dma((5,))],
        cost_estimate=pl.CostEstimate(flops=0, bytes_accessed=2 * student.size * 2, transcendentals=0),
    )(student, grad, loss)
    return student, loss.reshape(()), grad.T[None]


def fits_fused(mesh):
    return mesh.shape["ctx"] == 8 and mesh.shape["head"] == 4


def solution(mesh):
    return jax.shard_map(
        fused_local if fits_fused(mesh) else local,
        mesh=mesh,
        in_specs=(
            P("ctx", "head"),
            P("ctx", "head"),
            P("ctx", "head"),
            P("head", None, None),
            P("ctx", "head"),
            P("ctx", "head"),
        ),
        out_specs=(P("ctx", "head"), P(), P("head", None, None)),
        check_vma=False,
    )
```
